32 devices in a mesh: dp: 8 (over z, x), tp: 4 (over y, core).
Axes of the slice: x: 2, y: 2, z: 4, core: 2. Of those that a mesh axis runs over, the one named last changes fastest.
Arguments:
- tokens: bfloat16 [4096, 2048], P('dp'), may hold values from -6 to 6
- positions: int32 [4096], P('dp'), may hold values from 0 to 2047, as said below
- norm1_gain: float32 [2048], replicated, may hold values from 0.5 to 1.5
- w_query: bfloat16 [2048, 2048], P(None, 'tp'), may hold values from -0.125 to 0.125
- w_key: bfloat16 [2048, 256], P(None, 'tp'), may hold values from -0.125 to 0.125
- w_value: bfloat16 [2048, 256], P(None, 'tp'), may hold values from -0.125 to 0.125
- w_out: bfloat16 [2048, 2048], P('tp'), may hold values from -0.5 to 0.5
- norm2_gain: float32 [2048], replicated, may hold values from 0.5 to 1.5
- w_gate: bfloat16 [2048, 5632], P(None, 'tp'), may hold values from -0.125 to 0.125
- w_up: bfloat16 [2048, 5632], P(None, 'tp'), may hold values from -0.125 to 0.125
- w_down: bfloat16 [5632, 2048], P('tp'), may hold values from -0.078125 to 0.078125
- cotangent: bfloat16 [4096, 2048], P('dp'), may hold values from -6 to 6
Outputs:
- output: bfloat16 [4096, 2048], P(('dp', 'tp'))
- input_grad: float32 [4096, 2048], P(('dp', 'tp'))
- grad_norm1_gain: float32 [2048], P('dp')
- grad_query: float32 [2048, 2048], P('dp', 'tp')
- grad_key: float32 [2048, 256], P('dp', 'tp')
- grad_value: float32 [2048, 256], P('dp', 'tp')
- grad_out: float32 [2048, 2048], P('tp', 'dp')
- grad_norm2_gain: float32 [2048], P('dp')
- grad_gate: float32 [2048, 5632], P('dp', 'tp')
- grad_up: float32 [2048, 5632], P('dp', 'tp')
- grad_down: float32 [5632, 2048], P('tp', 'dp')
The draws below stay inside these ranges and needn't reach their ends.
Inputs may be any that keep to these rules, and one draw needn't show every extreme that they name: Each packed sequence of 2048 tokens holds whole documents; positions count up by one from 0 within a document, a position of 0 starts a document. Every sequence starts with a document, and documents other than that first one start only within the sequence's last 512 tokens. The first sequence is a single document.
All inputs are finite; a program needn't handle non-finite values.
Results may differ from the reference program's by a relative error of at most 0.015.
Values may be sent and summed in bfloat16 or wider, within the bound.
No kernel may reach another device: no remote copies, remote signals or barrier semaphores. Data moves between devices by JAX's collectives and lax.ppermute only.
A program may use at most 320 MiB of HBM per device.

```python
import jax
import jax.numpy as jnp
from jax import lax

D = 2048
H = 32
KV = 4
HD = 64
FF = 5632
SPAN = 4
TOK_DEV = 512
LENGTH = 2048
TOKENS = 4096


def draw_positions(key, part):
    length = LENGTH
    sequences = TOKENS // length
    spacing = max(TOK_DEV // 4, 2)
    places = jnp.arange(length, dtype=jnp.int32)[None, :]
    chosen = jax.random.randint(key, (sequences, length), 0, spacing) == 0
    in_tail = places >= (SPAN - 1) * TOK_DEV
    ordinal = jnp.arange(sequences, dtype=jnp.int32)[:, None]
    starting = (places == 0) | chosen & in_tail & (ordinal > 0)
    marks = jnp.where(starting, places, 0)
    return (places - lax.cummax(marks, axis=1)).reshape(-1).astype(jnp.int32)


def spiked(values, stream_key, source, target, shards_of, factor):
    def block_of(axis_at):
        return (jnp.arange(values.shape[axis_at]) // (values.shape[axis_at] // shards_of)).reshape((-1,) + (1,) * (values.ndim - 1 - axis_at))

    first = jax.random.permutation(stream_key, shards_of)[block_of(target)]
    other_side = (block_of(target) + shards_of // 2) % shards_of
    return jnp.where((block_of(source) == first) | (block_of(source) == other_side), factor * values, values)


def shard_levels(rng, extent, cuts, smallest, high):
    factor_of = 1.0
    for dim, parts in cuts:
        draws = jax.random.uniform(jax.random.fold_in(jax.random.fold_in(rng, 6), dim), (parts,), jnp.float32, smallest / len(cuts), high / len(cuts))
        factor_of = factor_of * jnp.repeat(jnp.exp(draws), extent[dim] // parts).reshape((-1,) + (1,) * (len(extent) - 1 - dim))
    return factor_of


def bell_draw(own_key, extent, spread, limit, split=(), kind=jnp.bfloat16):
    level = shard_levels(own_key, extent, split, -0.22, 0.18) if split else 1.0
    drawn = jax.random.normal(own_key, extent, jnp.float32) * spread * level
    return jnp.minimum(jnp.maximum(drawn, -limit), limit).astype(kind)


def heavy_noise(rng, extent, spread, most, split, heavy, held_as=jnp.bfloat16):
    values = spread * jax.random.normal(rng, extent, jnp.float32)
    if split:
        values = values * shard_levels(rng, extent, split, -0.22, 0.18)
    return jnp.clip(spiked(values, jax.random.fold_in(rng, 3), *heavy), -most, most).astype(held_as)


def setup_inputs(seed: int = 0) -> dict:
    splits = jax.random.split(jax.random.key(seed), 13)
    return {
        "tokens": bell_draw(splits[0], (TOKENS, D), 1.0, 6.0, ((0, 8),)),
        "positions": draw_positions(jax.random.fold_in(splits[12], 71), 0),
        "norm1_gain": jnp.clip(1.0 + 0.1 * jax.random.normal(splits[2], (D,), jnp.float32), 0.5, 1.5),
        "w_query": bell_draw(splits[3], (D, H * HD), D ** -0.5, 0.125, ((1, 4),)),
        "w_key": bell_draw(splits[4], (D, KV * HD), D ** -0.5, 0.125, ((1, 4),)),
        "w_value": bell_draw(splits[5], (D, KV * HD), D ** -0.5, 0.125, ((1, 4),)),
        "w_out": bell_draw(splits[6], (H * HD, D), (H * HD // 16) ** -0.5, 0.5, ((0, 4),)),
        "norm2_gain": jnp.clip(1.0 + 0.1 * jax.random.normal(splits[7], (D,), jnp.float32), 0.5, 1.5),
        "w_gate": bell_draw(splits[8], (D, FF), D ** -0.5, 0.125, ((1, 4),)),
        "w_up": bell_draw(splits[9], (D, FF), D ** -0.5, 0.125, ((1, 4),)),
        "w_down": bell_draw(splits[10], (FF, D), FF ** -0.5, 0.078125, ((0, 4),)),
        "cotangent": heavy_noise(splits[11], (TOKENS, D), 1.0, 6.0, ((0, 8),), (0, 1, 8, 2.0)),
    }


EPSILON = 1e-05
FAR_BELOW = -1e+30
HIGHEST = lax.Precision.HIGHEST

@jax.custom_vjp
def low(v):
    return lax.optimization_barrier(v.astype(jnp.bfloat16)).astype(jnp.float32)

@jax.custom_vjp
def low_back(v):
    return v

def low_keep(v):
    return (low(v), None)

def low_pass(kept, grad):
    return (grad,)

def back_keep(v):
    return (v, None)

def back_low(kept, grad):
    return (low(grad),)
low.defvjp(low_keep, low_pass)
low_back.defvjp(back_keep, back_low)

def product(left, right):
    return jnp.dot(left, right, precision=HIGHEST)

def angle_tables(positions, head_size):
    halfway = head_size // 2
    frequency = jnp.exp(-jnp.log(10000.0) * (2.0 * jnp.arange(halfway, dtype=jnp.float32) / head_size))
    angles = positions.astype(jnp.float32)[:, None] * frequency[None, :]
    return (jnp.concatenate([jnp.cos(angles), jnp.cos(angles)], -1), jnp.concatenate([jnp.sin(angles), jnp.sin(angles)], -1))

def rotate(values, cosine, sine_table):
    middle_at = values.shape[-1] // 2
    turned = jnp.concatenate([-values[..., middle_at:], values[..., :middle_at]], -1)
    return values * cosine + turned * sine_table

def rms_norm(rows_in, gain):
    return rows_in * lax.rsqrt(lax.optimization_barrier(jnp.mean(rows_in * rows_in, -1, keepdims=True)) + EPSILON) * gain

def layer_forward(rows_in, positions, norm1_gain, w_query, w_key, w_value, w_out, norm2_gain, w_gate, w_up, w_down):
    length = rows_in.shape[0]
    groups = H // KV
    normed_one = low(rms_norm(rows_in, norm1_gain))
    cosine, sine_table = angle_tables(positions, HD)
    queries = low_back(product(normed_one, w_query)).reshape(length, H, HD)
    queries = low(rotate(queries, cosine[:, None, :], sine_table[:, None, :]))
    key_rows = low_back(product(normed_one, w_key)).reshape(length, KV, HD)
    key_rows = low(rotate(key_rows, cosine[:, None, :], sine_table[:, None, :]))
    value_rows = low(low_back(product(normed_one, w_value))).reshape(length, KV, HD)
    places = jnp.arange(length, dtype=jnp.int32)
    begins = places - positions
    allowed = (places[None, :] <= places[:, None]) & (places[None, :] >= begins[:, None])
    grouped = queries.reshape(length, KV, groups, HD).transpose(1, 0, 2, 3)

    def attend(pieces):
        group_queries, group_keys, group_values = pieces
        scores = jnp.einsum('qhd,kd->qhk', group_queries, group_keys, precision=HIGHEST) * HD ** (-0.5)
        scores = low_back(scores)
        scores = jnp.where(allowed[:, None, :], scores, FAR_BELOW)
        probs_low = low(jax.nn.softmax(scores, axis=-1))
        return jnp.einsum('qhk,kd->qhd', probs_low, group_values, precision=HIGHEST)
    attended = lax.map(jax.checkpoint(attend), (grouped, key_rows.transpose(1, 0, 2), value_rows.transpose(1, 0, 2)))
    attended = attended.transpose(1, 0, 2, 3).reshape(length, H * HD)
    attended = low(low_back(attended))
    middle = rows_in + low_back(product(attended, w_out))
    normed_two = low(rms_norm(middle, norm2_gain))
    gate_pre = low_back(product(normed_two, w_gate))
    up_pre = low_back(product(normed_two, w_up))
    hidden = low(jax.nn.silu(gate_pre) * up_pre)
    return middle + low_back(product(hidden, w_down))

def reference(tokens, positions, norm1_gain, w_query, w_key, w_value, w_out, norm2_gain, w_gate, w_up, w_down, cotangent):
    length = LENGTH
    sequences = TOKENS // length
    params = tuple((weight.astype(jnp.float32) for weight in (norm1_gain, w_query, w_key, w_value, w_out, norm2_gain, w_gate, w_up, w_down)))
    rows_all = tokens.astype(jnp.float32).reshape(sequences, length, D)
    place_all = positions.reshape(sequences, length)
    pulled_all = cotangent.astype(jnp.float32).reshape(sequences, length, D)

    def one_sequence(totals, pieces):
        rows_in, places, pulled = pieces

        def forward(rows_arg, *weights):
            return layer_forward(rows_arg, places, *weights)
        result, backward = jax.vjp(forward, rows_in, *params)
        grads = backward(pulled)
        totals = jax.tree.map(jnp.add, totals, tuple(grads[1:]))
        return (totals, (result.astype(jnp.bfloat16), grads[0]))
    starting = tuple((jnp.zeros_like(weight) for weight in params))
    totals, (outputs, input_grads) = lax.scan(one_sequence, starting, (rows_all, place_all, pulled_all))
    return (outputs.reshape(TOKENS, D), input_grads.reshape(TOKENS, D), totals[0], totals[1], totals[2], totals[3], totals[4], totals[5], totals[6], totals[7], totals[8])
```

```python
import functools

import jax
import jax.numpy as jnp
from jax import lax
from jax.experimental import pallas as pl
from jax.experimental.pallas import tpu as pltpu
from jax.sharding import PartitionSpec as P

SPAN = 4
EPSILON = 1e-05
FAR_BELOW = -1e30
LOW = jnp.bfloat16
ROW_MASKS = (0, 2, 1, 3)


def flip(block, axis, mask):
    return lax.ppermute(block, axis, [(i, i ^ mask) for i in range(lax.axis_size(axis))])


def dot(left, right, left_dim, right_dim):
    return lax.dot_general(
        left,
        right,
        (((left_dim,), (right_dim,)), ((), ())),
        preferred_element_type=jnp.float32,
    )


def own_mask(pos, begin, keys, queries):
    key_at = lax.broadcasted_iota(jnp.int32, (keys, queries), 0)
    query_at = lax.broadcasted_iota(jnp.int32, (keys, queries), 1) + begin
    return (key_at <= query_at) & (key_at >= query_at - pos)


def forward_kernel(
    heads, size, rank_ref, pos_ref, q_ref, kv0, kv1, kv2, kv3, o_ref, lse_ref, keys, vals, top, acc
):
    rank = rank_ref[0]
    rows = pos_ref.shape[1]
    half = rows // 2

    @pl.when(pl.program_id(0) == 0)
    def _():
        for m, kv in enumerate((kv0, kv1, kv2, kv3)):
            keys[m] = kv[:size, :].T
            vals[m, :size, :] = kv[size:, :]
            vals[m, size:, :] = jnp.ones((16, rows), LOW)

    pos = pos_ref[...]
    for part in range(2):
        cols = slice(part * half, (part + 1) * half)
        count = (part + 1) * half
        mask = own_mask(pos[:, cols], part * half, count, half)
        for h in range(heads):
            scores = dot(keys[0, :count, :], q_ref[h * size : (h + 1) * size, cols], 1, 0)
            scores = jnp.where(mask, scores, FAR_BELOW)
            peak = jnp.max(scores, 0, keepdims=True)
            weights = jnp.exp(scores - peak).astype(LOW)
            acc[h, :, cols] = dot(vals[0, :, :count], weights, 1, 0)
            top[h, :, cols] = peak
    seen = pos > lax.broadcasted_iota(jnp.int32, (1, rows), 1)
    for m in range(1, SPAN):

        @pl.when((rank ^ m) < rank)
        def _():
            for h in range(heads):
                scores = dot(keys[m], q_ref[h * size : (h + 1) * size, :], 1, 0)
                old = top[h]
                peak = jnp.where(seen, jnp.maximum(old, jnp.max(scores, 0, keepdims=True)), old)
                weights = jnp.exp(scores - jnp.where(seen, peak, -FAR_BELOW)).astype(LOW)
                acc[h] = acc[h] * jnp.exp(old - peak) + dot(vals[m], weights, 1, 0)
                top[h] = peak

    for h in range(heads):
        total = acc[h, size : size + 1, :]
        o_ref[h * size : (h + 1) * size, :] = (acc[h, :size, :] / total).astype(LOW)
        lse_ref[h] = top[h] + jnp.log(total)


def backward_kernel(
    heads,
    size,
    rank_ref,
    pos_ref,
    q_ref,
    do_ref,
    o_ref,
    lse_ref,
    cos_ref,
    sin_ref,
    kv0,
    kv1,
    kv2,
    kv3,
    dq_ref,
    g0,
    g1,
    g2,
    g3,
    keys,
    vals,
    dq,
    total,
):
    rank = rank_ref[0]
    rows = pos_ref.shape[1]
    half = rows // 2
    blocks = (kv0, kv1, kv2, kv3)
    step = pl.program_id(0)

    @pl.when(step == 0)
    def _():
        for m, kv in enumerate(blocks):
            keys[m] = kv[:size, :].T
            vals[m] = kv[size:, :].T
        total[...] = jnp.zeros_like(total)

    pos = pos_ref[...]
    seen = pos > lax.broadcasted_iota(jnp.int32, (1, rows), 1)
    deltas = []
    for h in range(heads):
        span = slice(h * size, (h + 1) * size)
        deltas.append(
            jnp.sum(
                do_ref[span, :].astype(jnp.float32) * o_ref[span, :].astype(jnp.float32),
                0,
                keepdims=True,
            )
        )
    for part in range(2):
        cols = slice(part * half, (part + 1) * half)
        count = (part + 1) * half
        mask = own_mask(pos[:, cols], part * half, count, half)
        for h in range(heads):
            span = slice(h * size, (h + 1) * size)
            query, grad = q_ref[span, cols], do_ref[span, cols]
            scores = dot(keys[0, :count, :], query, 1, 0)
            probs = jnp.exp(jnp.where(mask, scores, FAR_BELOW) - lse_ref[h, :, cols])
            grad_probs = dot(vals[0, :count, :], grad, 1, 0)
            grad_scores = (probs * (grad_probs - deltas[h][:, cols])).astype(LOW)
            total[0, :size, :count] += dot(query, grad_scores, 1, 1)
            total[0, size:, :count] += dot(grad, probs.astype(LOW), 1, 1)
            dq[h, :, cols] = dot(kv0[:size, :count], grad_scores, 1, 0)
    for m in range(1, SPAN):

        @pl.when((rank ^ m) < rank)
        def _():
            for h in range(heads):
                span = slice(h * size, (h + 1) * size)
                query, grad = q_ref[span, :], do_ref[span, :]
                scores = dot(keys[m], query, 1, 0)
                probs = jnp.exp(scores - jnp.where(seen, lse_ref[h], -FAR_BELOW))
                grad_probs = dot(vals[m], grad, 1, 0)
                grad_scores = (probs * (grad_probs - deltas[h])).astype(LOW)
                total[m, :size, :] += dot(query, grad_scores, 1, 1)
                total[m, size:, :] += dot(grad, probs.astype(LOW), 1, 1)
                dq[h] += dot(blocks[m][:size, :], grad_scores, 1, 0)

    middle_at = size // 2
    cosine, sine = cos_ref[...], sin_ref[...]
    for h in range(heads):
        first = dq[h, :middle_at, :] * size ** (-0.5)
        second = dq[h, middle_at:, :] * size ** (-0.5)
        base = h * size
        dq_ref[base : base + middle_at, :] = (first * cosine + second * sine).astype(LOW)
        dq_ref[base + middle_at : base + size, :] = (second * cosine - first * sine).astype(LOW)

    @pl.when(step == pl.num_programs(0) - 1)
    def _():
        g0[...] = total[0]
        for m, out in ((1, g1), (2, g2), (3, g3)):
            out[...] = total[m].astype(LOW)


def attention_forward(rank, pos, queries, blocks, size, heads):
    wide, rows = queries.shape
    count = wide // size
    whole = pl.BlockSpec((2 * size, rows), lambda i, r: (0, 0))
    some = pl.BlockSpec((heads * size, rows), lambda i, r: (i, 0))
    return pl.pallas_call(
        functools.partial(forward_kernel, heads, size),
        out_shape=(
            jax.ShapeDtypeStruct((wide, rows), LOW),
            jax.ShapeDtypeStruct((count, 1, rows), jnp.float32),
        ),
        grid_spec=pltpu.PrefetchScalarGridSpec(
            num_scalar_prefetch=1,
            grid=(count // heads,),
            in_specs=[pl.BlockSpec((1, rows), lambda i, r: (0, 0)), some] + [whole] * SPAN,
            out_specs=[some, pl.BlockSpec((heads, 1, rows), lambda i, r: (i, 0, 0))],
            scratch_shapes=[
                pltpu.VMEM((SPAN, rows, size), LOW),
                pltpu.VMEM((SPAN, size + 16, rows), LOW),
                pltpu.VMEM((heads, 1, rows), jnp.float32),
                pltpu.VMEM((heads, size + 16, rows), jnp.float32),
            ],
        ),
        compiler_params=pltpu.CompilerParams(vmem_limit_bytes=48 << 20),
        cost_estimate=pl.CostEstimate(
            flops=16 * wide * rows * rows * SPAN // 2,
            bytes_accessed=4 * wide * rows,
            transcendentals=count * rows * rows * SPAN,
        ),
        name="attention_forward",
    )(rank, pos, queries, *blocks)


def attention_backward(rank, pos, queries, grads, attended, lse, cosine, sine, blocks, size, heads):
    wide, rows = queries.shape
    count = wide // size
    whole = pl.BlockSpec((2 * size, rows), lambda i, r: (0, 0))
    table = pl.BlockSpec((size // 2, rows), lambda i, r: (0, 0))
    some = pl.BlockSpec((heads * size, rows), lambda i, r: (i, 0))
    return pl.pallas_call(
        functools.partial(backward_kernel, heads, size),
        out_shape=(
            jax.ShapeDtypeStruct((wide, rows), LOW),
            jax.ShapeDtypeStruct((2 * size, rows), jnp.float32),
        )
        + (jax.ShapeDtypeStruct((2 * size, rows), LOW),) * (SPAN - 1),
        grid_spec=pltpu.PrefetchScalarGridSpec(
            num_scalar_prefetch=1,
            grid=(count // heads,),
            in_specs=[
                pl.BlockSpec((1, rows), lambda i, r: (0, 0)),
                some,
                some,
                some,
                pl.BlockSpec((heads, 1, rows), lambda i, r: (i, 0, 0)),
                table,
                table,
            ]
            + [whole] * SPAN,
            out_specs=[some] + [whole] * SPAN,
            scratch_shapes=[
                pltpu.VMEM((SPAN, rows, size), LOW),
                pltpu.VMEM((SPAN, rows, size), LOW),
                pltpu.VMEM((heads, size, rows), jnp.float32),
                pltpu.VMEM((SPAN, 2 * size, rows), jnp.float32),
            ],
        ),
        compiler_params=pltpu.CompilerParams(vmem_limit_bytes=48 << 20),
        cost_estimate=pl.CostEstimate(
            flops=40 * wide * rows * rows * SPAN // 2,
            bytes_accessed=10 * wide * rows,
            transcendentals=count * rows * rows * SPAN,
        ),
        name="attention_backward",
    )(rank, pos, queries, grads, attended, lse, cosine, sine, *blocks)


def block_order(bits, first):
    used = list(range(first, bits))
    count = 1 << len(used)
    return [
        sum(((j >> (len(used) - 1 - k)) & 1) << b for k, b in enumerate(used)) for j in range(count)
    ]


def pick(values, masks, place, blocks, dim):
    size = values.shape[dim] // blocks
    return jnp.concatenate(
        [lax.dynamic_slice_in_dim(values, (place ^ m) * size, size, dim) for m in masks], dim
    )


def exchange_sum(part, count, bits, first, dim):
    got = []
    size = None
    for bit in range(first, bits):
        lo = count // 2
        send = part(lo, count)
        size = send.shape[dim] // (count - lo)
        for other in got:
            send = send + lax.slice_in_dim(other, lo * size, count * size, axis=dim)
        got.append(flip(send.astype(LOW), "dp", 1 << bit))
        count = lo
    total = part(0, 1)
    for other in got:
        total = total + lax.slice_in_dim(other, 0, total.shape[dim], axis=dim)
    return total


def pair_terms(pairs, size, left_first):
    def part(lo, hi):
        total = None
        for x, g in pairs:
            cut = x[:, lo * size : hi * size]
            term = dot(cut, g, 0, 0) if left_first else dot(g, cut, 0, 0)
            total = term if total is None else total + term
        return total

    return part


def turn(values, cosine, sine):
    half = cosine.shape[0]
    heads = values.shape[0] // (2 * half)
    pieces = values.reshape(heads, 2, half, values.shape[1])
    first, second = pieces[:, 0], pieces[:, 1]
    return jnp.stack(
        [first * cosine - second * sine, second * cosine + first * sine], 1
    ).reshape(values.shape)


def turn_back(grads, cosine, sine):
    return turn(grads, cosine, -sine)


def norm_back(grad_rows, values, scale_rows, gain):
    scaled = grad_rows * gain
    inner_mean = jnp.mean(scaled * values, -1, keepdims=True)
    return (
        scale_rows * (scaled - values * scale_rows * scale_rows * inner_mean),
        jnp.sum(grad_rows * values * scale_rows, 0),
    )


def shards(
    tokens,
    positions,
    norm1_gain,
    w_query,
    w_key,
    w_value,
    w_out,
    norm2_gain,
    w_gate,
    w_up,
    w_down,
    cotangent,
):
    rows_here, width = tokens.shape
    size = w_key.shape[1]
    dp = lax.axis_size("dp")
    bits = dp.bit_length() - 1
    place = lax.axis_index("dp")
    spot = lax.axis_index("tp")
    tp_masks = range(lax.axis_size("tp"))
    own_rows = rows_here // lax.axis_size("tp")
    block = width // dp
    rank = (place % SPAN).astype(jnp.int32).reshape(1)
    pos = positions.reshape(1, rows_here)

    def own(values):
        return lax.dynamic_slice_in_dim(values, spot * own_rows, own_rows, 0)

    inputs = tokens.astype(jnp.float32)
    scale_one = lax.rsqrt(jnp.mean(inputs * inputs, -1, keepdims=True) + EPSILON)
    normed_one = (inputs * scale_one * norm1_gain).astype(LOW)
    half = size // 2
    frequency = jnp.exp(
        -jnp.log(10000.0) * (2.0 * jnp.arange(half, dtype=jnp.float32) / size)
    )
    angles = frequency[:, None] * positions.astype(jnp.float32)[None, :]
    cosine, sine = jnp.cos(angles), jnp.sin(angles)
    key_new = turn(dot(w_key, normed_one, 0, 1), cosine, sine)
    value_new = dot(w_value, normed_one, 0, 1)
    paired = jnp.concatenate([key_new, value_new], 0).astype(LOW)
    blocks = [paired] + [flip(paired, "dp", m) for m in range(1, SPAN)]
    queries = (turn(dot(w_query, normed_one, 0, 1), cosine, sine) * size ** (-0.5)).astype(LOW)

    out_core = flip(w_out, "tp", 1)
    out_far = flip(w_out, "tp", 2)
    outs = [w_out, out_core, out_far, flip(out_far, "tp", 1)]

    attended, lse = attention_forward(rank, pos, queries, blocks, size, 2)

    def token_block(values, mask):
        return lax.dynamic_slice_in_dim(values, (spot ^ mask) * own_rows, own_rows, 1)

    att_pieces = [token_block(attended, m) for m in tp_masks]
    att_mine = [att_pieces[0]] + [flip(att_pieces[m], "tp", m) for m in tp_masks if m]
    branch = sum(dot(a, w, 0, 0) for a, w in zip(att_mine, outs))

    middle = own(inputs) + branch
    scale_two = lax.rsqrt(jnp.mean(middle * middle, -1, keepdims=True) + EPSILON)

    def all_rows(mine):
        pair = jnp.concatenate([mine, flip(mine, "tp", 2)], 0)
        return jnp.concatenate([pair, flip(pair, "tp", 1)], 0)

    def sum_rows(part):
        near = flip(part(2, 4).astype(LOW), "tp", 1)
        pair = part(0, 2) + near
        return pair[:own_rows] + flip(pair[own_rows:].astype(LOW), "tp", 2)

    normed_two = all_rows((middle * scale_two * norm2_gain).astype(LOW))
    gate_pre = dot(normed_two, w_gate, 1, 0)
    up_pre = dot(normed_two, w_up, 1, 0)
    cot = pick(cotangent, ROW_MASKS, spot, len(tp_masks), 0)
    grad_hidden = dot(cot, w_down, 1, 1)
    sigma = jax.nn.sigmoid(gate_pre)
    active = gate_pre * sigma
    hidden = (active * up_pre).astype(LOW)
    grad_gate_pre = (grad_hidden * up_pre * sigma * (1.0 + gate_pre * (1.0 - sigma))).astype(LOW)
    grad_up_pre = (grad_hidden * active).astype(LOW)

    def rows_of(values, lo, hi):
        return values[lo * own_rows : hi * own_rows]

    grad_normed_two = sum_rows(
        lambda lo, hi: dot(rows_of(grad_gate_pre, lo, hi), w_gate, 1, 1)
        + dot(rows_of(grad_up_pre, lo, hi), w_up, 1, 1)
    )
    down = sum_rows(lambda lo, hi: dot(rows_of(hidden, lo, hi), w_down, 1, 0))
    output_rows = (middle + down).astype(LOW)

    half_order = block_order(bits, 1)
    half_count = len(half_order)

    def gathered(x, grads, left_first=True):
        mine = pick(x, half_order, place, dp, 1)
        theirs = flip(pick(x, half_order, place ^ 1, dp, 1), "dp", 1)
        return [
            exchange_sum(
                pair_terms([(mine, g), (theirs, flip(g, "dp", 1))], block, left_first),
                half_count,
                bits,
                1,
                0 if left_first else 1,
            )
            for g in grads
        ]

    (grad_down,) = gathered(cot, [hidden], False)
    grad_gate, grad_up = gathered(normed_two, [grad_gate_pre, grad_up_pre])

    grad_mid_norm, gain_two = norm_back(grad_normed_two, middle, scale_two, norm2_gain)
    grad_middle = own(cotangent).astype(jnp.float32) + grad_mid_norm
    branch_grad = grad_middle.astype(LOW)
    grad_pieces = [dot(w, branch_grad, 1, 1).astype(LOW) for w in outs]
    grad_mine = [grad_pieces[0]] + [flip(grad_pieces[m], "tp", m) for m in tp_masks if m]
    ordered = jnp.zeros(attended.shape, LOW)
    for m in tp_masks:
        ordered = lax.dynamic_update_slice_in_dim(
            ordered, grad_mine[m], (spot ^ m) * own_rows, 1
        )
    grads = attention_backward(
        rank, pos, queries, ordered, attended, lse, cosine, sine, blocks, size, 2
    )
    grad_query_rows, kv_total = grads[0], grads[1]

    branch_all = pick(all_rows(branch_grad), block_order(bits, 0), place, dp, 1)
    att_all = jnp.concatenate([att_pieces[m] for m in ROW_MASKS], 1)
    grad_out = exchange_sum(
        lambda lo, hi: dot(att_all, branch_all[:, lo * block : hi * block], 1, 0),
        dp,
        bits,
        0,
        1,
    )

    for m in range(1, SPAN):
        kv_total = kv_total + flip(grads[m + 1], "dp", m)
    key_grad = turn_back(kv_total[:size], cosine, sine)
    grad_kv_rows = jnp.concatenate([key_grad, kv_total[size:]], 0).astype(LOW)

    query_core = flip(w_query, "tp", 1)
    query_far = flip(w_query, "tp", 2)
    query_all = [w_query, query_core, query_far, flip(query_far, "tp", 1)]
    w_kv = jnp.concatenate([w_key, w_value], 1)
    kv_far = flip(w_kv, "tp", 2)
    kv_all = [w_kv, flip(w_kv, "tp", 1), kv_far, flip(kv_far, "tp", 1)]
    grad_normed_one = None
    for m in tp_masks:
        piece_q = token_block(grad_query_rows, m)
        piece_kv = token_block(grad_kv_rows, m)
        if m:
            piece_q, piece_kv = flip(piece_q, "tp", m), flip(piece_kv, "tp", m)
        term = dot(piece_q, query_all[m], 0, 1) + dot(piece_kv, kv_all[m], 0, 1)
        grad_normed_one = term if grad_normed_one is None else grad_normed_one + term
    grad_in_norm, gain_one = norm_back(
        grad_normed_one, own(inputs), own(scale_one), norm1_gain
    )
    input_rows = grad_middle + grad_in_norm

    grad_rows = jnp.concatenate([grad_query_rows, grad_kv_rows], 0).T
    (grad_proj,) = gathered(normed_one, [grad_rows])
    wide = w_query.shape[1]

    gains = pick(jnp.stack([gain_one, gain_two]), block_order(bits, 0), place, dp, 1)
    for m in (1, 2):
        gains = gains + flip(gains, "tp", m)
    count = dp
    for bit in range(bits):
        count //= 2
        gains = gains[:, : count * block] + flip(gains[:, count * block :], "dp", 1 << bit)

    return (
        output_rows,
        input_rows,
        gains[0],
        grad_proj[:, :wide],
        grad_proj[:, wide : wide + size],
        grad_proj[:, wide + size :],
        grad_out,
        gains[1],
        grad_gate,
        grad_up,
        grad_down,
    )


def solution(mesh):
    placed = (
        P("dp", None),
        P("dp"),
        P(),
        P(None, "tp"),
        P(None, "tp"),
        P(None, "tp"),
        P("tp", None),
        P(),
        P(None, "tp"),
        P(None, "tp"),
        P("tp", None),
        P("dp", None),
    )
    return jax.shard_map(
        shards,
        mesh=mesh,
        in_specs=placed,
        out_specs=(
            P(("dp", "tp"), None),
            P(("dp", "tp"), None),
            P("dp"),
            P("dp", "tp"),
            P("dp", "tp"),
            P("dp", "tp"),
            P("tp", "dp"),
            P("dp"),
            P("dp", "tp"),
            P("dp", "tp"),
            P("tp", "dp"),
        ),
        check_vma=False,
    )
```

```python
import functools

import jax
import jax.numpy as jnp
from jax import lax
from jax.experimental import pallas as pl
from jax.experimental.pallas import tpu as pltpu
from jax.sharding import PartitionSpec as P

SPAN = 4
EPSILON = 1e-05
FAR_BELOW = -1e30
LOW = jnp.bfloat16
ROW_MASKS = (0, 2, 1, 3)


def flip(block, axis, mask):
    return lax.ppermute(block, axis, [(i, i ^ mask) for i in range(lax.axis_size(axis))])


def dot(left, right, left_dim, right_dim):
    return lax.dot_general(
        left,
        right,
        (((left_dim,), (right_dim,)), ((), ())),
        preferred_element_type=jnp.float32,
    )


def own_mask(pos, begin, keys, queries):
    key_at = lax.broadcasted_iota(jnp.int32, (keys, queries), 0)
    query_at = lax.broadcasted_iota(jnp.int32, (keys, queries), 1) + begin
    return (key_at <= query_at) & (key_at >= query_at - pos)


def row_starts(spot, rows):
    part = rows // len(ROW_MASKS)
    return [pl.multiple_of((spot ^ m) * part, part) for m in ROW_MASKS]


def forward_kernel(
    heads,
    size,
    at_ref,
    pos_ref,
    q_ref,
    kv0,
    kv1,
    kv2,
    kv3,
    o_ref,
    lse_ref,
    keys,
    vals,
    top,
    acc,
    ordered,
):
    rank, spot = at_ref[0], at_ref[1]
    rows = pos_ref.shape[1]
    half = rows // 2

    @pl.when(pl.program_id(0) == 0)
    def _():
        for m, kv in enumerate((kv0, kv1, kv2, kv3)):
            keys[m] = kv[:size, :].T
            vals[m, :size, :] = kv[size:, :]
            vals[m, size:, :] = jnp.ones((16, rows), LOW)

    pos = pos_ref[...]
    for part in range(2):
        cols = slice(part * half, (part + 1) * half)
        count = (part + 1) * half
        mask = own_mask(pos[:, cols], part * half, count, half)
        for h in range(heads):
            scores = dot(keys[0, :count, :], q_ref[h * size : (h + 1) * size, cols], 1, 0)
            scores = jnp.where(mask, scores, FAR_BELOW)
            peak = jnp.max(scores, 0, keepdims=True)
            weights = jnp.exp(scores - peak).astype(LOW)
            acc[h, :, cols] = dot(vals[0, :, :count], weights, 1, 0)
            top[h, :, cols] = peak
    seen = pos > lax.broadcasted_iota(jnp.int32, (1, rows), 1)
    for m in range(1, SPAN):

        @pl.when((rank ^ m) < rank)
        def _():
            for h in range(heads):
                scores = dot(keys[m], q_ref[h * size : (h + 1) * size, :], 1, 0)
                old = top[h]
                peak = jnp.where(seen, jnp.maximum(old, jnp.max(scores, 0, keepdims=True)), old)
                weights = jnp.exp(scores - jnp.where(seen, peak, -FAR_BELOW)).astype(LOW)
                acc[h] = acc[h] * jnp.exp(old - peak) + dot(vals[m], weights, 1, 0)
                top[h] = peak

    for h in range(heads):
        total = acc[h, size : size + 1, :]
        ordered[h * size : (h + 1) * size, :] = (acc[h, :size, :] / total).astype(LOW)
        lse_ref[h] = top[h] + jnp.log(total)
    for j, start in enumerate(row_starts(spot, rows)):
        part = rows // len(ROW_MASKS)
        o_ref[:, j * part : (j + 1) * part] = ordered[:, pl.ds(start, part)]


def backward_kernel(
    heads,
    size,
    at_ref,
    pos_ref,
    q_ref,
    do_in,
    o_in,
    lse_ref,
    cos_ref,
    sin_ref,
    kv0,
    kv1,
    kv2,
    kv3,
    dq_ref,
    g0,
    g1,
    g2,
    g3,
    keys,
    vals,
    dq,
    total,
    do_ref,
    o_ref,
):
    rank, spot = at_ref[0], at_ref[1]
    rows = pos_ref.shape[1]
    half = rows // 2
    blocks = (kv0, kv1, kv2, kv3)
    step = pl.program_id(0)

    @pl.when(step == 0)
    def _():
        for m, kv in enumerate(blocks):
            keys[m] = kv[:size, :].T
            vals[m] = kv[size:, :].T
        total[...] = jnp.zeros_like(total)

    part = rows // len(ROW_MASKS)
    for j, start in enumerate(row_starts(spot, rows)):
        do_ref[:, pl.ds(start, part)] = do_in[:, j * part : (j + 1) * part]
        o_ref[:, pl.ds(start, part)] = o_in[:, j * part : (j + 1) * part]
    pos = pos_ref[...]
    seen = pos > lax.broadcasted_iota(jnp.int32, (1, rows), 1)
    deltas = []
    for h in range(heads):
        span = slice(h * size, (h + 1) * size)
        deltas.append(
            jnp.sum(
                do_ref[span, :].astype(jnp.float32) * o_ref[span, :].astype(jnp.float32),
                0,
                keepdims=True,
            )
        )
    for part in range(2):
        cols = slice(part * half, (part + 1) * half)
        count = (part + 1) * half
        mask = own_mask(pos[:, cols], part * half, count, half)
        for h in range(heads):
            span = slice(h * size, (h + 1) * size)
            query, grad = q_ref[span, cols], do_ref[span, cols]
            scores = dot(keys[0, :count, :], query, 1, 0)
            probs = jnp.exp(jnp.where(mask, scores, FAR_BELOW) - lse_ref[h, :, cols])
            grad_probs = dot(vals[0, :count, :], grad, 1, 0)
            grad_scores = (probs * (grad_probs - deltas[h][:, cols])).astype(LOW)
            total[0, :size, :count] += dot(query, grad_scores, 1, 1)
            total[0, size:, :count] += dot(grad, probs.astype(LOW), 1, 1)
            dq[h, :, cols] = dot(kv0[:size, :count], grad_scores, 1, 0)
    for m in range(1, SPAN):

        @pl.when((rank ^ m) < rank)
        def _():
            for h in range(heads):
                span = slice(h * size, (h + 1) * size)
                query, grad = q_ref[span, :], do_ref[span, :]
                scores = dot(keys[m], query, 1, 0)
                probs = jnp.exp(scores - jnp.where(seen, lse_ref[h], -FAR_BELOW))
                grad_probs = dot(vals[m], grad, 1, 0)
                grad_scores = (probs * (grad_probs - deltas[h])).astype(LOW)
                total[m, :size, :] += dot(query, grad_scores, 1, 1)
                total[m, size:, :] += dot(grad, probs.astype(LOW), 1, 1)
                dq[h] += dot(blocks[m][:size, :], grad_scores, 1, 0)

    middle_at = size // 2
    cosine, sine = cos_ref[...], sin_ref[...]
    for h in range(heads):
        first = dq[h, :middle_at, :] * size ** (-0.5)
        second = dq[h, middle_at:, :] * size ** (-0.5)
        base = h * size
        dq_ref[base : base + middle_at, :] = (first * cosine + second * sine).astype(LOW)
        dq_ref[base + middle_at : base + size, :] = (second * cosine - first * sine).astype(LOW)

    @pl.when(step == pl.num_programs(0) - 1)
    def _():
        g0[...] = total[0]
        for m, out in ((1, g1), (2, g2), (3, g3)):
            out[...] = total[m].astype(LOW)


def attention_forward(at, pos, queries, blocks, size, heads):
    wide, rows = queries.shape
    count = wide // size
    whole = pl.BlockSpec((2 * size, rows), lambda i, r: (0, 0))
    some = pl.BlockSpec((heads * size, rows), lambda i, r: (i, 0))
    return pl.pallas_call(
        functools.partial(forward_kernel, heads, size),
        out_shape=(
            jax.ShapeDtypeStruct((wide, rows), LOW),
            jax.ShapeDtypeStruct((count, 1, rows), jnp.float32),
        ),
        grid_spec=pltpu.PrefetchScalarGridSpec(
            num_scalar_prefetch=1,
            grid=(count // heads,),
            in_specs=[pl.BlockSpec((1, rows), lambda i, r: (0, 0)), some] + [whole] * SPAN,
            out_specs=[some, pl.BlockSpec((heads, 1, rows), lambda i, r: (i, 0, 0))],
            scratch_shapes=[
                pltpu.VMEM((SPAN, rows, size), LOW),
                pltpu.VMEM((SPAN, size + 16, rows), LOW),
                pltpu.VMEM((heads, 1, rows), jnp.float32),
                pltpu.VMEM((heads, size + 16, rows), jnp.float32),
                pltpu.VMEM((heads * size, rows), LOW),
            ],
        ),
        compiler_params=pltpu.CompilerParams(vmem_limit_bytes=48 << 20),
        cost_estimate=pl.CostEstimate(
            flops=wide * rows * rows,
            bytes_accessed=4 * wide * rows,
            transcendentals=0,
        ),
        name="attention_forward",
    )(at, pos, queries, *blocks)


def attention_backward(at, pos, queries, grads, attended, lse, cosine, sine, blocks, size, heads):
    wide, rows = queries.shape
    count = wide // size
    whole = pl.BlockSpec((2 * size, rows), lambda i, r: (0, 0))
    table = pl.BlockSpec((size // 2, rows), lambda i, r: (0, 0))
    some = pl.BlockSpec((heads * size, rows), lambda i, r: (i, 0))
    return pl.pallas_call(
        functools.partial(backward_kernel, heads, size),
        out_shape=(
            jax.ShapeDtypeStruct((wide, rows), LOW),
            jax.ShapeDtypeStruct((2 * size, rows), jnp.float32),
        )
        + (jax.ShapeDtypeStruct((2 * size, rows), LOW),) * (SPAN - 1),
        grid_spec=pltpu.PrefetchScalarGridSpec(
            num_scalar_prefetch=1,
            grid=(count // heads,),
            in_specs=[
                pl.BlockSpec((1, rows), lambda i, r: (0, 0)),
                some,
                some,
                some,
                pl.BlockSpec((heads, 1, rows), lambda i, r: (i, 0, 0)),
                table,
                table,
            ]
            + [whole] * SPAN,
            out_specs=[some] + [whole] * SPAN,
            scratch_shapes=[
                pltpu.VMEM((SPAN, rows, size), LOW),
                pltpu.VMEM((SPAN, rows, size), LOW),
                pltpu.VMEM((heads, size, rows), jnp.float32),
                pltpu.VMEM((SPAN, 2 * size, rows), jnp.float32),
                pltpu.VMEM((heads * size, rows), LOW),
                pltpu.VMEM((heads * size, rows), LOW),
            ],
        ),
        compiler_params=pltpu.CompilerParams(vmem_limit_bytes=48 << 20),
        cost_estimate=pl.CostEstimate(
            flops=wide * rows * rows,
            bytes_accessed=10 * wide * rows,
            transcendentals=0,
        ),
        name="attention_backward",
    )(at, pos, queries, grads, attended, lse, cosine, sine, *blocks)


def pick(values, places, blocks, dim):
    size = values.shape[dim] // blocks
    return jnp.concatenate(
        [lax.dynamic_slice_in_dim(values, p * size, size, dim) for p in places], dim
    )


def after(value, *others):
    return lax.optimization_barrier((value, *others))[0]


def parity_sum(terms, dim):
    count = lax.axis_size("dp")
    groups = [list(range(p, count, 2)) for p in range(2)]
    return lax.psum_scatter(
        terms.astype(LOW), "dp", scatter_dimension=dim, axis_index_groups=groups, tiled=True
    )


def turn(values, cosine, sine):
    half = cosine.shape[0]
    heads = values.shape[0] // (2 * half)
    pieces = values.reshape(heads, 2, half, values.shape[1])
    first, second = pieces[:, 0], pieces[:, 1]
    return jnp.stack(
        [first * cosine - second * sine, second * cosine + first * sine], 1
    ).reshape(values.shape)


def turn_back(grads, cosine, sine):
    return turn(grads, cosine, -sine)


def norm_back(grad_rows, values, scale_rows, gain):
    scaled = grad_rows * gain
    inner_mean = jnp.mean(scaled * values, -1, keepdims=True)
    return (
        scale_rows * (scaled - values * scale_rows * scale_rows * inner_mean),
        jnp.sum(grad_rows * values * scale_rows, 0),
    )


def shards(
    tokens,
    positions,
    norm1_gain,
    w_query,
    w_key,
    w_value,
    w_out,
    norm2_gain,
    w_gate,
    w_up,
    w_down,
    cotangent,
):
    rows_here, width = tokens.shape
    size = w_key.shape[1]
    dp = lax.axis_size("dp")
    place = lax.axis_index("dp")
    spot = lax.axis_index("tp")
    tp_masks = range(lax.axis_size("tp"))
    own_rows = rows_here // lax.axis_size("tp")
    block = width // dp
    at = jnp.stack([place % SPAN, spot]).astype(jnp.int32)
    pos = positions.reshape(1, rows_here)

    def own(values):
        return lax.dynamic_slice_in_dim(values, spot * own_rows, own_rows, 0)

    inputs = tokens.astype(jnp.float32)
    scale_one = lax.rsqrt(jnp.mean(inputs * inputs, -1, keepdims=True) + EPSILON)
    normed_one = (inputs * scale_one * norm1_gain).astype(LOW)
    half = size // 2
    frequency = jnp.exp(
        -jnp.log(10000.0) * (2.0 * jnp.arange(half, dtype=jnp.float32) / size)
    )
    angles = frequency[:, None] * positions.astype(jnp.float32)[None, :]
    cosine, sine = jnp.cos(angles), jnp.sin(angles)
    key_new = turn(dot(w_key, normed_one, 0, 1), cosine, sine)
    value_new = dot(w_value, normed_one, 0, 1)
    paired = jnp.concatenate([key_new, value_new], 0).astype(LOW)
    blocks = [paired] + [flip(paired, "dp", m) for m in range(1, SPAN)]
    queries = (turn(dot(w_query, normed_one, 0, 1), cosine, sine) * size ** (-0.5)).astype(LOW)

    bit = place % 2
    bits = dp.bit_length() - 1

    def columns(values, which):
        return pick(values, [2 * j + which for j in range(dp // 2)], dp, 1)

    near_bits = [0] + list(range(2, bits))
    near_masks = [
        sum(((j >> (len(near_bits) - 1 - k)) & 1) << b for k, b in enumerate(near_bits))
        for j in range(dp // 2)
    ]

    def near_columns(values, where):
        return pick(values, [where ^ m for m in near_masks], dp, 1)

    def rows_of(values, lo, hi):
        return values[lo * own_rows : hi * own_rows]

    def near_sum(part):
        send = part(2, 4).astype(LOW)
        near, kept = lax.optimization_barrier((flip(send, "tp", 1), part(0, 2)))
        pair = kept + near
        return pair[:own_rows], pair[own_rows:].astype(LOW)

    cot = pick(after(cotangent, paired), [spot ^ m for m in ROW_MASKS], len(tp_masks), 0)
    queries = after(queries, cot)
    attended, lse = attention_forward(at, pos, queries, blocks, size, 2)

    def branch_terms(lo, hi):
        return dot(attended[:, lo * own_rows : hi * own_rows], w_out, 0, 0)

    branch, branch_send = near_sum(branch_terms)
    branch_far = flip(branch_send, "tp", 2)
    one_rows = after(normed_one, branch_send)
    one_mine, one_send = columns(one_rows, bit), columns(one_rows, 1 - bit)
    one_theirs = flip(one_send, "dp", 1)
    branch = after(branch, one_mine, one_send)

    middle = own(inputs) + (branch + branch_far)
    scale_two = lax.rsqrt(jnp.mean(middle * middle, -1, keepdims=True) + EPSILON)
    own_two = (middle * scale_two * norm2_gain).astype(LOW)
    far_two = flip(own_two, "tp", 2)
    att_theirs = flip(after(attended, own_two), "dp", 1)
    cot_late = after(cot, own_two)
    cot_mine, cot_send = near_columns(cot_late, place), near_columns(cot_late, place ^ 2)
    cot_theirs = flip(cot_send, "dp", 2)
    own_two = after(own_two, cot_mine, cot_send)
    pair_two = jnp.concatenate([own_two, far_two], 0)
    core_two = flip(pair_two, "tp", 1)
    grad_hidden = dot(after(cot, pair_two), w_down, 1, 1)
    normed_two = jnp.concatenate([after(pair_two, grad_hidden), core_two], 0)
    two_send = columns(normed_two, 1 - bit)
    two_theirs = flip(two_send, "dp", 1)
    normed_two = after(normed_two, two_send, one_theirs)

    gate_pre = dot(normed_two, w_gate, 1, 0)
    up_pre = dot(normed_two, w_up, 1, 0)
    sigma = jax.nn.sigmoid(gate_pre)
    active = gate_pre * sigma
    hidden = (active * up_pre).astype(LOW)
    grad_gate_pre = (grad_hidden * up_pre * sigma * (1.0 + gate_pre * (1.0 - sigma))).astype(LOW)
    grad_up_pre = (grad_hidden * active).astype(LOW)
    hidden_theirs = flip(hidden, "dp", 2)
    gate_theirs = flip(grad_gate_pre, "dp", 1)

    gate_late, att_theirs, cot_theirs = lax.optimization_barrier(
        (grad_gate_pre, att_theirs, cot_theirs)
    )

    def two_terms(lo, hi):
        return dot(rows_of(gate_late, lo, hi), w_gate, 1, 1) + dot(
            rows_of(grad_up_pre, lo, hi), w_up, 1, 1
        )

    grad_normed_two, two_far_send = near_sum(two_terms)
    two_far = flip(two_far_send, "tp", 2)

    hidden_late = after(hidden, two_far_send)
    down, down_send = near_sum(lambda lo, hi: dot(rows_of(hidden_late, lo, hi), w_down, 1, 0))
    down_far = flip(down_send, "tp", 2)
    up_theirs = flip(after(grad_up_pre, down_send), "dp", 1)
    grad_normed_two = after(grad_normed_two, down_send) + two_far

    grad_mid_norm, gain_two = norm_back(grad_normed_two, middle, scale_two, norm2_gain)
    grad_middle = own(cotangent).astype(jnp.float32) + grad_mid_norm
    branch_grad = grad_middle.astype(LOW)
    output_rows = (middle + (down + after(down_far, branch_grad))).astype(LOW)
    grad_far = flip(branch_grad, "tp", 2)

    hidden_late, cot_mine = lax.optimization_barrier((hidden, cot_mine, branch_grad, output_rows))[:2]

    def down_terms(lo, hi):
        cut = slice(lo * block, hi * block)
        return dot(cot_mine[:, cut], hidden_late, 0, 0) + dot(
            cot_theirs[:, cut], hidden_theirs, 0, 0
        )

    count = dp // 2
    first_send = down_terms(count // 2, count).astype(LOW)
    grad_pair = jnp.concatenate([after(branch_grad, first_send), grad_far], 0)
    grad_core = flip(grad_pair, "tp", 1)

    two_mine = columns(after(normed_two, grad_pair), bit)
    gate_terms = dot(two_mine, grad_gate_pre, 0, 0) + dot(two_theirs, gate_theirs, 0, 0)
    gate_terms = gate_terms.astype(LOW)
    grad_gate = parity_sum(gate_terms, 0)
    branch_all = jnp.concatenate([after(grad_pair, gate_terms), grad_core], 0)
    grad_attended = dot(w_out, branch_all, 1, 1).astype(LOW)

    grads = attention_backward(
        at, pos, queries, grad_attended, attended, lse, cosine, sine, blocks, size, 2
    )
    grad_query_rows, kv_total = grads[0], grads[1]
    kv_back = [flip(grads[m + 1], "dp", m) for m in range(1, SPAN)]

    two_mine, up_late = lax.optimization_barrier((two_mine, grad_up_pre, grad_query_rows))[:2]
    up_terms = (dot(two_mine, up_late, 0, 0) + dot(two_theirs, up_theirs, 0, 0)).astype(LOW)
    grad_up = parity_sum(up_terms, 0)

    kv_total = after(kv_total, up_terms)
    for got in kv_back:
        kv_total = kv_total + got
    key_grad = turn_back(kv_total[:size], cosine, sine)
    grad_kv_rows = jnp.concatenate([key_grad, kv_total[size:]], 0).astype(LOW)
    proj_rows = jnp.concatenate([grad_query_rows, grad_kv_rows], 0)
    proj_theirs = flip(proj_rows, "dp", 1)

    w_proj = jnp.concatenate([w_query, w_key, w_value], 1)
    own_order = pick(proj_rows, [spot ^ m for m in ROW_MASKS], len(tp_masks), 1)

    def one_terms(lo, hi):
        return dot(own_order[:, lo * own_rows : hi * own_rows], w_proj, 0, 1)

    grad_normed_one, one_far_send = near_sum(one_terms)
    one_far = flip(one_far_send, "tp", 2)

    got = [flip(after(first_send, one_far_send), "dp", 1)]
    branch_late = after(branch_all, one_far_send)
    branch_mine = columns(branch_late, bit)
    branch_theirs = flip(columns(branch_late, 1 - bit), "dp", 1)
    grad_normed_one = after(grad_normed_one, branch_mine) + one_far
    grad_in_norm, gain_one = norm_back(
        grad_normed_one, own(inputs), own(scale_one), norm1_gain
    )
    input_rows = grad_middle + grad_in_norm
    grad_gate = grad_gate.astype(jnp.float32)

    proj_late = after(proj_rows, input_rows, grad_gate)
    proj_terms = dot(one_mine, proj_late, 0, 1) + dot(one_theirs, proj_theirs, 0, 1)
    proj_terms = proj_terms.astype(LOW)
    grad_proj = parity_sum(proj_terms, 0).astype(jnp.float32)
    wide = w_query.shape[1]

    count //= 2
    for b in near_bits[1:]:
        send = down_terms(count // 2, count)
        for other in got:
            send = send + other[count // 2 * block : count * block]
        got.append(flip(send.astype(LOW), "dp", 1 << b))
        count //= 2
    grad_down = down_terms(0, 1)
    for other in got:
        grad_down = grad_down + other[:block]

    out_terms = dot(attended, branch_mine, 1, 0) + dot(att_theirs, branch_theirs, 1, 0)
    grad_up = grad_up.astype(jnp.float32)
    grad_out = parity_sum(after(out_terms.astype(LOW), grad_up, proj_terms), 1)

    gains = jnp.stack([gain_one, gain_two])
    for m in (1, 2):
        gains = gains + flip(gains, "tp", m)
    gains = pick(gains, [place ^ m for m in range(dp)], dp, 1)
    count = dp
    while count > 1:
        count //= 2
        gains = gains[:, : count * block] + flip(gains[:, count * block :], "dp", count)

    return (
        output_rows,
        input_rows,
        gains[0],
        grad_proj[:, :wide],
        grad_proj[:, wide : wide + size],
        grad_proj[:, wide + size :],
        grad_out.astype(jnp.float32),
        gains[1],
        grad_gate,
        grad_up,
        grad_down.T,
    )


def solution(mesh):
    placed = (
        P("dp", None),
        P("dp"),
        P(),
        P(None, "tp"),
        P(None, "tp"),
        P(None, "tp"),
        P("tp", None),
        P(),
        P(None, "tp"),
        P(None, "tp"),
        P("tp", None),
        P("dp", None),
    )
    return jax.shard_map(
        shards,
        mesh=mesh,
        in_specs=placed,
        out_specs=(
            P(("dp", "tp"), None),
            P(("dp", "tp"), None),
            P("dp"),
            P("dp", "tp"),
            P("dp", "tp"),
            P("dp", "tp"),
            P("tp", "dp"),
            P("dp"),
            P("dp", "tp"),
            P("dp", "tp"),
            P("tp", "dp"),
        ),
        check_vma=False,
    )
```

```python
import functools

import jax
import jax.numpy as jnp
from jax import lax
from jax.experimental import pallas as pl
from jax.experimental.pallas import tpu as pltpu
from jax.sharding import PartitionSpec as P

SPAN = 4
EPSILON = 1e-05
FAR_BELOW = -1e30
LOW = jnp.bfloat16
ROW_MASKS = (0, 2, 1, 3)


def flip(block, axis, mask):
    return lax.ppermute(block, axis, [(i, i ^ mask) for i in range(lax.axis_size(axis))])


def dot(left, right, left_dim, right_dim):
    return lax.dot_general(
        left,
        right,
        (((left_dim,), (right_dim,)), ((), ())),
        preferred_element_type=jnp.float32,
    )


def own_mask(pos, begin, keys, queries):
    key_at = lax.broadcasted_iota(jnp.int32, (keys, queries), 0)
    query_at = lax.broadcasted_iota(jnp.int32, (keys, queries), 1) + begin
    return (key_at <= query_at) & (key_at >= query_at - pos)


def row_starts(spot, rows):
    part = rows // len(ROW_MASKS)
    return [pl.multiple_of((spot ^ m) * part, part) for m in ROW_MASKS]


def forward_kernel(
    heads,
    size,
    at_ref,
    pos_ref,
    q_ref,
    kv0,
    kv1,
    kv2,
    kv3,
    o_ref,
    lse_ref,
    keys,
    vals,
    top,
    acc,
    ordered,
):
    rank, spot = at_ref[0], at_ref[1]
    rows = pos_ref.shape[1]
    half = rows // 2

    @pl.when(pl.program_id(0) == 0)
    def _():
        for m, kv in enumerate((kv0, kv1, kv2, kv3)):
            keys[m] = kv[:size, :].T
            vals[m, :size, :] = kv[size:, :]
            vals[m, size:, :] = jnp.ones((16, rows), LOW)

    pos = pos_ref[...]
    for part in range(2):
        cols = slice(part * half, (part + 1) * half)
        count = (part + 1) * half
        mask = own_mask(pos[:, cols], part * half, count, half)
        for h in range(heads):
            scores = dot(keys[0, :count, :], q_ref[h * size : (h + 1) * size, cols], 1, 0)
            scores = jnp.where(mask, scores, FAR_BELOW)
            peak = jnp.max(scores, 0, keepdims=True)
            weights = jnp.exp(scores - peak).astype(LOW)
            acc[h, :, cols] = dot(vals[0, :, :count], weights, 1, 0)
            top[h, :, cols] = peak
    seen = pos > lax.broadcasted_iota(jnp.int32, (1, rows), 1)
    for m in range(1, SPAN):

        @pl.when((rank ^ m) < rank)
        def _():
            for h in range(heads):
                scores = dot(keys[m], q_ref[h * size : (h + 1) * size, :], 1, 0)
                old = top[h]
                peak = jnp.where(seen, jnp.maximum(old, jnp.max(scores, 0, keepdims=True)), old)
                weights = jnp.exp(scores - jnp.where(seen, peak, -FAR_BELOW)).astype(LOW)
                acc[h] = acc[h] * jnp.exp(old - peak) + dot(vals[m], weights, 1, 0)
                top[h] = peak

    for h in range(heads):
        total = acc[h, size : size + 1, :]
        ordered[h * size : (h + 1) * size, :] = (acc[h, :size, :] / total).astype(LOW)
        lse_ref[h] = top[h] + jnp.log(total)
    for j, start in enumerate(row_starts(spot, rows)):
        part = rows // len(ROW_MASKS)
        o_ref[:, j * part : (j + 1) * part] = ordered[:, pl.ds(start, part)]


def backward_kernel(
    heads,
    size,
    at_ref,
    pos_ref,
    q_ref,
    do_in,
    o_in,
    lse_ref,
    cos_ref,
    sin_ref,
    kv0,
    kv1,
    kv2,
    kv3,
    dq_ref,
    g0,
    g1,
    g2,
    g3,
    keys,
    vals,
    dq,
    total,
    do_ref,
    o_ref,
):
    rank, spot = at_ref[0], at_ref[1]
    rows = pos_ref.shape[1]
    half = rows // 2
    blocks = (kv0, kv1, kv2, kv3)
    step = pl.program_id(0)

    @pl.when(step == 0)
    def _():
        for m, kv in enumerate(blocks):
            keys[m] = kv[:size, :].T
            vals[m] = kv[size:, :].T
        total[...] = jnp.zeros_like(total)

    part = rows // len(ROW_MASKS)
    for j, start in enumerate(row_starts(spot, rows)):
        do_ref[:, pl.ds(start, part)] = do_in[:, j * part : (j + 1) * part]
        o_ref[:, pl.ds(start, part)] = o_in[:, j * part : (j + 1) * part]
    pos = pos_ref[...]
    seen = pos > lax.broadcasted_iota(jnp.int32, (1, rows), 1)
    deltas = []
    for h in range(heads):
        span = slice(h * size, (h + 1) * size)
        deltas.append(
            jnp.sum(
                do_ref[span, :].astype(jnp.float32) * o_ref[span, :].astype(jnp.float32),
                0,
                keepdims=True,
            )
        )
    for part in range(2):
        cols = slice(part * half, (part + 1) * half)
        count = (part + 1) * half
        mask = own_mask(pos[:, cols], part * half, count, half)
        for h in range(heads):
            span = slice(h * size, (h + 1) * size)
            query, grad = q_ref[span, cols], do_ref[span, cols]
            scores = dot(keys[0, :count, :], query, 1, 0)
            probs = jnp.exp(jnp.where(mask, scores, FAR_BELOW) - lse_ref[h, :, cols])
            grad_probs = dot(vals[0, :count, :], grad, 1, 0)
            grad_scores = (probs * (grad_probs - deltas[h][:, cols])).astype(LOW)
            total[0, :size, :count] += dot(query, grad_scores, 1, 1)
            total[0, size:, :count] += dot(grad, probs.astype(LOW), 1, 1)
            dq[h, :, cols] = dot(kv0[:size, :count], grad_scores, 1, 0)
    for m in range(1, SPAN):

        @pl.when((rank ^ m) < rank)
        def _():
            for h in range(heads):
                span = slice(h * size, (h + 1) * size)
                query, grad = q_ref[span, :], do_ref[span, :]
                scores = dot(keys[m], query, 1, 0)
                probs = jnp.exp(scores - jnp.where(seen, lse_ref[h], -FAR_BELOW))
                grad_probs = dot(vals[m], grad, 1, 0)
                grad_scores = (probs * (grad_probs - deltas[h])).astype(LOW)
                total[m, :size, :] += dot(query, grad_scores, 1, 1)
                total[m, size:, :] += dot(grad, probs.astype(LOW), 1, 1)
                dq[h] += dot(blocks[m][:size, :], grad_scores, 1, 0)

    middle_at = size // 2
    cosine, sine = cos_ref[...], sin_ref[...]
    for h in range(heads):
        first = dq[h, :middle_at, :] * size ** (-0.5)
        second = dq[h, middle_at:, :] * size ** (-0.5)
        base = h * size
        dq_ref[base : base + middle_at, :] = (first * cosine + second * sine).astype(LOW)
        dq_ref[base + middle_at : base + size, :] = (second * cosine - first * sine).astype(LOW)

    @pl.when(step == pl.num_programs(0) - 1)
    def _():
        g0[...] = total[0]
        for m, out in ((1, g1), (2, g2), (3, g3)):
            out[...] = total[m].astype(LOW)


def attention_forward(at, pos, queries, blocks, size, heads):
    wide, rows = queries.shape
    count = wide // size
    whole = pl.BlockSpec((2 * size, rows), lambda i, r: (0, 0))
    some = pl.BlockSpec((heads * size, rows), lambda i, r: (i, 0))
    return pl.pallas_call(
        functools.partial(forward_kernel, heads, size),
        out_shape=(
            jax.ShapeDtypeStruct((wide, rows), LOW),
            jax.ShapeDtypeStruct((count, 1, rows), jnp.float32),
        ),
        grid_spec=pltpu.PrefetchScalarGridSpec(
            num_scalar_prefetch=1,
            grid=(count // heads,),
            in_specs=[pl.BlockSpec((1, rows), lambda i, r: (0, 0)), some] + [whole] * SPAN,
            out_specs=[some, pl.BlockSpec((heads, 1, rows), lambda i, r: (i, 0, 0))],
            scratch_shapes=[
                pltpu.VMEM((SPAN, rows, size), LOW),
                pltpu.VMEM((SPAN, size + 16, rows), LOW),
                pltpu.VMEM((heads, 1, rows), jnp.float32),
                pltpu.VMEM((heads, size + 16, rows), jnp.float32),
                pltpu.VMEM((heads * size, rows), LOW),
            ],
        ),
        compiler_params=pltpu.CompilerParams(vmem_limit_bytes=24 << 20),
        cost_estimate=pl.CostEstimate(
            flops=wide * rows * rows,
            bytes_accessed=4 * wide * rows,
            transcendentals=0,
        ),
        name="attention_forward",
    )(at, pos, queries, *blocks)


def attention_backward(at, pos, queries, grads, attended, lse, cosine, sine, blocks, size, heads):
    wide, rows = queries.shape
    count = wide // size
    whole = pl.BlockSpec((2 * size, rows), lambda i, r: (0, 0))
    table = pl.BlockSpec((size // 2, rows), lambda i, r: (0, 0))
    some = pl.BlockSpec((heads * size, rows), lambda i, r: (i, 0))
    return pl.pallas_call(
        functools.partial(backward_kernel, heads, size),
        out_shape=(
            jax.ShapeDtypeStruct((wide, rows), LOW),
            jax.ShapeDtypeStruct((2 * size, rows), jnp.float32),
        )
        + (jax.ShapeDtypeStruct((2 * size, rows), LOW),) * (SPAN - 1),
        grid_spec=pltpu.PrefetchScalarGridSpec(
            num_scalar_prefetch=1,
            grid=(count // heads,),
            in_specs=[
                pl.BlockSpec((1, rows), lambda i, r: (0, 0)),
                some,
                some,
                some,
                pl.BlockSpec((heads, 1, rows), lambda i, r: (i, 0, 0)),
                table,
                table,
            ]
            + [whole] * SPAN,
            out_specs=[some] + [whole] * SPAN,
            scratch_shapes=[
                pltpu.VMEM((SPAN, rows, size), LOW),
                pltpu.VMEM((SPAN, rows, size), LOW),
                pltpu.VMEM((heads, size, rows), jnp.float32),
                pltpu.VMEM((SPAN, 2 * size, rows), jnp.float32),
                pltpu.VMEM((heads * size, rows), LOW),
                pltpu.VMEM((heads * size, rows), LOW),
            ],
        ),
        compiler_params=pltpu.CompilerParams(vmem_limit_bytes=24 << 20),
        cost_estimate=pl.CostEstimate(
            flops=wide * rows * rows,
            bytes_accessed=10 * wide * rows,
            transcendentals=0,
        ),
        name="attention_backward",
    )(at, pos, queries, grads, attended, lse, cosine, sine, *blocks)


def pick(values, places, blocks, dim):
    size = values.shape[dim] // blocks
    return jnp.concatenate(
        [lax.dynamic_slice_in_dim(values, p * size, size, dim) for p in places], dim
    )


def after(value, *others):
    return lax.optimization_barrier((value, *others))[0]


def parity_sum(terms, dim):
    count = lax.axis_size("dp")
    groups = [list(range(p, count, 2)) for p in range(2)]
    return lax.psum_scatter(
        terms.astype(LOW), "dp", scatter_dimension=dim, axis_index_groups=groups, tiled=True
    )


def terms_kernel(transposed, places, x, x_far, g, g_far, out):
    del places
    side = 1 if transposed else 0
    out[...] = (dot(x[...], g[...], 0, side) + dot(x_far[...], g_far[...], 0, side)).astype(LOW)


def weight_terms(places, first, x, x_far, g, g_far, transposed=False):
    count = len(places)
    blocks = lax.axis_size("dp")
    size = x.shape[1] // blocks
    rows = x.shape[0]
    units = g.shape[0] if transposed else g.shape[1]
    if size % 128:
        side = 1 if transposed else 0
        far = x_far[:, first * size : (first + count) * size]
        return (dot(pick(x, places, blocks, 1), g, 0, side) + dot(far, g_far, 0, side)).astype(LOW)
    whole = pl.BlockSpec(g.shape, lambda i, p: (0, 0))
    return pl.pallas_call(
        functools.partial(terms_kernel, transposed),
        out_shape=jax.ShapeDtypeStruct((count * size, units), LOW),
        grid_spec=pltpu.PrefetchScalarGridSpec(
            num_scalar_prefetch=1,
            grid=(count,),
            in_specs=[
                pl.BlockSpec((rows, size), lambda i, p: (0, p[i])),
                pl.BlockSpec((rows, size), lambda i, p: (0, first + i)),
                whole,
                whole,
            ],
            out_specs=pl.BlockSpec((size, units), lambda i, p: (i, 0)),
        ),
        compiler_params=pltpu.CompilerParams(vmem_limit_bytes=24 << 20),
        cost_estimate=pl.CostEstimate(
            flops=8 * rows * count * size * units, bytes_accessed=4 * rows * units, transcendentals=0
        ),
        name="weight_terms",
    )(jnp.stack(places).astype(jnp.int32), x, x_far, g, g_far)


def turn(values, cosine, sine):
    half = cosine.shape[0]
    heads = values.shape[0] // (2 * half)
    pieces = values.reshape(heads, 2, half, values.shape[1])
    first, second = pieces[:, 0], pieces[:, 1]
    return jnp.stack(
        [first * cosine - second * sine, second * cosine + first * sine], 1
    ).reshape(values.shape)


def turn_back(grads, cosine, sine):
    return turn(grads, cosine, -sine)


def norm_back(grad_rows, values, scale_rows, gain):
    scaled = grad_rows * gain
    inner_mean = jnp.mean(scaled * values, -1, keepdims=True)
    return (
        scale_rows * (scaled - values * scale_rows * scale_rows * inner_mean),
        jnp.sum(grad_rows * values * scale_rows, 0),
    )


def shards(
    tokens,
    positions,
    norm1_gain,
    w_query,
    w_key,
    w_value,
    w_out,
    norm2_gain,
    w_gate,
    w_up,
    w_down,
    cotangent,
):
    rows_here, width = tokens.shape
    size = w_key.shape[1]
    dp = lax.axis_size("dp")
    place = lax.axis_index("dp")
    spot = lax.axis_index("tp")
    tp_masks = range(lax.axis_size("tp"))
    own_rows = rows_here // lax.axis_size("tp")
    block = width // dp
    at = jnp.stack([place % SPAN, spot]).astype(jnp.int32)
    pos = positions.reshape(1, rows_here)

    def own(values):
        return lax.dynamic_slice_in_dim(values, spot * own_rows, own_rows, 0)

    inputs = tokens.astype(jnp.float32)
    scale_one = lax.rsqrt(jnp.mean(inputs * inputs, -1, keepdims=True) + EPSILON)
    normed_one = (inputs * scale_one * norm1_gain).astype(LOW)
    half = size // 2
    frequency = jnp.exp(
        -jnp.log(10000.0) * (2.0 * jnp.arange(half, dtype=jnp.float32) / size)
    )
    angles = frequency[:, None] * positions.astype(jnp.float32)[None, :]
    cosine, sine = jnp.cos(angles), jnp.sin(angles)
    w_kv = jnp.concatenate([w_key.T, w_value.T], 0)
    paired = dot(w_kv, normed_one, 1, 1)
    paired = jnp.concatenate([turn(paired[:size], cosine, sine), paired[size:]], 0).astype(LOW)
    blocks = [paired] + [flip(paired, "dp", m) for m in range(1, SPAN)]
    queries = (turn(dot(w_query, normed_one, 0, 1), cosine, sine) * size ** (-0.5)).astype(LOW)

    bit = place % 2
    bits = dp.bit_length() - 1

    halves = [[2 * j + which for j in range(dp // 2)] for which in (bit, 1 - bit)]

    def columns(values, which):
        return pick(values, halves[which], dp, 1)

    near_bits = [0] + list(range(2, bits))
    near_masks = [
        sum(((j >> (len(near_bits) - 1 - k)) & 1) << b for k, b in enumerate(near_bits))
        for j in range(dp // 2)
    ]

    near_halves = [[where ^ m for m in near_masks] for where in (place, place ^ 2)]

    def rows_of(values, lo, hi):
        return values[lo * own_rows : hi * own_rows]

    def near_sum(part):
        send = part(2, 4).astype(LOW)
        near, kept = lax.optimization_barrier((flip(send, "tp", 1), part(0, 2)))
        pair = kept + near
        return pair[:own_rows], pair[own_rows:].astype(LOW)

    cot = pick(after(cotangent, paired), [spot ^ m for m in ROW_MASKS], len(tp_masks), 0)
    queries = after(queries, cot)
    attended, lse = attention_forward(at, pos, queries, blocks, size, 2)

    def branch_terms(lo, hi):
        return dot(attended[:, lo * own_rows : hi * own_rows], w_out, 0, 0)

    branch, branch_send = near_sum(branch_terms)
    branch_far = flip(branch_send, "tp", 2)
    one_rows = after(normed_one, branch_send)
    one_send = columns(one_rows, 1)
    one_theirs = flip(one_send, "dp", 1)
    branch = after(branch, one_send)

    own_inputs = own(tokens).astype(jnp.float32)
    middle = own_inputs + (branch + branch_far)
    scale_two = lax.rsqrt(jnp.mean(middle * middle, -1, keepdims=True) + EPSILON)
    own_two = (middle * scale_two * norm2_gain).astype(LOW)
    far_two = flip(own_two, "tp", 2)
    att_theirs = flip(after(attended, own_two), "dp", 1)
    cot_late = after(cot, own_two)
    cot_send = pick(cot_late, near_halves[1], dp, 1)
    cot_theirs = flip(cot_send, "dp", 2)
    own_two = after(own_two, cot_send)
    pair_two = jnp.concatenate([own_two, far_two], 0)
    core_two = flip(pair_two, "tp", 1)
    two_send = columns(pair_two, 1)
    two_near = flip(two_send, "dp", 1)
    grad_hidden = dot(after(cot, two_send), w_down, 1, 1)
    normed_two = jnp.concatenate([after(pair_two, grad_hidden), core_two], 0)
    normed_two = after(normed_two, one_theirs)

    gate_pre = dot(normed_two, w_gate, 1, 0)
    up_pre = dot(normed_two, w_up, 1, 0)
    sigma = jax.nn.sigmoid(gate_pre)
    active = gate_pre * sigma
    hidden = (active * up_pre).astype(LOW)
    grad_gate_pre = (grad_hidden * up_pre * sigma * (1.0 + gate_pre * (1.0 - sigma))).astype(LOW)
    grad_up_pre = (grad_hidden * active).astype(LOW)
    hidden_theirs = flip(hidden, "dp", 2)
    gate_theirs = flip(grad_gate_pre, "dp", 1)

    gate_late, att_theirs, cot_theirs, two_near = lax.optimization_barrier(
        (grad_gate_pre, att_theirs, cot_theirs, two_near)
    )
    two_theirs = jnp.concatenate([two_near, flip(two_near, "tp", 1)], 0)

    def two_terms(lo, hi):
        return dot(rows_of(gate_late, lo, hi), w_gate, 1, 1) + dot(
            rows_of(grad_up_pre, lo, hi), w_up, 1, 1
        )

    grad_normed_two, two_far_send = near_sum(two_terms)
    two_far_send, two_theirs = lax.optimization_barrier((two_far_send, two_theirs))
    two_far = flip(two_far_send, "tp", 2)

    hidden_late = after(hidden, two_far_send)
    down, down_send = near_sum(lambda lo, hi: dot(rows_of(hidden_late, lo, hi), w_down, 1, 0))
    up_theirs = flip(after(grad_up_pre, two_far_send), "dp", 1)
    grad_normed_two = after(grad_normed_two, down_send) + two_far

    grad_mid_norm, gain_two = norm_back(grad_normed_two, middle, scale_two, norm2_gain)
    grad_middle = own(cotangent).astype(jnp.float32) + grad_mid_norm
    branch_grad = grad_middle.astype(LOW)
    grad_far = flip(branch_grad, "tp", 2)

    hidden_late = after(hidden, branch_grad)

    def down_terms(lo, hi):
        return weight_terms(
            near_halves[0][lo:hi], lo, cot, cot_theirs, hidden_late, hidden_theirs
        )

    count = dp // 2
    first_send = down_terms(count // 2, count)
    down_far = flip(after(down_send, first_send), "tp", 2)
    grad_pair = jnp.concatenate([after(branch_grad, first_send), grad_far], 0)
    grad_core = flip(grad_pair, "tp", 1)

    branch_send = columns(grad_pair, 1)
    branch_near = flip(branch_send, "dp", 1)
    two_late = after(normed_two, branch_send)
    gate_terms = weight_terms(halves[0], 0, two_late, two_theirs, grad_gate_pre, gate_theirs)
    grad_gate = parity_sum(gate_terms, 0)
    branch_all = jnp.concatenate([after(grad_pair, gate_terms), grad_core], 0)
    grad_attended = dot(w_out, branch_all, 1, 1).astype(LOW)

    grads = attention_backward(
        at, pos, queries, grad_attended, attended, lse, cosine, sine, blocks, size, 2
    )
    grad_query_rows, kv_total = grads[0], grads[1]
    kv_back = [flip(grads[m + 1], "dp", m) for m in range(1, SPAN)]

    up_late = after(grad_up_pre, grad_query_rows)
    up_terms = weight_terms(halves[0], 0, normed_two, two_theirs, up_late, up_theirs)
    output_rows = (middle + (down + after(down_far, grad_query_rows))).astype(LOW)
    got = [flip(first_send, "dp", 1)]

    kv_total, branch_near, got[0] = lax.optimization_barrier(
        (kv_total, branch_near, got[0], up_terms, output_rows)
    )[:3]
    for back in kv_back:
        kv_total = kv_total + back
    key_grad = turn_back(kv_total[:size], cosine, sine)
    grad_kv_rows = jnp.concatenate([key_grad, kv_total[size:]], 0).astype(LOW)
    proj_rows = jnp.concatenate([grad_query_rows, grad_kv_rows], 0)
    grad_up = parity_sum(after(up_terms, proj_rows), 0)
    proj_theirs = flip(proj_rows, "dp", 1)

    own_order = pick(proj_rows, [spot ^ m for m in ROW_MASKS], len(tp_masks), 1)
    wide = w_query.shape[1]

    def one_terms(lo, hi):
        cut = own_order[:, lo * own_rows : hi * own_rows]
        return dot(cut[:wide], w_query, 0, 1) + dot(cut[wide:], w_kv, 0, 0)

    grad_normed_one, one_far_send = near_sum(one_terms)
    one_far = flip(one_far_send, "tp", 2)

    branch_theirs = jnp.concatenate([branch_near, flip(branch_near, "tp", 1)], 0)
    hidden_late = after(hidden, one_far_send)
    count //= 2
    for b in near_bits[1:]:
        send = down_terms(count // 2, count).astype(jnp.float32)
        for other in got:
            send = send + other[count // 2 * block : count * block]
        got.append(flip(send.astype(LOW), "dp", 1 << b))
        count //= 2
    grad_down = down_terms(0, 1).astype(jnp.float32)
    grad_normed_one = after(grad_normed_one, send, grad_down) + one_far
    grad_in_norm, gain_one = norm_back(grad_normed_one, own_inputs, own(scale_one), norm1_gain)
    input_rows = grad_middle + grad_in_norm
    grad_gate = grad_gate.astype(jnp.float32)

    proj_late = after(proj_rows, input_rows, grad_gate)
    last_terms = jnp.concatenate(
        [
            weight_terms(halves[0], 0, normed_one, one_theirs, proj_late, proj_theirs, True),
            weight_terms(halves[0], 0, branch_all, branch_theirs, attended, att_theirs, True),
        ],
        1,
    )
    grad_up = grad_up.astype(jnp.float32)
    grad_last = parity_sum(last_terms, 0).astype(jnp.float32)
    narrow = wide + 2 * size

    for other in got:
        grad_down = grad_down + other[:block]

    gains = jnp.stack([gain_one, gain_two])
    for m in (1, 2):
        gains = gains + flip(gains, "tp", m)
    gains = pick(gains, [place ^ m for m in range(dp)], dp, 1)
    count = dp
    while count > 1:
        count //= 2
        gains = gains[:, : count * block] + flip(gains[:, count * block :], "dp", count)

    return (
        output_rows,
        input_rows,
        gains[0],
        grad_last[:, :wide],
        grad_last[:, wide : wide + size],
        grad_last[:, wide + size : narrow],
        grad_last[:, narrow:].T,
        gains[1],
        grad_gate,
        grad_up,
        grad_down.T,
    )


def solution(mesh):
    placed = (
        P("dp", None),
        P("dp"),
        P(),
        P(None, "tp"),
        P(None, "tp"),
        P(None, "tp"),
        P("tp", None),
        P(),
        P(None, "tp"),
        P(None, "tp"),
        P("tp", None),
        P("dp", None),
    )
    return jax.shard_map(
        shards,
        mesh=mesh,
        in_specs=placed,
        out_specs=(
            P(("dp", "tp"), None),
            P(("dp", "tp"), None),
            P("dp"),
            P("dp", "tp"),
            P("dp", "tp"),
            P("dp", "tp"),
            P("tp", "dp"),
            P("dp"),
            P("dp", "tp"),
            P("dp", "tp"),
            P("tp", "dp"),
        ),
        check_vma=False,
    )
```

```python
import functools

import jax
import jax.numpy as jnp
from jax import lax
from jax.experimental import pallas as pl
from jax.experimental.pallas import tpu as pltpu
from jax.sharding import PartitionSpec as P

SPAN = 4
EPSILON = 1e-05
FAR_BELOW = -1e30
LOW = jnp.bfloat16
ROW_MASKS = (0, 2, 1, 3)


def flip(block, axis, mask):
    return lax.ppermute(block, axis, [(i, i ^ mask) for i in range(lax.axis_size(axis))])


def dot(left, right, left_dim, right_dim):
    return lax.dot_general(
        left,
        right,
        (((left_dim,), (right_dim,)), ((), ())),
        preferred_element_type=jnp.float32,
    )


def own_mask(pos, begin, keys, queries):
    key_at = lax.broadcasted_iota(jnp.int32, (keys, queries), 0)
    query_at = lax.broadcasted_iota(jnp.int32, (keys, queries), 1) + begin
    return (key_at <= query_at) & (key_at >= query_at - pos)


def row_starts(spot, rows):
    part = rows // len(ROW_MASKS)
    return [pl.multiple_of((spot ^ m) * part, part) for m in ROW_MASKS]


def forward_kernel(
    heads,
    size,
    at_ref,
    pos_ref,
    q_ref,
    kv0,
    kv1,
    kv2,
    kv3,
    o_ref,
    lse_ref,
    keys,
    vals,
    top,
    acc,
    ordered,
):
    rank, spot = at_ref[0], at_ref[1]
    rows = pos_ref.shape[1]
    half = rows // 2

    @pl.when(pl.program_id(0) == 0)
    def _():
        for m, kv in enumerate((kv0, kv1, kv2, kv3)):
            keys[m] = kv[:size, :].T
            vals[m, :size, :] = kv[size:, :]
            vals[m, size:, :] = jnp.ones((16, rows), LOW)

    pos = pos_ref[...]
    for part in range(2):
        cols = slice(part * half, (part + 1) * half)
        count = (part + 1) * half
        mask = own_mask(pos[:, cols], part * half, count, half)
        for h in range(heads):
            scores = dot(keys[0, :count, :], q_ref[h * size : (h + 1) * size, cols], 1, 0)
            scores = jnp.where(mask, scores, FAR_BELOW)
            peak = jnp.max(scores, 0, keepdims=True)
            weights = jnp.exp(scores - peak).astype(LOW)
            acc[h, :, cols] = dot(vals[0, :, :count], weights, 1, 0)
            top[h, :, cols] = peak
    seen = pos > lax.broadcasted_iota(jnp.int32, (1, rows), 1)
    for m in range(1, SPAN):

        @pl.when((rank ^ m) < rank)
        def _():
            for h in range(heads):
                scores = dot(keys[m], q_ref[h * size : (h + 1) * size, :], 1, 0)
                old = top[h]
                peak = jnp.where(seen, jnp.maximum(old, jnp.max(scores, 0, keepdims=True)), old)
                weights = jnp.exp(scores - jnp.where(seen, peak, -FAR_BELOW)).astype(LOW)
                acc[h] = acc[h] * jnp.exp(old - peak) + dot(vals[m], weights, 1, 0)
                top[h] = peak

    for h in range(heads):
        total = acc[h, size : size + 1, :]
        ordered[h * size : (h + 1) * size, :] = (acc[h, :size, :] / total).astype(LOW)
        lse_ref[h] = top[h] + jnp.log(total)
    for j, start in enumerate(row_starts(spot, rows)):
        part = rows // len(ROW_MASKS)
        o_ref[:, j * part : (j + 1) * part] = ordered[:, pl.ds(start, part)]


def backward_kernel(
    heads,
    size,
    at_ref,
    pos_ref,
    q_ref,
    do_in,
    o_in,
    lse_ref,
    cos_ref,
    sin_ref,
    kv0,
    kv1,
    kv2,
    kv3,
    dq_ref,
    g0,
    g1,
    g2,
    g3,
    keys,
    vals,
    dq,
    total,
    do_ref,
    o_ref,
):
    rank, spot = at_ref[0], at_ref[1]
    rows = pos_ref.shape[1]
    half = rows // 2
    blocks = (kv0, kv1, kv2, kv3)
    step = pl.program_id(0)

    @pl.when(step == 0)
    def _():
        for m, kv in enumerate(blocks):
            keys[m] = kv[:size, :].T
            vals[m] = kv[size:, :].T
        total[...] = jnp.zeros_like(total)

    part = rows // len(ROW_MASKS)
    for j, start in enumerate(row_starts(spot, rows)):
        do_ref[:, pl.ds(start, part)] = do_in[:, j * part : (j + 1) * part]
        o_ref[:, pl.ds(start, part)] = o_in[:, j * part : (j + 1) * part]
    pos = pos_ref[...]
    seen = pos > lax.broadcasted_iota(jnp.int32, (1, rows), 1)
    deltas = []
    for h in range(heads):
        span = slice(h * size, (h + 1) * size)
        deltas.append(
            jnp.sum(
                do_ref[span, :].astype(jnp.float32) * o_ref[span, :].astype(jnp.float32),
                0,
                keepdims=True,
            )
        )
    for part in range(2):
        cols = slice(part * half, (part + 1) * half)
        count = (part + 1) * half
        mask = own_mask(pos[:, cols], part * half, count, half)
        for h in range(heads):
            span = slice(h * size, (h + 1) * size)
            query, grad = q_ref[span, cols], do_ref[span, cols]
            scores = dot(keys[0, :count, :], query, 1, 0)
            probs = jnp.exp(jnp.where(mask, scores, FAR_BELOW) - lse_ref[h, :, cols])
            grad_probs = dot(vals[0, :count, :], grad, 1, 0)
            grad_scores = (probs * (grad_probs - deltas[h][:, cols])).astype(LOW)
            total[0, :size, :count] += dot(query, grad_scores, 1, 1)
            total[0, size:, :count] += dot(grad, probs.astype(LOW), 1, 1)
            dq[h, :, cols] = dot(kv0[:size, :count], grad_scores, 1, 0)
    for m in range(1, SPAN):

        @pl.when((rank ^ m) < rank)
        def _():
            for h in range(heads):
                span = slice(h * size, (h + 1) * size)
                query, grad = q_ref[span, :], do_ref[span, :]
                scores = dot(keys[m], query, 1, 0)
                probs = jnp.exp(scores - jnp.where(seen, lse_ref[h], -FAR_BELOW))
                grad_probs = dot(vals[m], grad, 1, 0)
                grad_scores = (probs * (grad_probs - deltas[h])).astype(LOW)
                total[m, :size, :] += dot(query, grad_scores, 1, 1)
                total[m, size:, :] += dot(grad, probs.astype(LOW), 1, 1)
                dq[h] += dot(blocks[m][:size, :], grad_scores, 1, 0)

    middle_at = size // 2
    cosine, sine = cos_ref[...], sin_ref[...]
    for h in range(heads):
        first = dq[h, :middle_at, :] * size ** (-0.5)
        second = dq[h, middle_at:, :] * size ** (-0.5)
        base = h * size
        dq_ref[base : base + middle_at, :] = (first * cosine + second * sine).astype(LOW)
        dq_ref[base + middle_at : base + size, :] = (second * cosine - first * sine).astype(LOW)

    @pl.when(step == pl.num_programs(0) - 1)
    def _():
        g0[...] = total[0]
        for m, out in ((1, g1), (2, g2), (3, g3)):
            out[...] = total[m].astype(LOW)


def attention_forward(at, pos, queries, blocks, size, heads):
    wide, rows = queries.shape
    count = wide // size
    whole = pl.BlockSpec((2 * size, rows), lambda i, r: (0, 0))
    some = pl.BlockSpec((heads * size, rows), lambda i, r: (i, 0))
    return pl.pallas_call(
        functools.partial(forward_kernel, heads, size),
        out_shape=(
            jax.ShapeDtypeStruct((wide, rows), LOW),
            jax.ShapeDtypeStruct((count, 1, rows), jnp.float32),
        ),
        grid_spec=pltpu.PrefetchScalarGridSpec(
            num_scalar_prefetch=1,
            grid=(count // heads,),
            in_specs=[pl.BlockSpec((1, rows), lambda i, r: (0, 0)), some] + [whole] * SPAN,
            out_specs=[some, pl.BlockSpec((heads, 1, rows), lambda i, r: (i, 0, 0))],
            scratch_shapes=[
                pltpu.VMEM((SPAN, rows, size), LOW),
                pltpu.VMEM((SPAN, size + 16, rows), LOW),
                pltpu.VMEM((heads, 1, rows), jnp.float32),
                pltpu.VMEM((heads, size + 16, rows), jnp.float32),
                pltpu.VMEM((heads * size, rows), LOW),
            ],
        ),
        compiler_params=pltpu.CompilerParams(vmem_limit_bytes=24 << 20),
        cost_estimate=pl.CostEstimate(
            flops=32 * wide * rows * rows * SPAN,
            bytes_accessed=4 * wide * rows,
            transcendentals=0,
        ),
        name="attention_forward",
    )(at, pos, queries, *blocks)


def attention_backward(at, pos, queries, grads, attended, lse, cosine, sine, blocks, size, heads):
    wide, rows = queries.shape
    count = wide // size
    whole = pl.BlockSpec((2 * size, rows), lambda i, r: (0, 0))
    table = pl.BlockSpec((size // 2, rows), lambda i, r: (0, 0))
    some = pl.BlockSpec((heads * size, rows), lambda i, r: (i, 0))
    return pl.pallas_call(
        functools.partial(backward_kernel, heads, size),
        out_shape=(
            jax.ShapeDtypeStruct((wide, rows), LOW),
            jax.ShapeDtypeStruct((2 * size, rows), jnp.float32),
        )
        + (jax.ShapeDtypeStruct((2 * size, rows), LOW),) * (SPAN - 1),
        grid_spec=pltpu.PrefetchScalarGridSpec(
            num_scalar_prefetch=1,
            grid=(count // heads,),
            in_specs=[
                pl.BlockSpec((1, rows), lambda i, r: (0, 0)),
                some,
                some,
                some,
                pl.BlockSpec((heads, 1, rows), lambda i, r: (i, 0, 0)),
                table,
                table,
            ]
            + [whole] * SPAN,
            out_specs=[some] + [whole] * SPAN,
            scratch_shapes=[
                pltpu.VMEM((SPAN, rows, size), LOW),
                pltpu.VMEM((SPAN, rows, size), LOW),
                pltpu.VMEM((heads, size, rows), jnp.float32),
                pltpu.VMEM((SPAN, 2 * size, rows), jnp.float32),
                pltpu.VMEM((heads * size, rows), LOW),
                pltpu.VMEM((heads * size, rows), LOW),
            ],
        ),
        compiler_params=pltpu.CompilerParams(vmem_limit_bytes=24 << 20),
        cost_estimate=pl.CostEstimate(
            flops=48 * wide * rows * rows * SPAN,
            bytes_accessed=10 * wide * rows,
            transcendentals=0,
        ),
        name="attention_backward",
    )(at, pos, queries, grads, attended, lse, cosine, sine, *blocks)


def pick(values, places, blocks, dim):
    size = values.shape[dim] // blocks
    return jnp.concatenate(
        [lax.dynamic_slice_in_dim(values, p * size, size, dim) for p in places], dim
    )


def after(value, *others):
    return lax.optimization_barrier((value, *others))[0]


def parity_sum(terms, dim):
    count = lax.axis_size("dp")
    groups = [list(range(p, count, 2)) for p in range(2)]
    return lax.psum_scatter(
        terms.astype(LOW), "dp", scatter_dimension=dim, axis_index_groups=groups, tiled=True
    )


def terms_kernel(transposed, places, x, x_far, g, g_far, out):
    del places
    side = 1 if transposed else 0
    out[...] = (dot(x[...], g[...], 0, side) + dot(x_far[...], g_far[...], 0, side)).astype(LOW)


def weight_terms(places, first, x, x_far, g, g_far, transposed=False):
    count = len(places)
    blocks = lax.axis_size("dp")
    size = x.shape[1] // blocks
    rows = x.shape[0]
    units = g.shape[0] if transposed else g.shape[1]
    if size % 128:
        side = 1 if transposed else 0
        far = x_far[:, first * size : (first + count) * size]
        return (dot(pick(x, places, blocks, 1), g, 0, side) + dot(far, g_far, 0, side)).astype(LOW)
    whole = pl.BlockSpec(g.shape, lambda i, p: (0, 0))
    return pl.pallas_call(
        functools.partial(terms_kernel, transposed),
        out_shape=jax.ShapeDtypeStruct((count * size, units), LOW),
        grid_spec=pltpu.PrefetchScalarGridSpec(
            num_scalar_prefetch=1,
            grid=(count,),
            in_specs=[
                pl.BlockSpec((rows, size), lambda i, p: (0, p[i])),
                pl.BlockSpec((rows, size), lambda i, p: (0, first + i)),
                whole,
                whole,
            ],
            out_specs=pl.BlockSpec((size, units), lambda i, p: (i, 0)),
        ),
        compiler_params=pltpu.CompilerParams(vmem_limit_bytes=24 << 20),
        cost_estimate=pl.CostEstimate(
            flops=8 * rows * count * size * units, bytes_accessed=4 * rows * units, transcendentals=0
        ),
        name="weight_terms",
    )(jnp.stack(places).astype(jnp.int32), x, x_far, g, g_far)


def row_kernel(left, right, send, kept):
    half = left.shape[0] // 2
    send[...] = dot(left[half:, :], right[...], 1, 0).astype(LOW)
    kept[...] = dot(left[:half, :], right[...], 1, 0)


def row_terms(left, right):
    rows, units = left.shape
    half, width = rows // 2, right.shape[1]
    step = 256
    return pl.pallas_call(
        row_kernel,
        out_shape=(
            jax.ShapeDtypeStruct((half, width), LOW),
            jax.ShapeDtypeStruct((half, width), jnp.float32),
        ),
        grid=(width // step,),
        in_specs=[
            pl.BlockSpec((rows, units), lambda i: (0, 0)),
            pl.BlockSpec((units, step), lambda i: (0, i)),
        ],
        out_specs=[pl.BlockSpec((half, step), lambda i: (0, i))] * 2,
        compiler_params=pltpu.CompilerParams(vmem_limit_bytes=16 << 20),
        cost_estimate=pl.CostEstimate(
            flops=8 * rows * units * width, bytes_accessed=2 * units * width, transcendentals=0
        ),
        name="row_terms",
    )(left, right)


def turn(values, cosine, sine):
    half = cosine.shape[0]
    heads = values.shape[0] // (2 * half)
    pieces = values.reshape(heads, 2, half, values.shape[1])
    first, second = pieces[:, 0], pieces[:, 1]
    return jnp.stack(
        [first * cosine - second * sine, second * cosine + first * sine], 1
    ).reshape(values.shape)


def turn_back(grads, cosine, sine):
    return turn(grads, cosine, -sine)


def norm_back(grad_rows, values, scale_rows, gain):
    scaled = grad_rows * gain
    inner_mean = jnp.mean(scaled * values, -1, keepdims=True)
    return (
        scale_rows * (scaled - values * scale_rows * scale_rows * inner_mean),
        jnp.sum(grad_rows * values * scale_rows, 0),
    )


def shards(
    tokens,
    positions,
    norm1_gain,
    w_query,
    w_key,
    w_value,
    w_out,
    norm2_gain,
    w_gate,
    w_up,
    w_down,
    cotangent,
):
    rows_here, width = tokens.shape
    size = w_key.shape[1]
    dp = lax.axis_size("dp")
    place = lax.axis_index("dp")
    spot = lax.axis_index("tp")
    tp_masks = range(lax.axis_size("tp"))
    own_rows = rows_here // lax.axis_size("tp")
    block = width // dp
    at = jnp.stack([place % SPAN, spot]).astype(jnp.int32)
    pos = positions.reshape(1, rows_here)

    def own(values):
        return lax.dynamic_slice_in_dim(values, spot * own_rows, own_rows, 0)

    inputs = tokens.astype(jnp.float32)
    scale_one = lax.rsqrt(jnp.mean(inputs * inputs, -1, keepdims=True) + EPSILON)
    normed_one = (inputs * scale_one * norm1_gain).astype(LOW)
    half = size // 2
    frequency = jnp.exp(
        -jnp.log(10000.0) * (2.0 * jnp.arange(half, dtype=jnp.float32) / size)
    )
    angles = frequency[:, None] * positions.astype(jnp.float32)[None, :]
    cosine, sine = jnp.cos(angles), jnp.sin(angles)
    w_kv = jnp.concatenate([w_key.T, w_value.T], 0)
    paired = dot(w_kv, normed_one, 1, 1)
    paired = jnp.concatenate([turn(paired[:size], cosine, sine), paired[size:]], 0).astype(LOW)
    blocks = [paired] + [flip(paired, "dp", m) for m in range(1, SPAN)]
    queries = (turn(dot(w_query, normed_one, 0, 1), cosine, sine) * size ** (-0.5)).astype(LOW)

    bit = place % 2
    bits = dp.bit_length() - 1

    halves = [[2 * j + which for j in range(dp // 2)] for which in (bit, 1 - bit)]

    def columns(values, which):
        return pick(values, halves[which], dp, 1)

    near_bits = [0] + list(range(2, bits))
    near_masks = [
        sum(((j >> (len(near_bits) - 1 - k)) & 1) << b for k, b in enumerate(near_bits))
        for j in range(dp // 2)
    ]

    near_halves = [[where ^ m for m in near_masks] for where in (place, place ^ 2)]

    def rows_of(values, lo, hi):
        return values[lo * own_rows : hi * own_rows]

    def near_sum(part):
        send = part(2, 4).astype(LOW)
        near, kept = lax.optimization_barrier((flip(send, "tp", 1), part(0, 2)))
        pair = kept + near
        return pair[:own_rows], pair[own_rows:].astype(LOW)

    one_send = columns(after(normed_one, paired), 1)
    one_theirs = flip(one_send, "dp", 1)
    queries = after(queries, one_send)
    attended, lse = attention_forward(at, pos, queries, blocks, size, 2)
    attended = after(attended, one_theirs)

    def branch_terms(lo, hi):
        return dot(attended[:, lo * own_rows : hi * own_rows], w_out, 0, 0)

    branch, branch_send = near_sum(branch_terms)
    branch_far = flip(branch_send, "tp", 2)
    att_theirs = flip(after(attended, branch_send), "dp", 1)
    cot = pick(after(cotangent, branch_send), [spot ^ m for m in ROW_MASKS], len(tp_masks), 0)
    cot_send = pick(cot, near_halves[1], dp, 1)
    cot_theirs = flip(cot_send, "dp", 2)
    branch = after(branch, cot_send)

    own_inputs = own(tokens).astype(jnp.float32)
    middle = own_inputs + (branch + branch_far)
    scale_two = lax.rsqrt(jnp.mean(middle * middle, -1, keepdims=True) + EPSILON)
    own_two = (middle * scale_two * norm2_gain).astype(LOW)
    far_two = flip(own_two, "tp", 2)
    grad_hidden = dot(after(cot, own_two), w_down, 1, 1)
    pair_two = jnp.concatenate([after(own_two, grad_hidden, att_theirs), far_two], 0)
    core_two = flip(pair_two, "tp", 1)
    two_send = columns(pair_two, 1)
    two_near = flip(two_send, "dp", 1)
    normed_two = jnp.concatenate([after(pair_two, two_send), core_two], 0)

    gate_pre = dot(normed_two, w_gate, 1, 0)
    up_pre = dot(normed_two, w_up, 1, 0)
    sigma = jax.nn.sigmoid(gate_pre)
    active = gate_pre * sigma
    hidden = (active * up_pre).astype(LOW)
    grad_gate_pre = (grad_hidden * up_pre * sigma * (1.0 + gate_pre * (1.0 - sigma))).astype(LOW)
    grad_up_pre = (grad_hidden * active).astype(LOW)
    hidden_theirs = flip(hidden, "dp", 2)
    gate_theirs = flip(grad_gate_pre, "dp", 1)

    gate_late, cot_theirs, two_near = lax.optimization_barrier(
        (grad_gate_pre, cot_theirs, two_near)
    )
    two_theirs = jnp.concatenate([two_near, flip(two_near, "tp", 1)], 0)

    def two_terms(lo, hi):
        return dot(rows_of(gate_late, lo, hi), w_gate, 1, 1) + dot(
            rows_of(grad_up_pre, lo, hi), w_up, 1, 1
        )

    grad_normed_two, two_far_send = near_sum(two_terms)
    two_far_send, two_theirs = lax.optimization_barrier((two_far_send, two_theirs))
    two_far = flip(two_far_send, "tp", 2)

    hidden_late = after(hidden, two_far_send)
    down_near, down = row_terms(hidden_late, w_down)
    up_theirs = flip(grad_up_pre, "dp", 1)
    grad_normed_two = after(grad_normed_two, down) + two_far

    grad_mid_norm, gain_two = norm_back(grad_normed_two, middle, scale_two, norm2_gain)
    grad_middle = own(cotangent).astype(jnp.float32) + grad_mid_norm
    branch_grad = grad_middle.astype(LOW)
    grad_far = flip(branch_grad, "tp", 2)

    hidden_late = after(hidden, branch_grad)

    def down_terms(lo, hi):
        return weight_terms(
            near_halves[0][lo:hi], lo, cot, cot_theirs, hidden_late, hidden_theirs
        )

    count = dp // 2
    first_send = down_terms(count // 2, count)
    down_near = flip(after(down_near, branch_grad), "tp", 1)
    grad_pair = jnp.concatenate([after(branch_grad, first_send), grad_far], 0)
    grad_core = flip(grad_pair, "tp", 1)

    branch_send = columns(grad_pair, 1)
    branch_near = flip(branch_send, "dp", 1)
    two_late = after(normed_two, branch_send)
    gate_terms = weight_terms(halves[0], 0, two_late, two_theirs, grad_gate_pre, gate_theirs)
    branch_all = jnp.concatenate([after(grad_pair, gate_terms), grad_core], 0)
    grad_attended = dot(w_out, branch_all, 1, 1).astype(LOW)
    grad_gate = parity_sum(after(gate_terms, grad_attended), 0)

    grads = attention_backward(
        at, pos, queries, grad_attended, attended, lse, cosine, sine, blocks, size, 2
    )
    grad_query_rows, kv_total = grads[0], grads[1]
    kv_back = [flip(grads[m + 1], "dp", m) for m in range(1, SPAN)]

    up_late = after(grad_up_pre, grad_query_rows)
    up_terms = weight_terms(halves[0], 0, normed_two, two_theirs, up_late, up_theirs)
    down = down + after(down_near, grad_query_rows)
    down, down_send = down[:own_rows], down[own_rows:].astype(LOW)
    down_far = flip(down_send, "tp", 2)
    got = [flip(after(first_send, up_terms), "dp", 1)]

    kv_total, branch_near = lax.optimization_barrier(
        (kv_total, branch_near, up_terms, down_send)
    )[:2]
    for back in kv_back:
        kv_total = kv_total + back
    key_grad = turn_back(kv_total[:size], cosine, sine)
    grad_kv_rows = jnp.concatenate([key_grad, kv_total[size:]], 0).astype(LOW)
    proj_rows = jnp.concatenate([grad_query_rows, grad_kv_rows], 0)
    grad_up = parity_sum(after(up_terms, proj_rows), 0)
    proj_theirs = flip(proj_rows, "dp", 1)

    own_order = pick(proj_rows, [spot ^ m for m in ROW_MASKS], len(tp_masks), 1)
    wide = w_query.shape[1]

    def one_terms(lo, hi):
        cut = own_order[:, lo * own_rows : hi * own_rows]
        return dot(cut[:wide], w_query, 0, 1) + dot(cut[wide:], w_kv, 0, 0)

    grad_normed_one, one_far_send = near_sum(one_terms)
    one_far = flip(one_far_send, "tp", 2)

    branch_theirs = jnp.concatenate([branch_near, flip(branch_near, "tp", 1)], 0)
    hidden_late = after(hidden, one_far_send)
    count //= 2
    for b in near_bits[1:]:
        send = down_terms(count // 2, count).astype(jnp.float32)
        for other in got:
            send = send + other[count // 2 * block : count * block]
        got.append(flip(send.astype(LOW), "dp", 1 << b))
        count //= 2
    grad_down = down_terms(0, 1).astype(jnp.float32)
    output_rows = (middle + (down + after(down_far, one_far_send))).astype(LOW)
    grad_normed_one = after(grad_normed_one, send, grad_down, output_rows) + one_far
    grad_in_norm, gain_one = norm_back(grad_normed_one, own_inputs, own(scale_one), norm1_gain)
    input_rows = grad_middle + grad_in_norm
    grad_gate = grad_gate.astype(jnp.float32)

    proj_late = after(proj_rows, input_rows, grad_gate)
    last_terms = jnp.concatenate(
        [
            weight_terms(halves[0], 0, normed_one, one_theirs, proj_late, proj_theirs, True),
            weight_terms(halves[0], 0, branch_all, branch_theirs, attended, att_theirs, True),
        ],
        1,
    )
    grad_up = grad_up.astype(jnp.float32)
    grad_last = parity_sum(last_terms, 0).astype(jnp.float32)
    narrow = wide + 2 * size

    for other in got:
        grad_down = grad_down + other[:block]

    gains = jnp.stack([gain_one, gain_two])
    for m in (1, 2):
        gains = gains + flip(gains, "tp", m)
    gains = pick(gains, [place ^ m for m in range(dp)], dp, 1)
    count = dp
    while count > 1:
        count //= 2
        gains = gains[:, : count * block] + flip(gains[:, count * block :], "dp", count)

    return (
        output_rows,
        input_rows,
        gains[0],
        grad_last[:, :wide],
        grad_last[:, wide : wide + size],
        grad_last[:, wide + size : narrow],
        grad_last[:, narrow:].T,
        gains[1],
        grad_gate,
        grad_up,
        grad_down.T,
    )


def solution(mesh):
    placed = (
        P("dp", None),
        P("dp"),
        P(),
        P(None, "tp"),
        P(None, "tp"),
        P(None, "tp"),
        P("tp", None),
        P(),
        P(None, "tp"),
        P(None, "tp"),
        P("tp", None),
        P("dp", None),
    )
    return jax.shard_map(
        shards,
        mesh=mesh,
        in_specs=placed,
        out_specs=(
            P(("dp", "tp"), None),
            P(("dp", "tp"), None),
            P("dp"),
            P("dp", "tp"),
            P("dp", "tp"),
            P("dp", "tp"),
            P("tp", "dp"),
            P("dp"),
            P("dp", "tp"),
            P("dp", "tp"),
            P("tp", "dp"),
        ),
        check_vma=False,
    )
```

```python
import functools

import jax
import jax.numpy as jnp
from jax import lax
from jax.experimental import pallas as pl
from jax.experimental.pallas import tpu as pltpu
from jax.sharding import PartitionSpec as P

SPAN = 4
EPSILON = 1e-05
FAR_BELOW = -1e30
LOW = jnp.bfloat16
ROW_MASKS = (0, 2, 1, 3)


def flip(block, axis, mask):
    return lax.ppermute(block, axis, [(i, i ^ mask) for i in range(lax.axis_size(axis))])


def dot(left, right, left_dim, right_dim):
    return lax.dot_general(
        left,
        right,
        (((left_dim,), (right_dim,)), ((), ())),
        preferred_element_type=jnp.float32,
    )


def in_hbm(*arrays):
    return [pltpu.with_memory_space_constraint(a, pltpu.HBM) for a in arrays]


def own_mask(pos, begin, keys, queries):
    key_at = lax.broadcasted_iota(jnp.int32, (keys, queries), 0)
    query_at = lax.broadcasted_iota(jnp.int32, (keys, queries), 1) + begin
    return (key_at <= query_at) & (key_at >= query_at - pos)


def row_starts(spot, rows):
    part = rows // len(ROW_MASKS)
    return [pl.multiple_of((spot ^ m) * part, part) for m in ROW_MASKS]


def forward_kernel(
    heads,
    size,
    at_ref,
    pos_ref,
    q_ref,
    kv0,
    kv1,
    kv2,
    kv3,
    o_ref,
    lse_ref,
    keys,
    vals,
    top,
    acc,
    ordered,
):
    rank, spot = at_ref[0], at_ref[1]
    rows = pos_ref.shape[1]
    half = rows // 2

    @pl.when(pl.program_id(0) == 0)
    def _():
        for m, kv in enumerate((kv0, kv1, kv2, kv3)):
            keys[m] = kv[:size, :].T
            vals[m, :size, :] = kv[size:, :]
            vals[m, size:, :] = jnp.ones((16, rows), LOW)

    pos = pos_ref[...]
    for part in range(2):
        cols = slice(part * half, (part + 1) * half)
        count = (part + 1) * half
        mask = own_mask(pos[:, cols], part * half, count, half)
        for h in range(heads):
            scores = dot(keys[0, :count, :], q_ref[h * size : (h + 1) * size, cols], 1, 0)
            scores = jnp.where(mask, scores, FAR_BELOW)
            peak = jnp.max(scores, 0, keepdims=True)
            weights = jnp.exp(scores - peak).astype(LOW)
            acc[h, :, cols] = dot(vals[0, :, :count], weights, 1, 0)
            top[h, :, cols] = peak
    seen = pos > lax.broadcasted_iota(jnp.int32, (1, rows), 1)
    for m in range(1, SPAN):

        @pl.when((rank ^ m) < rank)
        def _():
            for h in range(heads):
                scores = dot(keys[m], q_ref[h * size : (h + 1) * size, :], 1, 0)
                old = top[h]
                peak = jnp.where(seen, jnp.maximum(old, jnp.max(scores, 0, keepdims=True)), old)
                weights = jnp.exp(scores - jnp.where(seen, peak, -FAR_BELOW)).astype(LOW)
                acc[h] = acc[h] * jnp.exp(old - peak) + dot(vals[m], weights, 1, 0)
                top[h] = peak

    for h in range(heads):
        total = acc[h, size : size + 1, :]
        ordered[h * size : (h + 1) * size, :] = (acc[h, :size, :] / total).astype(LOW)
        lse_ref[h] = top[h] + jnp.log(total)
    for j, start in enumerate(row_starts(spot, rows)):
        part = rows // len(ROW_MASKS)
        o_ref[:, j * part : (j + 1) * part] = ordered[:, pl.ds(start, part)]


def backward_kernel(
    heads,
    size,
    at_ref,
    pos_ref,
    q_ref,
    do_in,
    o_in,
    lse_ref,
    cos_ref,
    sin_ref,
    kv0,
    kv1,
    kv2,
    kv3,
    dq_ref,
    g0,
    g1,
    g2,
    g3,
    keys,
    vals,
    dq,
    total,
    do_ref,
    o_ref,
):
    rank, spot = at_ref[0], at_ref[1]
    rows = pos_ref.shape[1]
    half = rows // 2
    blocks = (kv0, kv1, kv2, kv3)
    step = pl.program_id(0)

    @pl.when(step == 0)
    def _():
        for m, kv in enumerate(blocks):
            keys[m] = kv[:size, :].T
            vals[m] = kv[size:, :].T
        total[...] = jnp.zeros_like(total)

    part = rows // len(ROW_MASKS)
    for j, start in enumerate(row_starts(spot, rows)):
        do_ref[:, pl.ds(start, part)] = do_in[:, j * part : (j + 1) * part]
        o_ref[:, pl.ds(start, part)] = o_in[:, j * part : (j + 1) * part]
    pos = pos_ref[...]
    seen = pos > lax.broadcasted_iota(jnp.int32, (1, rows), 1)
    deltas = []
    for h in range(heads):
        span = slice(h * size, (h + 1) * size)
        deltas.append(
            jnp.sum(
                do_ref[span, :].astype(jnp.float32) * o_ref[span, :].astype(jnp.float32),
                0,
                keepdims=True,
            )
        )
    for part in range(2):
        cols = slice(part * half, (part + 1) * half)
        count = (part + 1) * half
        mask = own_mask(pos[:, cols], part * half, count, half)
        for h in range(heads):
            span = slice(h * size, (h + 1) * size)
            query, grad = q_ref[span, cols], do_ref[span, cols]
            scores = dot(keys[0, :count, :], query, 1, 0)
            probs = jnp.exp(jnp.where(mask, scores, FAR_BELOW) - lse_ref[h, :, cols])
            grad_probs = dot(vals[0, :count, :], grad, 1, 0)
            grad_scores = (probs * (grad_probs - deltas[h][:, cols])).astype(LOW)
            total[0, :size, :count] += dot(query, grad_scores, 1, 1)
            total[0, size:, :count] += dot(grad, probs.astype(LOW), 1, 1)
            dq[h, :, cols] = dot(kv0[:size, :count], grad_scores, 1, 0)
    for m in range(1, SPAN):

        @pl.when((rank ^ m) < rank)
        def _():
            for h in range(heads):
                span = slice(h * size, (h + 1) * size)
                query, grad = q_ref[span, :], do_ref[span, :]
                scores = dot(keys[m], query, 1, 0)
                probs = jnp.exp(scores - jnp.where(seen, lse_ref[h], -FAR_BELOW))
                grad_probs = dot(vals[m], grad, 1, 0)
                grad_scores = (probs * (grad_probs - deltas[h])).astype(LOW)
                total[m, :size, :] += dot(query, grad_scores, 1, 1)
                total[m, size:, :] += dot(grad, probs.astype(LOW), 1, 1)
                dq[h] += dot(blocks[m][:size, :], grad_scores, 1, 0)

    middle_at = size // 2
    cosine, sine = cos_ref[...], sin_ref[...]
    for h in range(heads):
        first = dq[h, :middle_at, :] * size ** (-0.5)
        second = dq[h, middle_at:, :] * size ** (-0.5)
        base = h * size
        dq_ref[base : base + middle_at, :] = (first * cosine + second * sine).astype(LOW)
        dq_ref[base + middle_at : base + size, :] = (second * cosine - first * sine).astype(LOW)

    @pl.when(step == pl.num_programs(0) - 1)
    def _():
        g0[...] = total[0]
        for m, out in ((1, g1), (2, g2), (3, g3)):
            out[...] = total[m].astype(LOW)


def attention_forward(at, pos, queries, blocks, size, heads):
    wide, rows = queries.shape
    count = wide // size
    whole = pl.BlockSpec((2 * size, rows), lambda i, r: (0, 0))
    some = pl.BlockSpec((heads * size, rows), lambda i, r: (i, 0))
    return pl.pallas_call(
        functools.partial(forward_kernel, heads, size),
        out_shape=(
            jax.ShapeDtypeStruct((wide, rows), LOW),
            jax.ShapeDtypeStruct((count, 1, rows), jnp.float32),
        ),
        grid_spec=pltpu.PrefetchScalarGridSpec(
            num_scalar_prefetch=1,
            grid=(count // heads,),
            in_specs=[pl.BlockSpec((1, rows), lambda i, r: (0, 0)), some] + [whole] * SPAN,
            out_specs=[some, pl.BlockSpec((heads, 1, rows), lambda i, r: (i, 0, 0))],
            scratch_shapes=[
                pltpu.VMEM((SPAN, rows, size), LOW),
                pltpu.VMEM((SPAN, size + 16, rows), LOW),
                pltpu.VMEM((heads, 1, rows), jnp.float32),
                pltpu.VMEM((heads, size + 16, rows), jnp.float32),
                pltpu.VMEM((heads * size, rows), LOW),
            ],
        ),
        compiler_params=pltpu.CompilerParams(vmem_limit_bytes=24 << 20),
        cost_estimate=pl.CostEstimate(
            flops=32 * wide * rows * rows * SPAN,
            bytes_accessed=4 * wide * rows,
            transcendentals=0,
        ),
        name="attention_forward",
    )(at, pos, queries, *blocks)


def attention_backward(at, pos, queries, grads, attended, lse, cosine, sine, blocks, size, heads):
    wide, rows = queries.shape
    count = wide // size
    whole = pl.BlockSpec((2 * size, rows), lambda i, r: (0, 0))
    table = pl.BlockSpec((size // 2, rows), lambda i, r: (0, 0))
    some = pl.BlockSpec((heads * size, rows), lambda i, r: (i, 0))
    return pl.pallas_call(
        functools.partial(backward_kernel, heads, size),
        out_shape=(
            jax.ShapeDtypeStruct((wide, rows), LOW),
            jax.ShapeDtypeStruct((2 * size, rows), jnp.float32),
        )
        + (jax.ShapeDtypeStruct((2 * size, rows), LOW),) * (SPAN - 1),
        grid_spec=pltpu.PrefetchScalarGridSpec(
            num_scalar_prefetch=1,
            grid=(count // heads,),
            in_specs=[
                pl.BlockSpec((1, rows), lambda i, r: (0, 0)),
                some,
                some,
                some,
                pl.BlockSpec((heads, 1, rows), lambda i, r: (i, 0, 0)),
                table,
                table,
            ]
            + [whole] * SPAN,
            out_specs=[some] + [whole] * SPAN,
            scratch_shapes=[
                pltpu.VMEM((SPAN, rows, size), LOW),
                pltpu.VMEM((SPAN, rows, size), LOW),
                pltpu.VMEM((heads, size, rows), jnp.float32),
                pltpu.VMEM((SPAN, 2 * size, rows), jnp.float32),
                pltpu.VMEM((heads * size, rows), LOW),
                pltpu.VMEM((heads * size, rows), LOW),
            ],
        ),
        compiler_params=pltpu.CompilerParams(vmem_limit_bytes=24 << 20),
        cost_estimate=pl.CostEstimate(
            flops=48 * wide * rows * rows * SPAN,
            bytes_accessed=10 * wide * rows,
            transcendentals=0,
        ),
        name="attention_backward",
    )(at, pos, *in_hbm(queries, grads, attended, lse, cosine, sine, *blocks))


def pick(values, places, blocks, dim):
    size = values.shape[dim] // blocks
    return jnp.concatenate(
        [lax.dynamic_slice_in_dim(values, p * size, size, dim) for p in places], dim
    )


def after(value, *others):
    return lax.optimization_barrier((value, *others))[0]


def parity_sum(terms, dim):
    count = lax.axis_size("dp")
    groups = [list(range(p, count, 2)) for p in range(2)]
    return lax.psum_scatter(
        terms.astype(LOW), "dp", scatter_dimension=dim, axis_index_groups=groups, tiled=True
    )


def terms_kernel(transposed, places, x, x_far, g, g_far, out):
    del places
    side = 1 if transposed else 0
    out[...] = (dot(x[...], g[...], 0, side) + dot(x_far[...], g_far[...], 0, side)).astype(LOW)


def weight_terms(places, first, x, x_far, g, g_far, transposed=False):
    count = len(places)
    blocks = lax.axis_size("dp")
    size = x.shape[1] // blocks
    rows = x.shape[0]
    units = g.shape[0] if transposed else g.shape[1]
    if size % 128:
        side = 1 if transposed else 0
        far = x_far[:, first * size : (first + count) * size]
        return (dot(pick(x, places, blocks, 1), g, 0, side) + dot(far, g_far, 0, side)).astype(LOW)
    whole = pl.BlockSpec(g.shape, lambda i, p: (0, 0))
    return pl.pallas_call(
        functools.partial(terms_kernel, transposed),
        out_shape=pltpu.HBM((count * size, units), LOW),
        grid_spec=pltpu.PrefetchScalarGridSpec(
            num_scalar_prefetch=1,
            grid=(count,),
            in_specs=[
                pl.BlockSpec((rows, size), lambda i, p: (0, p[i])),
                pl.BlockSpec((rows, size), lambda i, p: (0, first + i)),
                whole,
                whole,
            ],
            out_specs=pl.BlockSpec((size, units), lambda i, p: (i, 0)),
        ),
        compiler_params=pltpu.CompilerParams(vmem_limit_bytes=24 << 20),
        cost_estimate=pl.CostEstimate(
            flops=8 * rows * count * size * units, bytes_accessed=4 * rows * units, transcendentals=0
        ),
        name="weight_terms",
    )(jnp.stack(places).astype(jnp.int32), x, x_far, g, g_far)


def row_kernel(left, right, send, kept):
    half = left.shape[0] // 2
    send[...] = dot(left[half:, :], right[...], 1, 0).astype(LOW)
    kept[...] = dot(left[:half, :], right[...], 1, 0)


def row_terms(left, right):
    rows, units = left.shape
    half, width = rows // 2, right.shape[1]
    step = 256
    return pl.pallas_call(
        row_kernel,
        out_shape=(
            jax.ShapeDtypeStruct((half, width), LOW),
            jax.ShapeDtypeStruct((half, width), jnp.float32),
        ),
        grid=(width // step,),
        in_specs=[
            pl.BlockSpec((rows, units), lambda i: (0, 0)),
            pl.BlockSpec((units, step), lambda i: (0, i)),
        ],
        out_specs=[pl.BlockSpec((half, step), lambda i: (0, i))] * 2,
        compiler_params=pltpu.CompilerParams(vmem_limit_bytes=16 << 20),
        cost_estimate=pl.CostEstimate(
            flops=8 * rows * units * width, bytes_accessed=2 * units * width, transcendentals=0
        ),
        name="row_terms",
    )(left, right)


def turn(values, cosine, sine):
    half = cosine.shape[0]
    heads = values.shape[0] // (2 * half)
    pieces = values.reshape(heads, 2, half, values.shape[1])
    first, second = pieces[:, 0], pieces[:, 1]
    return jnp.stack(
        [first * cosine - second * sine, second * cosine + first * sine], 1
    ).reshape(values.shape)


def turn_back(grads, cosine, sine):
    return turn(grads, cosine, -sine)


def norm_back(grad_rows, values, scale_rows, gain):
    scaled = grad_rows * gain
    inner_mean = jnp.mean(scaled * values, -1, keepdims=True)
    return (
        scale_rows * (scaled - values * scale_rows * scale_rows * inner_mean),
        jnp.sum(grad_rows * values * scale_rows, 0),
    )


def shards(
    tokens,
    positions,
    norm1_gain,
    w_query,
    w_key,
    w_value,
    w_out,
    norm2_gain,
    w_gate,
    w_up,
    w_down,
    cotangent,
):
    rows_here, width = tokens.shape
    size = w_key.shape[1]
    dp = lax.axis_size("dp")
    place = lax.axis_index("dp")
    spot = lax.axis_index("tp")
    tp_masks = range(lax.axis_size("tp"))
    own_rows = rows_here // lax.axis_size("tp")
    block = width // dp
    at = jnp.stack([place % SPAN, spot]).astype(jnp.int32)
    pos = positions.reshape(1, rows_here)

    def own(values):
        return lax.dynamic_slice_in_dim(values, spot * own_rows, own_rows, 0)

    inputs = tokens.astype(jnp.float32)
    scale_one = lax.rsqrt(jnp.mean(inputs * inputs, -1, keepdims=True) + EPSILON)
    normed_one = (inputs * scale_one * norm1_gain).astype(LOW)
    half = size // 2
    frequency = jnp.exp(
        -jnp.log(10000.0) * (2.0 * jnp.arange(half, dtype=jnp.float32) / size)
    )
    angles = frequency[:, None] * positions.astype(jnp.float32)[None, :]
    cosine, sine = jnp.cos(angles), jnp.sin(angles)
    w_kv = jnp.concatenate([w_key.T, w_value.T], 0)
    paired = dot(w_kv, normed_one, 1, 1)
    paired = jnp.concatenate([turn(paired[:size], cosine, sine), paired[size:]], 0).astype(LOW)
    blocks = [paired] + [flip(paired, "dp", m) for m in range(1, SPAN)]
    queries = (turn(dot(w_query, normed_one, 0, 1), cosine, sine) * size ** (-0.5)).astype(LOW)

    bit = place % 2
    bits = dp.bit_length() - 1

    halves = [[2 * j + which for j in range(dp // 2)] for which in (bit, 1 - bit)]

    def columns(values, which):
        return pick(values, halves[which], dp, 1)

    near_bits = [0] + list(range(2, bits))
    near_masks = [
        sum(((j >> (len(near_bits) - 1 - k)) & 1) << b for k, b in enumerate(near_bits))
        for j in range(dp // 2)
    ]

    near_halves = [[where ^ m for m in near_masks] for where in (place, place ^ 2)]

    def rows_of(values, lo, hi):
        return values[lo * own_rows : hi * own_rows]

    def near_sum(part):
        send = part(2, 4).astype(LOW)
        near, kept = lax.optimization_barrier((flip(send, "tp", 1), part(0, 2)))
        pair = kept + near
        return pair[:own_rows], pair[own_rows:].astype(LOW)

    one_send = columns(after(normed_one, paired), 1)
    one_theirs = flip(one_send, "dp", 1)
    queries = after(queries, one_send)
    attended, lse = attention_forward(at, pos, queries, blocks, size, 2)
    attended = after(attended, one_theirs)

    def branch_terms(lo, hi):
        return dot(attended[:, lo * own_rows : hi * own_rows], w_out, 0, 0)

    branch, branch_send = near_sum(branch_terms)
    branch_far = flip(branch_send, "tp", 2)
    att_theirs = flip(after(attended, branch_send), "dp", 1)
    cot = pick(after(cotangent, branch_send), [spot ^ m for m in ROW_MASKS], len(tp_masks), 0)
    cot_send = pick(cot, near_halves[1], dp, 1)
    cot_theirs = flip(cot_send, "dp", 2)
    branch = after(branch, cot_send)

    own_inputs = own(tokens).astype(jnp.float32)
    middle = own_inputs + (branch + branch_far)
    scale_two = lax.rsqrt(jnp.mean(middle * middle, -1, keepdims=True) + EPSILON)
    own_two = (middle * scale_two * norm2_gain).astype(LOW)
    far_two = flip(own_two, "tp", 2)
    grad_hidden = dot(after(cot, own_two), w_down, 1, 1)
    pair_two = jnp.concatenate([after(own_two, grad_hidden, att_theirs), far_two], 0)
    core_two = flip(pair_two, "tp", 1)
    two_send, two_far_half = columns(pair_two, 1), pick(pair_two, near_halves[1], dp, 1)
    two_near, two_far_near = flip(two_send, "dp", 1), flip(two_far_half, "dp", 2)
    normed_two = jnp.concatenate([after(pair_two, two_send, two_far_half), core_two], 0)

    gate_pre = dot(normed_two, w_gate, 1, 0)
    up_pre = dot(normed_two, w_up, 1, 0)
    sigma = jax.nn.sigmoid(gate_pre)
    active = gate_pre * sigma
    hidden = (active * up_pre).astype(LOW)
    grad_gate_pre = (grad_hidden * up_pre * sigma * (1.0 + gate_pre * (1.0 - sigma))).astype(LOW)
    grad_up_pre = (grad_hidden * active).astype(LOW)
    hidden_theirs = flip(hidden, "dp", 2)
    gate_theirs = flip(grad_gate_pre, "dp", 1)

    gate_late, cot_theirs, two_near, two_far_near = lax.optimization_barrier(
        (grad_gate_pre, cot_theirs, two_near, two_far_near)
    )
    two_near = jnp.concatenate([two_near, two_far_near], 1)
    two_theirs = jnp.concatenate([two_near, flip(two_near, "tp", 1)], 0)

    def two_terms(lo, hi):
        return dot(rows_of(gate_late, lo, hi), w_gate, 1, 1) + dot(
            rows_of(grad_up_pre, lo, hi), w_up, 1, 1
        )

    grad_normed_two, two_far_send = near_sum(two_terms)
    two_far_send, two_theirs = lax.optimization_barrier((two_far_send, two_theirs))
    far_first = dp // 2
    two_far = flip(two_far_send, "tp", 2)

    hidden_late = after(hidden, two_far_send)
    down_near, down = row_terms(hidden_late, w_down)
    up_theirs = flip(grad_up_pre, "dp", 2)
    grad_normed_two = after(grad_normed_two, down) + two_far

    grad_mid_norm, gain_two = norm_back(grad_normed_two, middle, scale_two, norm2_gain)
    grad_middle = own(cotangent).astype(jnp.float32) + grad_mid_norm
    branch_grad = grad_middle.astype(LOW)
    grad_far = flip(branch_grad, "tp", 2)

    down_near = flip(after(down_near, branch_grad), "tp", 1)
    two_late = after(normed_two, branch_grad)
    gate_terms = weight_terms(halves[0], 0, two_late, two_theirs, grad_gate_pre, gate_theirs)
    grad_gate = parity_sum(gate_terms, 0)
    grad_pair = jnp.concatenate([after(branch_grad, gate_terms), grad_far], 0)
    grad_core = flip(grad_pair, "tp", 1)
    branch_send = columns(grad_pair, 1)
    branch_near = flip(branch_send, "dp", 1)

    def down_terms(lo, hi, *late):
        return weight_terms(
            near_halves[0][lo:hi], lo, cot, cot_theirs, after(hidden, *late), hidden_theirs
        )

    def up_terms(lo, hi, *late):
        return weight_terms(
            near_halves[0][lo:hi],
            far_first + lo,
            normed_two,
            two_theirs,
            after(grad_up_pre, *late),
            up_theirs,
        )

    count = dp // 2
    down_sent = [down_terms(count // 2, count, branch_send)]

    branch_all = jnp.concatenate([after(grad_pair, down_sent[0]), grad_core], 0)
    grad_attended = dot(w_out, branch_all, 1, 1).astype(LOW)

    grads = attention_backward(
        at, pos, queries, grad_attended, attended, lse, cosine, sine, blocks, size, 2
    )
    grad_query_rows, kv_total = grads[0], grads[1]
    kv_back = [flip(grads[m + 1], "dp", m) for m in range(1, SPAN)]

    down = down + after(down_near, grad_query_rows)
    down, down_send = down[:own_rows], down[own_rows:].astype(LOW)
    down_far = flip(down_send, "tp", 2)
    up_sent = [up_terms(count // 2, count, grad_query_rows)]
    down_got = [flip(down_sent[0], "dp", 1)]
    kv_total, branch_near, down_got[0] = lax.optimization_barrier(
        (kv_total, branch_near, down_got[0], up_sent[0], down_send)
    )[:3]
    for back in kv_back:
        kv_total = kv_total + back
    key_grad = turn_back(kv_total[:size], cosine, sine)
    grad_kv_rows = jnp.concatenate([key_grad, kv_total[size:]], 0).astype(LOW)
    proj_rows = jnp.concatenate([grad_query_rows, grad_kv_rows], 0)
    proj_theirs = flip(proj_rows, "dp", 1)

    own_order = pick(proj_rows, [spot ^ m for m in ROW_MASKS], len(tp_masks), 1)
    wide = w_query.shape[1]

    def one_terms(lo, hi):
        cut = own_order[:, lo * own_rows : hi * own_rows]
        return dot(cut[:wide], w_query, 0, 1) + dot(cut[wide:], w_kv, 0, 0)

    grad_normed_one, one_far_send = near_sum(one_terms)
    one_far = flip(one_far_send, "tp", 2)

    up_got = [flip(after(up_sent[0], one_far_send), "dp", 1)]
    branch_theirs = jnp.concatenate([branch_near, flip(branch_near, "tp", 1)], 0)
    out_late = after(attended, one_far_send)
    out_terms = weight_terms(halves[0], 0, branch_all, branch_theirs, out_late, att_theirs, True)
    grad_out = parity_sum(out_terms, 0)

    def exchange_rest(terms, got, late):
        left = count // 2
        for b in near_bits[1:]:
            send = terms(left // 2, left, late).astype(jnp.float32)
            for other in got:
                send = send + other[left // 2 * block : left * block]
            got.append(flip(send.astype(LOW), "dp", 1 << b))
            left //= 2
        return terms(0, 1, late), send

    grad_down, down_last = exchange_rest(down_terms, down_got, out_terms)
    output_rows = (middle + (down + after(down_far, one_far_send))).astype(LOW)
    grad_normed_one = after(grad_normed_one, down_last, grad_down, output_rows) + one_far
    grad_in_norm, gain_one = norm_back(grad_normed_one, own_inputs, own(scale_one), norm1_gain)
    input_rows = grad_middle + grad_in_norm
    grad_gate = grad_gate.astype(jnp.float32)

    proj_late = after(proj_rows, input_rows, grad_gate)
    proj_terms = weight_terms(halves[0], 0, normed_one, one_theirs, proj_late, proj_theirs, True)
    grad_out = grad_out.astype(jnp.float32)
    grad_proj = parity_sum(proj_terms, 0).astype(jnp.float32)

    grad_up, up_last = exchange_rest(up_terms, up_got, proj_terms)

    def total(kept, got):
        kept = kept.astype(jnp.float32)
        for other in got:
            kept = kept + other[:block]
        return kept

    gains = jnp.stack([gain_one, gain_two])
    for m in (1, 2):
        gains = gains + flip(gains, "tp", m)
    gains = pick(gains, [place ^ m for m in range(dp)], dp, 1)
    count = dp
    while count > 1:
        count //= 2
        gains = gains[:, : count * block] + flip(gains[:, count * block :], "dp", count)

    return (
        output_rows,
        input_rows,
        gains[0],
        grad_proj[:, :wide],
        grad_proj[:, wide : wide + size],
        grad_proj[:, wide + size :],
        grad_out.T,
        gains[1],
        grad_gate,
        total(grad_up, up_got),
        total(grad_down, down_got).T,
    )


def solution(mesh):
    placed = (
        P("dp", None),
        P("dp"),
        P(),
        P(None, "tp"),
        P(None, "tp"),
        P(None, "tp"),
        P("tp", None),
        P(),
        P(None, "tp"),
        P(None, "tp"),
        P("tp", None),
        P("dp", None),
    )
    return jax.shard_map(
        shards,
        mesh=mesh,
        in_specs=placed,
        out_specs=(
            P(("dp", "tp"), None),
            P(("dp", "tp"), None),
            P("dp"),
            P("dp", "tp"),
            P("dp", "tp"),
            P("dp", "tp"),
            P("tp", "dp"),
            P("dp"),
            P("dp", "tp"),
            P("dp", "tp"),
            P("tp", "dp"),
        ),
        check_vma=False,
    )
```

```python
import functools

import jax
import jax.numpy as jnp
from jax import lax
from jax.experimental import pallas as pl
from jax.experimental.pallas import tpu as pltpu
from jax.sharding import PartitionSpec as P

SPAN = 4
EPSILON = 1e-05
FAR_BELOW = -1e30
LOW = jnp.bfloat16
ROW_MASKS = (0, 2, 1, 3)


def flip(block, axis, mask):
    return lax.ppermute(block, axis, [(i, i ^ mask) for i in range(lax.axis_size(axis))])


def dot(left, right, left_dim, right_dim):
    return lax.dot_general(
        left,
        right,
        (((left_dim,), (right_dim,)), ((), ())),
        preferred_element_type=jnp.float32,
    )


def in_hbm(*arrays):
    return [pltpu.with_memory_space_constraint(a, pltpu.HBM) for a in arrays]


def own_mask(pos, begin, keys, queries):
    key_at = lax.broadcasted_iota(jnp.int32, (keys, queries), 0)
    query_at = lax.broadcasted_iota(jnp.int32, (keys, queries), 1) + begin
    return (key_at <= query_at) & (key_at >= query_at - pos)


def row_starts(spot, rows):
    part = rows // len(ROW_MASKS)
    return [pl.multiple_of((spot ^ m) * part, part) for m in ROW_MASKS]


def forward_kernel(
    heads,
    size,
    at_ref,
    pos_ref,
    q_ref,
    kv0,
    kv1,
    kv2,
    kv3,
    o_ref,
    lse_ref,
    keys,
    vals,
    top,
    acc,
    ordered,
):
    rank, spot = at_ref[0], at_ref[1]
    rows = pos_ref.shape[1]
    half = rows // 2

    @pl.when(pl.program_id(0) == 0)
    def _():
        for m, kv in enumerate((kv0, kv1, kv2, kv3)):
            keys[m] = kv[:size, :].T
            vals[m, :size, :] = kv[size:, :]
            vals[m, size:, :] = jnp.ones((16, rows), LOW)

    pos = pos_ref[...]
    for part in range(2):
        cols = slice(part * half, (part + 1) * half)
        count = (part + 1) * half
        mask = own_mask(pos[:, cols], part * half, count, half)
        for h in range(heads):
            scores = dot(keys[0, :count, :], q_ref[h * size : (h + 1) * size, cols], 1, 0)
            scores = jnp.where(mask, scores, FAR_BELOW)
            peak = jnp.max(scores, 0, keepdims=True)
            weights = jnp.exp(scores - peak).astype(LOW)
            acc[h, :, cols] = dot(vals[0, :, :count], weights, 1, 0)
            top[h, :, cols] = peak
    seen = pos > lax.broadcasted_iota(jnp.int32, (1, rows), 1)
    for m in range(1, SPAN):

        @pl.when((rank ^ m) < rank)
        def _():
            for h in range(heads):
                scores = dot(keys[m], q_ref[h * size : (h + 1) * size, :], 1, 0)
                old = top[h]
                peak = jnp.where(seen, jnp.maximum(old, jnp.max(scores, 0, keepdims=True)), old)
                weights = jnp.exp(scores - jnp.where(seen, peak, -FAR_BELOW)).astype(LOW)
                acc[h] = acc[h] * jnp.exp(old - peak) + dot(vals[m], weights, 1, 0)
                top[h] = peak

    for h in range(heads):
        total = acc[h, size : size + 1, :]
        ordered[h * size : (h + 1) * size, :] = (acc[h, :size, :] / total).astype(LOW)
        lse_ref[h] = top[h] + jnp.log(total)
    for j, start in enumerate(row_starts(spot, rows)):
        part = rows // len(ROW_MASKS)
        o_ref[:, j * part : (j + 1) * part] = ordered[:, pl.ds(start, part)]


def backward_kernel(
    heads,
    size,
    at_ref,
    pos_ref,
    q_ref,
    do_in,
    o_in,
    lse_ref,
    cos_ref,
    sin_ref,
    kv0,
    kv1,
    kv2,
    kv3,
    dq_ref,
    g0,
    g1,
    g2,
    g3,
    keys,
    vals,
    dq,
    total,
    do_ref,
    o_ref,
):
    rank, spot = at_ref[0], at_ref[1]
    rows = pos_ref.shape[1]
    half = rows // 2
    blocks = (kv0, kv1, kv2, kv3)
    step = pl.program_id(0)

    @pl.when(step == 0)
    def _():
        for m, kv in enumerate(blocks):
            keys[m] = kv[:size, :].T
            vals[m] = kv[size:, :].T
        total[...] = jnp.zeros_like(total)

    part = rows // len(ROW_MASKS)
    for j, start in enumerate(row_starts(spot, rows)):
        do_ref[:, pl.ds(start, part)] = do_in[:, j * part : (j + 1) * part]
        o_ref[:, pl.ds(start, part)] = o_in[:, j * part : (j + 1) * part]
    pos = pos_ref[...]
    seen = pos > lax.broadcasted_iota(jnp.int32, (1, rows), 1)
    deltas = []
    for h in range(heads):
        span = slice(h * size, (h + 1) * size)
        deltas.append(
            jnp.sum(
                do_ref[span, :].astype(jnp.float32) * o_ref[span, :].astype(jnp.float32),
                0,
                keepdims=True,
            )
        )
    for part in range(2):
        cols = slice(part * half, (part + 1) * half)
        count = (part + 1) * half
        mask = own_mask(pos[:, cols], part * half, count, half)
        for h in range(heads):
            span = slice(h * size, (h + 1) * size)
            query, grad = q_ref[span, cols], do_ref[span, cols]
            scores = dot(keys[0, :count, :], query, 1, 0)
            probs = jnp.exp(jnp.where(mask, scores, FAR_BELOW) - lse_ref[h, :, cols])
            grad_probs = dot(vals[0, :count, :], grad, 1, 0)
            grad_scores = (probs * (grad_probs - deltas[h][:, cols])).astype(LOW)
            total[0, :size, :count] += dot(query, grad_scores, 1, 1)
            total[0, size:, :count] += dot(grad, probs.astype(LOW), 1, 1)
            dq[h, :, cols] = dot(kv0[:size, :count], grad_scores, 1, 0)
    for m in range(1, SPAN):

        @pl.when((rank ^ m) < rank)
        def _():
            for h in range(heads):
                span = slice(h * size, (h + 1) * size)
                query, grad = q_ref[span, :], do_ref[span, :]
                scores = dot(keys[m], query, 1, 0)
                probs = jnp.exp(scores - jnp.where(seen, lse_ref[h], -FAR_BELOW))
                grad_probs = dot(vals[m], grad, 1, 0)
                grad_scores = (probs * (grad_probs - deltas[h])).astype(LOW)
                total[m, :size, :] += dot(query, grad_scores, 1, 1)
                total[m, size:, :] += dot(grad, probs.astype(LOW), 1, 1)
                dq[h] += dot(blocks[m][:size, :], grad_scores, 1, 0)

    middle_at = size // 2
    cosine, sine = cos_ref[...], sin_ref[...]
    for h in range(heads):
        first = dq[h, :middle_at, :] * size ** (-0.5)
        second = dq[h, middle_at:, :] * size ** (-0.5)
        base = h * size
        dq_ref[base : base + middle_at, :] = (first * cosine + second * sine).astype(LOW)
        dq_ref[base + middle_at : base + size, :] = (second * cosine - first * sine).astype(LOW)

    @pl.when(step == pl.num_programs(0) - 1)
    def _():
        g0[...] = total[0]
        for m, out in ((1, g1), (2, g2), (3, g3)):
            out[...] = total[m].astype(LOW)


def attention_forward(at, pos, queries, blocks, size, heads):
    wide, rows = queries.shape
    count = wide // size
    whole = pl.BlockSpec((2 * size, rows), lambda i, r: (0, 0))
    some = pl.BlockSpec((heads * size, rows), lambda i, r: (i, 0))
    return pl.pallas_call(
        functools.partial(forward_kernel, heads, size),
        out_shape=(
            jax.ShapeDtypeStruct((wide, rows), LOW),
            jax.ShapeDtypeStruct((count, 1, rows), jnp.float32),
        ),
        grid_spec=pltpu.PrefetchScalarGridSpec(
            num_scalar_prefetch=1,
            grid=(count // heads,),
            in_specs=[pl.BlockSpec((1, rows), lambda i, r: (0, 0)), some] + [whole] * SPAN,
            out_specs=[some, pl.BlockSpec((heads, 1, rows), lambda i, r: (i, 0, 0))],
            scratch_shapes=[
                pltpu.VMEM((SPAN, rows, size), LOW),
                pltpu.VMEM((SPAN, size + 16, rows), LOW),
                pltpu.VMEM((heads, 1, rows), jnp.float32),
                pltpu.VMEM((heads, size + 16, rows), jnp.float32),
                pltpu.VMEM((heads * size, rows), LOW),
            ],
        ),
        compiler_params=pltpu.CompilerParams(vmem_limit_bytes=24 << 20),
        cost_estimate=pl.CostEstimate(
            flops=32 * wide * rows * rows * SPAN,
            bytes_accessed=4 * wide * rows,
            transcendentals=0,
        ),
        name="attention_forward",
    )(at, pos, queries, *blocks)


def attention_backward(at, pos, queries, grads, attended, lse, cosine, sine, blocks, size, heads):
    wide, rows = queries.shape
    count = wide // size
    whole = pl.BlockSpec((2 * size, rows), lambda i, r: (0, 0))
    table = pl.BlockSpec((size // 2, rows), lambda i, r: (0, 0))
    some = pl.BlockSpec((heads * size, rows), lambda i, r: (i, 0))
    return pl.pallas_call(
        functools.partial(backward_kernel, heads, size),
        out_shape=(
            jax.ShapeDtypeStruct((wide, rows), LOW),
            jax.ShapeDtypeStruct((2 * size, rows), jnp.float32),
        )
        + (jax.ShapeDtypeStruct((2 * size, rows), LOW),) * (SPAN - 1),
        grid_spec=pltpu.PrefetchScalarGridSpec(
            num_scalar_prefetch=1,
            grid=(count // heads,),
            in_specs=[
                pl.BlockSpec((1, rows), lambda i, r: (0, 0)),
                some,
                some,
                some,
                pl.BlockSpec((heads, 1, rows), lambda i, r: (i, 0, 0)),
                table,
                table,
            ]
            + [whole] * SPAN,
            out_specs=[some] + [whole] * SPAN,
            scratch_shapes=[
                pltpu.VMEM((SPAN, rows, size), LOW),
                pltpu.VMEM((SPAN, rows, size), LOW),
                pltpu.VMEM((heads, size, rows), jnp.float32),
                pltpu.VMEM((SPAN, 2 * size, rows), jnp.float32),
                pltpu.VMEM((heads * size, rows), LOW),
                pltpu.VMEM((heads * size, rows), LOW),
            ],
        ),
        compiler_params=pltpu.CompilerParams(vmem_limit_bytes=24 << 20),
        cost_estimate=pl.CostEstimate(
            flops=48 * wide * rows * rows * SPAN,
            bytes_accessed=10 * wide * rows,
            transcendentals=0,
        ),
        name="attention_backward",
    )(at, pos, *in_hbm(queries, grads, attended, lse, cosine, sine, *blocks))


def pick(values, places, blocks, dim):
    size = values.shape[dim] // blocks
    return jnp.concatenate(
        [lax.dynamic_slice_in_dim(values, p * size, size, dim) for p in places], dim
    )


def after(value, *others):
    return lax.optimization_barrier((value, *others))[0]


def parity_sum(terms, dim):
    count = lax.axis_size("dp")
    groups = [list(range(p, count, 2)) for p in range(2)]
    return lax.psum_scatter(
        terms.astype(LOW), "dp", scatter_dimension=dim, axis_index_groups=groups, tiled=True
    )


def terms_kernel(transposed, places, x, x_far, g, g_far, out):
    del places
    side = 1 if transposed else 0
    out[...] = (dot(x[...], g[...], 0, side) + dot(x_far[...], g_far[...], 0, side)).astype(LOW)


def weight_terms(places, first, x, x_far, g, g_far, transposed=False, part=None, keep=False):
    count = len(places)
    blocks = lax.axis_size("dp")
    size = x.shape[1] // blocks
    rows = x.shape[0]
    units = g.shape[0] if transposed else g.shape[1]
    if part is not None:
        units //= 2
    if size % 128:
        side = 1 if transposed else 0
        far = x_far[:, first * size : (first + count) * size]
        if part is not None:
            g, g_far = (v[:, part * units : (part + 1) * units] for v in (g, g_far))
        return (dot(pick(x, places, blocks, 1), g, 0, side) + dot(far, g_far, 0, side)).astype(LOW)
    whole = pl.BlockSpec(
        (units, rows) if transposed else (rows, units), lambda i, p: (0, part or 0)
    )
    return pl.pallas_call(
        functools.partial(terms_kernel, transposed),
        out_shape=(jax.ShapeDtypeStruct if keep else pltpu.HBM)((count * size, units), LOW),
        grid_spec=pltpu.PrefetchScalarGridSpec(
            num_scalar_prefetch=1,
            grid=(count,),
            in_specs=[
                pl.BlockSpec((rows, size), lambda i, p: (0, p[i])),
                pl.BlockSpec((rows, size), lambda i, p: (0, first + i)),
                whole,
                whole,
            ],
            out_specs=pl.BlockSpec((size, units), lambda i, p: (i, 0)),
        ),
        compiler_params=pltpu.CompilerParams(vmem_limit_bytes=24 << 20),
        cost_estimate=pl.CostEstimate(
            flops=8 * rows * count * size * units, bytes_accessed=4 * rows * units, transcendentals=0
        ),
        name="weight_terms",
    )(jnp.stack(places).astype(jnp.int32), x, x_far, g, g_far)


def row_kernel(left, right, send, kept):
    half = left.shape[0] // 2
    send[...] = dot(left[half:, :], right[...], 1, 0).astype(LOW)
    kept[...] = dot(left[:half, :], right[...], 1, 0)


def row_terms(left, right):
    rows, units = left.shape
    half, width = rows // 2, right.shape[1]
    step = 256
    return pl.pallas_call(
        row_kernel,
        out_shape=(
            jax.ShapeDtypeStruct((half, width), LOW),
            jax.ShapeDtypeStruct((half, width), jnp.float32),
        ),
        grid=(width // step,),
        in_specs=[
            pl.BlockSpec((rows, units), lambda i: (0, 0)),
            pl.BlockSpec((units, step), lambda i: (0, i)),
        ],
        out_specs=[pl.BlockSpec((half, step), lambda i: (0, i))] * 2,
        compiler_params=pltpu.CompilerParams(vmem_limit_bytes=16 << 20),
        cost_estimate=pl.CostEstimate(
            flops=8 * rows * units * width, bytes_accessed=2 * units * width, transcendentals=0
        ),
        name="row_terms",
    )(left, right)


def turn(values, cosine, sine):
    half = cosine.shape[0]
    heads = values.shape[0] // (2 * half)
    pieces = values.reshape(heads, 2, half, values.shape[1])
    first, second = pieces[:, 0], pieces[:, 1]
    return jnp.stack(
        [first * cosine - second * sine, second * cosine + first * sine], 1
    ).reshape(values.shape)


def turn_back(grads, cosine, sine):
    return turn(grads, cosine, -sine)


def norm_back(grad_rows, values, scale_rows, gain):
    scaled = grad_rows * gain
    inner_mean = jnp.mean(scaled * values, -1, keepdims=True)
    return (
        scale_rows * (scaled - values * scale_rows * scale_rows * inner_mean),
        jnp.sum(grad_rows * values * scale_rows, 0),
    )


def shards(
    tokens,
    positions,
    norm1_gain,
    w_query,
    w_key,
    w_value,
    w_out,
    norm2_gain,
    w_gate,
    w_up,
    w_down,
    cotangent,
):
    rows_here, width = tokens.shape
    size = w_key.shape[1]
    dp = lax.axis_size("dp")
    place = lax.axis_index("dp")
    spot = lax.axis_index("tp")
    tp_masks = range(lax.axis_size("tp"))
    own_rows = rows_here // lax.axis_size("tp")
    block = width // dp
    at = jnp.stack([place % SPAN, spot]).astype(jnp.int32)
    pos = positions.reshape(1, rows_here)

    def own(values):
        return lax.dynamic_slice_in_dim(values, spot * own_rows, own_rows, 0)

    inputs = tokens.astype(jnp.float32)
    scale_one = lax.rsqrt(jnp.mean(inputs * inputs, -1, keepdims=True) + EPSILON)
    normed_one = (inputs * scale_one * norm1_gain).astype(LOW)
    half = size // 2
    frequency = jnp.exp(
        -jnp.log(10000.0) * (2.0 * jnp.arange(half, dtype=jnp.float32) / size)
    )
    angles = frequency[:, None] * positions.astype(jnp.float32)[None, :]
    cosine, sine = jnp.cos(angles), jnp.sin(angles)
    w_kv = jnp.concatenate([w_key.T, w_value.T], 0)
    paired = dot(w_kv, normed_one, 1, 1)
    paired = jnp.concatenate([turn(paired[:size], cosine, sine), paired[size:]], 0).astype(LOW)
    blocks = [paired] + [flip(paired, "dp", m) for m in range(1, SPAN)]
    queries = (turn(dot(w_query, normed_one, 0, 1), cosine, sine) * size ** (-0.5)).astype(LOW)

    bit = place % 2
    bits = dp.bit_length() - 1
    half_count = dp // 2
    wide = w_query.shape[1]

    halves = [[2 * j + which for j in range(half_count)] for which in (bit, 1 - bit)]
    near_bits = [0] + list(range(2, bits))
    near_masks = [
        sum(((j >> (len(near_bits) - 1 - k)) & 1) << b for k, b in enumerate(near_bits))
        for j in range(half_count)
    ]
    near_halves = [[where ^ m for m in near_masks] for where in (place, place ^ 2)]
    row_order = [spot ^ m for m in ROW_MASKS]

    def near_sum(part):
        send = part(2, 4).astype(LOW)
        near, kept = lax.optimization_barrier((flip(send, "tp", 1), part(0, 2)))
        pair = kept + near
        return pair[:own_rows], pair[own_rows:].astype(LOW)

    one_send = pick(after(normed_one, paired), halves[1], dp, 1)
    one_theirs = flip(one_send, "dp", 1)
    queries = after(queries, one_send)
    attended, lse = attention_forward(at, pos, queries, blocks, size, 2)
    attended = after(attended, one_theirs)

    branch, branch_out = near_sum(
        lambda lo, hi: dot(attended[:, lo * own_rows : hi * own_rows], w_out, 0, 0)
    )
    branch_far = flip(branch_out, "tp", 2)
    att_theirs = flip(after(attended, branch_out), "dp", 1)
    cot = pick(after(cotangent, branch_out), row_order, len(ROW_MASKS), 0)
    cot_send = pick(cot, near_halves[1], dp, 1)
    cot_theirs = flip(cot_send, "dp", 2)
    own_inputs = own(tokens).astype(jnp.float32)
    middle = own_inputs + (after(branch, cot_send) + branch_far)

    scale_two = lax.rsqrt(jnp.mean(middle * middle, -1, keepdims=True) + EPSILON)
    own_two = (middle * scale_two * norm2_gain).astype(LOW)
    far_two = flip(own_two, "tp", 2)
    grad_hidden = dot(after(cot, own_two), w_down, 1, 1)
    pair_two = jnp.concatenate([after(own_two, grad_hidden, att_theirs), far_two], 0)
    core_two = flip(pair_two, "tp", 1)
    two_send = pick(pair_two, halves[1], dp, 1)
    two_near_send = pick(pair_two, near_halves[1], dp, 1)
    two_near = [flip(two_send, "dp", 1), flip(two_near_send, "dp", 2)]
    normed_two = jnp.concatenate([after(pair_two, two_send, two_near_send), core_two], 0)

    gate_pre = dot(normed_two, w_gate, 1, 0)
    up_pre = dot(normed_two, w_up, 1, 0)
    sigma = jax.nn.sigmoid(gate_pre)
    active = gate_pre * sigma
    hidden = (active * up_pre).astype(LOW)
    grad_gate_pre = (grad_hidden * up_pre * sigma * (1.0 + gate_pre * (1.0 - sigma))).astype(LOW)
    grad_up_pre = (grad_hidden * active).astype(LOW)
    gate_theirs = flip(grad_gate_pre, "dp", 1)
    far_rows = jnp.concatenate([hidden, grad_up_pre], 1)
    far_theirs = flip(far_rows, "dp", 2)
    gate_late = after(grad_gate_pre, far_rows)

    def two_terms(lo, hi):
        rows = slice(lo * own_rows, hi * own_rows)
        return dot(gate_late[rows], w_gate, 1, 1) + dot(grad_up_pre[rows], w_up, 1, 1)

    grad_normed_two, two_out = near_sum(two_terms)
    two_out, cot_theirs, *two_near = lax.optimization_barrier((two_out, cot_theirs, *two_near))
    two_far = flip(two_out, "tp", 2)
    two_near = jnp.concatenate(two_near, 1)
    two_theirs = jnp.concatenate([two_near, flip(two_near, "tp", 1)], 0)

    down_near, down = row_terms(after(hidden, two_out), w_down)
    grad_normed_two = after(grad_normed_two, down) + two_far

    grad_mid_norm, gain_two = norm_back(grad_normed_two, middle, scale_two, norm2_gain)
    grad_middle = own(cotangent).astype(jnp.float32) + grad_mid_norm
    branch_grad = grad_middle.astype(LOW)
    grad_far = flip(branch_grad, "tp", 2)

    down_near = flip(after(down_near, branch_grad), "tp", 1)
    two_late = after(normed_two, branch_grad)
    gate_terms = weight_terms(halves[0], 0, two_late, two_theirs, grad_gate_pre, gate_theirs)
    grad_gate = parity_sum(gate_terms, 0)
    grad_pair = jnp.concatenate([after(branch_grad, gate_terms), grad_far], 0)
    grad_core = flip(grad_pair, "tp", 1)
    branch_send = pick(grad_pair, halves[1], dp, 1)
    branch_near = flip(branch_send, "dp", 1)
    branch_all = jnp.concatenate([after(grad_pair, branch_send), grad_core], 0)
    grad_attended = dot(w_out, branch_all, 1, 1).astype(LOW)

    def down_terms(lo, hi, *late):
        rows = after(far_rows, *late)
        return weight_terms(
            near_halves[0][lo:hi], lo, cot, cot_theirs, rows, far_theirs, part=0, keep=True
        )

    def up_terms(lo, hi, *late):
        rows = after(far_rows, *late)
        first = half_count + lo
        return weight_terms(
            near_halves[0][lo:hi], first, normed_two, two_theirs, rows, far_theirs, part=1, keep=True
        )

    down_sent = down_terms(half_count // 2, half_count, grad_attended)
    down_got = [flip(down_sent, "dp", 1)]
    grads = attention_backward(
        at,
        pos,
        queries,
        after(grad_attended, down_sent),
        attended,
        lse,
        cosine,
        sine,
        blocks,
        size,
        2,
    )
    grad_query_rows, kv_total = grads[0], grads[1]
    kv_back = [flip(grads[m + 1], "dp", m) for m in range(1, SPAN)]

    down = down + after(down_near, grad_query_rows)
    down, down_out = down[:own_rows], down[own_rows:].astype(LOW)
    down_far = flip(down_out, "tp", 2)
    up_sent = up_terms(half_count // 2, half_count, grad_query_rows)
    kv_total, branch_near, down_got[0] = lax.optimization_barrier(
        (kv_total, branch_near, down_got[0], up_sent, down_out)
    )[:3]
    for back in kv_back:
        kv_total = kv_total + back
    key_grad = turn_back(kv_total[:size], cosine, sine)
    grad_kv_rows = jnp.concatenate([key_grad, kv_total[size:]], 0).astype(LOW)
    proj_rows = jnp.concatenate([grad_query_rows, grad_kv_rows], 0)
    proj_theirs = flip(proj_rows, "dp", 1)

    def exchange_rest(terms, got, *late):
        left = half_count // 2
        for b in near_bits[1:]:
            send = terms(left // 2, left, *late).astype(jnp.float32)
            for other in got:
                send = send + other[left // 2 * block : left * block]
            send = send.astype(LOW)
            got.append(flip(send, "dp", 1 << b))
            left //= 2
        return send

    def exchange_end(terms, got, *late):
        kept = terms(0, 1, *late).astype(jnp.float32)
        for other in got:
            kept = kept + other[:block]
        return kept

    down_last = exchange_rest(down_terms, down_got, proj_rows)
    proj_rows = after(proj_rows, down_last)

    own_order = pick(proj_rows, row_order, len(ROW_MASKS), 1)

    def one_terms(lo, hi):
        cut = own_order[:, lo * own_rows : hi * own_rows]
        return dot(cut[:wide], w_query, 0, 1) + dot(cut[wide:], w_kv, 0, 0)

    grad_normed_one, one_out = near_sum(one_terms)
    one_far = flip(one_out, "tp", 2)

    up_got = [flip(after(up_sent, one_out), "dp", 1)]
    branch_theirs = jnp.concatenate([branch_near, flip(branch_near, "tp", 1)], 0)
    out_late = after(attended, one_out)
    out_terms = weight_terms(halves[0], 0, branch_all, branch_theirs, out_late, att_theirs, True)
    grad_out = parity_sum(out_terms, 0)
    output_rows = (middle + (down + after(down_far, one_out))).astype(LOW)
    grad_normed_one = after(grad_normed_one, out_terms, output_rows) + one_far
    grad_in_norm, gain_one = norm_back(grad_normed_one, own_inputs, own(scale_one), norm1_gain)
    input_rows = grad_middle + grad_in_norm

    gains = jnp.stack([gain_one, gain_two])
    for m in (1, 2):
        gains = gains + flip(gains, "tp", m)
    gains = pick(gains, [place ^ m for m in range(dp)], dp, 1)
    left = dp
    while left > 1:
        left //= 2
        gains = gains[:, : left * block] + flip(gains[:, left * block :], "dp", left)

    grad_down = exchange_end(down_terms, down_got, input_rows)
    grad_gate = grad_gate.astype(jnp.float32)

    proj_late = after(proj_rows, input_rows, grad_gate)
    proj_terms = weight_terms(halves[0], 0, normed_one, one_theirs, proj_late, proj_theirs, True)
    grad_out = grad_out.astype(jnp.float32)
    grad_proj = parity_sum(proj_terms, 0).astype(jnp.float32)
    exchange_rest(up_terms, up_got, gains, proj_terms)
    grad_up = exchange_end(up_terms, up_got, proj_terms)

    return (
        output_rows,
        input_rows,
        gains[0],
        grad_proj[:, :wide],
        grad_proj[:, wide : wide + size],
        grad_proj[:, wide + size :],
        grad_out.T,
        gains[1],
        grad_gate,
        grad_up,
        grad_down.T,
    )


def solution(mesh):
    placed = (
        P("dp", None),
        P("dp"),
        P(),
        P(None, "tp"),
        P(None, "tp"),
        P(None, "tp"),
        P("tp", None),
        P(),
        P(None, "tp"),
        P(None, "tp"),
        P("tp", None),
        P("dp", None),
    )
    return jax.shard_map(
        shards,
        mesh=mesh,
        in_specs=placed,
        out_specs=(
            P(("dp", "tp"), None),
            P(("dp", "tp"), None),
            P("dp"),
            P("dp", "tp"),
            P("dp", "tp"),
            P("dp", "tp"),
            P("tp", "dp"),
            P("dp"),
            P("dp", "tp"),
            P("dp", "tp"),
            P("tp", "dp"),
        ),
        check_vma=False,
    )
```

```python
import functools

import jax
import jax.numpy as jnp
from jax import lax
from jax.experimental import pallas as pl
from jax.experimental.pallas import tpu as pltpu
from jax.sharding import PartitionSpec as P

SPAN = 4
EPSILON = 1e-05
FAR_BELOW = -1e30
LOW = jnp.bfloat16
ROW_MASKS = (0, 2, 1, 3)


def flip(block, axis, mask):
    return lax.ppermute(block, axis, [(i, i ^ mask) for i in range(lax.axis_size(axis))])


def dot(left, right, left_dim, right_dim):
    return lax.dot_general(
        left,
        right,
        (((left_dim,), (right_dim,)), ((), ())),
        preferred_element_type=jnp.float32,
    )


def in_hbm(*arrays):
    return [pltpu.with_memory_space_constraint(a, pltpu.HBM) for a in arrays]


def own_mask(pos, begin, keys, queries):
    key_at = lax.broadcasted_iota(jnp.int32, (keys, queries), 0)
    query_at = lax.broadcasted_iota(jnp.int32, (keys, queries), 1) + begin
    return (key_at <= query_at) & (key_at >= query_at - pos)


def row_starts(spot, rows):
    part = rows // len(ROW_MASKS)
    return [pl.multiple_of((spot ^ m) * part, part) for m in ROW_MASKS]


def forward_kernel(
    heads,
    size,
    at_ref,
    pos_ref,
    q_ref,
    kv0,
    kv1,
    kv2,
    kv3,
    o_ref,
    lse_ref,
    keys,
    vals,
    top,
    acc,
    ordered,
):
    rank, spot = at_ref[0], at_ref[1]
    rows = pos_ref.shape[1]
    half = rows // 2

    @pl.when(pl.program_id(0) == 0)
    def _():
        for m, kv in enumerate((kv0, kv1, kv2, kv3)):
            keys[m] = kv[:size, :].T
            vals[m, :size, :] = kv[size:, :]
            vals[m, size:, :] = jnp.ones((16, rows), LOW)

    pos = pos_ref[...]
    for part in range(2):
        cols = slice(part * half, (part + 1) * half)
        count = (part + 1) * half
        mask = own_mask(pos[:, cols], part * half, count, half)
        for h in range(heads):
            scores = dot(keys[0, :count, :], q_ref[h * size : (h + 1) * size, cols], 1, 0)
            scores = jnp.where(mask, scores, FAR_BELOW)
            peak = jnp.max(scores, 0, keepdims=True)
            weights = jnp.exp(scores - peak).astype(LOW)
            acc[h, :, cols] = dot(vals[0, :, :count], weights, 1, 0)
            top[h, :, cols] = peak
    seen = pos > lax.broadcasted_iota(jnp.int32, (1, rows), 1)
    for m in range(1, SPAN):

        @pl.when((rank ^ m) < rank)
        def _():
            for h in range(heads):
                scores = dot(keys[m], q_ref[h * size : (h + 1) * size, :], 1, 0)
                old = top[h]
                peak = jnp.where(seen, jnp.maximum(old, jnp.max(scores, 0, keepdims=True)), old)
                weights = jnp.exp(scores - jnp.where(seen, peak, -FAR_BELOW)).astype(LOW)
                acc[h] = acc[h] * jnp.exp(old - peak) + dot(vals[m], weights, 1, 0)
                top[h] = peak

    for h in range(heads):
        total = acc[h, size : size + 1, :]
        ordered[h * size : (h + 1) * size, :] = (acc[h, :size, :] / total).astype(LOW)
        lse_ref[h] = top[h] + jnp.log(total)
    for j, start in enumerate(row_starts(spot, rows)):
        part = rows // len(ROW_MASKS)
        o_ref[:, j * part : (j + 1) * part] = ordered[:, pl.ds(start, part)]


def backward_kernel(
    heads,
    size,
    at_ref,
    pos_ref,
    q_ref,
    do_in,
    o_in,
    lse_ref,
    cos_ref,
    sin_ref,
    kv0,
    kv1,
    kv2,
    kv3,
    dq_ref,
    g0,
    g1,
    g2,
    g3,
    keys,
    vals,
    dq,
    total,
    do_ref,
    o_ref,
):
    rank, spot = at_ref[0], at_ref[1]
    rows = pos_ref.shape[1]
    half = rows // 2
    blocks = (kv0, kv1, kv2, kv3)
    step = pl.program_id(0)

    @pl.when(step == 0)
    def _():
        for m, kv in enumerate(blocks):
            keys[m] = kv[:size, :].T
            vals[m] = kv[size:, :].T
        total[...] = jnp.zeros_like(total)

    part = rows // len(ROW_MASKS)
    for j, start in enumerate(row_starts(spot, rows)):
        do_ref[:, pl.ds(start, part)] = do_in[:, j * part : (j + 1) * part]
        o_ref[:, pl.ds(start, part)] = o_in[:, j * part : (j + 1) * part]
    pos = pos_ref[...]
    seen = pos > lax.broadcasted_iota(jnp.int32, (1, rows), 1)
    deltas = []
    for h in range(heads):
        span = slice(h * size, (h + 1) * size)
        deltas.append(
            jnp.sum(
                do_ref[span, :].astype(jnp.float32) * o_ref[span, :].astype(jnp.float32),
                0,
                keepdims=True,
            )
        )
    for part in range(2):
        cols = slice(part * half, (part + 1) * half)
        count = (part + 1) * half
        mask = own_mask(pos[:, cols], part * half, count, half)
        for h in range(heads):
            span = slice(h * size, (h + 1) * size)
            query, grad = q_ref[span, cols], do_ref[span, cols]
            scores = dot(keys[0, :count, :], query, 1, 0)
            probs = jnp.exp(jnp.where(mask, scores, FAR_BELOW) - lse_ref[h, :, cols])
            grad_probs = dot(vals[0, :count, :], grad, 1, 0)
            grad_scores = (probs * (grad_probs - deltas[h][:, cols])).astype(LOW)
            total[0, :size, :count] += dot(query, grad_scores, 1, 1)
            total[0, size:, :count] += dot(grad, probs.astype(LOW), 1, 1)
            dq[h, :, cols] = dot(kv0[:size, :count], grad_scores, 1, 0)
    for m in range(1, SPAN):

        @pl.when((rank ^ m) < rank)
        def _():
            for h in range(heads):
                span = slice(h * size, (h + 1) * size)
                query, grad = q_ref[span, :], do_ref[span, :]
                scores = dot(keys[m], query, 1, 0)
                probs = jnp.exp(scores - jnp.where(seen, lse_ref[h], -FAR_BELOW))
                grad_probs = dot(vals[m], grad, 1, 0)
                grad_scores = (probs * (grad_probs - deltas[h])).astype(LOW)
                total[m, :size, :] += dot(query, grad_scores, 1, 1)
                total[m, size:, :] += dot(grad, probs.astype(LOW), 1, 1)
                dq[h] += dot(blocks[m][:size, :], grad_scores, 1, 0)

    middle_at = size // 2
    cosine, sine = cos_ref[...], sin_ref[...]
    for h in range(heads):
        first = dq[h, :middle_at, :] * size ** (-0.5)
        second = dq[h, middle_at:, :] * size ** (-0.5)
        base = h * size
        dq_ref[base : base + middle_at, :] = (first * cosine + second * sine).astype(LOW)
        dq_ref[base + middle_at : base + size, :] = (second * cosine - first * sine).astype(LOW)

    @pl.when(step == pl.num_programs(0) - 1)
    def _():
        g0[...] = total[0]
        for m, out in ((1, g1), (2, g2), (3, g3)):
            out[...] = total[m].astype(LOW)


def attention_forward(at, pos, queries, blocks, size, heads):
    wide, rows = queries.shape
    count = wide // size
    whole = pl.BlockSpec((2 * size, rows), lambda i, r: (0, 0))
    some = pl.BlockSpec((heads * size, rows), lambda i, r: (i, 0))
    return pl.pallas_call(
        functools.partial(forward_kernel, heads, size),
        out_shape=(
            jax.ShapeDtypeStruct((wide, rows), LOW),
            jax.ShapeDtypeStruct((count, 1, rows), jnp.float32),
        ),
        grid_spec=pltpu.PrefetchScalarGridSpec(
            num_scalar_prefetch=1,
            grid=(count // heads,),
            in_specs=[pl.BlockSpec((1, rows), lambda i, r: (0, 0)), some] + [whole] * SPAN,
            out_specs=[some, pl.BlockSpec((heads, 1, rows), lambda i, r: (i, 0, 0))],
            scratch_shapes=[
                pltpu.VMEM((SPAN, rows, size), LOW),
                pltpu.VMEM((SPAN, size + 16, rows), LOW),
                pltpu.VMEM((heads, 1, rows), jnp.float32),
                pltpu.VMEM((heads, size + 16, rows), jnp.float32),
                pltpu.VMEM((heads * size, rows), LOW),
            ],
        ),
        compiler_params=pltpu.CompilerParams(vmem_limit_bytes=24 << 20),
        cost_estimate=pl.CostEstimate(
            flops=32 * wide * rows * rows * SPAN,
            bytes_accessed=4 * wide * rows,
            transcendentals=0,
        ),
        name="attention_forward",
    )(at, pos, queries, *blocks)


def attention_backward(at, pos, queries, grads, attended, lse, cosine, sine, blocks, size, heads):
    wide, rows = queries.shape
    count = wide // size
    whole = pl.BlockSpec((2 * size, rows), lambda i, r: (0, 0))
    table = pl.BlockSpec((size // 2, rows), lambda i, r: (0, 0))
    some = pl.BlockSpec((heads * size, rows), lambda i, r: (i, 0))
    return pl.pallas_call(
        functools.partial(backward_kernel, heads, size),
        out_shape=(
            jax.ShapeDtypeStruct((wide, rows), LOW),
            jax.ShapeDtypeStruct((2 * size, rows), jnp.float32),
        )
        + (jax.ShapeDtypeStruct((2 * size, rows), LOW),) * (SPAN - 1),
        grid_spec=pltpu.PrefetchScalarGridSpec(
            num_scalar_prefetch=1,
            grid=(count // heads,),
            in_specs=[
                pl.BlockSpec((1, rows), lambda i, r: (0, 0)),
                some,
                some,
                some,
                pl.BlockSpec((heads, 1, rows), lambda i, r: (i, 0, 0)),
                table,
                table,
            ]
            + [whole] * SPAN,
            out_specs=[some] + [whole] * SPAN,
            scratch_shapes=[
                pltpu.VMEM((SPAN, rows, size), LOW),
                pltpu.VMEM((SPAN, rows, size), LOW),
                pltpu.VMEM((heads, size, rows), jnp.float32),
                pltpu.VMEM((SPAN, 2 * size, rows), jnp.float32),
                pltpu.VMEM((heads * size, rows), LOW),
                pltpu.VMEM((heads * size, rows), LOW),
            ],
        ),
        compiler_params=pltpu.CompilerParams(vmem_limit_bytes=24 << 20),
        cost_estimate=pl.CostEstimate(
            flops=48 * wide * rows * rows * SPAN,
            bytes_accessed=10 * wide * rows,
            transcendentals=0,
        ),
        name="attention_backward",
    )(at, pos, *in_hbm(queries, grads, attended, lse, cosine, sine, *blocks))


def pick(values, places, blocks, dim):
    size = values.shape[dim] // blocks
    return jnp.concatenate(
        [lax.dynamic_slice_in_dim(values, p * size, size, dim) for p in places], dim
    )


def after(value, *others):
    return lax.optimization_barrier((value, *others))[0]


def parity_sum(terms, dim):
    count = lax.axis_size("dp")
    groups = [list(range(p, count, 2)) for p in range(2)]
    return lax.psum_scatter(
        terms.astype(LOW), "dp", scatter_dimension=dim, axis_index_groups=groups, tiled=True
    )


def terms_kernel(transposed, places, x, x_far, g, g_far, out):
    del places
    side = 1 if transposed else 0
    out[...] = (dot(x[...], g[...], 0, side) + dot(x_far[...], g_far[...], 0, side)).astype(LOW)


def weight_terms(places, far_places, x, x_far, g, g_far, transposed=False, keep=True):
    count = len(places)
    size = x.shape[1] // lax.axis_size("dp")
    rows = x.shape[0]
    units = g.shape[0] if transposed else g.shape[1]
    if size % 128:
        side = 1 if transposed else 0
        mine = pick(x, places, x.shape[1] // size, 1)
        theirs = pick(x_far, far_places, x_far.shape[1] // size, 1)
        return (dot(mine, g, 0, side) + dot(theirs, g_far, 0, side)).astype(LOW)
    whole = pl.BlockSpec(g.shape, lambda i, p: (0, 0))
    return pl.pallas_call(
        functools.partial(terms_kernel, transposed),
        out_shape=(jax.ShapeDtypeStruct if keep else pltpu.HBM)((count * size, units), LOW),
        grid_spec=pltpu.PrefetchScalarGridSpec(
            num_scalar_prefetch=1,
            grid=(count,),
            in_specs=[
                pl.BlockSpec((rows, size), lambda i, p: (0, p[i])),
                pl.BlockSpec((rows, size), lambda i, p: (0, p[count + i])),
                whole,
                whole,
            ],
            out_specs=pl.BlockSpec((size, units), lambda i, p: (i, 0)),
        ),
        compiler_params=pltpu.CompilerParams(vmem_limit_bytes=24 << 20),
        cost_estimate=pl.CostEstimate(
            flops=8 * rows * count * size * units, bytes_accessed=4 * rows * units, transcendentals=0
        ),
        name="weight_terms",
    )(jnp.stack([*places, *far_places]).astype(jnp.int32), x, x_far, g, g_far)


def row_kernel(left, right, send, kept):
    half = left.shape[0] // 2
    send[...] = dot(left[half:, :], right[...], 1, 0).astype(LOW)
    kept[...] = dot(left[:half, :], right[...], 1, 0)


def row_terms(left, right):
    rows, units = left.shape
    half, width = rows // 2, right.shape[1]
    step = 256
    return pl.pallas_call(
        row_kernel,
        out_shape=(
            jax.ShapeDtypeStruct((half, width), LOW),
            jax.ShapeDtypeStruct((half, width), jnp.float32),
        ),
        grid=(width // step,),
        in_specs=[
            pl.BlockSpec((rows, units), lambda i: (0, 0)),
            pl.BlockSpec((units, step), lambda i: (0, i)),
        ],
        out_specs=[pl.BlockSpec((half, step), lambda i: (0, i))] * 2,
        compiler_params=pltpu.CompilerParams(vmem_limit_bytes=16 << 20),
        cost_estimate=pl.CostEstimate(
            flops=8 * rows * units * width, bytes_accessed=2 * units * width, transcendentals=0
        ),
        name="row_terms",
    )(left, right)


def turn(values, cosine, sine):
    half = cosine.shape[0]
    heads = values.shape[0] // (2 * half)
    pieces = values.reshape(heads, 2, half, values.shape[1])
    first, second = pieces[:, 0], pieces[:, 1]
    return jnp.stack(
        [first * cosine - second * sine, second * cosine + first * sine], 1
    ).reshape(values.shape)


def turn_back(grads, cosine, sine):
    return turn(grads, cosine, -sine)


def norm_back(grad_rows, values, scale_rows, gain):
    scaled = grad_rows * gain
    inner_mean = jnp.mean(scaled * values, -1, keepdims=True)
    return (
        scale_rows * (scaled - values * scale_rows * scale_rows * inner_mean),
        jnp.sum(grad_rows * values * scale_rows, 0),
    )


def shards(
    tokens,
    positions,
    norm1_gain,
    w_query,
    w_key,
    w_value,
    w_out,
    norm2_gain,
    w_gate,
    w_up,
    w_down,
    cotangent,
):
    rows_here, width = tokens.shape
    size = w_key.shape[1]
    dp = lax.axis_size("dp")
    place = lax.axis_index("dp")
    spot = lax.axis_index("tp")
    tp_masks = range(lax.axis_size("tp"))
    own_rows = rows_here // lax.axis_size("tp")
    block = width // dp
    at = jnp.stack([place % SPAN, spot]).astype(jnp.int32)
    pos = positions.reshape(1, rows_here)

    def own(values):
        return lax.dynamic_slice_in_dim(values, spot * own_rows, own_rows, 0)

    inputs = tokens.astype(jnp.float32)
    scale_one = lax.rsqrt(jnp.mean(inputs * inputs, -1, keepdims=True) + EPSILON)
    normed_one = (inputs * scale_one * norm1_gain).astype(LOW)
    half = size // 2
    frequency = jnp.exp(
        -jnp.log(10000.0) * (2.0 * jnp.arange(half, dtype=jnp.float32) / size)
    )
    angles = frequency[:, None] * positions.astype(jnp.float32)[None, :]
    cosine, sine = jnp.cos(angles), jnp.sin(angles)
    w_kv = jnp.concatenate([w_key.T, w_value.T], 0)
    paired = dot(w_kv, normed_one, 1, 1)
    paired = jnp.concatenate([turn(paired[:size], cosine, sine), paired[size:]], 0).astype(LOW)
    blocks = [paired] + [flip(paired, "dp", m) for m in range(1, SPAN)]
    queries = (turn(dot(w_query, normed_one, 0, 1), cosine, sine) * size ** (-0.5)).astype(LOW)

    bit = place % 2
    bits = dp.bit_length() - 1
    half_count = dp // 2
    wide = w_query.shape[1]

    halves = [[2 * j + which for j in range(half_count)] for which in (bit, 1 - bit)]

    def exchange_order(order):
        return [
            sum(((j >> (len(order) - 1 - k)) & 1) << b for k, b in enumerate(order))
            for j in range(1 << len(order))
        ]

    down_bits = [0] + list(range(2, bits))
    down_places = [[where ^ m for m in exchange_order(down_bits)] for where in (place, place ^ 2)]
    rest_bits = list(range(1, bits))
    rest_places = [[where ^ m for m in exchange_order(rest_bits)] for where in (place, place ^ 1)]
    row_order = [spot ^ m for m in ROW_MASKS]

    def near_sum(part):
        send = part(2, 4).astype(LOW)
        near, kept = lax.optimization_barrier((flip(send, "tp", 1), part(0, 2)))
        pair = kept + near
        return pair[:own_rows], pair[own_rows:].astype(LOW)

    one_send = pick(after(normed_one, paired), halves[1], dp, 1)
    one_theirs = flip(one_send, "dp", 1)
    queries = after(queries, one_send)
    attended, lse = attention_forward(at, pos, queries, blocks, size, 2)
    attended = after(attended, one_theirs)

    branch, branch_out = near_sum(
        lambda lo, hi: dot(attended[:, lo * own_rows : hi * own_rows], w_out, 0, 0)
    )
    branch_far = flip(branch_out, "tp", 2)
    att_theirs = flip(after(attended, branch_out), "dp", 1)
    cot = pick(after(cotangent, branch_out), row_order, len(ROW_MASKS), 0)
    cot_send = pick(cot, down_places[1], dp, 1)
    cot_theirs = flip(cot_send, "dp", 2)
    own_inputs = own(tokens).astype(jnp.float32)
    middle = own_inputs + (after(branch, cot_send) + branch_far)

    scale_two = lax.rsqrt(jnp.mean(middle * middle, -1, keepdims=True) + EPSILON)
    own_two = (middle * scale_two * norm2_gain).astype(LOW)
    far_two = flip(own_two, "tp", 2)
    pair_two = jnp.concatenate([after(own_two, att_theirs), far_two], 0)
    core_two = flip(pair_two, "tp", 1)
    two_send = pick(pair_two, halves[1], dp, 1)
    two_near = flip(two_send, "dp", 1)
    grad_hidden = dot(after(cot, two_send), w_down, 1, 1)
    normed_two = jnp.concatenate([after(pair_two, grad_hidden), core_two], 0)

    gate_pre = dot(normed_two, w_gate, 1, 0)
    up_pre = dot(normed_two, w_up, 1, 0)
    sigma = jax.nn.sigmoid(gate_pre)
    active = gate_pre * sigma
    hidden = (active * up_pre).astype(LOW)
    grad_gate_pre = (grad_hidden * up_pre * sigma * (1.0 + gate_pre * (1.0 - sigma))).astype(LOW)
    grad_up_pre = (grad_hidden * active).astype(LOW)
    gate_theirs = flip(grad_gate_pre, "dp", 1)
    hidden_theirs = flip(hidden, "dp", 2)
    up_theirs = flip(grad_up_pre, "dp", 1)
    gate_late, cot_theirs, two_near = lax.optimization_barrier((grad_gate_pre, cot_theirs, two_near))

    def two_terms(lo, hi):
        rows = slice(lo * own_rows, hi * own_rows)
        return dot(gate_late[rows], w_gate, 1, 1) + dot(grad_up_pre[rows], w_up, 1, 1)

    grad_normed_two, two_out = near_sum(two_terms)
    two_far = flip(two_out, "tp", 2)
    two_theirs = jnp.concatenate([two_near, flip(two_near, "tp", 1)], 0)

    down_near, down = row_terms(after(hidden, two_out), w_down)
    grad_normed_two = after(grad_normed_two, down) + two_far

    grad_mid_norm, gain_two = norm_back(grad_normed_two, middle, scale_two, norm2_gain)
    grad_middle = own(cotangent).astype(jnp.float32) + grad_mid_norm
    branch_grad = grad_middle.astype(LOW)
    grad_far = flip(branch_grad, "tp", 2)

    down_near = flip(after(down_near, branch_grad), "tp", 1)
    natural = list(range(half_count))
    gate_terms = weight_terms(
        halves[0],
        natural,
        after(normed_two, branch_grad),
        two_theirs,
        grad_gate_pre,
        gate_theirs,
        keep=False,
    )
    grad_gate = parity_sum(gate_terms, 0)
    grad_pair = jnp.concatenate([after(branch_grad, gate_terms), grad_far], 0)
    grad_core = flip(grad_pair, "tp", 1)
    branch_send = pick(grad_pair, halves[1], dp, 1)
    branch_near = flip(branch_send, "dp", 1)

    def down_terms(lo, hi, *late):
        g = after(hidden, *late)
        return weight_terms(
            down_places[0][lo:hi], range(lo, hi), cot, cot_theirs, g, hidden_theirs
        )

    down_sent = down_terms(half_count // 2, half_count, branch_send)
    branch_all = jnp.concatenate([after(grad_pair, down_sent), grad_core], 0)
    grad_attended = dot(w_out, branch_all, 1, 1).astype(LOW)
    grads = attention_backward(
        at, pos, queries, grad_attended, attended, lse, cosine, sine, blocks, size, 2
    )
    grad_query_rows, kv_total = grads[0], grads[1]
    kv_back = [flip(grads[m + 1], "dp", m) for m in range(1, SPAN)]

    def rest_terms(lo, hi, x, x_far, g, g_far, transposed=False):
        return weight_terms(
            rest_places[0][lo:hi],
            [p // 2 for p in rest_places[0][lo:hi]],
            x,
            x_far,
            g,
            g_far,
            transposed,
        )

    down = down + after(down_near, grad_query_rows)
    down, down_out = down[:own_rows], down[own_rows:].astype(LOW)
    down_far = flip(down_out, "tp", 2)

    def up_terms(lo, hi, *late):
        return rest_terms(lo, hi, normed_two, two_theirs, after(grad_up_pre, *late), up_theirs)

    up_sent = up_terms(half_count // 2, half_count, grad_query_rows)
    up_got = [flip(up_sent, "dp", 2)]
    kv_total, branch_near = lax.optimization_barrier((kv_total, branch_near, up_sent, down_out))[:2]
    for back in kv_back:
        kv_total = kv_total + back
    key_grad = turn_back(kv_total[:size], cosine, sine)
    grad_kv_rows = jnp.concatenate([key_grad, kv_total[size:]], 0).astype(LOW)
    proj_rows = jnp.concatenate([grad_query_rows, grad_kv_rows], 0)
    proj_theirs = flip(proj_rows, "dp", 1)

    own_order = pick(proj_rows, row_order, len(ROW_MASKS), 1)

    def one_terms(lo, hi):
        cut = own_order[:, lo * own_rows : hi * own_rows]
        return dot(cut[:wide], w_query, 0, 1) + dot(cut[wide:], w_kv, 0, 0)

    grad_normed_one, one_out = near_sum(one_terms)
    one_far = flip(one_out, "tp", 2)
    down_got = [flip(after(down_sent, one_out), "dp", 1)]
    branch_theirs = jnp.concatenate([branch_near, flip(branch_near, "tp", 1)], 0)
    output_rows = (middle + (down + after(down_far, one_out))).astype(LOW)
    up_kept = up_terms(0, 1, one_out)
    out_kept = rest_terms(
        0, 1, branch_all, branch_theirs, after(attended, one_out), att_theirs, True
    )
    grad_normed_one = after(grad_normed_one, output_rows, up_kept, out_kept) + one_far
    grad_in_norm, gain_one = norm_back(grad_normed_one, own_inputs, own(scale_one), norm1_gain)
    input_rows = grad_middle + grad_in_norm

    def exchange_rest(terms, got, order, *late):
        left = half_count // 2
        for b in order[1:]:
            send = terms(left // 2, left, *late)
            rows = send.shape[0]
            for other in got:
                keep = rows * (left // 2) // (left - left // 2)
                send = send.astype(jnp.float32) + other[keep : keep + rows]
            send = send.astype(LOW)
            got.append(flip(send, "dp", 1 << b))
            left //= 2
        return send

    def exchange_end(kept, got):
        kept = kept.astype(jnp.float32)
        for other in got:
            kept = kept + other[:block]
        return kept

    up_last = exchange_rest(up_terms, up_got, rest_bits, input_rows)
    down_last = exchange_rest(down_terms, down_got, down_bits, up_last)

    gains = jnp.stack([after(gain_one, down_last), gain_two])
    for m in (1, 2):
        gains = gains + flip(gains, "tp", m)
    gains = pick(gains, rest_places[0], dp, 1) + flip(pick(gains, rest_places[1], dp, 1), "dp", 1)

    out_late, proj_late = lax.optimization_barrier((attended, proj_rows, up_last))[:2]

    def last_terms(lo, hi):
        return jnp.concatenate(
            [
                rest_terms(lo, hi, normed_one, one_theirs, proj_late, proj_theirs, True),
                rest_terms(lo, hi, branch_all, branch_theirs, out_late, att_theirs, True),
            ],
            1,
        )

    last_got, gains_got = [], []
    left = half_count
    for b in rest_bits:
        send = last_terms(left // 2, left)
        rows, columns = send.shape
        extra = gains[:, left // 2 * block : left * block]
        for other, other_gains in zip(last_got, gains_got):
            send = send.astype(jnp.float32) + other[left // 2 * block : left * block]
            extra = extra + other_gains[:, left // 2 * block : left * block]
        extra = jnp.pad(extra, ((0, 14), (0, columns - extra.shape[1] % columns)))[:, :columns]
        whole = jnp.concatenate([send.astype(LOW), extra.astype(LOW)], 0)
        got = flip(whole, "dp", 1 << b)
        last_got.append(got[:rows])
        gains_got.append(got[rows : rows + 2])
        left //= 2
    proj_kept = rest_terms(0, 1, normed_one, one_theirs, after(proj_late, whole), proj_theirs, True)
    down_kept = down_terms(0, 1, whole)
    grad_last = exchange_end(jnp.concatenate([proj_kept, out_kept], 1), last_got)
    gains = gains[:, :block]
    for other in gains_got:
        gains = gains + other[:, :block]
    grad_up = exchange_end(up_kept, up_got)
    grad_down = exchange_end(down_kept, down_got)
    narrow = wide + 2 * size

    return (
        output_rows,
        input_rows,
        gains[0],
        grad_last[:, :wide],
        grad_last[:, wide : wide + size],
        grad_last[:, wide + size : narrow],
        grad_last[:, narrow:].T,
        gains[1],
        grad_gate.astype(jnp.float32),
        grad_up,
        grad_down.T,
    )


def solution(mesh):
    placed = (
        P("dp", None),
        P("dp"),
        P(),
        P(None, "tp"),
        P(None, "tp"),
        P(None, "tp"),
        P("tp", None),
        P(),
        P(None, "tp"),
        P(None, "tp"),
        P("tp", None),
        P("dp", None),
    )
    return jax.shard_map(
        shards,
        mesh=mesh,
        in_specs=placed,
        out_specs=(
            P(("dp", "tp"), None),
            P(("dp", "tp"), None),
            P("dp"),
            P("dp", "tp"),
            P("dp", "tp"),
            P("dp", "tp"),
            P("tp", "dp"),
            P("dp"),
            P("dp", "tp"),
            P("dp", "tp"),
            P("tp", "dp"),
        ),
        check_vma=False,
    )
```

```python
import functools

import jax
import jax.numpy as jnp
from jax import lax
from jax.experimental import pallas as pl
from jax.experimental.pallas import tpu as pltpu
from jax.sharding import PartitionSpec as P

SPAN = 4
EPSILON = 1e-05
FAR_BELOW = -1e30
LOW = jnp.bfloat16
ROW_MASKS = (0, 2, 1, 3)


def flip(block, axis, mask):
    return lax.ppermute(block, axis, [(i, i ^ mask) for i in range(lax.axis_size(axis))])


def dot(left, right, left_dim, right_dim):
    return lax.dot_general(
        left,
        right,
        (((left_dim,), (right_dim,)), ((), ())),
        preferred_element_type=jnp.float32,
    )


def in_hbm(*arrays):
    return [pltpu.with_memory_space_constraint(a, pltpu.HBM) for a in arrays]


def own_mask(pos, begin, keys, queries):
    key_at = lax.broadcasted_iota(jnp.int32, (keys, queries), 0)
    query_at = lax.broadcasted_iota(jnp.int32, (keys, queries), 1) + begin
    return (key_at <= query_at) & (key_at >= query_at - pos)


def row_starts(spot, rows):
    part = rows // len(ROW_MASKS)
    return [pl.multiple_of((spot ^ m) * part, part) for m in ROW_MASKS]


def forward_kernel(
    heads,
    size,
    at_ref,
    pos_ref,
    q_ref,
    kv0,
    kv1,
    kv2,
    kv3,
    o_ref,
    lse_ref,
    keys,
    vals,
    top,
    acc,
    ordered,
):
    rank, spot = at_ref[0], at_ref[1]
    rows = pos_ref.shape[1]
    half = rows // 2

    @pl.when(pl.program_id(0) == 0)
    def _():
        for m, kv in enumerate((kv0, kv1, kv2, kv3)):
            keys[m] = kv[:size, :].T
            vals[m, :size, :] = kv[size:, :]
            vals[m, size:, :] = jnp.ones((16, rows), LOW)

    pos = pos_ref[...]
    for part in range(2):
        cols = slice(part * half, (part + 1) * half)
        count = (part + 1) * half
        mask = own_mask(pos[:, cols], part * half, count, half)
        for h in range(heads):
            scores = dot(keys[0, :count, :], q_ref[h * size : (h + 1) * size, cols], 1, 0)
            scores = jnp.where(mask, scores, FAR_BELOW)
            peak = jnp.max(scores, 0, keepdims=True)
            weights = jnp.exp(scores - peak).astype(LOW)
            acc[h, :, cols] = dot(vals[0, :, :count], weights, 1, 0)
            top[h, :, cols] = peak
    seen = pos > lax.broadcasted_iota(jnp.int32, (1, rows), 1)
    for m in range(1, SPAN):

        @pl.when((rank ^ m) < rank)
        def _():
            for h in range(heads):
                scores = dot(keys[m], q_ref[h * size : (h + 1) * size, :], 1, 0)
                old = top[h]
                peak = jnp.where(seen, jnp.maximum(old, jnp.max(scores, 0, keepdims=True)), old)
                weights = jnp.exp(scores - jnp.where(seen, peak, -FAR_BELOW)).astype(LOW)
                acc[h] = acc[h] * jnp.exp(old - peak) + dot(vals[m], weights, 1, 0)
                top[h] = peak

    for h in range(heads):
        total = acc[h, size : size + 1, :]
        ordered[h * size : (h + 1) * size, :] = (acc[h, :size, :] / total).astype(LOW)
        lse_ref[h] = top[h] + jnp.log(total)
    for j, start in enumerate(row_starts(spot, rows)):
        part = rows // len(ROW_MASKS)
        o_ref[:, j * part : (j + 1) * part] = ordered[:, pl.ds(start, part)]


def backward_kernel(
    heads,
    size,
    at_ref,
    pos_ref,
    q_ref,
    do_in,
    o_in,
    lse_ref,
    cos_ref,
    sin_ref,
    kv0,
    kv1,
    kv2,
    kv3,
    dq_ref,
    g0,
    g1,
    g2,
    g3,
    keys,
    vals,
    dq,
    total,
    do_ref,
    o_ref,
):
    rank, spot = at_ref[0], at_ref[1]
    rows = pos_ref.shape[1]
    half = rows // 2
    blocks = (kv0, kv1, kv2, kv3)
    step = pl.program_id(0)

    @pl.when(step == 0)
    def _():
        for m, kv in enumerate(blocks):
            keys[m] = kv[:size, :].T
            vals[m] = kv[size:, :].T
        total[...] = jnp.zeros_like(total)

    part = rows // len(ROW_MASKS)
    for j, start in enumerate(row_starts(spot, rows)):
        do_ref[:, pl.ds(start, part)] = do_in[:, j * part : (j + 1) * part]
        o_ref[:, pl.ds(start, part)] = o_in[:, j * part : (j + 1) * part]
    pos = pos_ref[...]
    seen = pos > lax.broadcasted_iota(jnp.int32, (1, rows), 1)
    deltas = []
    for h in range(heads):
        span = slice(h * size, (h + 1) * size)
        deltas.append(
            jnp.sum(
                do_ref[span, :].astype(jnp.float32) * o_ref[span, :].astype(jnp.float32),
                0,
                keepdims=True,
            )
        )
    for part in range(2):
        cols = slice(part * half, (part + 1) * half)
        count = (part + 1) * half
        mask = own_mask(pos[:, cols], part * half, count, half)
        for h in range(heads):
            span = slice(h * size, (h + 1) * size)
            query, grad = q_ref[span, cols], do_ref[span, cols]
            scores = dot(keys[0, :count, :], query, 1, 0)
            probs = jnp.exp(jnp.where(mask, scores, FAR_BELOW) - lse_ref[h, :, cols])
            grad_probs = dot(vals[0, :count, :], grad, 1, 0)
            grad_scores = (probs * (grad_probs - deltas[h][:, cols])).astype(LOW)
            total[0, :size, :count] += dot(query, grad_scores, 1, 1)
            total[0, size:, :count] += dot(grad, probs.astype(LOW), 1, 1)
            dq[h, :, cols] = dot(kv0[:size, :count], grad_scores, 1, 0)
    for m in range(1, SPAN):

        @pl.when((rank ^ m) < rank)
        def _():
            for h in range(heads):
                span = slice(h * size, (h + 1) * size)
                query, grad = q_ref[span, :], do_ref[span, :]
                scores = dot(keys[m], query, 1, 0)
                probs = jnp.exp(scores - jnp.where(seen, lse_ref[h], -FAR_BELOW))
                grad_probs = dot(vals[m], grad, 1, 0)
                grad_scores = (probs * (grad_probs - deltas[h])).astype(LOW)
                total[m, :size, :] += dot(query, grad_scores, 1, 1)
                total[m, size:, :] += dot(grad, probs.astype(LOW), 1, 1)
                dq[h] += dot(blocks[m][:size, :], grad_scores, 1, 0)

    middle_at = size // 2
    cosine, sine = cos_ref[...], sin_ref[...]
    for h in range(heads):
        first = dq[h, :middle_at, :] * size ** (-0.5)
        second = dq[h, middle_at:, :] * size ** (-0.5)
        base = h * size
        dq_ref[base : base + middle_at, :] = (first * cosine + second * sine).astype(LOW)
        dq_ref[base + middle_at : base + size, :] = (second * cosine - first * sine).astype(LOW)

    @pl.when(step == pl.num_programs(0) - 1)
    def _():
        g0[...] = total[0]
        for m, out in ((1, g1), (2, g2), (3, g3)):
            out[...] = total[m].astype(LOW)


def attention_forward(at, pos, queries, blocks, size, heads):
    wide, rows = queries.shape
    count = wide // size
    whole = pl.BlockSpec((2 * size, rows), lambda i, r: (0, 0))
    some = pl.BlockSpec((heads * size, rows), lambda i, r: (i, 0))
    return pl.pallas_call(
        functools.partial(forward_kernel, heads, size),
        out_shape=(
            jax.ShapeDtypeStruct((wide, rows), LOW),
            jax.ShapeDtypeStruct((count, 1, rows), jnp.float32),
        ),
        grid_spec=pltpu.PrefetchScalarGridSpec(
            num_scalar_prefetch=1,
            grid=(count // heads,),
            in_specs=[pl.BlockSpec((1, rows), lambda i, r: (0, 0)), some] + [whole] * SPAN,
            out_specs=[some, pl.BlockSpec((heads, 1, rows), lambda i, r: (i, 0, 0))],
            scratch_shapes=[
                pltpu.VMEM((SPAN, rows, size), LOW),
                pltpu.VMEM((SPAN, size + 16, rows), LOW),
                pltpu.VMEM((heads, 1, rows), jnp.float32),
                pltpu.VMEM((heads, size + 16, rows), jnp.float32),
                pltpu.VMEM((heads * size, rows), LOW),
            ],
        ),
        compiler_params=pltpu.CompilerParams(vmem_limit_bytes=24 << 20),
        cost_estimate=pl.CostEstimate(
            flops=32 * wide * rows * rows * SPAN,
            bytes_accessed=4 * wide * rows,
            transcendentals=0,
        ),
        name="attention_forward",
    )(at, pos, queries, *blocks)


def attention_backward(at, pos, queries, grads, attended, lse, cosine, sine, blocks, size, heads):
    wide, rows = queries.shape
    count = wide // size
    whole = pl.BlockSpec((2 * size, rows), lambda i, r: (0, 0))
    table = pl.BlockSpec((size // 2, rows), lambda i, r: (0, 0))
    some = pl.BlockSpec((heads * size, rows), lambda i, r: (i, 0))
    return pl.pallas_call(
        functools.partial(backward_kernel, heads, size),
        out_shape=(
            jax.ShapeDtypeStruct((wide, rows), LOW),
            jax.ShapeDtypeStruct((2 * size, rows), jnp.float32),
        )
        + (jax.ShapeDtypeStruct((2 * size, rows), LOW),) * (SPAN - 1),
        grid_spec=pltpu.PrefetchScalarGridSpec(
            num_scalar_prefetch=1,
            grid=(count // heads,),
            in_specs=[
                pl.BlockSpec((1, rows), lambda i, r: (0, 0)),
                some,
                some,
                some,
                pl.BlockSpec((heads, 1, rows), lambda i, r: (i, 0, 0)),
                table,
                table,
            ]
            + [whole] * SPAN,
            out_specs=[some] + [whole] * SPAN,
            scratch_shapes=[
                pltpu.VMEM((SPAN, rows, size), LOW),
                pltpu.VMEM((SPAN, rows, size), LOW),
                pltpu.VMEM((heads, size, rows), jnp.float32),
                pltpu.VMEM((SPAN, 2 * size, rows), jnp.float32),
                pltpu.VMEM((heads * size, rows), LOW),
                pltpu.VMEM((heads * size, rows), LOW),
            ],
        ),
        compiler_params=pltpu.CompilerParams(vmem_limit_bytes=24 << 20),
        cost_estimate=pl.CostEstimate(
            flops=48 * wide * rows * rows * SPAN,
            bytes_accessed=10 * wide * rows,
            transcendentals=0,
        ),
        name="attention_backward",
    )(at, pos, *in_hbm(queries, grads, attended, lse, cosine, sine, *blocks))


def pick(values, places, blocks, dim):
    size = values.shape[dim] // blocks
    return jnp.concatenate(
        [lax.dynamic_slice_in_dim(values, p * size, size, dim) for p in places], dim
    )


def after(value, *others):
    return lax.optimization_barrier((value, *others))[0]


def parity_sum(terms, dim):
    count = lax.axis_size("dp")
    groups = [list(range(p, count, 2)) for p in range(2)]
    return lax.psum_scatter(
        terms.astype(LOW), "dp", scatter_dimension=dim, axis_index_groups=groups, tiled=True
    )


def terms_kernel(transposed, places, x, x_far, g, g_far, out):
    del places
    side = 1 if transposed else 0
    out[...] = (dot(x[...], g[...], 0, side) + dot(x_far[...], g_far[...], 0, side)).astype(LOW)


def weight_terms(places, far_places, x, x_far, g, g_far, transposed=False, keep=True):
    count = len(places)
    size = x.shape[1] // lax.axis_size("dp")
    rows = x.shape[0]
    units = g.shape[0] if transposed else g.shape[1]
    if size % 128:
        side = 1 if transposed else 0
        mine = pick(x, places, x.shape[1] // size, 1)
        theirs = pick(x_far, far_places, x_far.shape[1] // size, 1)
        return (dot(mine, g, 0, side) + dot(theirs, g_far, 0, side)).astype(LOW)
    whole = pl.BlockSpec(g.shape, lambda i, p: (0, 0))
    return pl.pallas_call(
        functools.partial(terms_kernel, transposed),
        out_shape=(jax.ShapeDtypeStruct if keep else pltpu.HBM)((count * size, units), LOW),
        grid_spec=pltpu.PrefetchScalarGridSpec(
            num_scalar_prefetch=1,
            grid=(count,),
            in_specs=[
                pl.BlockSpec((rows, size), lambda i, p: (0, p[i])),
                pl.BlockSpec((rows, size), lambda i, p: (0, p[count + i])),
                whole,
                whole,
            ],
            out_specs=pl.BlockSpec((size, units), lambda i, p: (i, 0)),
        ),
        compiler_params=pltpu.CompilerParams(vmem_limit_bytes=24 << 20),
        cost_estimate=pl.CostEstimate(
            flops=8 * rows * count * size * units, bytes_accessed=4 * rows * units, transcendentals=0
        ),
        name="weight_terms",
    )(jnp.stack([*places, *far_places]).astype(jnp.int32), x, x_far, g, g_far)


def row_kernel(left, right, send, kept):
    half = left.shape[0] // 2
    send[...] = dot(left[half:, :], right[...], 1, 0).astype(LOW)
    kept[...] = dot(left[:half, :], right[...], 1, 0)


def row_terms(left, right):
    rows, units = left.shape
    half, width = rows // 2, right.shape[1]
    step = 256
    return pl.pallas_call(
        row_kernel,
        out_shape=(
            jax.ShapeDtypeStruct((half, width), LOW),
            jax.ShapeDtypeStruct((half, width), jnp.float32),
        ),
        grid=(width // step,),
        in_specs=[
            pl.BlockSpec((rows, units), lambda i: (0, 0)),
            pl.BlockSpec((units, step), lambda i: (0, i)),
        ],
        out_specs=[pl.BlockSpec((half, step), lambda i: (0, i))] * 2,
        compiler_params=pltpu.CompilerParams(vmem_limit_bytes=16 << 20),
        cost_estimate=pl.CostEstimate(
            flops=8 * rows * units * width, bytes_accessed=2 * units * width, transcendentals=0
        ),
        name="row_terms",
    )(left, right)


def turn(values, cosine, sine):
    half = cosine.shape[0]
    heads = values.shape[0] // (2 * half)
    pieces = values.reshape(heads, 2, half, values.shape[1])
    first, second = pieces[:, 0], pieces[:, 1]
    return jnp.stack(
        [first * cosine - second * sine, second * cosine + first * sine], 1
    ).reshape(values.shape)


def turn_back(grads, cosine, sine):
    return turn(grads, cosine, -sine)


def norm_back(grad_rows, values, scale_rows, gain):
    scaled = grad_rows * gain
    inner_mean = jnp.mean(scaled * values, -1, keepdims=True)
    return (
        scale_rows * (scaled - values * scale_rows * scale_rows * inner_mean),
        jnp.sum(grad_rows * values * scale_rows, 0),
    )


def shards(
    tokens,
    positions,
    norm1_gain,
    w_query,
    w_key,
    w_value,
    w_out,
    norm2_gain,
    w_gate,
    w_up,
    w_down,
    cotangent,
):
    rows_here, width = tokens.shape
    size = w_key.shape[1]
    dp = lax.axis_size("dp")
    place = lax.axis_index("dp")
    spot = lax.axis_index("tp")
    tp_masks = range(lax.axis_size("tp"))
    own_rows = rows_here // lax.axis_size("tp")
    block = width // dp
    at = jnp.stack([place % SPAN, spot]).astype(jnp.int32)
    pos = positions.reshape(1, rows_here)

    def own(values):
        return lax.dynamic_slice_in_dim(values, spot * own_rows, own_rows, 0)

    inputs = tokens.astype(jnp.float32)
    scale_one = lax.rsqrt(jnp.mean(inputs * inputs, -1, keepdims=True) + EPSILON)
    normed_one = (inputs * scale_one * norm1_gain).astype(LOW)
    half = size // 2
    frequency = jnp.exp(
        -jnp.log(10000.0) * (2.0 * jnp.arange(half, dtype=jnp.float32) / size)
    )
    angles = frequency[:, None] * positions.astype(jnp.float32)[None, :]
    cosine, sine = jnp.cos(angles), jnp.sin(angles)
    w_kv = jnp.concatenate([w_key.T, w_value.T], 0)
    paired = dot(w_kv, normed_one, 1, 1)
    paired = jnp.concatenate([turn(paired[:size], cosine, sine), paired[size:]], 0).astype(LOW)
    blocks = [paired] + [flip(paired, "dp", m) for m in range(1, SPAN)]
    queries = (turn(dot(w_query, normed_one, 0, 1), cosine, sine) * size ** (-0.5)).astype(LOW)

    bit = place % 2
    bits = dp.bit_length() - 1
    half_count = dp // 2
    wide = w_query.shape[1]

    halves = [[2 * j + which for j in range(half_count)] for which in (bit, 1 - bit)]

    def exchange_order(order):
        return [
            sum(((j >> (len(order) - 1 - k)) & 1) << b for k, b in enumerate(order))
            for j in range(1 << len(order))
        ]

    down_bits = [0] + list(range(2, bits))
    down_places = [[where ^ m for m in exchange_order(down_bits)] for where in (place, place ^ 2)]
    rest_bits = list(range(1, bits))
    rest_places = [[where ^ m for m in exchange_order(rest_bits)] for where in (place, place ^ 1)]
    row_order = [spot ^ m for m in ROW_MASKS]

    def near_sum(part):
        send = part(2, 4).astype(LOW)
        near, kept = lax.optimization_barrier((flip(send, "tp", 1), part(0, 2)))
        pair = kept + near
        return pair[:own_rows], pair[own_rows:].astype(LOW)

    one_send = pick(after(normed_one, paired), halves[1], dp, 1)
    one_theirs = flip(one_send, "dp", 1)
    queries = after(queries, one_send)
    attended, lse = attention_forward(at, pos, queries, blocks, size, 2)
    attended = after(attended, one_theirs)

    branch, branch_out = near_sum(
        lambda lo, hi: dot(attended[:, lo * own_rows : hi * own_rows], w_out, 0, 0)
    )
    branch_far = flip(branch_out, "tp", 2)
    att_theirs = flip(after(attended, branch_out), "dp", 1)
    cot = pick(after(cotangent, branch_out), row_order, len(ROW_MASKS), 0)
    cot_send = pick(cot, down_places[1], dp, 1)
    cot_theirs = flip(cot_send, "dp", 2)
    own_inputs = own(tokens).astype(jnp.float32)
    middle = own_inputs + (after(branch, cot_send) + branch_far)

    scale_two = lax.rsqrt(jnp.mean(middle * middle, -1, keepdims=True) + EPSILON)
    own_two = (middle * scale_two * norm2_gain).astype(LOW)
    far_two = flip(own_two, "tp", 2)
    pair_two = jnp.concatenate([after(own_two, att_theirs), far_two], 0)
    core_two = flip(pair_two, "tp", 1)
    two_send = pick(pair_two, halves[1], dp, 1)
    two_near = flip(two_send, "dp", 1)
    grad_hidden = dot(after(cot, two_send), w_down, 1, 1)
    normed_two = jnp.concatenate([after(pair_two, grad_hidden), core_two], 0)

    gate_pre = dot(normed_two, w_gate, 1, 0)
    up_pre = dot(normed_two, w_up, 1, 0)
    sigma = jax.nn.sigmoid(gate_pre)
    active = gate_pre * sigma
    hidden = (active * up_pre).astype(LOW)
    grad_gate_pre = (grad_hidden * up_pre * sigma * (1.0 + gate_pre * (1.0 - sigma))).astype(LOW)
    grad_up_pre = (grad_hidden * active).astype(LOW)
    gate_theirs = flip(grad_gate_pre, "dp", 1)
    hidden_theirs = flip(hidden, "dp", 2)
    up_theirs = flip(grad_up_pre, "dp", 1)
    gate_late, cot_theirs, two_near = lax.optimization_barrier((grad_gate_pre, cot_theirs, two_near))

    def two_terms(lo, hi):
        rows = slice(lo * own_rows, hi * own_rows)
        return dot(gate_late[rows], w_gate, 1, 1) + dot(grad_up_pre[rows], w_up, 1, 1)

    grad_normed_two, two_out = near_sum(two_terms)
    two_far = flip(two_out, "tp", 2)
    two_theirs = jnp.concatenate([two_near, flip(two_near, "tp", 1)], 0)

    down_near, down = row_terms(after(hidden, two_out), w_down)
    grad_normed_two = after(grad_normed_two, down) + two_far

    grad_mid_norm, gain_two = norm_back(grad_normed_two, middle, scale_two, norm2_gain)
    grad_middle = own(cotangent).astype(jnp.float32) + grad_mid_norm
    branch_grad = grad_middle.astype(LOW)
    grad_far = flip(branch_grad, "tp", 2)

    down_near = flip(after(down_near, branch_grad), "tp", 1)
    natural = list(range(half_count))
    gate_terms = weight_terms(
        halves[0],
        natural,
        after(normed_two, branch_grad),
        two_theirs,
        grad_gate_pre,
        gate_theirs,
        keep=False,
    )
    grad_gate = parity_sum(gate_terms, 0)
    grad_pair = jnp.concatenate([after(branch_grad, gate_terms), grad_far], 0)
    grad_core = flip(grad_pair, "tp", 1)
    branch_send = pick(grad_pair, halves[1], dp, 1)
    branch_near = flip(branch_send, "dp", 1)

    def down_terms(lo, hi, *late):
        g = after(hidden, *late)
        return weight_terms(
            down_places[0][lo:hi], range(lo, hi), cot, cot_theirs, g, hidden_theirs
        )

    down_sent = down_terms(half_count // 2, half_count, branch_send)
    branch_all = jnp.concatenate([after(grad_pair, down_sent), grad_core], 0)
    grad_attended = dot(w_out, branch_all, 1, 1).astype(LOW)
    grads = attention_backward(
        at, pos, queries, grad_attended, attended, lse, cosine, sine, blocks, size, 2
    )
    grad_query_rows, kv_total = grads[0], grads[1]
    kv_back = [flip(grads[m + 1], "dp", m) for m in range(1, SPAN)]

    def rest_terms(lo, hi, x, x_far, g, g_far, transposed=False):
        return weight_terms(
            rest_places[0][lo:hi],
            [p // 2 for p in rest_places[0][lo:hi]],
            x,
            x_far,
            g,
            g_far,
            transposed,
        )

    down = down + after(down_near, grad_query_rows)
    down, down_out = down[:own_rows], down[own_rows:].astype(LOW)
    down_far = flip(down_out, "tp", 2)

    def up_terms(lo, hi, *late):
        return rest_terms(lo, hi, normed_two, two_theirs, after(grad_up_pre, *late), up_theirs)

    up_sent = up_terms(half_count // 2, half_count, grad_query_rows)
    up_got = [flip(up_sent, "dp", 2)]
    kv_total, branch_near = lax.optimization_barrier((kv_total, branch_near, up_sent, down_out))[:2]
    for back in kv_back:
        kv_total = kv_total + back
    key_grad = turn_back(kv_total[:size], cosine, sine)
    grad_kv_rows = jnp.concatenate([key_grad, kv_total[size:]], 0).astype(LOW)
    proj_rows = jnp.concatenate([grad_query_rows, grad_kv_rows], 0)
    proj_theirs = flip(proj_rows, "dp", 1)

    own_order = pick(proj_rows, row_order, len(ROW_MASKS), 1)

    def one_terms(lo, hi):
        cut = own_order[:, lo * own_rows : hi * own_rows]
        return dot(cut[:wide], w_query, 0, 1) + dot(cut[wide:], w_kv, 0, 0)

    grad_normed_one, one_out = near_sum(one_terms)
    one_far = flip(one_out, "tp", 2)
    down_got = [flip(after(down_sent, one_out), "dp", 1)]
    branch_theirs = jnp.concatenate([branch_near, flip(branch_near, "tp", 1)], 0)
    output_rows = (middle + (down + after(down_far, one_out))).astype(LOW)
    up_kept = up_terms(0, 1, one_out)
    out_kept = rest_terms(
        0, 1, branch_all, branch_theirs, after(attended, one_out), att_theirs, True
    )
    grad_gate = grad_gate.astype(jnp.float32)
    grad_normed_one = after(grad_normed_one, output_rows, up_kept, out_kept, grad_gate) + one_far
    grad_in_norm, gain_one = norm_back(grad_normed_one, own_inputs, own(scale_one), norm1_gain)
    input_rows = grad_middle + grad_in_norm

    def exchange_rest(terms, got, order, *late):
        left = half_count // 2
        for b in order[1:]:
            send = terms(left // 2, left, *late)
            rows = send.shape[0]
            for other in got:
                keep = rows * (left // 2) // (left - left // 2)
                send = send.astype(jnp.float32) + other[keep : keep + rows]
            send = send.astype(LOW)
            got.append(flip(send, "dp", 1 << b))
            left //= 2
        return send

    def exchange_end(kept, got):
        kept = kept.astype(jnp.float32)
        for other in got:
            kept = kept + other[:block]
        return kept

    up_last = exchange_rest(up_terms, up_got, rest_bits, input_rows)
    down_last = exchange_rest(down_terms, down_got, down_bits, up_last)

    gains = jnp.stack([after(gain_one, down_last), gain_two])
    for m in (1, 2):
        gains = gains + flip(gains, "tp", m)
    gains = pick(gains, rest_places[0], dp, 1) + flip(pick(gains, rest_places[1], dp, 1), "dp", 1)

    out_late, proj_late = lax.optimization_barrier((attended, proj_rows, up_last))[:2]

    def last_terms(lo, hi):
        return jnp.concatenate(
            [
                rest_terms(lo, hi, normed_one, one_theirs, proj_late, proj_theirs, True),
                rest_terms(lo, hi, branch_all, branch_theirs, out_late, att_theirs, True),
            ],
            1,
        )

    last_got, gains_got = [], []
    left = half_count
    for b in rest_bits:
        send = last_terms(left // 2, left)
        rows, columns = send.shape
        extra = gains[:, left // 2 * block : left * block]
        for other, other_gains in zip(last_got, gains_got):
            send = send.astype(jnp.float32) + other[left // 2 * block : left * block]
            extra = extra + other_gains[:, left // 2 * block : left * block]
        extra = jnp.pad(extra, ((0, 14), (0, columns - extra.shape[1] % columns)))[:, :columns]
        whole = jnp.concatenate([send.astype(LOW), extra.astype(LOW)], 0)
        got = flip(whole, "dp", 1 << b)
        last_got.append(got[:rows])
        gains_got.append(got[rows : rows + 2])
        left //= 2
    proj_kept = rest_terms(0, 1, normed_one, one_theirs, after(proj_late, whole), proj_theirs, True)
    down_kept = down_terms(0, 1, whole)
    grad_last = exchange_end(jnp.concatenate([proj_kept, out_kept], 1), last_got)
    gains = gains[:, :block]
    for other in gains_got:
        gains = gains + other[:, :block]
    grad_up = exchange_end(up_kept, up_got)
    grad_down = exchange_end(down_kept, down_got)
    narrow = wide + 2 * size

    return (
        output_rows,
        input_rows,
        gains[0],
        grad_last[:, :wide],
        grad_last[:, wide : wide + size],
        grad_last[:, wide + size : narrow],
        grad_last[:, narrow:].T,
        gains[1],
        grad_gate,
        grad_up,
        grad_down.T,
    )


def solution(mesh):
    placed = (
        P("dp", None),
        P("dp"),
        P(),
        P(None, "tp"),
        P(None, "tp"),
        P(None, "tp"),
        P("tp", None),
        P(),
        P(None, "tp"),
        P(None, "tp"),
        P("tp", None),
        P("dp", None),
    )
    return jax.shard_map(
        shards,
        mesh=mesh,
        in_specs=placed,
        out_specs=(
            P(("dp", "tp"), None),
            P(("dp", "tp"), None),
            P("dp"),
            P("dp", "tp"),
            P("dp", "tp"),
            P("dp", "tp"),
            P("tp", "dp"),
            P("dp"),
            P("dp", "tp"),
            P("dp", "tp"),
            P("tp", "dp"),
        ),
        check_vma=False,
    )
```

```python
import functools

import jax
import jax.numpy as jnp
from jax import lax
from jax.experimental import pallas as pl
from jax.experimental.pallas import tpu as pltpu
from jax.sharding import PartitionSpec as P

SPAN = 4
EPSILON = 1e-05
FAR_BELOW = -1e30
LOW = jnp.bfloat16
ROW_MASKS = (0, 2, 1, 3)


def flip(block, axis, mask):
    return lax.ppermute(block, axis, [(i, i ^ mask) for i in range(lax.axis_size(axis))])


def dot(left, right, left_dim, right_dim):
    return lax.dot_general(
        left,
        right,
        (((left_dim,), (right_dim,)), ((), ())),
        preferred_element_type=jnp.float32,
    )


def in_hbm(*arrays):
    return [pltpu.with_memory_space_constraint(a, pltpu.HBM) for a in arrays]


def own_mask(pos, begin, keys, queries):
    key_at = lax.broadcasted_iota(jnp.int32, (keys, queries), 0)
    query_at = lax.broadcasted_iota(jnp.int32, (keys, queries), 1) + begin
    return (key_at <= query_at) & (key_at >= query_at - pos)


def row_starts(spot, rows):
    part = rows // len(ROW_MASKS)
    return [pl.multiple_of((spot ^ m) * part, part) for m in ROW_MASKS]


def forward_kernel(
    heads,
    size,
    at_ref,
    pos_ref,
    q_ref,
    kv0,
    kv1,
    kv2,
    kv3,
    o_ref,
    lse_ref,
    keys,
    vals,
    top,
    acc,
    ordered,
):
    rank, spot = at_ref[0], at_ref[1]
    rows = pos_ref.shape[1]
    half = rows // 2

    @pl.when(pl.program_id(0) == 0)
    def _():
        for m, kv in enumerate((kv0, kv1, kv2, kv3)):
            keys[m] = kv[:size, :].T
            vals[m, :size, :] = kv[size:, :]
            vals[m, size:, :] = jnp.ones((16, rows), LOW)

    pos = pos_ref[...]
    for part in range(2):
        cols = slice(part * half, (part + 1) * half)
        count = (part + 1) * half
        mask = own_mask(pos[:, cols], part * half, count, half)
        for h in range(heads):
            scores = dot(keys[0, :count, :], q_ref[h * size : (h + 1) * size, cols], 1, 0)
            scores = jnp.where(mask, scores, FAR_BELOW)
            peak = jnp.max(scores, 0, keepdims=True)
            weights = jnp.exp(scores - peak).astype(LOW)
            acc[h, :, cols] = dot(vals[0, :, :count], weights, 1, 0)
            top[h, :, cols] = peak
    seen = pos > lax.broadcasted_iota(jnp.int32, (1, rows), 1)
    for m in range(1, SPAN):

        @pl.when((rank ^ m) < rank)
        def _():
            for h in range(heads):
                scores = dot(keys[m], q_ref[h * size : (h + 1) * size, :], 1, 0)
                old = top[h]
                peak = jnp.where(seen, jnp.maximum(old, jnp.max(scores, 0, keepdims=True)), old)
                weights = jnp.exp(scores - jnp.where(seen, peak, -FAR_BELOW)).astype(LOW)
                acc[h] = acc[h] * jnp.exp(old - peak) + dot(vals[m], weights, 1, 0)
                top[h] = peak

    for h in range(heads):
        total = acc[h, size : size + 1, :]
        ordered[h * size : (h + 1) * size, :] = (acc[h, :size, :] / total).astype(LOW)
        lse_ref[h] = top[h] + jnp.log(total)
    for j, start in enumerate(row_starts(spot, rows)):
        part = rows // len(ROW_MASKS)
        o_ref[:, j * part : (j + 1) * part] = ordered[:, pl.ds(start, part)]


def backward_kernel(
    heads,
    size,
    at_ref,
    pos_ref,
    q_ref,
    do_in,
    o_in,
    lse_ref,
    cos_ref,
    sin_ref,
    kv0,
    kv1,
    kv2,
    kv3,
    dq_ref,
    g0,
    g1,
    g2,
    g3,
    keys,
    vals,
    dq,
    total,
    do_ref,
    o_ref,
):
    rank, spot = at_ref[0], at_ref[1]
    rows = pos_ref.shape[1]
    half = rows // 2
    blocks = (kv0, kv1, kv2, kv3)
    step = pl.program_id(0)

    @pl.when(step == 0)
    def _():
        for m, kv in enumerate(blocks):
            keys[m] = kv[:size, :].T
            vals[m] = kv[size:, :].T
        total[...] = jnp.zeros_like(total)

    part = rows // len(ROW_MASKS)
    for j, start in enumerate(row_starts(spot, rows)):
        do_ref[:, pl.ds(start, part)] = do_in[:, j * part : (j + 1) * part]
        o_ref[:, pl.ds(start, part)] = o_in[:, j * part : (j + 1) * part]
    pos = pos_ref[...]
    seen = pos > lax.broadcasted_iota(jnp.int32, (1, rows), 1)
    deltas = []
    for h in range(heads):
        span = slice(h * size, (h + 1) * size)
        deltas.append(
            jnp.sum(
                do_ref[span, :].astype(jnp.float32) * o_ref[span, :].astype(jnp.float32),
                0,
                keepdims=True,
            )
        )
    for part in range(2):
        cols = slice(part * half, (part + 1) * half)
        count = (part + 1) * half
        mask = own_mask(pos[:, cols], part * half, count, half)
        for h in range(heads):
            span = slice(h * size, (h + 1) * size)
            query, grad = q_ref[span, cols], do_ref[span, cols]
            scores = dot(keys[0, :count, :], query, 1, 0)
            probs = jnp.exp(jnp.where(mask, scores, FAR_BELOW) - lse_ref[h, :, cols])
            grad_probs = dot(vals[0, :count, :], grad, 1, 0)
            grad_scores = (probs * (grad_probs - deltas[h][:, cols])).astype(LOW)
            total[0, :size, :count] += dot(query, grad_scores, 1, 1)
            total[0, size:, :count] += dot(grad, probs.astype(LOW), 1, 1)
            dq[h, :, cols] = dot(kv0[:size, :count], grad_scores, 1, 0)
    for m in range(1, SPAN):

        @pl.when((rank ^ m) < rank)
        def _():
            for h in range(heads):
                span = slice(h * size, (h + 1) * size)
                query, grad = q_ref[span, :], do_ref[span, :]
                scores = dot(keys[m], query, 1, 0)
                probs = jnp.exp(scores - jnp.where(seen, lse_ref[h], -FAR_BELOW))
                grad_probs = dot(vals[m], grad, 1, 0)
                grad_scores = (probs * (grad_probs - deltas[h])).astype(LOW)
                total[m, :size, :] += dot(query, grad_scores, 1, 1)
                total[m, size:, :] += dot(grad, probs.astype(LOW), 1, 1)
                dq[h] += dot(blocks[m][:size, :], grad_scores, 1, 0)

    middle_at = size // 2
    cosine, sine = cos_ref[...], sin_ref[...]
    for h in range(heads):
        first = dq[h, :middle_at, :] * size ** (-0.5)
        second = dq[h, middle_at:, :] * size ** (-0.5)
        base = h * size
        dq_ref[base : base + middle_at, :] = (first * cosine + second * sine).astype(LOW)
        dq_ref[base + middle_at : base + size, :] = (second * cosine - first * sine).astype(LOW)

    @pl.when(step == pl.num_programs(0) - 1)
    def _():
        g0[...] = total[0]
        for m, out in ((1, g1), (2, g2), (3, g3)):
            out[...] = total[m].astype(LOW)


def attention_forward(at, pos, queries, blocks, size, heads):
    wide, rows = queries.shape
    count = wide // size
    whole = pl.BlockSpec((2 * size, rows), lambda i, r: (0, 0))
    some = pl.BlockSpec((heads * size, rows), lambda i, r: (i, 0))
    return pl.pallas_call(
        functools.partial(forward_kernel, heads, size),
        out_shape=(
            jax.ShapeDtypeStruct((wide, rows), LOW),
            jax.ShapeDtypeStruct((count, 1, rows), jnp.float32),
        ),
        grid_spec=pltpu.PrefetchScalarGridSpec(
            num_scalar_prefetch=1,
            grid=(count // heads,),
            in_specs=[pl.BlockSpec((1, rows), lambda i, r: (0, 0)), some] + [whole] * SPAN,
            out_specs=[some, pl.BlockSpec((heads, 1, rows), lambda i, r: (i, 0, 0))],
            scratch_shapes=[
                pltpu.VMEM((SPAN, rows, size), LOW),
                pltpu.VMEM((SPAN, size + 16, rows), LOW),
                pltpu.VMEM((heads, 1, rows), jnp.float32),
                pltpu.VMEM((heads, size + 16, rows), jnp.float32),
                pltpu.VMEM((heads * size, rows), LOW),
            ],
        ),
        compiler_params=pltpu.CompilerParams(vmem_limit_bytes=24 << 20),
        cost_estimate=pl.CostEstimate(
            flops=32 * wide * rows * rows * SPAN,
            bytes_accessed=4 * wide * rows,
            transcendentals=0,
        ),
        name="attention_forward",
    )(at, pos, queries, *blocks)


def attention_backward(at, pos, queries, grads, attended, lse, cosine, sine, blocks, size, heads):
    wide, rows = queries.shape
    count = wide // size
    whole = pl.BlockSpec((2 * size, rows), lambda i, r: (0, 0))
    table = pl.BlockSpec((size // 2, rows), lambda i, r: (0, 0))
    some = pl.BlockSpec((heads * size, rows), lambda i, r: (i, 0))
    return pl.pallas_call(
        functools.partial(backward_kernel, heads, size),
        out_shape=(
            jax.ShapeDtypeStruct((wide, rows), LOW),
            jax.ShapeDtypeStruct((2 * size, rows), jnp.float32),
        )
        + (jax.ShapeDtypeStruct((2 * size, rows), LOW),) * (SPAN - 1),
        grid_spec=pltpu.PrefetchScalarGridSpec(
            num_scalar_prefetch=1,
            grid=(count // heads,),
            in_specs=[
                pl.BlockSpec((1, rows), lambda i, r: (0, 0)),
                some,
                some,
                some,
                pl.BlockSpec((heads, 1, rows), lambda i, r: (i, 0, 0)),
                table,
                table,
            ]
            + [whole] * SPAN,
            out_specs=[some] + [whole] * SPAN,
            scratch_shapes=[
                pltpu.VMEM((SPAN, rows, size), LOW),
                pltpu.VMEM((SPAN, rows, size), LOW),
                pltpu.VMEM((heads, size, rows), jnp.float32),
                pltpu.VMEM((SPAN, 2 * size, rows), jnp.float32),
                pltpu.VMEM((heads * size, rows), LOW),
                pltpu.VMEM((heads * size, rows), LOW),
            ],
        ),
        compiler_params=pltpu.CompilerParams(vmem_limit_bytes=24 << 20),
        cost_estimate=pl.CostEstimate(
            flops=48 * wide * rows * rows * SPAN,
            bytes_accessed=10 * wide * rows,
            transcendentals=0,
        ),
        name="attention_backward",
    )(at, pos, *in_hbm(queries, grads, attended, lse, cosine, sine, *blocks))


def pick(values, places, blocks, dim):
    size = values.shape[dim] // blocks
    return jnp.concatenate(
        [lax.dynamic_slice_in_dim(values, p * size, size, dim) for p in places], dim
    )


def after(value, *others):
    return lax.optimization_barrier((value, *others))[0]


def parity_sum(terms, dim):
    count = lax.axis_size("dp")
    groups = [list(range(p, count, 2)) for p in range(2)]
    return lax.psum_scatter(
        terms.astype(LOW), "dp", scatter_dimension=dim, axis_index_groups=groups, tiled=True
    )


def terms_kernel(transposed, places, x, x_far, g, g_far, out):
    del places
    side = 1 if transposed else 0
    out[...] = (dot(x[...], g[...], 0, side) + dot(x_far[...], g_far[...], 0, side)).astype(LOW)


def weight_terms(places, far_places, x, x_far, g, g_far, transposed=False, keep=True):
    count = len(places)
    size = x.shape[1] // lax.axis_size("dp")
    rows = x.shape[0]
    units = g.shape[0] if transposed else g.shape[1]
    if size % 128:
        side = 1 if transposed else 0
        mine = pick(x, places, x.shape[1] // size, 1)
        theirs = pick(x_far, far_places, x_far.shape[1] // size, 1)
        return (dot(mine, g, 0, side) + dot(theirs, g_far, 0, side)).astype(LOW)
    whole = pl.BlockSpec(g.shape, lambda i, p: (0, 0))
    return pl.pallas_call(
        functools.partial(terms_kernel, transposed),
        out_shape=(jax.ShapeDtypeStruct if keep else pltpu.HBM)((count * size, units), LOW),
        grid_spec=pltpu.PrefetchScalarGridSpec(
            num_scalar_prefetch=1,
            grid=(count,),
            in_specs=[
                pl.BlockSpec((rows, size), lambda i, p: (0, p[i])),
                pl.BlockSpec((rows, size), lambda i, p: (0, p[count + i])),
                whole,
                whole,
            ],
            out_specs=pl.BlockSpec((size, units), lambda i, p: (i, 0)),
        ),
        compiler_params=pltpu.CompilerParams(vmem_limit_bytes=24 << 20),
        cost_estimate=pl.CostEstimate(
            flops=24 * rows * count * size * units, bytes_accessed=4 * rows * units, transcendentals=0
        ),
        name="weight_terms",
    )(jnp.stack([*places, *far_places]).astype(jnp.int32), x, x_far, g, g_far)


def row_kernel(left, right, send, kept):
    half = left.shape[0] // 2
    send[...] = dot(left[half:, :], right[...], 1, 0).astype(LOW)
    kept[...] = dot(left[:half, :], right[...], 1, 0)


def row_terms(left, right):
    rows, units = left.shape
    half, width = rows // 2, right.shape[1]
    step = 256
    return pl.pallas_call(
        row_kernel,
        out_shape=(
            jax.ShapeDtypeStruct((half, width), LOW),
            jax.ShapeDtypeStruct((half, width), jnp.float32),
        ),
        grid=(width // step,),
        in_specs=[
            pl.BlockSpec((rows, units), lambda i: (0, 0)),
            pl.BlockSpec((units, step), lambda i: (0, i)),
        ],
        out_specs=[pl.BlockSpec((half, step), lambda i: (0, i))] * 2,
        compiler_params=pltpu.CompilerParams(vmem_limit_bytes=16 << 20),
        cost_estimate=pl.CostEstimate(
            flops=8 * rows * units * width, bytes_accessed=2 * units * width, transcendentals=0
        ),
        name="row_terms",
    )(left, right)


def turn(values, cosine, sine):
    half = cosine.shape[0]
    heads = values.shape[0] // (2 * half)
    pieces = values.reshape(heads, 2, half, values.shape[1])
    first, second = pieces[:, 0], pieces[:, 1]
    return jnp.stack(
        [first * cosine - second * sine, second * cosine + first * sine], 1
    ).reshape(values.shape)


def turn_back(grads, cosine, sine):
    return turn(grads, cosine, -sine)


def norm_back(grad_rows, values, scale_rows, gain):
    scaled = grad_rows * gain
    inner_mean = jnp.mean(scaled * values, -1, keepdims=True)
    return (
        scale_rows * (scaled - values * scale_rows * scale_rows * inner_mean),
        jnp.sum(grad_rows * values * scale_rows, 0),
    )


def shards(
    tokens,
    positions,
    norm1_gain,
    w_query,
    w_key,
    w_value,
    w_out,
    norm2_gain,
    w_gate,
    w_up,
    w_down,
    cotangent,
):
    rows_here, width = tokens.shape
    size = w_key.shape[1]
    dp = lax.axis_size("dp")
    place = lax.axis_index("dp")
    spot = lax.axis_index("tp")
    tp_masks = range(lax.axis_size("tp"))
    own_rows = rows_here // lax.axis_size("tp")
    block = width // dp
    at = jnp.stack([place % SPAN, spot]).astype(jnp.int32)
    pos = positions.reshape(1, rows_here)

    def own(values):
        return lax.dynamic_slice_in_dim(values, spot * own_rows, own_rows, 0)

    inputs = tokens.astype(jnp.float32)
    scale_one = lax.rsqrt(jnp.mean(inputs * inputs, -1, keepdims=True) + EPSILON)
    normed_one = (inputs * scale_one * norm1_gain).astype(LOW)
    half = size // 2
    frequency = jnp.exp(
        -jnp.log(10000.0) * (2.0 * jnp.arange(half, dtype=jnp.float32) / size)
    )
    angles = frequency[:, None] * positions.astype(jnp.float32)[None, :]
    cosine, sine = jnp.cos(angles), jnp.sin(angles)
    w_kv = jnp.concatenate([w_key.T, w_value.T], 0)
    paired = dot(w_kv, normed_one, 1, 1)
    paired = jnp.concatenate([turn(paired[:size], cosine, sine), paired[size:]], 0).astype(LOW)
    blocks = [paired] + [flip(paired, "dp", m) for m in range(1, SPAN)]
    queries = (turn(dot(w_query, normed_one, 0, 1), cosine, sine) * size ** (-0.5)).astype(LOW)

    bit = place % 2
    bits = dp.bit_length() - 1
    half_count = dp // 2
    wide = w_query.shape[1]

    halves = [[2 * j + which for j in range(half_count)] for which in (bit, 1 - bit)]

    def exchange_order(order):
        return [
            sum(((j >> (len(order) - 1 - k)) & 1) << b for k, b in enumerate(order))
            for j in range(1 << len(order))
        ]

    down_bits = [0] + list(range(2, bits))
    down_places = [[where ^ m for m in exchange_order(down_bits)] for where in (place, place ^ 2)]
    rest_bits = list(range(1, bits))
    rest_places = [[where ^ m for m in exchange_order(rest_bits)] for where in (place, place ^ 1)]
    row_order = [spot ^ m for m in ROW_MASKS]

    def near_sum(part):
        send = part(2, 4).astype(LOW)
        near, kept = lax.optimization_barrier((flip(send, "tp", 1), part(0, 2)))
        pair = kept + near
        return pair[:own_rows], pair[own_rows:].astype(LOW)

    one_send = pick(after(normed_one, paired), halves[1], dp, 1)
    one_theirs = flip(one_send, "dp", 1)
    queries = after(queries, one_send)
    attended, lse = attention_forward(at, pos, queries, blocks, size, 2)
    attended = after(attended, one_theirs)

    branch, branch_out = near_sum(
        lambda lo, hi: dot(attended[:, lo * own_rows : hi * own_rows], w_out, 0, 0)
    )
    branch_far = flip(branch_out, "tp", 2)
    att_theirs = flip(after(attended, branch_out), "dp", 1)
    cot = pick(after(cotangent, branch_out), row_order, len(ROW_MASKS), 0)
    cot_send = pick(cot, down_places[1], dp, 1)
    cot_theirs = flip(cot_send, "dp", 2)
    own_inputs = own(tokens).astype(jnp.float32)
    grad_hidden = dot(after(cot, cot_send), w_down, 1, 1)
    middle = own_inputs + (after(branch, cot_send, grad_hidden) + branch_far)

    scale_two = lax.rsqrt(jnp.mean(middle * middle, -1, keepdims=True) + EPSILON)
    own_two = (middle * scale_two * norm2_gain).astype(LOW)
    far_two = flip(own_two, "tp", 2)
    pair_two = jnp.concatenate([after(own_two, att_theirs), far_two], 0)
    core_two = flip(pair_two, "tp", 1)
    two_send = pick(pair_two, halves[1], dp, 1)
    two_near = flip(two_send, "dp", 1)
    normed_two = jnp.concatenate([after(pair_two, two_send), core_two], 0)

    gate_pre = dot(normed_two, w_gate, 1, 0)
    up_pre = dot(normed_two, w_up, 1, 0)
    sigma = jax.nn.sigmoid(gate_pre)
    active = gate_pre * sigma
    hidden = (active * up_pre).astype(LOW)
    grad_gate_pre = (grad_hidden * up_pre * sigma * (1.0 + gate_pre * (1.0 - sigma))).astype(LOW)
    grad_up_pre = (grad_hidden * active).astype(LOW)
    gate_theirs = flip(grad_gate_pre, "dp", 1)
    hidden_theirs = flip(hidden, "dp", 2)
    up_theirs = flip(grad_up_pre, "dp", 1)
    gate_late, cot_theirs, two_near = lax.optimization_barrier((grad_gate_pre, cot_theirs, two_near))

    def two_terms(lo, hi):
        rows = slice(lo * own_rows, hi * own_rows)
        return dot(gate_late[rows], w_gate, 1, 1) + dot(grad_up_pre[rows], w_up, 1, 1)

    grad_normed_two, two_out = near_sum(two_terms)
    two_far = flip(two_out, "tp", 2)
    two_theirs = jnp.concatenate([two_near, flip(two_near, "tp", 1)], 0)

    down_near, down = row_terms(after(hidden, two_out), w_down)
    grad_normed_two = after(grad_normed_two, down) + two_far

    grad_mid_norm, gain_two = norm_back(grad_normed_two, middle, scale_two, norm2_gain)
    grad_middle = own(cotangent).astype(jnp.float32) + grad_mid_norm
    branch_grad = grad_middle.astype(LOW)
    grad_far = flip(branch_grad, "tp", 2)

    down_near = flip(after(down_near, branch_grad), "tp", 1)
    natural = list(range(half_count))
    gate_terms = weight_terms(
        halves[0],
        natural,
        after(normed_two, branch_grad),
        two_theirs,
        grad_gate_pre,
        gate_theirs,
        keep=False,
    )
    grad_gate = parity_sum(gate_terms, 0)
    grad_pair = jnp.concatenate([after(branch_grad, gate_terms), grad_far], 0)
    grad_core = flip(grad_pair, "tp", 1)
    branch_send = pick(grad_pair, halves[1], dp, 1)

    def near_flip(terms, bit):
        half = terms.shape[0] // 2
        return [flip(terms[half:], "dp", 1 << bit), flip(terms[:half], "dp", 1 << bit)]

    def down_terms(lo, hi, *late):
        g = after(hidden, *late)
        return weight_terms(
            down_places[0][lo:hi], range(lo, hi), cot, cot_theirs, g, hidden_theirs
        )

    down_sent = down_terms(half_count // 2, half_count, branch_send)
    half = down_sent.shape[0] // 2
    down_first = flip(down_sent[half:], "dp", 1)
    branch_all = jnp.concatenate([after(grad_pair, down_sent), grad_core], 0)
    grad_attended = dot(w_out, branch_all, 1, 1).astype(LOW)
    grads = attention_backward(
        at, pos, queries, grad_attended, attended, lse, cosine, sine, blocks, size, 2
    )
    grad_query_rows, kv_total = grads[0], grads[1]
    kv_back = [flip(grads[m + 1], "dp", m) for m in range(1, SPAN)]

    def rest_terms(lo, hi, x, x_far, g, g_far, transposed=False):
        return weight_terms(
            rest_places[0][lo:hi],
            [p // 2 for p in rest_places[0][lo:hi]],
            x,
            x_far,
            g,
            g_far,
            transposed,
        )

    down = down + after(down_near, grad_query_rows)
    down, down_out = down[:own_rows], down[own_rows:].astype(LOW)
    down_far = flip(down_out, "tp", 2)

    def up_terms(lo, hi, *late):
        return rest_terms(lo, hi, normed_two, two_theirs, after(grad_up_pre, *late), up_theirs)

    up_sent = up_terms(half_count // 2, half_count, grad_query_rows)
    up_first = flip(up_sent[half:], "dp", 2)

    def exchange_mid(terms, first, order, *late):
        got, left = [first], half_count // 2
        for b in order[1:]:
            send = terms(left // 2, left, *late).astype(jnp.float32)
            rows = send.shape[0]
            for other in got:
                send = send + other[other.shape[0] - rows :]
            send = send.astype(LOW)
            got.append(flip(send, "dp", 1 << b))
            left //= 2
        return got[1:], send

    down_late, down_last = exchange_mid(down_terms, down_first, down_bits, grad_query_rows)
    kv_total = lax.optimization_barrier((kv_total, up_sent, down_out, down_last))[0]
    for back in kv_back:
        kv_total = kv_total + back
    key_grad = turn_back(kv_total[:size], cosine, sine)
    grad_kv_rows = jnp.concatenate([key_grad, kv_total[size:]], 0).astype(LOW)
    proj_rows = jnp.concatenate([grad_query_rows, grad_kv_rows], 0)
    proj_theirs = flip(proj_rows, "dp", 1)
    branch_near = flip(after(branch_send, proj_rows), "dp", 1)

    own_order = pick(proj_rows, row_order, len(ROW_MASKS), 1)

    def one_terms(lo, hi):
        cut = own_order[:, lo * own_rows : hi * own_rows]
        return dot(cut[:wide], w_query, 0, 1) + dot(cut[wide:], w_kv, 0, 0)

    grad_normed_one, one_out = near_sum(one_terms)
    one_far = flip(one_out, "tp", 2)
    branch_theirs = jnp.concatenate([branch_near, flip(branch_near, "tp", 1)], 0)
    output_rows = (middle + (down + after(down_far, one_out))).astype(LOW)
    up_kept = up_terms(0, 1, one_out)
    out_kept = rest_terms(
        0, 1, branch_all, branch_theirs, after(attended, one_out), att_theirs, True
    )
    grad_gate = grad_gate.astype(jnp.float32)
    grad_normed_one = after(grad_normed_one, output_rows, up_kept, out_kept, grad_gate) + one_far
    grad_in_norm, gain_one = norm_back(grad_normed_one, own_inputs, own(scale_one), norm1_gain)
    input_rows = grad_middle + grad_in_norm

    up_late, up_last = exchange_mid(up_terms, up_first, rest_bits, input_rows)
    gain_one, *down_late = lax.optimization_barrier((gain_one, *down_late, up_last))[:-1]
    gains = jnp.stack([gain_one, gain_two])
    for m in (1, 2):
        gains = gains + flip(gains, "tp", m)
    gains = pick(gains, rest_places[0], dp, 1) + flip(pick(gains, rest_places[1], dp, 1), "dp", 1)

    out_late, proj_late = lax.optimization_barrier((attended, proj_rows, up_last))[:2]

    def last_terms(lo, hi, *late):
        first, second = after(proj_late, *late), after(out_late, *late)
        return jnp.concatenate(
            [
                rest_terms(lo, hi, normed_one, one_theirs, first, proj_theirs, True),
                rest_terms(lo, hi, branch_all, branch_theirs, second, att_theirs, True),
            ],
            1,
        )

    def with_gains(terms, lo, hi, *others):
        extra = gains[:, lo * block : hi * block]
        for other, other_gains in others:
            terms = terms.astype(jnp.float32) + other
            extra = extra + other_gains
        columns = terms.shape[1]
        extra = jnp.pad(extra, ((0, 14), (0, -extra.shape[1] % columns)))[:, :columns]
        return jnp.concatenate([terms.astype(LOW), extra.astype(LOW)], 0)

    def split(message, count):
        rows = count * block
        return message[:rows], message[rows : rows + 2, :rows]

    quarter = half_count // 4
    sent = last_terms(half_count // 2, half_count)
    cut = quarter * block
    firsts = with_gains(sent[cut:], 3 * quarter, half_count)
    seconds = with_gains(sent[:cut], 2 * quarter, 3 * quarter)
    mids = [split(flip(firsts, "dp", 2), quarter)]
    proj_kept = rest_terms(0, 1, normed_one, one_theirs, after(proj_late, firsts), proj_theirs, True)
    down_kept = down_terms(0, 1, firsts)
    left = half_count // 2
    for b in rest_bits[1:]:
        count = left // 2
        terms = last_terms(count, left, firsts)
        terms, *up_late = lax.optimization_barrier((terms, *up_late, proj_kept, down_kept))[:-2]
        send = with_gains(
            terms, count, left, *((o[-count * block :], g[:, -count * block :]) for o, g in mids)
        )
        mids.append(split(flip(send, "dp", 1 << b), count))
        left = count
    last_second = split(flip(after(seconds, send), "dp", 2), quarter)
    up_second, down_second = lax.optimization_barrier((up_sent[:half], down_sent[:half], send))[:2]
    up_second, down_second = flip(up_second, "dp", 2), flip(down_second, "dp", 1)

    def ending(kept, *others):
        kept = kept.astype(jnp.float32)
        for other in others:
            kept = kept + other[:block]
        return kept

    grad_last = ending(
        jnp.concatenate([proj_kept, out_kept], 1), last_second[0], *(m[0] for m in mids[1:])
    )
    gains = gains[:, :block] + last_second[1][:, :block]
    for _, other in mids[1:]:
        gains = gains + other[:, :block]
    grad_up = ending(up_kept, up_second, *up_late)
    grad_down = ending(down_kept, down_second, *down_late)
    narrow = wide + 2 * size

    return (
        output_rows,
        input_rows,
        gains[0],
        grad_last[:, :wide],
        grad_last[:, wide : wide + size],
        grad_last[:, wide + size : narrow],
        grad_last[:, narrow:].T,
        gains[1],
        grad_gate,
        grad_up,
        grad_down.T,
    )


def solution(mesh):
    placed = (
        P("dp", None),
        P("dp"),
        P(),
        P(None, "tp"),
        P(None, "tp"),
        P(None, "tp"),
        P("tp", None),
        P(),
        P(None, "tp"),
        P(None, "tp"),
        P("tp", None),
        P("dp", None),
    )
    return jax.shard_map(
        shards,
        mesh=mesh,
        in_specs=placed,
        out_specs=(
            P(("dp", "tp"), None),
            P(("dp", "tp"), None),
            P("dp"),
            P("dp", "tp"),
            P("dp", "tp"),
            P("dp", "tp"),
            P("tp", "dp"),
            P("dp"),
            P("dp", "tp"),
            P("dp", "tp"),
            P("tp", "dp"),
        ),
        check_vma=False,
    )
```

```python
import functools

import jax
import jax.numpy as jnp
from jax import lax
from jax.experimental import pallas as pl
from jax.experimental.pallas import tpu as pltpu
from jax.sharding import PartitionSpec as P

SPAN = 4
EPSILON = 1e-05
FAR_BELOW = -1e30
LOW = jnp.bfloat16
ROW_MASKS = (0, 2, 1, 3)


def flip(block, axis, mask):
    return lax.ppermute(block, axis, [(i, i ^ mask) for i in range(lax.axis_size(axis))])


def dot(left, right, left_dim, right_dim):
    return lax.dot_general(
        left,
        right,
        (((left_dim,), (right_dim,)), ((), ())),
        preferred_element_type=jnp.float32,
    )


def in_hbm(*arrays):
    return [pltpu.with_memory_space_constraint(a, pltpu.HBM) for a in arrays]


def own_mask(pos, begin, keys, queries):
    key_at = lax.broadcasted_iota(jnp.int32, (keys, queries), 0)
    query_at = lax.broadcasted_iota(jnp.int32, (keys, queries), 1) + begin
    return (key_at <= query_at) & (key_at >= query_at - pos)


def row_starts(spot, rows):
    part = rows // len(ROW_MASKS)
    return [pl.multiple_of((spot ^ m) * part, part) for m in ROW_MASKS]


def forward_kernel(
    heads,
    size,
    at_ref,
    pos_ref,
    q_ref,
    kv0,
    kv1,
    kv2,
    kv3,
    o_ref,
    lse_ref,
    keys,
    vals,
    top,
    acc,
    ordered,
):
    rank, spot = at_ref[0], at_ref[1]
    rows = pos_ref.shape[1]
    half = rows // 2

    @pl.when(pl.program_id(0) == 0)
    def _():
        for m, kv in enumerate((kv0, kv1, kv2, kv3)):
            keys[m] = kv[:size, :].T
            vals[m, :size, :] = kv[size:, :]
            vals[m, size:, :] = jnp.ones((16, rows), LOW)

    pos = pos_ref[...]
    for part in range(2):
        cols = slice(part * half, (part + 1) * half)
        count = (part + 1) * half
        mask = own_mask(pos[:, cols], part * half, count, half)
        for h in range(heads):
            scores = dot(keys[0, :count, :], q_ref[h * size : (h + 1) * size, cols], 1, 0)
            scores = jnp.where(mask, scores, FAR_BELOW)
            peak = jnp.max(scores, 0, keepdims=True)
            weights = jnp.exp(scores - peak).astype(LOW)
            acc[h, :, cols] = dot(vals[0, :, :count], weights, 1, 0)
            top[h, :, cols] = peak
    seen = pos > lax.broadcasted_iota(jnp.int32, (1, rows), 1)
    for m in range(1, SPAN):

        @pl.when((rank ^ m) < rank)
        def _():
            for h in range(heads):
                scores = dot(keys[m], q_ref[h * size : (h + 1) * size, :], 1, 0)
                old = top[h]
                peak = jnp.where(seen, jnp.maximum(old, jnp.max(scores, 0, keepdims=True)), old)
                weights = jnp.exp(scores - jnp.where(seen, peak, -FAR_BELOW)).astype(LOW)
                acc[h] = acc[h] * jnp.exp(old - peak) + dot(vals[m], weights, 1, 0)
                top[h] = peak

    for h in range(heads):
        total = acc[h, size : size + 1, :]
        ordered[h * size : (h + 1) * size, :] = (acc[h, :size, :] / total).astype(LOW)
        lse_ref[h] = top[h] + jnp.log(total)
    for j, start in enumerate(row_starts(spot, rows)):
        part = rows // len(ROW_MASKS)
        o_ref[:, j * part : (j + 1) * part] = ordered[:, pl.ds(start, part)]


def backward_kernel(
    heads,
    size,
    at_ref,
    pos_ref,
    q_ref,
    do_in,
    o_in,
    lse_ref,
    cos_ref,
    sin_ref,
    kv0,
    kv1,
    kv2,
    kv3,
    dq_ref,
    g0,
    g1,
    g2,
    g3,
    keys,
    vals,
    dq,
    total,
    do_ref,
    o_ref,
):
    rank, spot = at_ref[0], at_ref[1]
    rows = pos_ref.shape[1]
    half = rows // 2
    blocks = (kv0, kv1, kv2, kv3)
    step = pl.program_id(0)

    @pl.when(step == 0)
    def _():
        for m, kv in enumerate(blocks):
            keys[m] = kv[:size, :].T
            vals[m] = kv[size:, :].T
        total[...] = jnp.zeros_like(total)

    part = rows // len(ROW_MASKS)
    for j, start in enumerate(row_starts(spot, rows)):
        do_ref[:, pl.ds(start, part)] = do_in[:, j * part : (j + 1) * part]
        o_ref[:, pl.ds(start, part)] = o_in[:, j * part : (j + 1) * part]
    pos = pos_ref[...]
    seen = pos > lax.broadcasted_iota(jnp.int32, (1, rows), 1)
    deltas = []
    for h in range(heads):
        span = slice(h * size, (h + 1) * size)
        deltas.append(
            jnp.sum(
                do_ref[span, :].astype(jnp.float32) * o_ref[span, :].astype(jnp.float32),
                0,
                keepdims=True,
            )
        )
    for part in range(2):
        cols = slice(part * half, (part + 1) * half)
        count = (part + 1) * half
        mask = own_mask(pos[:, cols], part * half, count, half)
        for h in range(heads):
            span = slice(h * size, (h + 1) * size)
            query, grad = q_ref[span, cols], do_ref[span, cols]
            scores = dot(keys[0, :count, :], query, 1, 0)
            probs = jnp.exp(jnp.where(mask, scores, FAR_BELOW) - lse_ref[h, :, cols])
            grad_probs = dot(vals[0, :count, :], grad, 1, 0)
            grad_scores = (probs * (grad_probs - deltas[h][:, cols])).astype(LOW)
            total[0, :size, :count] += dot(query, grad_scores, 1, 1)
            total[0, size:, :count] += dot(grad, probs.astype(LOW), 1, 1)
            dq[h, :, cols] = dot(kv0[:size, :count], grad_scores, 1, 0)
    for m in range(1, SPAN):

        @pl.when((rank ^ m) < rank)
        def _():
            for h in range(heads):
                span = slice(h * size, (h + 1) * size)
                query, grad = q_ref[span, :], do_ref[span, :]
                scores = dot(keys[m], query, 1, 0)
                probs = jnp.exp(scores - jnp.where(seen, lse_ref[h], -FAR_BELOW))
                grad_probs = dot(vals[m], grad, 1, 0)
                grad_scores = (probs * (grad_probs - deltas[h])).astype(LOW)
                total[m, :size, :] += dot(query, grad_scores, 1, 1)
                total[m, size:, :] += dot(grad, probs.astype(LOW), 1, 1)
                dq[h] += dot(blocks[m][:size, :], grad_scores, 1, 0)

    middle_at = size // 2
    cosine, sine = cos_ref[...], sin_ref[...]
    for h in range(heads):
        first = dq[h, :middle_at, :] * size ** (-0.5)
        second = dq[h, middle_at:, :] * size ** (-0.5)
        base = h * size
        dq_ref[base : base + middle_at, :] = (first * cosine + second * sine).astype(LOW)
        dq_ref[base + middle_at : base + size, :] = (second * cosine - first * sine).astype(LOW)

    @pl.when(step == pl.num_programs(0) - 1)
    def _():
        g0[...] = total[0]
        for m, out in ((1, g1), (2, g2), (3, g3)):
            out[...] = total[m].astype(LOW)


def attention_forward(at, pos, queries, blocks, size, heads):
    wide, rows = queries.shape
    count = wide // size
    whole = pl.BlockSpec((2 * size, rows), lambda i, r: (0, 0))
    some = pl.BlockSpec((heads * size, rows), lambda i, r: (i, 0))
    return pl.pallas_call(
        functools.partial(forward_kernel, heads, size),
        out_shape=(
            jax.ShapeDtypeStruct((wide, rows), LOW),
            jax.ShapeDtypeStruct((count, 1, rows), jnp.float32),
        ),
        grid_spec=pltpu.PrefetchScalarGridSpec(
            num_scalar_prefetch=1,
            grid=(count // heads,),
            in_specs=[pl.BlockSpec((1, rows), lambda i, r: (0, 0)), some] + [whole] * SPAN,
            out_specs=[some, pl.BlockSpec((heads, 1, rows), lambda i, r: (i, 0, 0))],
            scratch_shapes=[
                pltpu.VMEM((SPAN, rows, size), LOW),
                pltpu.VMEM((SPAN, size + 16, rows), LOW),
                pltpu.VMEM((heads, 1, rows), jnp.float32),
                pltpu.VMEM((heads, size + 16, rows), jnp.float32),
                pltpu.VMEM((heads * size, rows), LOW),
            ],
        ),
        compiler_params=pltpu.CompilerParams(vmem_limit_bytes=24 << 20),
        cost_estimate=pl.CostEstimate(
            flops=32 * wide * rows * rows * SPAN,
            bytes_accessed=4 * wide * rows,
            transcendentals=0,
        ),
        name="attention_forward",
    )(at, pos, queries, *blocks)


def attention_backward(at, pos, queries, grads, attended, lse, cosine, sine, blocks, size, heads):
    wide, rows = queries.shape
    count = wide // size
    whole = pl.BlockSpec((2 * size, rows), lambda i, r: (0, 0))
    table = pl.BlockSpec((size // 2, rows), lambda i, r: (0, 0))
    some = pl.BlockSpec((heads * size, rows), lambda i, r: (i, 0))
    return pl.pallas_call(
        functools.partial(backward_kernel, heads, size),
        out_shape=(
            jax.ShapeDtypeStruct((wide, rows), LOW),
            jax.ShapeDtypeStruct((2 * size, rows), jnp.float32),
        )
        + (jax.ShapeDtypeStruct((2 * size, rows), LOW),) * (SPAN - 1),
        grid_spec=pltpu.PrefetchScalarGridSpec(
            num_scalar_prefetch=1,
            grid=(count // heads,),
            in_specs=[
                pl.BlockSpec((1, rows), lambda i, r: (0, 0)),
                some,
                some,
                some,
                pl.BlockSpec((heads, 1, rows), lambda i, r: (i, 0, 0)),
                table,
                table,
            ]
            + [whole] * SPAN,
            out_specs=[some] + [whole] * SPAN,
            scratch_shapes=[
                pltpu.VMEM((SPAN, rows, size), LOW),
                pltpu.VMEM((SPAN, rows, size), LOW),
                pltpu.VMEM((heads, size, rows), jnp.float32),
                pltpu.VMEM((SPAN, 2 * size, rows), jnp.float32),
                pltpu.VMEM((heads * size, rows), LOW),
                pltpu.VMEM((heads * size, rows), LOW),
            ],
        ),
        compiler_params=pltpu.CompilerParams(vmem_limit_bytes=24 << 20),
        cost_estimate=pl.CostEstimate(
            flops=48 * wide * rows * rows * SPAN,
            bytes_accessed=10 * wide * rows,
            transcendentals=0,
        ),
        name="attention_backward",
    )(at, pos, *in_hbm(queries, grads, attended, lse, cosine, sine, *blocks))


def pick(values, places, blocks, dim):
    size = values.shape[dim] // blocks
    return jnp.concatenate(
        [lax.dynamic_slice_in_dim(values, p * size, size, dim) for p in places], dim
    )


def after(value, *others):
    return lax.optimization_barrier((value, *others))[0]


def parity_sum(terms, dim):
    count = lax.axis_size("dp")
    groups = [list(range(p, count, 2)) for p in range(2)]
    return lax.psum_scatter(
        terms.astype(LOW), "dp", scatter_dimension=dim, axis_index_groups=groups, tiled=True
    )


def terms_kernel(transposed, places, x, x_far, g, g_far, out):
    del places
    side = 1 if transposed else 0
    out[...] = (dot(x[...], g[...], 0, side) + dot(x_far[...], g_far[...], 0, side)).astype(LOW)


def weight_terms(places, far_places, x, x_far, g, g_far, transposed=False, keep=True):
    count = len(places)
    size = x.shape[1] // lax.axis_size("dp")
    rows = x.shape[0]
    units = g.shape[0] if transposed else g.shape[1]
    if size % 128:
        side = 1 if transposed else 0
        mine = pick(x, places, x.shape[1] // size, 1)
        theirs = pick(x_far, far_places, x_far.shape[1] // size, 1)
        return (dot(mine, g, 0, side) + dot(theirs, g_far, 0, side)).astype(LOW)
    whole = pl.BlockSpec(g.shape, lambda i, p: (0, 0))
    return pl.pallas_call(
        functools.partial(terms_kernel, transposed),
        out_shape=(jax.ShapeDtypeStruct if keep else pltpu.HBM)((count * size, units), LOW),
        grid_spec=pltpu.PrefetchScalarGridSpec(
            num_scalar_prefetch=1,
            grid=(count,),
            in_specs=[
                pl.BlockSpec((rows, size), lambda i, p: (0, p[i])),
                pl.BlockSpec((rows, size), lambda i, p: (0, p[count + i])),
                whole,
                whole,
            ],
            out_specs=pl.BlockSpec((size, units), lambda i, p: (i, 0)),
        ),
        compiler_params=pltpu.CompilerParams(vmem_limit_bytes=24 << 20),
        cost_estimate=pl.CostEstimate(
            flops=24 * rows * count * size * units, bytes_accessed=4 * rows * units, transcendentals=0
        ),
        name="weight_terms",
    )(jnp.stack([*places, *far_places]).astype(jnp.int32), x, x_far, g, g_far)


def copy_kernel(places, source, target):
    del places
    target[...] = source[...]


def pick_columns(values, places):
    rows, count = values.shape[0], len(places)
    blocks = lax.axis_size("dp")
    size = values.shape[1] // blocks
    if size % 128:
        return pick(values, places, blocks, 1)
    return pl.pallas_call(
        copy_kernel,
        out_shape=jax.ShapeDtypeStruct((rows, count * size), values.dtype),
        grid_spec=pltpu.PrefetchScalarGridSpec(
            num_scalar_prefetch=1,
            grid=(count,),
            in_specs=[pl.BlockSpec((rows, size), lambda i, p: (0, p[i]))],
            out_specs=pl.BlockSpec((rows, size), lambda i, p: (0, i)),
        ),
        compiler_params=pltpu.CompilerParams(vmem_limit_bytes=8 << 20),
        cost_estimate=pl.CostEstimate(
            flops=65536 * rows * count * size, bytes_accessed=4 * rows * count * size, transcendentals=0
        ),
        name="pick_columns",
    )(jnp.stack(places).astype(jnp.int32), values)


def row_kernel(left, right, send, kept):
    half = left.shape[0] // 2
    send[...] = dot(left[half:, :], right[...], 1, 0).astype(LOW)
    kept[...] = dot(left[:half, :], right[...], 1, 0)


def row_terms(left, right):
    rows, units = left.shape
    half, width = rows // 2, right.shape[1]
    step = 256
    return pl.pallas_call(
        row_kernel,
        out_shape=(
            jax.ShapeDtypeStruct((half, width), LOW),
            jax.ShapeDtypeStruct((half, width), jnp.float32),
        ),
        grid=(width // step,),
        in_specs=[
            pl.BlockSpec((rows, units), lambda i: (0, 0)),
            pl.BlockSpec((units, step), lambda i: (0, i)),
        ],
        out_specs=[pl.BlockSpec((half, step), lambda i: (0, i))] * 2,
        compiler_params=pltpu.CompilerParams(vmem_limit_bytes=16 << 20),
        cost_estimate=pl.CostEstimate(
            flops=8 * rows * units * width, bytes_accessed=2 * units * width, transcendentals=0
        ),
        name="row_terms",
    )(left, right)


def turn(values, cosine, sine):
    half = cosine.shape[0]
    heads = values.shape[0] // (2 * half)
    pieces = values.reshape(heads, 2, half, values.shape[1])
    first, second = pieces[:, 0], pieces[:, 1]
    return jnp.stack(
        [first * cosine - second * sine, second * cosine + first * sine], 1
    ).reshape(values.shape)


def turn_back(grads, cosine, sine):
    return turn(grads, cosine, -sine)


def norm_back(grad_rows, values, scale_rows, gain):
    scaled = grad_rows * gain
    inner_mean = jnp.mean(scaled * values, -1, keepdims=True)
    return (
        scale_rows * (scaled - values * scale_rows * scale_rows * inner_mean),
        jnp.sum(grad_rows * values * scale_rows, 0),
    )


def shards(
    tokens,
    positions,
    norm1_gain,
    w_query,
    w_key,
    w_value,
    w_out,
    norm2_gain,
    w_gate,
    w_up,
    w_down,
    cotangent,
):
    rows_here, width = tokens.shape
    size = w_key.shape[1]
    dp = lax.axis_size("dp")
    place = lax.axis_index("dp")
    spot = lax.axis_index("tp")
    tp_masks = range(lax.axis_size("tp"))
    own_rows = rows_here // lax.axis_size("tp")
    block = width // dp
    at = jnp.stack([place % SPAN, spot]).astype(jnp.int32)
    pos = positions.reshape(1, rows_here)

    def own(values):
        return lax.dynamic_slice_in_dim(values, spot * own_rows, own_rows, 0)

    inputs = tokens.astype(jnp.float32)
    scale_one = lax.rsqrt(jnp.mean(inputs * inputs, -1, keepdims=True) + EPSILON)
    normed_one = (inputs * scale_one * norm1_gain).astype(LOW)
    half = size // 2
    frequency = jnp.exp(
        -jnp.log(10000.0) * (2.0 * jnp.arange(half, dtype=jnp.float32) / size)
    )
    angles = frequency[:, None] * positions.astype(jnp.float32)[None, :]
    cosine, sine = jnp.cos(angles), jnp.sin(angles)
    w_kv = jnp.concatenate([w_key.T, w_value.T], 0)
    paired = dot(w_kv, normed_one, 1, 1)
    paired = jnp.concatenate([turn(paired[:size], cosine, sine), paired[size:]], 0).astype(LOW)
    blocks = [paired] + [flip(paired, "dp", m) for m in range(1, SPAN)]
    queries = (turn(dot(w_query, normed_one, 0, 1), cosine, sine) * size ** (-0.5)).astype(LOW)

    bit = place % 2
    bits = dp.bit_length() - 1
    half_count = dp // 2
    wide = w_query.shape[1]

    halves = [[2 * j + which for j in range(half_count)] for which in (bit, 1 - bit)]

    def exchange_order(order):
        return [
            sum(((j >> (len(order) - 1 - k)) & 1) << b for k, b in enumerate(order))
            for j in range(1 << len(order))
        ]

    down_bits = [0] + list(range(2, bits))
    down_places = [[where ^ m for m in exchange_order(down_bits)] for where in (place, place ^ 2)]
    rest_bits = list(range(1, bits))
    rest_places = [[where ^ m for m in exchange_order(rest_bits)] for where in (place, place ^ 1)]
    row_order = [spot ^ m for m in ROW_MASKS]

    def near_sum(part):
        send = part(2, 4).astype(LOW)
        near, kept = lax.optimization_barrier((flip(send, "tp", 1), part(0, 2)))
        pair = kept + near
        return pair[:own_rows], pair[own_rows:].astype(LOW)

    one_send = pick_columns(after(normed_one, paired), halves[1])
    one_theirs = flip(one_send, "dp", 1)
    queries = after(queries, one_send)
    attended, lse = attention_forward(at, pos, queries, blocks, size, 2)
    attended = after(attended, one_theirs)

    branch, branch_out = near_sum(
        lambda lo, hi: dot(attended[:, lo * own_rows : hi * own_rows], w_out, 0, 0)
    )
    branch_far = flip(branch_out, "tp", 2)
    att_theirs = flip(after(attended, branch_out), "dp", 1)
    cot = pick(after(cotangent, branch_out), row_order, len(ROW_MASKS), 0)
    cot_send = pick_columns(cot, down_places[1])
    cot_theirs = flip(cot_send, "dp", 2)
    own_inputs = own(tokens).astype(jnp.float32)
    grad_hidden = dot(after(cot, cot_send), w_down, 1, 1)
    middle = own_inputs + (after(branch, cot_send, grad_hidden) + branch_far)

    scale_two = lax.rsqrt(jnp.mean(middle * middle, -1, keepdims=True) + EPSILON)
    own_two = (middle * scale_two * norm2_gain).astype(LOW)
    far_two = flip(own_two, "tp", 2)
    pair_two = jnp.concatenate([after(own_two, att_theirs), far_two], 0)
    core_two = flip(pair_two, "tp", 1)
    two_send = pick_columns(pair_two, halves[1])
    two_near = flip(two_send, "dp", 1)
    normed_two = jnp.concatenate([after(pair_two, two_send), core_two], 0)

    gate_pre = dot(normed_two, w_gate, 1, 0)
    up_pre = dot(normed_two, w_up, 1, 0)
    sigma = jax.nn.sigmoid(gate_pre)
    active = gate_pre * sigma
    hidden = (active * up_pre).astype(LOW)
    grad_gate_pre = (grad_hidden * up_pre * sigma * (1.0 + gate_pre * (1.0 - sigma))).astype(LOW)
    grad_up_pre = (grad_hidden * active).astype(LOW)
    gate_theirs = flip(grad_gate_pre, "dp", 1)
    hidden_theirs = flip(hidden, "dp", 2)
    up_theirs = flip(grad_up_pre, "dp", 1)
    gate_late, cot_theirs, two_near = lax.optimization_barrier((grad_gate_pre, cot_theirs, two_near))

    def two_terms(lo, hi):
        rows = slice(lo * own_rows, hi * own_rows)
        return dot(gate_late[rows], w_gate, 1, 1) + dot(grad_up_pre[rows], w_up, 1, 1)

    grad_normed_two, two_out = near_sum(two_terms)
    two_far = flip(two_out, "tp", 2)
    two_theirs = jnp.concatenate([two_near, flip(two_near, "tp", 1)], 0)

    down_near, down = row_terms(after(hidden, two_out), w_down)
    grad_normed_two = after(grad_normed_two, down) + two_far

    grad_mid_norm, gain_two = norm_back(grad_normed_two, middle, scale_two, norm2_gain)
    grad_middle = own(cotangent).astype(jnp.float32) + grad_mid_norm
    branch_grad = grad_middle.astype(LOW)
    grad_far = flip(branch_grad, "tp", 2)

    down_near = flip(after(down_near, branch_grad), "tp", 1)
    natural = list(range(half_count))
    gate_terms = weight_terms(
        halves[0],
        natural,
        after(normed_two, branch_grad),
        two_theirs,
        grad_gate_pre,
        gate_theirs,
        keep=False,
    )
    grad_gate = parity_sum(gate_terms, 0)
    grad_pair = jnp.concatenate([after(branch_grad, gate_terms), grad_far], 0)
    grad_core = flip(grad_pair, "tp", 1)
    branch_send = pick_columns(grad_pair, halves[1])

    def near_flip(terms, bit):
        half = terms.shape[0] // 2
        return [flip(terms[half:], "dp", 1 << bit), flip(terms[:half], "dp", 1 << bit)]

    def down_terms(lo, hi, *late):
        g = after(hidden, *late)
        return weight_terms(
            down_places[0][lo:hi], range(lo, hi), cot, cot_theirs, g, hidden_theirs
        )

    down_sent = down_terms(half_count // 2, half_count, branch_send)
    half = down_sent.shape[0] // 2
    down_first = flip(down_sent[half:], "dp", 1)
    branch_all = jnp.concatenate([after(grad_pair, down_sent), grad_core], 0)
    grad_attended = dot(w_out, branch_all, 1, 1).astype(LOW)
    grads = attention_backward(
        at, pos, queries, grad_attended, attended, lse, cosine, sine, blocks, size, 2
    )
    grad_query_rows, kv_total = grads[0], grads[1]
    kv_back = [flip(grads[m + 1], "dp", m) for m in range(1, SPAN)]

    def rest_terms(lo, hi, x, x_far, g, g_far, transposed=False):
        return weight_terms(
            rest_places[0][lo:hi],
            [p // 2 for p in rest_places[0][lo:hi]],
            x,
            x_far,
            g,
            g_far,
            transposed,
        )

    down = down + after(down_near, grad_query_rows)
    down, down_out = down[:own_rows], down[own_rows:].astype(LOW)
    down_far = flip(down_out, "tp", 2)

    def up_terms(lo, hi, *late):
        return rest_terms(lo, hi, normed_two, two_theirs, after(grad_up_pre, *late), up_theirs)

    up_sent = up_terms(half_count // 2, half_count, grad_query_rows)
    up_first = flip(up_sent[half:], "dp", 2)

    def exchange_mid(terms, first, order, *late):
        got, left = [first], half_count // 2
        for b in order[1:]:
            send = terms(left // 2, left, *late).astype(jnp.float32)
            rows = send.shape[0]
            for other in got:
                send = send + other[other.shape[0] - rows :]
            send = send.astype(LOW)
            got.append(flip(send, "dp", 1 << b))
            left //= 2
        return got[1:], send

    down_late, down_last = exchange_mid(down_terms, down_first, down_bits, grad_query_rows)
    kv_total = lax.optimization_barrier((kv_total, up_sent, down_out, down_last))[0]
    for back in kv_back:
        kv_total = kv_total + back
    key_grad = turn_back(kv_total[:size], cosine, sine)
    grad_kv_rows = jnp.concatenate([key_grad, kv_total[size:]], 0).astype(LOW)
    proj_rows = jnp.concatenate([grad_query_rows, grad_kv_rows], 0)
    proj_theirs = flip(proj_rows, "dp", 1)
    branch_near = flip(after(branch_send, proj_rows), "dp", 1)

    own_order = pick(proj_rows, row_order, len(ROW_MASKS), 1)

    def one_terms(lo, hi):
        cut = own_order[:, lo * own_rows : hi * own_rows]
        return dot(cut[:wide], w_query, 0, 1) + dot(cut[wide:], w_kv, 0, 0)

    grad_normed_one, one_out = near_sum(one_terms)
    one_far = flip(one_out, "tp", 2)
    output_rows = (middle + (down + after(down_far, one_out))).astype(LOW)
    up_kept = up_terms(0, 1, one_out)
    grad_gate = grad_gate.astype(jnp.float32)
    grad_normed_one = after(grad_normed_one, output_rows, up_kept, grad_gate) + one_far
    grad_in_norm, gain_one = norm_back(grad_normed_one, own_inputs, own(scale_one), norm1_gain)
    input_rows = grad_middle + grad_in_norm

    up_late, up_last = exchange_mid(up_terms, up_first, rest_bits, input_rows)
    branch_near, down_second = lax.optimization_barrier((branch_near, down_sent[:half], up_last))[:2]
    branch_theirs = jnp.concatenate([branch_near, flip(branch_near, "tp", 1)], 0)
    down_second = flip(down_second, "dp", 1)
    gain_one, *down_late = lax.optimization_barrier((gain_one, *down_late, up_last))[:-1]
    gains = jnp.stack([gain_one, gain_two])
    for m in (1, 2):
        gains = gains + flip(gains, "tp", m)
    gains = pick(gains, rest_places[0], dp, 1) + flip(pick(gains, rest_places[1], dp, 1), "dp", 1)

    out_late, proj_late = lax.optimization_barrier((attended, proj_rows, up_last))[:2]

    def last_terms(lo, hi, *late):
        first, second = after(proj_late, *late), after(out_late, *late)
        return jnp.concatenate(
            [
                rest_terms(lo, hi, normed_one, one_theirs, first, proj_theirs, True),
                rest_terms(lo, hi, branch_all, branch_theirs, second, att_theirs, True),
            ],
            1,
        )

    def with_gains(terms, lo, hi, *others):
        extra = gains[:, lo * block : hi * block]
        for other, other_gains in others:
            terms = terms.astype(jnp.float32) + other
            extra = extra + other_gains
        columns = terms.shape[1]
        extra = jnp.pad(extra, ((0, 14), (0, -extra.shape[1] % columns)))[:, :columns]
        return jnp.concatenate([terms.astype(LOW), extra.astype(LOW)], 0)

    def split(message, count):
        rows = count * block
        return message[:rows], message[rows : rows + 2, :rows]

    quarter = half_count // 4
    sent = last_terms(half_count // 2, half_count)
    cut = quarter * block
    firsts = with_gains(sent[cut:], 3 * quarter, half_count)
    seconds = with_gains(sent[:cut], 2 * quarter, 3 * quarter)
    mids = [split(flip(firsts, "dp", 2), quarter)]
    last_second = split(flip(after(seconds, firsts), "dp", 2), quarter)
    proj_kept = rest_terms(0, 1, normed_one, one_theirs, after(proj_late, firsts), proj_theirs, True)
    out_kept = rest_terms(0, 1, branch_all, branch_theirs, after(out_late, firsts), att_theirs, True)
    down_kept = down_terms(0, 1, firsts)
    left = half_count // 2
    for b in rest_bits[1:]:
        count = left // 2
        terms = last_terms(count, left, firsts)
        terms, *up_late = lax.optimization_barrier((terms, *up_late, proj_kept, out_kept, down_kept))[
            :-3
        ]
        send = with_gains(
            terms, count, left, *((o[-count * block :], g[:, -count * block :]) for o, g in mids)
        )
        mids.append(split(flip(send, "dp", 1 << b), count))
        left = count
    up_second = flip(after(up_sent[:half], send), "dp", 2)

    def ending(kept, *others):
        kept = kept.astype(jnp.float32)
        for other in others:
            kept = kept + other[:block]
        return kept

    down_kept, down_second = lax.optimization_barrier((down_kept, down_second, send))[:2]
    grad_down = ending(down_kept, down_second, *down_late)
    grad_last = ending(
        jnp.concatenate([proj_kept, out_kept], 1), last_second[0], *(m[0] for m in mids[1:])
    )
    gains = gains[:, :block] + last_second[1][:, :block]
    for _, other in mids[1:]:
        gains = gains + other[:, :block]
    grad_up = ending(up_kept, up_second, *up_late)
    narrow = wide + 2 * size

    return (
        output_rows,
        input_rows,
        gains[0],
        grad_last[:, :wide],
        grad_last[:, wide : wide + size],
        grad_last[:, wide + size : narrow],
        grad_last[:, narrow:].T,
        gains[1],
        grad_gate,
        grad_up,
        grad_down.T,
    )


def solution(mesh):
    placed = (
        P("dp", None),
        P("dp"),
        P(),
        P(None, "tp"),
        P(None, "tp"),
        P(None, "tp"),
        P("tp", None),
        P(),
        P(None, "tp"),
        P(None, "tp"),
        P("tp", None),
        P("dp", None),
    )
    return jax.shard_map(
        shards,
        mesh=mesh,
        in_specs=placed,
        out_specs=(
            P(("dp", "tp"), None),
            P(("dp", "tp"), None),
            P("dp"),
            P("dp", "tp"),
            P("dp", "tp"),
            P("dp", "tp"),
            P("tp", "dp"),
            P("dp"),
            P("dp", "tp"),
            P("dp", "tp"),
            P("tp", "dp"),
        ),
        check_vma=False,
    )
```

```python
import functools

import jax
import jax.numpy as jnp
from jax import lax
from jax.experimental import pallas as pl
from jax.experimental.pallas import tpu as pltpu
from jax.sharding import PartitionSpec as P

SPAN = 4
EPSILON = 1e-05
FAR_BELOW = -1e30
LOW = jnp.bfloat16
ROW_MASKS = (0, 2, 1, 3)


def flip(block, axis, mask):
    return lax.ppermute(block, axis, [(i, i ^ mask) for i in range(lax.axis_size(axis))])


def dot(left, right, left_dim, right_dim):
    return lax.dot_general(
        left,
        right,
        (((left_dim,), (right_dim,)), ((), ())),
        preferred_element_type=jnp.float32,
    )


def in_hbm(*arrays):
    return [pltpu.with_memory_space_constraint(a, pltpu.HBM) for a in arrays]


def own_mask(pos, begin, keys, queries):
    key_at = lax.broadcasted_iota(jnp.int32, (keys, queries), 0)
    query_at = lax.broadcasted_iota(jnp.int32, (keys, queries), 1) + begin
    return (key_at <= query_at) & (key_at >= query_at - pos)


def row_starts(spot, rows):
    part = rows // len(ROW_MASKS)
    return [pl.multiple_of((spot ^ m) * part, part) for m in ROW_MASKS]


def forward_kernel(
    heads,
    size,
    at_ref,
    pos_ref,
    q_ref,
    kv0,
    kv1,
    kv2,
    kv3,
    o_ref,
    lse_ref,
    keys,
    vals,
    top,
    acc,
    ordered,
):
    rank, spot = at_ref[0], at_ref[1]
    rows = pos_ref.shape[1]
    half = rows // 2

    @pl.when(pl.program_id(0) == 0)
    def _():
        for m, kv in enumerate((kv0, kv1, kv2, kv3)):
            keys[m] = kv[:size, :].T
            vals[m, :size, :] = kv[size:, :]
            vals[m, size:, :] = jnp.ones((16, rows), LOW)

    pos = pos_ref[...]
    for part in range(2):
        cols = slice(part * half, (part + 1) * half)
        count = (part + 1) * half
        mask = own_mask(pos[:, cols], part * half, count, half)
        for h in range(heads):
            scores = dot(keys[0, :count, :], q_ref[h * size : (h + 1) * size, cols], 1, 0)
            scores = jnp.where(mask, scores, FAR_BELOW)
            peak = jnp.max(scores, 0, keepdims=True)
            weights = jnp.exp(scores - peak).astype(LOW)
            acc[h, :, cols] = dot(vals[0, :, :count], weights, 1, 0)
            top[h, :, cols] = peak
    seen = pos > lax.broadcasted_iota(jnp.int32, (1, rows), 1)
    for m in range(1, SPAN):

        @pl.when((rank ^ m) < rank)
        def _():
            for h in range(heads):
                scores = dot(keys[m], q_ref[h * size : (h + 1) * size, :], 1, 0)
                old = top[h]
                peak = jnp.where(seen, jnp.maximum(old, jnp.max(scores, 0, keepdims=True)), old)
                weights = jnp.exp(scores - jnp.where(seen, peak, -FAR_BELOW)).astype(LOW)
                acc[h] = acc[h] * jnp.exp(old - peak) + dot(vals[m], weights, 1, 0)
                top[h] = peak

    for h in range(heads):
        total = acc[h, size : size + 1, :]
        ordered[h * size : (h + 1) * size, :] = (acc[h, :size, :] / total).astype(LOW)
        lse_ref[h] = top[h] + jnp.log(total)
    for j, start in enumerate(row_starts(spot, rows)):
        part = rows // len(ROW_MASKS)
        o_ref[:, j * part : (j + 1) * part] = ordered[:, pl.ds(start, part)]


def backward_kernel(
    heads,
    size,
    at_ref,
    pos_ref,
    q_ref,
    do_in,
    o_in,
    lse_ref,
    cos_ref,
    sin_ref,
    kv0,
    kv1,
    kv2,
    kv3,
    dq_ref,
    g0,
    g1,
    g2,
    g3,
    keys,
    vals,
    dq,
    total,
    do_ref,
    o_ref,
):
    rank, spot = at_ref[0], at_ref[1]
    rows = pos_ref.shape[1]
    half = rows // 2
    blocks = (kv0, kv1, kv2, kv3)
    step = pl.program_id(0)

    @pl.when(step == 0)
    def _():
        for m, kv in enumerate(blocks):
            keys[m] = kv[:size, :].T
            vals[m] = kv[size:, :].T
        total[...] = jnp.zeros_like(total)

    part = rows // len(ROW_MASKS)
    for j, start in enumerate(row_starts(spot, rows)):
        do_ref[:, pl.ds(start, part)] = do_in[:, j * part : (j + 1) * part]
        o_ref[:, pl.ds(start, part)] = o_in[:, j * part : (j + 1) * part]
    pos = pos_ref[...]
    seen = pos > lax.broadcasted_iota(jnp.int32, (1, rows), 1)
    deltas = []
    for h in range(heads):
        span = slice(h * size, (h + 1) * size)
        deltas.append(
            jnp.sum(
                do_ref[span, :].astype(jnp.float32) * o_ref[span, :].astype(jnp.float32),
                0,
                keepdims=True,
            )
        )
    for part in range(2):
        cols = slice(part * half, (part + 1) * half)
        count = (part + 1) * half
        mask = own_mask(pos[:, cols], part * half, count, half)
        for h in range(heads):
            span = slice(h * size, (h + 1) * size)
            query, grad = q_ref[span, cols], do_ref[span, cols]
            scores = dot(keys[0, :count, :], query, 1, 0)
            probs = jnp.exp(jnp.where(mask, scores, FAR_BELOW) - lse_ref[h, :, cols])
            grad_probs = dot(vals[0, :count, :], grad, 1, 0)
            grad_scores = (probs * (grad_probs - deltas[h][:, cols])).astype(LOW)
            total[0, :size, :count] += dot(query, grad_scores, 1, 1)
            total[0, size:, :count] += dot(grad, probs.astype(LOW), 1, 1)
            dq[h, :, cols] = dot(kv0[:size, :count], grad_scores, 1, 0)
    for m in range(1, SPAN):

        @pl.when((rank ^ m) < rank)
        def _():
            for h in range(heads):
                span = slice(h * size, (h + 1) * size)
                query, grad = q_ref[span, :], do_ref[span, :]
                scores = dot(keys[m], query, 1, 0)
                probs = jnp.exp(scores - jnp.where(seen, lse_ref[h], -FAR_BELOW))
                grad_probs = dot(vals[m], grad, 1, 0)
                grad_scores = (probs * (grad_probs - deltas[h])).astype(LOW)
                total[m, :size, :] += dot(query, grad_scores, 1, 1)
                total[m, size:, :] += dot(grad, probs.astype(LOW), 1, 1)
                dq[h] += dot(blocks[m][:size, :], grad_scores, 1, 0)

    middle_at = size // 2
    cosine, sine = cos_ref[...], sin_ref[...]
    for h in range(heads):
        first = dq[h, :middle_at, :] * size ** (-0.5)
        second = dq[h, middle_at:, :] * size ** (-0.5)
        base = h * size
        dq_ref[base : base + middle_at, :] = (first * cosine + second * sine).astype(LOW)
        dq_ref[base + middle_at : base + size, :] = (second * cosine - first * sine).astype(LOW)

    @pl.when(step == pl.num_programs(0) - 1)
    def _():
        g0[...] = total[0]
        for m, out in ((1, g1), (2, g2), (3, g3)):
            out[...] = total[m].astype(LOW)


def attention_forward(at, pos, queries, blocks, size, heads):
    wide, rows = queries.shape
    count = wide // size
    whole = pl.BlockSpec((2 * size, rows), lambda i, r: (0, 0))
    some = pl.BlockSpec((heads * size, rows), lambda i, r: (i, 0))
    return pl.pallas_call(
        functools.partial(forward_kernel, heads, size),
        out_shape=(
            jax.ShapeDtypeStruct((wide, rows), LOW),
            jax.ShapeDtypeStruct((count, 1, rows), jnp.float32),
        ),
        grid_spec=pltpu.PrefetchScalarGridSpec(
            num_scalar_prefetch=1,
            grid=(count // heads,),
            in_specs=[pl.BlockSpec((1, rows), lambda i, r: (0, 0)), some] + [whole] * SPAN,
            out_specs=[some, pl.BlockSpec((heads, 1, rows), lambda i, r: (i, 0, 0))],
            scratch_shapes=[
                pltpu.VMEM((SPAN, rows, size), LOW),
                pltpu.VMEM((SPAN, size + 16, rows), LOW),
                pltpu.VMEM((heads, 1, rows), jnp.float32),
                pltpu.VMEM((heads, size + 16, rows), jnp.float32),
                pltpu.VMEM((heads * size, rows), LOW),
            ],
        ),
        compiler_params=pltpu.CompilerParams(vmem_limit_bytes=24 << 20),
        cost_estimate=pl.CostEstimate(
            flops=32 * wide * rows * rows * SPAN,
            bytes_accessed=4 * wide * rows,
            transcendentals=0,
        ),
        name="attention_forward",
    )(at, pos, queries, *blocks)


def attention_backward(at, pos, queries, grads, attended, lse, cosine, sine, blocks, size, heads):
    wide, rows = queries.shape
    count = wide // size
    whole = pl.BlockSpec((2 * size, rows), lambda i, r: (0, 0))
    table = pl.BlockSpec((size // 2, rows), lambda i, r: (0, 0))
    some = pl.BlockSpec((heads * size, rows), lambda i, r: (i, 0))
    return pl.pallas_call(
        functools.partial(backward_kernel, heads, size),
        out_shape=(
            jax.ShapeDtypeStruct((wide, rows), LOW),
            jax.ShapeDtypeStruct((2 * size, rows), jnp.float32),
        )
        + (jax.ShapeDtypeStruct((2 * size, rows), LOW),) * (SPAN - 1),
        grid_spec=pltpu.PrefetchScalarGridSpec(
            num_scalar_prefetch=1,
            grid=(count // heads,),
            in_specs=[
                pl.BlockSpec((1, rows), lambda i, r: (0, 0)),
                some,
                some,
                some,
                pl.BlockSpec((heads, 1, rows), lambda i, r: (i, 0, 0)),
                table,
                table,
            ]
            + [whole] * SPAN,
            out_specs=[some] + [whole] * SPAN,
            scratch_shapes=[
                pltpu.VMEM((SPAN, rows, size), LOW),
                pltpu.VMEM((SPAN, rows, size), LOW),
                pltpu.VMEM((heads, size, rows), jnp.float32),
                pltpu.VMEM((SPAN, 2 * size, rows), jnp.float32),
                pltpu.VMEM((heads * size, rows), LOW),
                pltpu.VMEM((heads * size, rows), LOW),
            ],
        ),
        compiler_params=pltpu.CompilerParams(vmem_limit_bytes=24 << 20),
        cost_estimate=pl.CostEstimate(
            flops=48 * wide * rows * rows * SPAN,
            bytes_accessed=10 * wide * rows,
            transcendentals=0,
        ),
        name="attention_backward",
    )(at, pos, *in_hbm(queries, grads, attended, lse, cosine, sine, *blocks))


def pick(values, places, blocks, dim):
    size = values.shape[dim] // blocks
    return jnp.concatenate(
        [lax.dynamic_slice_in_dim(values, p * size, size, dim) for p in places], dim
    )


def after(value, *others):
    return lax.optimization_barrier((value, *others))[0]


def parity_sum(terms, dim):
    count = lax.axis_size("dp")
    groups = [list(range(p, count, 2)) for p in range(2)]
    return lax.psum_scatter(
        terms.astype(LOW), "dp", scatter_dimension=dim, axis_index_groups=groups, tiled=True
    )


def terms_kernel(transposed, places, x, x_far, g, g_far, out):
    del places
    side = 1 if transposed else 0
    out[...] = (dot(x[...], g[...], 0, side) + dot(x_far[...], g_far[...], 0, side)).astype(LOW)


def weight_terms(places, far_places, x, x_far, g, g_far, transposed=False, keep=True):
    count = len(places)
    size = x.shape[1] // lax.axis_size("dp")
    rows = x.shape[0]
    units = g.shape[0] if transposed else g.shape[1]
    if size % 128:
        side = 1 if transposed else 0
        mine = pick(x, places, x.shape[1] // size, 1)
        theirs = pick(x_far, far_places, x_far.shape[1] // size, 1)
        return (dot(mine, g, 0, side) + dot(theirs, g_far, 0, side)).astype(LOW)
    whole = pl.BlockSpec(g.shape, lambda i, p: (0, 0))
    return pl.pallas_call(
        functools.partial(terms_kernel, transposed),
        out_shape=(jax.ShapeDtypeStruct if keep else pltpu.HBM)((count * size, units), LOW),
        grid_spec=pltpu.PrefetchScalarGridSpec(
            num_scalar_prefetch=1,
            grid=(count,),
            in_specs=[
                pl.BlockSpec((rows, size), lambda i, p: (0, p[i])),
                pl.BlockSpec((rows, size), lambda i, p: (0, p[count + i])),
                whole,
                whole,
            ],
            out_specs=pl.BlockSpec((size, units), lambda i, p: (i, 0)),
        ),
        compiler_params=pltpu.CompilerParams(vmem_limit_bytes=24 << 20),
        cost_estimate=pl.CostEstimate(
            flops=24 * rows * count * size * units, bytes_accessed=4 * rows * units, transcendentals=0
        ),
        name="weight_terms",
    )(jnp.stack([*places, *far_places]).astype(jnp.int32), x, x_far, g, g_far)


def copy_kernel(places, source, target):
    del places
    target[...] = source[...]


def pick_columns(values, places, part=0, parts=1):
    rows, count = values.shape[0] // parts, len(places)
    blocks = lax.axis_size("dp")
    size = values.shape[1] // blocks
    if size % 128:
        return pick(lax.dynamic_slice_in_dim(values, part * rows, rows, 0), places, blocks, 1)
    return pl.pallas_call(
        copy_kernel,
        out_shape=jax.ShapeDtypeStruct((rows, count * size), values.dtype),
        grid_spec=pltpu.PrefetchScalarGridSpec(
            num_scalar_prefetch=1,
            grid=(count,),
            in_specs=[pl.BlockSpec((rows, size), lambda i, p: (p[count], p[i]))],
            out_specs=pl.BlockSpec((rows, size), lambda i, p: (0, i)),
        ),
        compiler_params=pltpu.CompilerParams(vmem_limit_bytes=8 << 20),
        cost_estimate=pl.CostEstimate(
            flops=65536 * rows * count * size, bytes_accessed=4 * rows * count * size, transcendentals=0
        ),
        name="pick_columns",
    )(jnp.stack([*places, part]).astype(jnp.int32), values)


def ffn_kernel(rows, gate_w, up_w, grad_in, hidden, grad_gate, grad_up):
    step = gate_w.shape[1]
    both = dot(rows[...], jnp.concatenate([gate_w[...], up_w[...]], 1), 1, 0)
    gate, up = both[:, :step], both[:, step:]
    grad = grad_in[...]
    sigma = jax.nn.sigmoid(gate)
    active = gate * sigma
    hidden[...] = (active * up).astype(LOW)
    grad_gate[...] = (grad * up * sigma * (1.0 + gate * (1.0 - sigma))).astype(LOW)
    grad_up[...] = (grad * active).astype(LOW)


def feed_forward(rows, w_gate, w_up, grad_hidden):
    count, width = rows.shape
    units = w_gate.shape[1]
    step = 128
    weights = pl.BlockSpec((width, step), lambda i: (0, i))
    wide = pl.BlockSpec((count, step), lambda i: (0, i))
    return pl.pallas_call(
        ffn_kernel,
        out_shape=(jax.ShapeDtypeStruct((count, units), LOW),) * 3,
        grid=(units // step,),
        in_specs=[pl.BlockSpec((count, width), lambda i: (0, 0)), weights, weights, wide],
        out_specs=[wide] * 3,
        compiler_params=pltpu.CompilerParams(vmem_limit_bytes=20 << 20),
        cost_estimate=pl.CostEstimate(
            flops=6 * count * width * units,
            bytes_accessed=4 * width * units,
            transcendentals=count * units,
        ),
        name="feed_forward",
    )(rows, w_gate, w_up, grad_hidden)


def back_kernel(gate_rows, up_rows, gate_w, up_w, out):
    out[...] = dot(gate_rows[...], gate_w[...], 1, 1) + dot(up_rows[...], up_w[...], 1, 1)


def back_send_kernel(steps, added, gate_rows, up_rows, gate_w, up_w, *refs):
    *more, out = refs
    step = pl.program_id(0)

    @pl.when(step < steps)
    def _():
        total = dot(gate_rows[...], gate_w[...], 1, 1) + dot(up_rows[...], up_w[...], 1, 1)
        out[...] = total.astype(LOW)

    for j, ref in enumerate(more):
        begin = steps + j * added

        @pl.when((step >= begin) & (step < begin + added))
        def _():
            out[...] = ref[...]


def feed_forward_back(grad_gate, grad_up, w_gate, w_up, half, more=()):
    count, units = grad_gate.shape
    width = w_gate.shape[0]
    step = 256
    steps = width // step
    added = more[0].shape[1] // step if more else 0
    rows = pl.BlockSpec((count // 2, units), lambda i: (half, 0))
    weights = pl.BlockSpec((step, units), lambda i: (jnp.minimum(i, steps - 1), 0))
    specs, kernel, kind = [rows, rows, weights, weights], back_kernel, jnp.float32
    for j in range(len(more)):
        begin = steps + j * added
        specs.append(
            pl.BlockSpec(
                (count // 2, step), lambda i, b=begin: (0, jnp.clip(i - b, 0, added - 1))
            )
        )
    if more:
        kernel, kind = functools.partial(back_send_kernel, steps, added), LOW
    added *= len(more)
    return pl.pallas_call(
        kernel,
        out_shape=jax.ShapeDtypeStruct((count // 2, width + added * step), kind),
        grid=(steps + added,),
        in_specs=specs,
        out_specs=pl.BlockSpec((count // 2, step), lambda i: (0, i)),
        compiler_params=pltpu.CompilerParams(vmem_limit_bytes=16 << 20),
        cost_estimate=pl.CostEstimate(
            flops=8 * count * width * units, bytes_accessed=4 * width * units, transcendentals=0
        ),
        name="feed_forward_back",
    )(grad_gate, grad_up, w_gate, w_up, *more)


def row_kernel(left, right, send, kept):
    half = left.shape[0] // 2
    send[...] = dot(left[half:, :], right[...], 1, 0).astype(LOW)
    kept[...] = dot(left[:half, :], right[...], 1, 0)


def row_terms(left, right):
    rows, units = left.shape
    half, width = rows // 2, right.shape[1]
    step = 256
    return pl.pallas_call(
        row_kernel,
        out_shape=(
            jax.ShapeDtypeStruct((half, width), LOW),
            jax.ShapeDtypeStruct((half, width), jnp.float32),
        ),
        grid=(width // step,),
        in_specs=[
            pl.BlockSpec((rows, units), lambda i: (0, 0)),
            pl.BlockSpec((units, step), lambda i: (0, i)),
        ],
        out_specs=[pl.BlockSpec((half, step), lambda i: (0, i))] * 2,
        compiler_params=pltpu.CompilerParams(vmem_limit_bytes=16 << 20),
        cost_estimate=pl.CostEstimate(
            flops=8 * rows * units * width, bytes_accessed=2 * units * width, transcendentals=0
        ),
        name="row_terms",
    )(left, right)


def turn(values, cosine, sine):
    half = cosine.shape[0]
    heads = values.shape[0] // (2 * half)
    pieces = values.reshape(heads, 2, half, values.shape[1])
    first, second = pieces[:, 0], pieces[:, 1]
    return jnp.stack(
        [first * cosine - second * sine, second * cosine + first * sine], 1
    ).reshape(values.shape)


def turn_back(grads, cosine, sine):
    return turn(grads, cosine, -sine)


def norm_back(grad_rows, values, scale_rows, gain):
    scaled = grad_rows * gain
    inner_mean = jnp.mean(scaled * values, -1, keepdims=True)
    return (
        scale_rows * (scaled - values * scale_rows * scale_rows * inner_mean),
        jnp.sum(grad_rows * values * scale_rows, 0),
    )


def shards(
    tokens,
    positions,
    norm1_gain,
    w_query,
    w_key,
    w_value,
    w_out,
    norm2_gain,
    w_gate,
    w_up,
    w_down,
    cotangent,
):
    rows_here, width = tokens.shape
    size = w_key.shape[1]
    dp = lax.axis_size("dp")
    place = lax.axis_index("dp")
    spot = lax.axis_index("tp")
    tp_masks = range(lax.axis_size("tp"))
    own_rows = rows_here // lax.axis_size("tp")
    block = width // dp
    at = jnp.stack([place % SPAN, spot]).astype(jnp.int32)
    pos = positions.reshape(1, rows_here)

    def own(values):
        return lax.dynamic_slice_in_dim(values, spot * own_rows, own_rows, 0)

    inputs = tokens.astype(jnp.float32)
    scale_one = lax.rsqrt(jnp.mean(inputs * inputs, -1, keepdims=True) + EPSILON)
    normed_one = (inputs * scale_one * norm1_gain).astype(LOW)
    half = size // 2
    frequency = jnp.exp(
        -jnp.log(10000.0) * (2.0 * jnp.arange(half, dtype=jnp.float32) / size)
    )
    angles = frequency[:, None] * positions.astype(jnp.float32)[None, :]
    cosine, sine = jnp.cos(angles), jnp.sin(angles)
    w_kv = jnp.concatenate([w_key.T, w_value.T], 0)
    paired = dot(w_kv, normed_one, 1, 1)
    paired = jnp.concatenate([turn(paired[:size], cosine, sine), paired[size:]], 0).astype(LOW)
    blocks = [paired] + [flip(paired, "dp", m) for m in range(1, SPAN)]
    queries = (turn(dot(w_query, normed_one, 0, 1), cosine, sine) * size ** (-0.5)).astype(LOW)

    bit = place % 2
    bits = dp.bit_length() - 1
    half_count = dp // 2
    wide = w_query.shape[1]

    halves = [[2 * j + which for j in range(half_count)] for which in (bit, 1 - bit)]

    def exchange_order(order):
        return [
            sum(((j >> (len(order) - 1 - k)) & 1) << b for k, b in enumerate(order))
            for j in range(1 << len(order))
        ]

    down_bits = [0] + list(range(2, bits))
    down_places = [[where ^ m for m in exchange_order(down_bits)] for where in (place, place ^ 2)]
    rest_bits = list(range(1, bits))
    rest_places = [[where ^ m for m in exchange_order(rest_bits)] for where in (place, place ^ 1)]
    row_order = [spot ^ m for m in ROW_MASKS]

    def near_sum(part):
        send = part(2, 4).astype(LOW)
        near, kept = lax.optimization_barrier((flip(send, "tp", 1), part(0, 2)))
        pair = kept + near
        return pair[:own_rows], pair[own_rows:].astype(LOW)

    attended, lse = attention_forward(at, pos, queries, blocks, size, 8)

    branch, branch_out = near_sum(
        lambda lo, hi: dot(attended[:, lo * own_rows : hi * own_rows], w_out, 0, 0)
    )
    branch_far = flip(branch_out, "tp", 2)
    att_theirs = flip(after(attended, branch_out), "dp", 1)
    cot = pick(after(cotangent, branch_out), row_order, len(ROW_MASKS), 0)
    cot_send = pick_columns(cot, down_places[1])
    cot_theirs = flip(cot_send, "dp", 2)
    own_inputs = own(tokens).astype(jnp.float32)
    core = spot % 2
    one_send = pick_columns(after(normed_one, cot_send), halves[1], core, 2)
    one_near = flip(one_send, "dp", 1)
    grad_hidden = dot(after(cot, one_send), w_down, 1, 1)
    middle = own_inputs + (after(branch, grad_hidden) + branch_far)

    scale_two = lax.rsqrt(jnp.mean(middle * middle, -1, keepdims=True) + EPSILON)
    own_two = (middle * scale_two * norm2_gain).astype(LOW)
    far_two = flip(own_two, "tp", 2)
    pair_two = jnp.concatenate([after(own_two, att_theirs), far_two], 0)
    core_two = flip(pair_two, "tp", 1)
    two_send = pick_columns(pair_two, halves[1])
    two_near = flip(two_send, "dp", 1)
    normed_two = jnp.concatenate([after(pair_two, two_send), core_two], 0)

    hidden, grad_gate_pre, grad_up_pre = feed_forward(normed_two, w_gate, w_up, grad_hidden)
    gate_theirs = flip(grad_gate_pre, "dp", 1)
    hidden_theirs = flip(hidden, "dp", 2)
    up_theirs = flip(grad_up_pre, "dp", 1)
    gate_late, cot_theirs, two_near, one_near = lax.optimization_barrier(
        (grad_gate_pre, cot_theirs, two_near, one_near)
    )

    two_back = functools.partial(feed_forward_back, gate_late, grad_up_pre, w_gate, w_up)
    core_send = two_back(1, (two_near, one_near))
    core_got, kept = lax.optimization_barrier((flip(core_send, "tp", 1), two_back(0)))
    pair = kept + core_got[:, :width]
    grad_normed_two, two_out = pair[:own_rows], pair[own_rows:].astype(LOW)
    two_far = flip(two_out, "tp", 2)
    two_theirs = jnp.concatenate([two_near, core_got[:, width : width + width // 2]], 0)

    down_near, down = row_terms(after(hidden, two_out), w_down)
    grad_normed_two = after(grad_normed_two, down) + two_far

    grad_mid_norm, gain_two = norm_back(grad_normed_two, middle, scale_two, norm2_gain)
    grad_middle = own(cotangent).astype(jnp.float32) + grad_mid_norm
    branch_grad = grad_middle.astype(LOW)
    grad_far = flip(branch_grad, "tp", 2)

    down_near = flip(after(down_near, branch_grad), "tp", 1)
    natural = list(range(half_count))
    gate_terms = weight_terms(
        halves[0],
        natural,
        after(normed_two, branch_grad),
        two_theirs,
        grad_gate_pre,
        gate_theirs,
        keep=False,
    )
    grad_gate = parity_sum(gate_terms, 0)
    one_near, one_core = lax.optimization_barrier(
        (one_near, core_got[:, width + width // 2 :], gate_terms)
    )[:2]
    one_theirs = jnp.zeros((rows_here, width // 2), LOW)
    for piece, where in ((one_near, core), (one_core, 1 - core)):
        one_theirs = lax.dynamic_update_slice_in_dim(one_theirs, piece, where * (rows_here // 2), 0)
    branch_grad = after(branch_grad, one_theirs)
    grad_pair = jnp.concatenate([after(branch_grad, gate_terms), grad_far], 0)
    grad_core = flip(grad_pair, "tp", 1)
    branch_send = pick_columns(grad_pair, halves[1])

    def near_flip(terms, bit):
        half = terms.shape[0] // 2
        return [flip(terms[half:], "dp", 1 << bit), flip(terms[:half], "dp", 1 << bit)]

    def down_terms(lo, hi, *late):
        g = after(hidden, *late)
        return weight_terms(
            down_places[0][lo:hi], range(lo, hi), cot, cot_theirs, g, hidden_theirs
        )

    down_sent = down_terms(half_count // 2, half_count, branch_send)
    half = down_sent.shape[0] // 2
    down_first = flip(down_sent[half:], "dp", 1)
    branch_all = jnp.concatenate([after(grad_pair, down_sent), grad_core], 0)
    grad_attended = dot(w_out, branch_all, 1, 1).astype(LOW)
    grads = attention_backward(
        at, pos, queries, grad_attended, attended, lse, cosine, sine, blocks, size, 2
    )
    grad_query_rows, kv_total = grads[0], grads[1]
    kv_back = [flip(grads[m + 1], "dp", m) for m in range(1, SPAN)]

    def rest_terms(lo, hi, x, x_far, g, g_far, transposed=False):
        return weight_terms(
            rest_places[0][lo:hi],
            [p // 2 for p in rest_places[0][lo:hi]],
            x,
            x_far,
            g,
            g_far,
            transposed,
        )

    down = down + after(down_near, grad_query_rows)
    down, down_out = down[:own_rows], down[own_rows:].astype(LOW)
    down_far = flip(down_out, "tp", 2)

    def up_terms(lo, hi, *late):
        return rest_terms(lo, hi, normed_two, two_theirs, after(grad_up_pre, *late), up_theirs)

    up_sent = up_terms(half_count // 2, half_count, grad_query_rows)
    up_first = flip(up_sent[half:], "dp", 2)

    def exchange_mid(terms, first, order, *late):
        got, left = [first], half_count // 2
        for b in order[1:]:
            send = terms(left // 2, left, *late).astype(jnp.float32)
            rows = send.shape[0]
            for other in got:
                send = send + other[other.shape[0] - rows :]
            send = send.astype(LOW)
            got.append(flip(send, "dp", 1 << b))
            left //= 2
        return got[1:], send

    down_late, down_last = exchange_mid(down_terms, down_first, down_bits, grad_query_rows)
    kv_total = lax.optimization_barrier((kv_total, up_sent, down_out, down_last))[0]
    for back in kv_back:
        kv_total = kv_total + back
    key_grad = turn_back(kv_total[:size], cosine, sine)
    grad_kv_rows = jnp.concatenate([key_grad, kv_total[size:]], 0).astype(LOW)
    proj_rows = jnp.concatenate([grad_query_rows, grad_kv_rows], 0)
    proj_theirs = flip(proj_rows, "dp", 1)
    branch_near = flip(after(branch_send, proj_rows), "dp", 1)

    own_order = pick(proj_rows, row_order, len(ROW_MASKS), 1)

    def one_terms(lo, hi):
        cut = own_order[:, lo * own_rows : hi * own_rows]
        return dot(cut[:wide], w_query, 0, 1) + dot(cut[wide:], w_kv, 0, 0)

    grad_normed_one, one_out = near_sum(one_terms)
    one_far = flip(one_out, "tp", 2)
    output_rows = (middle + (down + after(down_far, one_out))).astype(LOW)
    up_kept = up_terms(0, 1, one_out)
    grad_gate = grad_gate.astype(jnp.float32)
    grad_normed_one = after(grad_normed_one, output_rows, up_kept, grad_gate) + one_far
    grad_in_norm, gain_one = norm_back(grad_normed_one, own_inputs, own(scale_one), norm1_gain)
    input_rows = grad_middle + grad_in_norm

    up_late, up_last = exchange_mid(up_terms, up_first, rest_bits, input_rows)
    branch_near, down_second = lax.optimization_barrier((branch_near, down_sent[:half], up_last))[:2]
    branch_theirs = jnp.concatenate([branch_near, flip(branch_near, "tp", 1)], 0)
    down_second = flip(down_second, "dp", 1)
    gain_one, *down_late = lax.optimization_barrier((gain_one, *down_late, up_last))[:-1]
    gains = jnp.stack([gain_one, gain_two])
    for m in (1, 2):
        gains = gains + flip(gains, "tp", m)
    gains = pick(gains, rest_places[0], dp, 1) + flip(pick(gains, rest_places[1], dp, 1), "dp", 1)

    out_late, proj_late = lax.optimization_barrier((attended, proj_rows, up_last))[:2]

    def last_terms(lo, hi, *late):
        first, second = after(proj_late, *late), after(out_late, *late)
        return jnp.concatenate(
            [
                rest_terms(lo, hi, normed_one, one_theirs, first, proj_theirs, True),
                rest_terms(lo, hi, branch_all, branch_theirs, second, att_theirs, True),
            ],
            1,
        )

    def with_gains(terms, lo, hi, *others):
        extra = gains[:, lo * block : hi * block]
        for other, other_gains in others:
            terms = terms.astype(jnp.float32) + other
            extra = extra + other_gains
        columns = terms.shape[1]
        extra = jnp.pad(extra, ((0, 14), (0, -extra.shape[1] % columns)))[:, :columns]
        return jnp.concatenate([terms.astype(LOW), extra.astype(LOW)], 0)

    def split(message, count):
        rows = count * block
        return message[:rows], message[rows : rows + 2, :rows]

    quarter = half_count // 4
    sent = last_terms(half_count // 2, half_count)
    cut = quarter * block
    firsts = with_gains(sent[cut:], 3 * quarter, half_count)
    seconds = with_gains(sent[:cut], 2 * quarter, 3 * quarter)
    mids = [split(flip(firsts, "dp", 2), quarter)]
    last_second = split(flip(after(seconds, firsts), "dp", 2), quarter)
    proj_kept = rest_terms(0, 1, normed_one, one_theirs, after(proj_late, firsts), proj_theirs, True)
    out_kept = rest_terms(0, 1, branch_all, branch_theirs, after(out_late, firsts), att_theirs, True)
    down_kept = down_terms(0, 1, firsts)
    left = half_count // 2
    for b in rest_bits[1:]:
        count = left // 2
        terms = last_terms(count, left, firsts)
        terms, *up_late = lax.optimization_barrier((terms, *up_late, proj_kept, out_kept, down_kept))[
            :-3
        ]
        send = with_gains(
            terms, count, left, *((o[-count * block :], g[:, -count * block :]) for o, g in mids)
        )
        mids.append(split(flip(send, "dp", 1 << b), count))
        left = count
    up_second = flip(after(up_sent[:half], send), "dp", 2)

    def ending(kept, *others):
        kept = kept.astype(jnp.float32)
        for other in others:
            kept = kept + other[:block]
        return kept

    down_kept, down_second = lax.optimization_barrier((down_kept, down_second, send))[:2]
    grad_down = ending(down_kept, down_second, *down_late)
    grad_last = ending(
        jnp.concatenate([proj_kept, out_kept], 1), last_second[0], *(m[0] for m in mids[1:])
    )
    gains = gains[:, :block] + last_second[1][:, :block]
    for _, other in mids[1:]:
        gains = gains + other[:, :block]
    grad_up = ending(up_kept, up_second, *up_late)
    narrow = wide + 2 * size

    return (
        output_rows,
        input_rows,
        gains[0],
        grad_last[:, :wide],
        grad_last[:, wide : wide + size],
        grad_last[:, wide + size : narrow],
        grad_last[:, narrow:].T,
        gains[1],
        grad_gate,
        grad_up,
        grad_down.T,
    )


def solution(mesh):
    placed = (
        P("dp", None),
        P("dp"),
        P(),
        P(None, "tp"),
        P(None, "tp"),
        P(None, "tp"),
        P("tp", None),
        P(),
        P(None, "tp"),
        P(None, "tp"),
        P("tp", None),
        P("dp", None),
    )
    return jax.shard_map(
        shards,
        mesh=mesh,
        in_specs=placed,
        out_specs=(
            P(("dp", "tp"), None),
            P(("dp", "tp"), None),
            P("dp"),
            P("dp", "tp"),
            P("dp", "tp"),
            P("dp", "tp"),
            P("tp", "dp"),
            P("dp"),
            P("dp", "tp"),
            P("dp", "tp"),
            P("tp", "dp"),
        ),
        check_vma=False,
    )
```

```python
import functools

import jax
import jax.numpy as jnp
import numpy as np
from jax import lax
from jax.experimental import pallas as pl
from jax.experimental.pallas import tpu as pltpu
from jax.sharding import PartitionSpec as P

SPAN = 4
EPSILON = 1e-05
FAR_BELOW = -1e30
LOW = jnp.bfloat16
ROW_MASKS = (0, 2, 1, 3)


def flip(block, axis, mask):
    return lax.ppermute(block, axis, [(i, i ^ mask) for i in range(lax.axis_size(axis))])


def dot(left, right, left_dim, right_dim):
    return lax.dot_general(
        left,
        right,
        (((left_dim,), (right_dim,)), ((), ())),
        preferred_element_type=jnp.float32,
    )


def in_hbm(*arrays):
    return [pltpu.with_memory_space_constraint(a, pltpu.HBM) for a in arrays]


def own_mask(pos, begin, keys, queries):
    key_at = lax.broadcasted_iota(jnp.int32, (keys, queries), 0)
    query_at = lax.broadcasted_iota(jnp.int32, (keys, queries), 1) + begin
    return (key_at <= query_at) & (key_at >= query_at - pos)


def row_starts(spot, rows):
    part = rows // len(ROW_MASKS)
    return [pl.multiple_of((spot ^ m) * part, part) for m in ROW_MASKS]


def forward_kernel(
    heads,
    size,
    at_ref,
    pos_ref,
    q_ref,
    kv0,
    kv1,
    kv2,
    kv3,
    o_ref,
    lse_ref,
    keys,
    vals,
    top,
    acc,
    ordered,
):
    rank, spot = at_ref[0], at_ref[1]
    rows = pos_ref.shape[1]
    half = rows // 2

    @pl.when(pl.program_id(0) == 0)
    def _():
        for m, kv in enumerate((kv0, kv1, kv2, kv3)):
            keys[m] = kv[:size, :].T
            vals[m, :size, :] = kv[size:, :]
            vals[m, size:, :] = jnp.ones((16, rows), LOW)

    pos = pos_ref[...]
    for part in range(2):
        cols = slice(part * half, (part + 1) * half)
        count = (part + 1) * half
        mask = own_mask(pos[:, cols], part * half, count, half)
        for h in range(heads):
            scores = dot(keys[0, :count, :], q_ref[h * size : (h + 1) * size, cols], 1, 0)
            scores = jnp.where(mask, scores, FAR_BELOW)
            peak = jnp.max(scores, 0, keepdims=True)
            weights = jnp.exp(scores - peak).astype(LOW)
            acc[h, :, cols] = dot(vals[0, :, :count], weights, 1, 0)
            top[h, :, cols] = peak
    seen = pos > lax.broadcasted_iota(jnp.int32, (1, rows), 1)
    for m in range(1, SPAN):

        @pl.when((rank ^ m) < rank)
        def _():
            for h in range(heads):
                scores = dot(keys[m], q_ref[h * size : (h + 1) * size, :], 1, 0)
                old = top[h]
                peak = jnp.where(seen, jnp.maximum(old, jnp.max(scores, 0, keepdims=True)), old)
                weights = jnp.exp(scores - jnp.where(seen, peak, -FAR_BELOW)).astype(LOW)
                acc[h] = acc[h] * jnp.exp(old - peak) + dot(vals[m], weights, 1, 0)
                top[h] = peak

    for h in range(heads):
        total = acc[h, size : size + 1, :]
        ordered[h * size : (h + 1) * size, :] = (acc[h, :size, :] / total).astype(LOW)
        lse_ref[h] = top[h] + jnp.log(total)
    for j, start in enumerate(row_starts(spot, rows)):
        part = rows // len(ROW_MASKS)
        o_ref[:, j * part : (j + 1) * part] = ordered[:, pl.ds(start, part)]


def backward_kernel(
    heads,
    size,
    at_ref,
    pos_ref,
    q_ref,
    do_in,
    o_in,
    lse_ref,
    cos_ref,
    sin_ref,
    kv0,
    kv1,
    kv2,
    kv3,
    dq_ref,
    g0,
    g1,
    g2,
    g3,
    keys,
    vals,
    dq,
    total,
    do_ref,
    o_ref,
):
    rank, spot = at_ref[0], at_ref[1]
    rows = pos_ref.shape[1]
    half = rows // 2
    blocks = (kv0, kv1, kv2, kv3)
    step = pl.program_id(0)

    @pl.when(step == 0)
    def _():
        for m, kv in enumerate(blocks):
            keys[m] = kv[:size, :].T
            vals[m] = kv[size:, :].T
        total[...] = jnp.zeros_like(total)

    part = rows // len(ROW_MASKS)
    for j, start in enumerate(row_starts(spot, rows)):
        do_ref[:, pl.ds(start, part)] = do_in[:, j * part : (j + 1) * part]
        o_ref[:, pl.ds(start, part)] = o_in[:, j * part : (j + 1) * part]
    pos = pos_ref[...]
    seen = pos > lax.broadcasted_iota(jnp.int32, (1, rows), 1)
    deltas = []
    for h in range(heads):
        span = slice(h * size, (h + 1) * size)
        deltas.append(
            jnp.sum(
                do_ref[span, :].astype(jnp.float32) * o_ref[span, :].astype(jnp.float32),
                0,
                keepdims=True,
            )
        )
    for part in range(2):
        cols = slice(part * half, (part + 1) * half)
        count = (part + 1) * half
        mask = own_mask(pos[:, cols], part * half, count, half)
        for h in range(heads):
            span = slice(h * size, (h + 1) * size)
            query, grad = q_ref[span, cols], do_ref[span, cols]
            scores = dot(keys[0, :count, :], query, 1, 0)
            probs = jnp.exp(jnp.where(mask, scores, FAR_BELOW) - lse_ref[h, :, cols])
            grad_probs = dot(vals[0, :count, :], grad, 1, 0)
            grad_scores = (probs * (grad_probs - deltas[h][:, cols])).astype(LOW)
            total[0, :size, :count] += dot(query, grad_scores, 1, 1)
            total[0, size:, :count] += dot(grad, probs.astype(LOW), 1, 1)
            dq[h, :, cols] = dot(kv0[:size, :count], grad_scores, 1, 0)
    for m in range(1, SPAN):

        @pl.when((rank ^ m) < rank)
        def _():
            for h in range(heads):
                span = slice(h * size, (h + 1) * size)
                query, grad = q_ref[span, :], do_ref[span, :]
                scores = dot(keys[m], query, 1, 0)
                probs = jnp.exp(scores - jnp.where(seen, lse_ref[h], -FAR_BELOW))
                grad_probs = dot(vals[m], grad, 1, 0)
                grad_scores = (probs * (grad_probs - deltas[h])).astype(LOW)
                total[m, :size, :] += dot(query, grad_scores, 1, 1)
                total[m, size:, :] += dot(grad, probs.astype(LOW), 1, 1)
                dq[h] += dot(blocks[m][:size, :], grad_scores, 1, 0)

    middle_at = size // 2
    cosine, sine = cos_ref[...], sin_ref[...]
    for h in range(heads):
        first = dq[h, :middle_at, :] * size ** (-0.5)
        second = dq[h, middle_at:, :] * size ** (-0.5)
        base = h * size
        dq_ref[base : base + middle_at, :] = (first * cosine + second * sine).astype(LOW)
        dq_ref[base + middle_at : base + size, :] = (second * cosine - first * sine).astype(LOW)

    @pl.when(step == pl.num_programs(0) - 1)
    def _():
        g0[...] = total[0]
        for m, out in ((1, g1), (2, g2), (3, g3)):
            out[...] = total[m].astype(LOW)


def attention_forward(at, pos, queries, blocks, size, heads):
    wide, rows = queries.shape
    count = wide // size
    whole = pl.BlockSpec((2 * size, rows), lambda i, r: (0, 0))
    some = pl.BlockSpec((heads * size, rows), lambda i, r: (i, 0))
    return pl.pallas_call(
        functools.partial(forward_kernel, heads, size),
        out_shape=(
            jax.ShapeDtypeStruct((wide, rows), LOW),
            jax.ShapeDtypeStruct((count, 1, rows), jnp.float32),
        ),
        grid_spec=pltpu.PrefetchScalarGridSpec(
            num_scalar_prefetch=1,
            grid=(count // heads,),
            in_specs=[pl.BlockSpec((1, rows), lambda i, r: (0, 0)), some] + [whole] * SPAN,
            out_specs=[some, pl.BlockSpec((heads, 1, rows), lambda i, r: (i, 0, 0))],
            scratch_shapes=[
                pltpu.VMEM((SPAN, rows, size), LOW),
                pltpu.VMEM((SPAN, size + 16, rows), LOW),
                pltpu.VMEM((heads, 1, rows), jnp.float32),
                pltpu.VMEM((heads, size + 16, rows), jnp.float32),
                pltpu.VMEM((heads * size, rows), LOW),
            ],
        ),
        compiler_params=pltpu.CompilerParams(vmem_limit_bytes=24 << 20),
        cost_estimate=pl.CostEstimate(
            flops=32 * wide * rows * rows * SPAN,
            bytes_accessed=4 * wide * rows,
            transcendentals=0,
        ),
        name="attention_forward",
    )(at, pos, queries, *blocks)


def attention_backward(at, pos, queries, grads, attended, lse, cosine, sine, blocks, size, heads):
    wide, rows = queries.shape
    count = wide // size
    whole = pl.BlockSpec((2 * size, rows), lambda i, r: (0, 0))
    table = pl.BlockSpec((size // 2, rows), lambda i, r: (0, 0))
    some = pl.BlockSpec((heads * size, rows), lambda i, r: (i, 0))
    return pl.pallas_call(
        functools.partial(backward_kernel, heads, size),
        out_shape=(
            jax.ShapeDtypeStruct((wide, rows), LOW),
            jax.ShapeDtypeStruct((2 * size, rows), jnp.float32),
        )
        + (jax.ShapeDtypeStruct((2 * size, rows), LOW),) * (SPAN - 1),
        grid_spec=pltpu.PrefetchScalarGridSpec(
            num_scalar_prefetch=1,
            grid=(count // heads,),
            in_specs=[
                pl.BlockSpec((1, rows), lambda i, r: (0, 0)),
                some,
                some,
                some,
                pl.BlockSpec((heads, 1, rows), lambda i, r: (i, 0, 0)),
                table,
                table,
            ]
            + [whole] * SPAN,
            out_specs=[some] + [whole] * SPAN,
            scratch_shapes=[
                pltpu.VMEM((SPAN, rows, size), LOW),
                pltpu.VMEM((SPAN, rows, size), LOW),
                pltpu.VMEM((heads, size, rows), jnp.float32),
                pltpu.VMEM((SPAN, 2 * size, rows), jnp.float32),
                pltpu.VMEM((heads * size, rows), LOW),
                pltpu.VMEM((heads * size, rows), LOW),
            ],
        ),
        compiler_params=pltpu.CompilerParams(vmem_limit_bytes=24 << 20),
        cost_estimate=pl.CostEstimate(
            flops=48 * wide * rows * rows * SPAN,
            bytes_accessed=10 * wide * rows,
            transcendentals=0,
        ),
        name="attention_backward",
    )(at, pos, *in_hbm(queries, grads, attended, lse, cosine, sine, *blocks))


def take(values, start, size, dim):
    starts = [np.uint32(0)] * values.ndim
    starts[dim] = start
    sizes = list(values.shape)
    sizes[dim] = size
    return lax.dynamic_slice(values, starts, sizes)


def pick(values, places, blocks, dim):
    size = values.shape[dim] // blocks
    return jnp.concatenate(
        [lax.dynamic_slice_in_dim(values, p * size, size, dim) for p in places], dim
    )


class Table:
    def __init__(self, **parts):
        self.begin, at = {}, 0
        for name, part in parts.items():
            self.begin[name] = at
            at += part.shape[0]
        self.values = jnp.concatenate([p.astype(jnp.int32) for p in parts.values()])

    def list(self, name, lo, hi):
        return [self.values[self.begin[name] + j] for j in range(lo, hi)]


def after(value, *others):
    return lax.optimization_barrier((value, *others))[0]


def parity_sum(terms, dim):
    count = lax.axis_size("dp")
    groups = [list(range(p, count, 2)) for p in range(2)]
    return lax.psum_scatter(
        terms.astype(LOW), "dp", scatter_dimension=dim, axis_index_groups=groups, tiled=True
    )


def terms_kernel(transposed, places, x, x_far, g, g_far, out):
    del places
    side = 1 if transposed else 0
    out[...] = (dot(x[...], g[...], 0, side) + dot(x_far[...], g_far[...], 0, side)).astype(LOW)


def weight_terms(table, name, far, lo, hi, x, x_far, g, g_far, transposed=False, keep=True):
    count = hi - lo
    size = x.shape[1] // lax.axis_size("dp")
    rows = x.shape[0]
    units = g.shape[0] if transposed else g.shape[1]
    if size % 128:
        side = 1 if transposed else 0
        mine = pick(x, table.list(name, lo, hi), x.shape[1] // size, 1)
        theirs = pick(x_far, table.list(far, lo, hi), x_far.shape[1] // size, 1)
        return (dot(mine, g, 0, side) + dot(theirs, g_far, 0, side)).astype(LOW)
    whole = pl.BlockSpec(g.shape, lambda i, p: (0, 0))
    begin, far_begin = table.begin[name] + lo, table.begin[far] + lo
    return pl.pallas_call(
        functools.partial(terms_kernel, transposed),
        out_shape=(jax.ShapeDtypeStruct if keep else pltpu.HBM)((count * size, units), LOW),
        grid_spec=pltpu.PrefetchScalarGridSpec(
            num_scalar_prefetch=1,
            grid=(count,),
            in_specs=[
                pl.BlockSpec((rows, size), lambda i, p: (0, p[begin + i])),
                pl.BlockSpec((rows, size), lambda i, p: (0, p[far_begin + i])),
                whole,
                whole,
            ],
            out_specs=pl.BlockSpec((size, units), lambda i, p: (i, 0)),
        ),
        compiler_params=pltpu.CompilerParams(vmem_limit_bytes=20 << 20),
        cost_estimate=pl.CostEstimate(
            flops=24 * rows * count * size * units, bytes_accessed=4 * rows * units, transcendentals=0
        ),
        name="weight_terms",
    )(table.values, x, x_far, g, g_far)


def copy_kernel(places, source, target):
    del places
    target[...] = source[...]


def pick_columns(table, name, values, part=None, parts=1):
    blocks = lax.axis_size("dp")
    rows, count = values.shape[0] // parts, blocks // 2
    size = values.shape[1] // blocks
    if size % 128:
        if part is not None:
            values = lax.dynamic_slice_in_dim(values, table.list(part, 0, 1)[0] * rows, rows, 0)
        return pick(values, table.list(name, 0, count), blocks, 1)
    begin = table.begin[name]
    row = 0 if part is None else table.begin[part]
    return pl.pallas_call(
        copy_kernel,
        out_shape=jax.ShapeDtypeStruct((rows, count * size), values.dtype),
        grid_spec=pltpu.PrefetchScalarGridSpec(
            num_scalar_prefetch=1,
            grid=(count,),
            in_specs=[
                pl.BlockSpec(
                    (rows, size), lambda i, p: (0 if part is None else p[row], p[begin + i])
                )
            ],
            out_specs=pl.BlockSpec((rows, size), lambda i, p: (0, i)),
        ),
        compiler_params=pltpu.CompilerParams(vmem_limit_bytes=8 << 20),
        cost_estimate=pl.CostEstimate(
            flops=65536 * rows * count * size, bytes_accessed=4 * rows * count * size, transcendentals=0
        ),
        name="pick_columns",
    )(table.values, values)


def load_kernel(*refs):
    *pairs, sems = refs
    half = len(pairs) // 2
    copies = [
        pltpu.make_async_copy(source, target, sems.at[j])
        for j, (source, target) in enumerate(zip(pairs[:half], pairs[half:]))
    ]
    for copy in copies:
        copy.start()
    for copy in copies:
        copy.wait()


def load_weights(*weights):
    return pl.pallas_call(
        load_kernel,
        out_shape=tuple(pltpu.VMEM(w.shape, w.dtype) for w in weights),
        in_specs=[pl.BlockSpec(memory_space=pl.ANY)] * len(weights),
        out_specs=[pl.BlockSpec(memory_space=pltpu.VMEM)] * len(weights),
        scratch_shapes=[pltpu.SemaphoreType.DMA((len(weights),))],
        compiler_params=pltpu.CompilerParams(vmem_limit_bytes=2 << 20),
        cost_estimate=pl.CostEstimate(
            flops=20_000_000_000,
            bytes_accessed=2 * sum(w.size for w in weights),
            transcendentals=0,
        ),
        name="load_weights",
    )(*in_hbm(*weights))


def in_vmem(*arrays):
    return [pltpu.with_memory_space_constraint(a, pltpu.VMEM) for a in arrays]


def ffn_kernel(rows, gate_w, up_w, grad_in, hidden, grad_gate, grad_up):
    step = hidden.shape[1]
    cut = pl.ds(pl.multiple_of(pl.program_id(0) * step, step), step)
    both = dot(rows[...], jnp.concatenate([gate_w[:, cut], up_w[:, cut]], 1), 1, 0)
    gate, up = both[:, :step], both[:, step:]
    grad = grad_in[...]
    sigma = jax.nn.sigmoid(gate)
    active = gate * sigma
    hidden[...] = (active * up).astype(LOW)
    grad_gate[...] = (grad * up * sigma * (1.0 + gate * (1.0 - sigma))).astype(LOW)
    grad_up[...] = (grad * active).astype(LOW)


def feed_forward(rows, w_gate, w_up, grad_hidden):
    count, width = rows.shape
    units = w_gate.shape[1]
    step = 128
    weights = pl.BlockSpec(memory_space=pltpu.VMEM)
    wide = pl.BlockSpec((count, step), lambda i: (0, i))
    return pl.pallas_call(
        ffn_kernel,
        out_shape=(jax.ShapeDtypeStruct((count, units), LOW),) * 3,
        grid=(units // step,),
        in_specs=[pl.BlockSpec((count, width), lambda i: (0, 0)), weights, weights, wide],
        out_specs=[wide] * 3,
        compiler_params=pltpu.CompilerParams(vmem_limit_bytes=16 << 20),
        cost_estimate=pl.CostEstimate(
            flops=6 * count * width * units,
            bytes_accessed=4 * width * units,
            transcendentals=count * units,
        ),
        name="feed_forward",
    )(rows, *in_vmem(w_gate, w_up), grad_hidden)


def back_terms(gate_rows, up_rows, gate_w, up_w, step, size):
    cut = pl.ds(pl.multiple_of(step * size, size), size)
    return dot(gate_rows[...], gate_w[cut, :], 1, 1) + dot(up_rows[...], up_w[cut, :], 1, 1)


def back_kernel(gate_rows, up_rows, gate_w, up_w, out):
    out[...] = back_terms(gate_rows, up_rows, gate_w, up_w, pl.program_id(0), out.shape[1])


def back_send_kernel(steps, added, gate_rows, up_rows, gate_w, up_w, *refs):
    *more, out = refs
    step = pl.program_id(0)

    @pl.when(step < steps)
    def _():
        out[...] = back_terms(gate_rows, up_rows, gate_w, up_w, step, out.shape[1]).astype(LOW)

    for j, ref in enumerate(more):
        begin = steps + j * added

        @pl.when((step >= begin) & (step < begin + added))
        def _():
            out[...] = ref[...]


def feed_forward_back(grad_gate, grad_up, w_gate, w_up, half, more=()):
    count, units = grad_gate.shape
    width = w_gate.shape[0]
    step = 256
    steps = width // step
    added = more[0].shape[1] // step if more else 0
    rows = pl.BlockSpec((count // 2, units), lambda i: (half, 0))
    weights = pl.BlockSpec(memory_space=pltpu.VMEM)
    specs, kernel, kind = [rows, rows, weights, weights], back_kernel, jnp.float32
    for j in range(len(more)):
        begin = steps + j * added
        specs.append(
            pl.BlockSpec(
                (count // 2, step), lambda i, b=begin: (0, jnp.clip(i - b, 0, added - 1))
            )
        )
    if more:
        kernel, kind = functools.partial(back_send_kernel, steps, added), LOW
    added *= len(more)
    return pl.pallas_call(
        kernel,
        out_shape=jax.ShapeDtypeStruct((count // 2, width + added * step), kind),
        grid=(steps + added,),
        in_specs=specs,
        out_specs=pl.BlockSpec((count // 2, step), lambda i: (0, i)),
        compiler_params=pltpu.CompilerParams(vmem_limit_bytes=16 << 20),
        cost_estimate=pl.CostEstimate(
            flops=8 * count * width * units, bytes_accessed=4 * width * units, transcendentals=0
        ),
        name="feed_forward_back",
    )(grad_gate, grad_up, *in_vmem(w_gate, w_up), *more)


def row_kernel(left, right, send, kept):
    half = left.shape[0] // 2
    send[...] = dot(left[half:, :], right[...], 1, 0).astype(LOW)
    kept[...] = dot(left[:half, :], right[...], 1, 0)


def row_terms(left, right):
    rows, units = left.shape
    half, width = rows // 2, right.shape[1]
    step = 256
    return pl.pallas_call(
        row_kernel,
        out_shape=(
            jax.ShapeDtypeStruct((half, width), LOW),
            jax.ShapeDtypeStruct((half, width), jnp.float32),
        ),
        grid=(width // step,),
        in_specs=[
            pl.BlockSpec((rows, units), lambda i: (0, 0)),
            pl.BlockSpec((units, step), lambda i: (0, i)),
        ],
        out_specs=[pl.BlockSpec((half, step), lambda i: (0, i))] * 2,
        compiler_params=pltpu.CompilerParams(vmem_limit_bytes=16 << 20),
        cost_estimate=pl.CostEstimate(
            flops=8 * rows * units * width, bytes_accessed=2 * units * width, transcendentals=0
        ),
        name="row_terms",
    )(left, right)


def turn(values, cosine, sine):
    half = cosine.shape[0]
    heads = values.shape[0] // (2 * half)
    pieces = values.reshape(heads, 2, half, values.shape[1])
    first, second = pieces[:, 0], pieces[:, 1]
    return jnp.stack(
        [first * cosine - second * sine, second * cosine + first * sine], 1
    ).reshape(values.shape)


def turn_back(grads, cosine, sine):
    return turn(grads, cosine, -sine)


def norm_back(grad_rows, values, scale_rows, gain):
    scaled = grad_rows * gain
    inner_mean = jnp.mean(scaled * values, -1, keepdims=True)
    return (
        scale_rows * (scaled - values * scale_rows * scale_rows * inner_mean),
        jnp.sum(grad_rows * values * scale_rows, 0),
    )


def shards(
    tokens,
    positions,
    norm1_gain,
    w_query,
    w_key,
    w_value,
    w_out,
    norm2_gain,
    w_gate,
    w_up,
    w_down,
    cotangent,
):
    rows_here, width = tokens.shape
    size = w_key.shape[1]
    dp = lax.axis_size("dp")
    tp_count = len(ROW_MASKS)
    own_rows = rows_here // tp_count
    block = width // dp
    bits = dp.bit_length() - 1
    half_count = dp // 2

    def exchange_order(order):
        return np.array(
            [
                sum(((j >> (len(order) - 1 - k)) & 1) << b for k, b in enumerate(order))
                for j in range(1 << len(order))
            ],
            np.int32,
        )

    down_bits = [0] + list(range(2, bits))
    rest_bits = list(range(1, bits))

    place = lax.axis_index("dp").astype(jnp.int32)
    spot = lax.axis_index("tp").astype(jnp.int32)
    natural = np.arange(half_count, dtype=np.int32)
    down_here, rest_here = place ^ exchange_order(down_bits), place ^ exchange_order(rest_bits)
    table = Table(
        mine=2 * natural + (place & 1),
        theirs=2 * natural + (1 - (place & 1)),
        natural=jnp.asarray(natural),
        down=down_here,
        down_far=down_here ^ 2,
        rest=rest_here,
        rest_far=rest_here ^ 1,
        rest_block=rest_here >> 1,
        core=(spot & 1)[None],
    )
    at = jnp.stack([place & (SPAN - 1), spot])
    row_starts = [((spot ^ m) * own_rows).astype(jnp.uint32) for m in ROW_MASKS]
    core_starts = [(c * (rows_here // 2)).astype(jnp.uint32) for c in (spot & 1, 1 - (spot & 1))]
    tokens, table.values, at, row_starts, core_starts = lax.optimization_barrier(
        (tokens, table.values, at, row_starts, core_starts)
    )
    pos = positions.reshape(1, rows_here)

    def own(values):
        return take(values, row_starts[0], own_rows, 0)

    inputs = tokens.astype(jnp.float32)
    scale_one = lax.rsqrt(jnp.mean(inputs * inputs, -1, keepdims=True) + EPSILON)
    normed_one = (inputs * scale_one * norm1_gain).astype(LOW)
    half = size // 2
    frequency = jnp.exp(
        -jnp.log(10000.0) * (2.0 * jnp.arange(half, dtype=jnp.float32) / size)
    )
    angles = frequency[:, None] * positions.astype(jnp.float32)[None, :]
    cosine, sine = jnp.cos(angles), jnp.sin(angles)
    w_kv = jnp.concatenate([w_key.T, w_value.T], 0)
    paired = dot(w_kv, normed_one, 1, 1)
    paired = jnp.concatenate([turn(paired[:size], cosine, sine), paired[size:]], 0).astype(LOW)
    blocks = [paired] + [flip(paired, "dp", m) for m in range(1, SPAN)]
    queries = (turn(dot(w_query, normed_one, 0, 1), cosine, sine) * size ** (-0.5)).astype(LOW)

    wide = w_query.shape[1]

    def near_sum(part):
        send = part(2, 4).astype(LOW)
        near, kept = lax.optimization_barrier((flip(send, "tp", 1), part(0, 2)))
        pair = kept + near
        return pair[:own_rows], pair[own_rows:].astype(LOW)

    attended, lse = attention_forward(at, pos, queries, blocks, size, 8)

    branch, branch_out = near_sum(
        lambda lo, hi: dot(attended[:, lo * own_rows : hi * own_rows], w_out, 0, 0)
    )
    branch_far = flip(branch_out, "tp", 2)
    att_theirs = flip(after(attended, branch_out), "dp", 1)
    cot = jnp.concatenate(
        [take(after(cotangent, branch_out), start, own_rows, 0) for start in row_starts], 0
    )
    cot_send = pick_columns(table, "down_far", cot)
    cot_theirs = flip(cot_send, "dp", 2)
    own_inputs = own(tokens).astype(jnp.float32)
    one_send = pick_columns(table, "theirs", after(normed_one, cot_send), "core", 2)
    one_near = flip(one_send, "dp", 1)
    grad_hidden = dot(after(cot, one_send), w_down, 1, 1)
    middle = own_inputs + (after(branch, grad_hidden) + branch_far)

    scale_two = lax.rsqrt(jnp.mean(middle * middle, -1, keepdims=True) + EPSILON)
    own_two = (middle * scale_two * norm2_gain).astype(LOW)
    far_two = flip(own_two, "tp", 2)
    gate_w, up_w = load_weights(after(w_gate, own_two), w_up)
    pair_two = jnp.concatenate([after(own_two, att_theirs, gate_w), far_two], 0)
    core_two = flip(pair_two, "tp", 1)
    two_send = pick_columns(table, "theirs", pair_two)
    two_near = flip(two_send, "dp", 1)
    normed_two = jnp.concatenate([after(pair_two, two_send), core_two], 0)

    hidden, grad_gate_pre, grad_up_pre = feed_forward(normed_two, gate_w, up_w, grad_hidden)
    gate_theirs = flip(grad_gate_pre, "dp", 1)
    hidden_theirs = flip(hidden, "dp", 2)
    up_theirs = flip(grad_up_pre, "dp", 1)
    gate_late, cot_theirs, two_near, one_near = lax.optimization_barrier(
        (grad_gate_pre, cot_theirs, two_near, one_near)
    )

    two_back = functools.partial(feed_forward_back, gate_late, grad_up_pre, gate_w, up_w)
    core_send = two_back(1, (two_near, one_near))
    core_got, kept = lax.optimization_barrier((flip(core_send, "tp", 1), two_back(0)))
    pair = kept + core_got[:, :width]
    grad_normed_two, two_out = pair[:own_rows], pair[own_rows:].astype(LOW)
    two_far = flip(two_out, "tp", 2)
    two_theirs = jnp.concatenate([two_near, core_got[:, width : width + width // 2]], 0)

    down_near, down = row_terms(after(hidden, two_out), w_down)
    grad_normed_two = after(grad_normed_two, down) + two_far

    grad_mid_norm, gain_two = norm_back(grad_normed_two, middle, scale_two, norm2_gain)
    grad_middle = own(cotangent).astype(jnp.float32) + grad_mid_norm
    branch_grad = grad_middle.astype(LOW)
    grad_far = flip(branch_grad, "tp", 2)

    down_near = flip(after(down_near, branch_grad), "tp", 1)
    gate_terms = weight_terms(
        table,
        "mine",
        "natural",
        0,
        half_count,
        after(normed_two, branch_grad),
        two_theirs,
        grad_gate_pre,
        gate_theirs,
        keep=False,
    )
    grad_gate = parity_sum(gate_terms, 0)
    one_near, one_core = lax.optimization_barrier(
        (one_near, core_got[:, width + width // 2 :], gate_terms)
    )[:2]
    one_theirs = jnp.zeros((rows_here, width // 2), LOW)
    for piece, start in zip((one_near, one_core), core_starts):
        one_theirs = lax.dynamic_update_slice(one_theirs, piece, (start, np.uint32(0)))
    branch_grad = after(branch_grad, one_theirs)
    grad_pair = jnp.concatenate([after(branch_grad, gate_terms), grad_far], 0)
    grad_core = flip(grad_pair, "tp", 1)
    branch_send = pick_columns(table, "theirs", grad_pair)

    def near_flip(terms, bit):
        half = terms.shape[0] // 2
        return [flip(terms[half:], "dp", 1 << bit), flip(terms[:half], "dp", 1 << bit)]

    def down_terms(lo, hi, *late):
        g = after(hidden, *late)
        return weight_terms(table, "down", "natural", lo, hi, cot, cot_theirs, g, hidden_theirs)

    down_sent = down_terms(half_count // 2, half_count, branch_send)
    half = down_sent.shape[0] // 2
    down_first = flip(down_sent[half:], "dp", 1)
    branch_all = jnp.concatenate([after(grad_pair, down_sent), grad_core], 0)
    grad_attended = dot(w_out, branch_all, 1, 1).astype(LOW)
    grads = attention_backward(
        at, pos, queries, grad_attended, attended, lse, cosine, sine, blocks, size, 2
    )
    grad_query_rows, kv_total = grads[0], grads[1]
    kv_back = [flip(grads[m + 1], "dp", m) for m in range(1, SPAN)]

    def rest_terms(lo, hi, x, x_far, g, g_far, transposed=False):
        return weight_terms(
            table, "rest", "rest_block", lo, hi, x, x_far, g, g_far, transposed
        )

    down = down + after(down_near, grad_query_rows)
    down, down_out = down[:own_rows], down[own_rows:].astype(LOW)
    down_far = flip(down_out, "tp", 2)

    def up_terms(lo, hi, *late):
        return rest_terms(lo, hi, normed_two, two_theirs, after(grad_up_pre, *late), up_theirs)

    up_sent = up_terms(half_count // 2, half_count, grad_query_rows)
    up_first = flip(up_sent[half:], "dp", 2)

    def exchange_mid(terms, first, order, *late):
        got, left = [first], half_count // 2
        for b in order[1:]:
            send = terms(left // 2, left, *late).astype(jnp.float32)
            rows = send.shape[0]
            for other in got:
                send = send + other[other.shape[0] - rows :]
            send = send.astype(LOW)
            got.append(flip(send, "dp", 1 << b))
            left //= 2
        return got[1:], send

    down_late, down_last = exchange_mid(down_terms, down_first, down_bits, grad_query_rows)
    kv_total = lax.optimization_barrier((kv_total, up_sent, down_out, down_last))[0]
    for back in kv_back:
        kv_total = kv_total + back
    key_grad = turn_back(kv_total[:size], cosine, sine)
    grad_kv_rows = jnp.concatenate([key_grad, kv_total[size:]], 0).astype(LOW)
    proj_rows = jnp.concatenate([grad_query_rows, grad_kv_rows], 0)
    proj_theirs = flip(proj_rows, "dp", 1)
    branch_near = flip(after(branch_send, proj_rows), "dp", 1)

    own_order = jnp.concatenate(
        [take(proj_rows, start, own_rows, 1) for start in row_starts], 1
    )

    def one_terms(lo, hi):
        cut = own_order[:, lo * own_rows : hi * own_rows]
        return dot(cut[:wide], w_query, 0, 1) + dot(cut[wide:], w_kv, 0, 0)

    grad_normed_one, one_out = near_sum(one_terms)
    one_far = flip(one_out, "tp", 2)
    output_rows = (middle + (down + after(down_far, one_out))).astype(LOW)
    up_kept = up_terms(0, 1, one_out)
    grad_gate = grad_gate.astype(jnp.float32)
    grad_normed_one = after(grad_normed_one, output_rows, up_kept, grad_gate) + one_far
    grad_in_norm, gain_one = norm_back(grad_normed_one, own_inputs, own(scale_one), norm1_gain)
    input_rows = grad_middle + grad_in_norm

    up_late, up_last = exchange_mid(up_terms, up_first, rest_bits, input_rows)
    branch_near, down_second = lax.optimization_barrier((branch_near, down_sent[:half], up_last))[:2]
    branch_theirs = jnp.concatenate([branch_near, flip(branch_near, "tp", 1)], 0)
    down_second = flip(down_second, "dp", 1)
    gain_one, *down_late = lax.optimization_barrier((gain_one, *down_late, up_last))[:-1]
    gains = jnp.stack([gain_one, gain_two])
    for m in (1, 2):
        gains = gains + flip(gains, "tp", m)
    gains = pick_columns(table, "rest", gains) + flip(
        pick_columns(table, "rest_far", gains), "dp", 1
    )

    out_late, proj_late = lax.optimization_barrier((attended, proj_rows, up_last))[:2]

    def last_terms(lo, hi, *late):
        first, second = after(proj_late, *late), after(out_late, *late)
        return jnp.concatenate(
            [
                rest_terms(lo, hi, normed_one, one_theirs, first, proj_theirs, True),
                rest_terms(lo, hi, branch_all, branch_theirs, second, att_theirs, True),
            ],
            1,
        )

    def with_gains(terms, lo, hi, *others):
        extra = gains[:, lo * block : hi * block]
        for other, other_gains in others:
            terms = terms.astype(jnp.float32) + other
            extra = extra + other_gains
        columns = terms.shape[1]
        extra = jnp.pad(extra, ((0, 14), (0, -extra.shape[1] % columns)))[:, :columns]
        return jnp.concatenate([terms.astype(LOW), extra.astype(LOW)], 0)

    def split(message, count):
        rows = count * block
        return message[:rows], message[rows : rows + 2, :rows]

    quarter = half_count // 4
    sent = last_terms(half_count // 2, half_count)
    cut = quarter * block
    firsts = with_gains(sent[cut:], 3 * quarter, half_count)
    seconds = with_gains(sent[:cut], 2 * quarter, 3 * quarter)
    mids = [split(flip(firsts, "dp", 2), quarter)]
    last_second = split(flip(after(seconds, firsts), "dp", 2), quarter)
    proj_kept = rest_terms(0, 1, normed_one, one_theirs, after(proj_late, firsts), proj_theirs, True)
    out_kept = rest_terms(0, 1, branch_all, branch_theirs, after(out_late, firsts), att_theirs, True)
    down_kept = down_terms(0, 1, firsts)
    left = half_count // 2
    for b in rest_bits[1:]:
        count = left // 2
        terms = last_terms(count, left, firsts)
        terms, *up_late = lax.optimization_barrier((terms, *up_late, proj_kept, out_kept, down_kept))[
            :-3
        ]
        send = with_gains(
            terms, count, left, *((o[-count * block :], g[:, -count * block :]) for o, g in mids)
        )
        mids.append(split(flip(send, "dp", 1 << b), count))
        left = count
    up_second = flip(after(up_sent[:half], send), "dp", 2)

    def ending(kept, *others):
        kept = kept.astype(jnp.float32)
        for other in others:
            kept = kept + other[:block]
        return kept

    down_kept, down_second = lax.optimization_barrier((down_kept, down_second, send))[:2]
    grad_down = ending(down_kept, down_second, *down_late)
    grad_last = ending(
        jnp.concatenate([proj_kept, out_kept], 1), last_second[0], *(m[0] for m in mids[1:])
    )
    gains = gains[:, :block] + last_second[1][:, :block]
    for _, other in mids[1:]:
        gains = gains + other[:, :block]
    grad_up = ending(up_kept, up_second, *up_late)
    narrow = wide + 2 * size

    return (
        output_rows,
        input_rows,
        gains[0],
        grad_last[:, :wide],
        grad_last[:, wide : wide + size],
        grad_last[:, wide + size : narrow],
        grad_last[:, narrow:].T,
        gains[1],
        grad_gate,
        grad_up,
        grad_down.T,
    )


def solution(mesh):
    placed = (
        P("dp", None),
        P("dp"),
        P(),
        P(None, "tp"),
        P(None, "tp"),
        P(None, "tp"),
        P("tp", None),
        P(),
        P(None, "tp"),
        P(None, "tp"),
        P("tp", None),
        P("dp", None),
    )
    return jax.shard_map(
        shards,
        mesh=mesh,
        in_specs=placed,
        out_specs=(
            P(("dp", "tp"), None),
            P(("dp", "tp"), None),
            P("dp"),
            P("dp", "tp"),
            P("dp", "tp"),
            P("dp", "tp"),
            P("tp", "dp"),
            P("dp"),
            P("dp", "tp"),
            P("dp", "tp"),
            P("tp", "dp"),
        ),
        check_vma=False,
    )
```

```python
import functools

import jax
import jax.numpy as jnp
import numpy as np
from jax import lax
from jax.experimental import pallas as pl
from jax.experimental.pallas import tpu as pltpu
from jax.sharding import PartitionSpec as P

SPAN = 4
EPSILON = 1e-05
FAR_BELOW = -1e30
LOW = jnp.bfloat16
ROW_MASKS = (0, 2, 1, 3)


def flip(block, axis, mask):
    return lax.ppermute(block, axis, [(i, i ^ mask) for i in range(lax.axis_size(axis))])


def dot(left, right, left_dim, right_dim):
    return lax.dot_general(
        left,
        right,
        (((left_dim,), (right_dim,)), ((), ())),
        preferred_element_type=jnp.float32,
    )


def in_hbm(*arrays):
    return [pltpu.with_memory_space_constraint(a, pltpu.HBM) for a in arrays]


def own_mask(pos, begin, keys, queries):
    key_at = lax.broadcasted_iota(jnp.int32, (keys, queries), 0)
    query_at = lax.broadcasted_iota(jnp.int32, (keys, queries), 1) + begin
    return (key_at <= query_at) & (key_at >= query_at - pos)


def row_starts(spot, rows):
    part = rows // len(ROW_MASKS)
    return [pl.multiple_of((spot ^ m) * part, part) for m in ROW_MASKS]


def forward_kernel(
    heads,
    size,
    at_ref,
    pos_ref,
    q_ref,
    kv0,
    kv1,
    kv2,
    kv3,
    o_ref,
    lse_ref,
    keys,
    vals,
    top,
    acc,
    ordered,
):
    rank, spot = at_ref[0], at_ref[1]
    rows = pos_ref.shape[1]
    half = rows // 2

    @pl.when(pl.program_id(0) == 0)
    def _():
        for m, kv in enumerate((kv0, kv1, kv2, kv3)):
            keys[m] = kv[:size, :].T
            vals[m, :size, :] = kv[size:, :]
            vals[m, size:, :] = jnp.ones((16, rows), LOW)

    pos = pos_ref[...]
    for part in range(2):
        cols = slice(part * half, (part + 1) * half)
        count = (part + 1) * half
        mask = own_mask(pos[:, cols], part * half, count, half)
        for h in range(heads):
            scores = dot(keys[0, :count, :], q_ref[h * size : (h + 1) * size, cols], 1, 0)
            scores = jnp.where(mask, scores, FAR_BELOW)
            peak = jnp.max(scores, 0, keepdims=True)
            weights = jnp.exp(scores - peak).astype(LOW)
            acc[h, :, cols] = dot(vals[0, :, :count], weights, 1, 0)
            top[h, :, cols] = peak
    seen = pos > lax.broadcasted_iota(jnp.int32, (1, rows), 1)
    for m in range(1, SPAN):

        @pl.when((rank ^ m) < rank)
        def _():
            for h in range(heads):
                scores = dot(keys[m], q_ref[h * size : (h + 1) * size, :], 1, 0)
                old = top[h]
                peak = jnp.where(seen, jnp.maximum(old, jnp.max(scores, 0, keepdims=True)), old)
                weights = jnp.exp(scores - jnp.where(seen, peak, -FAR_BELOW)).astype(LOW)
                acc[h] = acc[h] * jnp.exp(old - peak) + dot(vals[m], weights, 1, 0)
                top[h] = peak

    for h in range(heads):
        total = acc[h, size : size + 1, :]
        ordered[h * size : (h + 1) * size, :] = (acc[h, :size, :] / total).astype(LOW)
        lse_ref[h] = top[h] + jnp.log(total)
    for j, start in enumerate(row_starts(spot, rows)):
        part = rows // len(ROW_MASKS)
        o_ref[:, j * part : (j + 1) * part] = ordered[:, pl.ds(start, part)]


def backward_kernel(
    heads,
    size,
    at_ref,
    pos_ref,
    q_ref,
    do_in,
    o_in,
    lse_ref,
    cos_ref,
    sin_ref,
    kv0,
    kv1,
    kv2,
    kv3,
    dq_ref,
    g0,
    g1,
    g2,
    g3,
    keys,
    vals,
    dq,
    total,
    do_ref,
    o_ref,
):
    rank, spot = at_ref[0], at_ref[1]
    rows = pos_ref.shape[1]
    half = rows // 2
    blocks = (kv0, kv1, kv2, kv3)
    step = pl.program_id(0)

    @pl.when(step == 0)
    def _():
        for m, kv in enumerate(blocks):
            keys[m] = kv[:size, :].T
            vals[m] = kv[size:, :].T
        total[...] = jnp.zeros_like(total)

    part = rows // len(ROW_MASKS)
    for j, start in enumerate(row_starts(spot, rows)):
        do_ref[:, pl.ds(start, part)] = do_in[:, j * part : (j + 1) * part]
        o_ref[:, pl.ds(start, part)] = o_in[:, j * part : (j + 1) * part]
    pos = pos_ref[...]
    seen = pos > lax.broadcasted_iota(jnp.int32, (1, rows), 1)
    deltas = []
    for h in range(heads):
        span = slice(h * size, (h + 1) * size)
        deltas.append(
            jnp.sum(
                do_ref[span, :].astype(jnp.float32) * o_ref[span, :].astype(jnp.float32),
                0,
                keepdims=True,
            )
        )
    for part in range(2):
        cols = slice(part * half, (part + 1) * half)
        count = (part + 1) * half
        mask = own_mask(pos[:, cols], part * half, count, half)
        for h in range(heads):
            span = slice(h * size, (h + 1) * size)
            query, grad = q_ref[span, cols], do_ref[span, cols]
            scores = dot(keys[0, :count, :], query, 1, 0)
            probs = jnp.exp(jnp.where(mask, scores, FAR_BELOW) - lse_ref[h, :, cols])
            grad_probs = dot(vals[0, :count, :], grad, 1, 0)
            grad_scores = (probs * (grad_probs - deltas[h][:, cols])).astype(LOW)
            total[0, :size, :count] += dot(query, grad_scores, 1, 1)
            total[0, size:, :count] += dot(grad, probs.astype(LOW), 1, 1)
            dq[h, :, cols] = dot(kv0[:size, :count], grad_scores, 1, 0)
    for m in range(1, SPAN):

        @pl.when((rank ^ m) < rank)
        def _():
            for h in range(heads):
                span = slice(h * size, (h + 1) * size)
                query, grad = q_ref[span, :], do_ref[span, :]
                scores = dot(keys[m], query, 1, 0)
                probs = jnp.exp(scores - jnp.where(seen, lse_ref[h], -FAR_BELOW))
                grad_probs = dot(vals[m], grad, 1, 0)
                grad_scores = (probs * (grad_probs - deltas[h])).astype(LOW)
                total[m, :size, :] += dot(query, grad_scores, 1, 1)
                total[m, size:, :] += dot(grad, probs.astype(LOW), 1, 1)
                dq[h] += dot(blocks[m][:size, :], grad_scores, 1, 0)

    middle_at = size // 2
    cosine, sine = cos_ref[...], sin_ref[...]
    for h in range(heads):
        first = dq[h, :middle_at, :] * size ** (-0.5)
        second = dq[h, middle_at:, :] * size ** (-0.5)
        base = h * size
        dq_ref[base : base + middle_at, :] = (first * cosine + second * sine).astype(LOW)
        dq_ref[base + middle_at : base + size, :] = (second * cosine - first * sine).astype(LOW)

    @pl.when(step == pl.num_programs(0) - 1)
    def _():
        g0[...] = total[0]
        for m, out in ((1, g1), (2, g2), (3, g3)):
            out[...] = total[m].astype(LOW)


def attention_forward(at, pos, queries, blocks, size, heads):
    wide, rows = queries.shape
    count = wide // size
    whole = pl.BlockSpec((2 * size, rows), lambda i, r: (0, 0))
    some = pl.BlockSpec((heads * size, rows), lambda i, r: (i, 0))
    return pl.pallas_call(
        functools.partial(forward_kernel, heads, size),
        out_shape=(
            jax.ShapeDtypeStruct((wide, rows), LOW),
            jax.ShapeDtypeStruct((count, 1, rows), jnp.float32),
        ),
        grid_spec=pltpu.PrefetchScalarGridSpec(
            num_scalar_prefetch=1,
            grid=(count // heads,),
            in_specs=[pl.BlockSpec((1, rows), lambda i, r: (0, 0)), some] + [whole] * SPAN,
            out_specs=[some, pl.BlockSpec((heads, 1, rows), lambda i, r: (i, 0, 0))],
            scratch_shapes=[
                pltpu.VMEM((SPAN, rows, size), LOW),
                pltpu.VMEM((SPAN, size + 16, rows), LOW),
                pltpu.VMEM((heads, 1, rows), jnp.float32),
                pltpu.VMEM((heads, size + 16, rows), jnp.float32),
                pltpu.VMEM((heads * size, rows), LOW),
            ],
        ),
        compiler_params=pltpu.CompilerParams(vmem_limit_bytes=24 << 20),
        cost_estimate=pl.CostEstimate(
            flops=32 * wide * rows * rows * SPAN,
            bytes_accessed=4 * wide * rows,
            transcendentals=0,
        ),
        name="attention_forward",
    )(at, pos, queries, *blocks)


def attention_backward(at, pos, queries, grads, attended, lse, cosine, sine, blocks, size, heads):
    wide, rows = queries.shape
    count = wide // size
    whole = pl.BlockSpec((2 * size, rows), lambda i, r: (0, 0))
    table = pl.BlockSpec((size // 2, rows), lambda i, r: (0, 0))
    some = pl.BlockSpec((heads * size, rows), lambda i, r: (i, 0))
    return pl.pallas_call(
        functools.partial(backward_kernel, heads, size),
        out_shape=(
            jax.ShapeDtypeStruct((wide, rows), LOW),
            jax.ShapeDtypeStruct((2 * size, rows), jnp.float32),
        )
        + (jax.ShapeDtypeStruct((2 * size, rows), LOW),) * (SPAN - 1),
        grid_spec=pltpu.PrefetchScalarGridSpec(
            num_scalar_prefetch=1,
            grid=(count // heads,),
            in_specs=[
                pl.BlockSpec((1, rows), lambda i, r: (0, 0)),
                some,
                some,
                some,
                pl.BlockSpec((heads, 1, rows), lambda i, r: (i, 0, 0)),
                table,
                table,
            ]
            + [whole] * SPAN,
            out_specs=[some] + [whole] * SPAN,
            scratch_shapes=[
                pltpu.VMEM((SPAN, rows, size), LOW),
                pltpu.VMEM((SPAN, rows, size), LOW),
                pltpu.VMEM((heads, size, rows), jnp.float32),
                pltpu.VMEM((SPAN, 2 * size, rows), jnp.float32),
                pltpu.VMEM((heads * size, rows), LOW),
                pltpu.VMEM((heads * size, rows), LOW),
            ],
        ),
        compiler_params=pltpu.CompilerParams(vmem_limit_bytes=24 << 20),
        cost_estimate=pl.CostEstimate(
            flops=48 * wide * rows * rows * SPAN,
            bytes_accessed=10 * wide * rows,
            transcendentals=0,
        ),
        name="attention_backward",
    )(at, pos, *in_hbm(queries, grads, attended, lse, cosine, sine, *blocks))


def take(values, start, size, dim):
    starts = [np.uint32(0)] * values.ndim
    starts[dim] = start
    sizes = list(values.shape)
    sizes[dim] = size
    return lax.dynamic_slice(values, starts, sizes)


def pick(values, places, blocks, dim):
    size = values.shape[dim] // blocks
    return jnp.concatenate(
        [lax.dynamic_slice_in_dim(values, p * size, size, dim) for p in places], dim
    )


class Table:
    def __init__(self, **parts):
        self.begin, at = {}, 0
        for name, part in parts.items():
            self.begin[name] = at
            at += part.shape[0]
        self.values = jnp.concatenate([p.astype(jnp.int32) for p in parts.values()])

    def list(self, name, lo, hi):
        return [self.values[self.begin[name] + j] for j in range(lo, hi)]


def after(value, *others):
    return lax.optimization_barrier((value, *others))[0]


def parity_sum(terms, dim):
    count = lax.axis_size("dp")
    groups = [list(range(p, count, 2)) for p in range(2)]
    return lax.psum_scatter(
        terms.astype(LOW), "dp", scatter_dimension=dim, axis_index_groups=groups, tiled=True
    )


def terms_kernel(transposed, places, x, x_far, g, g_far, out):
    del places
    side = 1 if transposed else 0
    out[...] = (dot(x[...], g[...], 0, side) + dot(x_far[...], g_far[...], 0, side)).astype(LOW)


def weight_terms(table, name, far, lo, hi, x, x_far, g, g_far, transposed=False, keep=True):
    count = hi - lo
    size = x.shape[1] // lax.axis_size("dp")
    rows = x.shape[0]
    units = g.shape[0] if transposed else g.shape[1]
    if size % 128:
        side = 1 if transposed else 0
        mine = pick(x, table.list(name, lo, hi), x.shape[1] // size, 1)
        theirs = pick(x_far, table.list(far, lo, hi), x_far.shape[1] // size, 1)
        return (dot(mine, g, 0, side) + dot(theirs, g_far, 0, side)).astype(LOW)
    whole = pl.BlockSpec(g.shape, lambda i, p: (0, 0))
    begin, far_begin = table.begin[name] + lo, table.begin[far] + lo
    return pl.pallas_call(
        functools.partial(terms_kernel, transposed),
        out_shape=(jax.ShapeDtypeStruct if keep else pltpu.HBM)((count * size, units), LOW),
        grid_spec=pltpu.PrefetchScalarGridSpec(
            num_scalar_prefetch=1,
            grid=(count,),
            in_specs=[
                pl.BlockSpec((rows, size), lambda i, p: (0, p[begin + i])),
                pl.BlockSpec((rows, size), lambda i, p: (0, p[far_begin + i])),
                whole,
                whole,
            ],
            out_specs=pl.BlockSpec((size, units), lambda i, p: (i, 0)),
        ),
        compiler_params=pltpu.CompilerParams(vmem_limit_bytes=20 << 20),
        cost_estimate=pl.CostEstimate(
            flops=24 * rows * count * size * units, bytes_accessed=4 * rows * units, transcendentals=0
        ),
        name="weight_terms",
    )(table.values, x, x_far, g, g_far)


def copy_kernel(places, source, target):
    del places
    target[...] = source[...]


def pick_columns(table, name, values, part=None, parts=1):
    blocks = lax.axis_size("dp")
    rows, count = values.shape[0] // parts, blocks // 2
    size = values.shape[1] // blocks
    if size % 128:
        if part is not None:
            values = lax.dynamic_slice_in_dim(values, table.list(part, 0, 1)[0] * rows, rows, 0)
        return pick(values, table.list(name, 0, count), blocks, 1)
    begin = table.begin[name]
    row = 0 if part is None else table.begin[part]
    return pl.pallas_call(
        copy_kernel,
        out_shape=jax.ShapeDtypeStruct((rows, count * size), values.dtype),
        grid_spec=pltpu.PrefetchScalarGridSpec(
            num_scalar_prefetch=1,
            grid=(count,),
            in_specs=[
                pl.BlockSpec(
                    (rows, size), lambda i, p: (0 if part is None else p[row], p[begin + i])
                )
            ],
            out_specs=pl.BlockSpec((rows, size), lambda i, p: (0, i)),
        ),
        compiler_params=pltpu.CompilerParams(vmem_limit_bytes=8 << 20),
        cost_estimate=pl.CostEstimate(
            flops=65536 * rows * count * size, bytes_accessed=4 * rows * count * size, transcendentals=0
        ),
        name="pick_columns",
    )(table.values, values)


def load_kernel(*refs):
    *pairs, sems = refs
    half = len(pairs) // 2
    copies = [
        pltpu.make_async_copy(source, target, sems.at[j])
        for j, (source, target) in enumerate(zip(pairs[:half], pairs[half:]))
    ]
    for copy in copies:
        copy.start()
    for copy in copies:
        copy.wait()


def load_weights(*weights):
    return pl.pallas_call(
        load_kernel,
        out_shape=tuple(pltpu.VMEM(w.shape, w.dtype) for w in weights),
        in_specs=[pl.BlockSpec(memory_space=pl.ANY)] * len(weights),
        out_specs=[pl.BlockSpec(memory_space=pltpu.VMEM)] * len(weights),
        scratch_shapes=[pltpu.SemaphoreType.DMA((len(weights),))],
        compiler_params=pltpu.CompilerParams(vmem_limit_bytes=2 << 20),
        cost_estimate=pl.CostEstimate(
            flops=20_000_000_000,
            bytes_accessed=2 * sum(w.size for w in weights),
            transcendentals=0,
        ),
        name="load_weights",
    )(*in_hbm(*weights))


def in_vmem(*arrays):
    return [pltpu.with_memory_space_constraint(a, pltpu.VMEM) for a in arrays]


def ffn_kernel(rows, gate_w, up_w, grad_in, hidden, grad_gate, grad_up):
    step = hidden.shape[1]
    cut = pl.ds(pl.multiple_of(pl.program_id(0) * step, step), step)
    both = dot(rows[...], jnp.concatenate([gate_w[:, cut], up_w[:, cut]], 1), 1, 0)
    gate, up = both[:, :step], both[:, step:]
    grad = grad_in[...]
    sigma = jax.nn.sigmoid(gate)
    active = gate * sigma
    hidden[...] = (active * up).astype(LOW)
    grad_gate[...] = (grad * up * sigma * (1.0 + gate * (1.0 - sigma))).astype(LOW)
    grad_up[...] = (grad * active).astype(LOW)


def feed_forward(rows, w_gate, w_up, grad_hidden):
    count, width = rows.shape
    units = w_gate.shape[1]
    step = 128
    weights = pl.BlockSpec(memory_space=pltpu.VMEM)
    wide = pl.BlockSpec((count, step), lambda i: (0, i))
    return pl.pallas_call(
        ffn_kernel,
        out_shape=(jax.ShapeDtypeStruct((count, units), LOW),) * 3,
        grid=(units // step,),
        in_specs=[pl.BlockSpec((count, width), lambda i: (0, 0)), weights, weights, wide],
        out_specs=[wide] * 3,
        compiler_params=pltpu.CompilerParams(vmem_limit_bytes=16 << 20),
        cost_estimate=pl.CostEstimate(
            flops=6 * count * width * units,
            bytes_accessed=4 * width * units,
            transcendentals=count * units,
        ),
        name="feed_forward",
    )(rows, *in_vmem(w_gate, w_up), grad_hidden)


def join_kernel(places, first, second, out):
    del places

    @pl.when(pl.program_id(0) == 0)
    def _():
        out[...] = first[...]

    @pl.when(pl.program_id(0) == 1)
    def _():
        out[...] = second[...]


def join_rows(table, first, second):
    rows, width = first.shape
    core = table.begin["core"]
    whole = pl.BlockSpec((rows, width), lambda i, p: (0, 0))
    return pl.pallas_call(
        join_kernel,
        out_shape=jax.ShapeDtypeStruct((2 * rows, width), first.dtype),
        grid_spec=pltpu.PrefetchScalarGridSpec(
            num_scalar_prefetch=1,
            grid=(2,),
            in_specs=[whole, whole],
            out_specs=pl.BlockSpec((rows, width), lambda i, p: (p[core] ^ i, 0)),
        ),
        compiler_params=pltpu.CompilerParams(vmem_limit_bytes=8 << 20),
        cost_estimate=pl.CostEstimate(
            flops=1_000_000_000, bytes_accessed=8 * rows * width, transcendentals=0
        ),
        name="join_rows",
    )(table.values, first, second)


def row_kernel(left, right, send, kept):
    half = left.shape[0] // 2
    send[...] = dot(left[half:, :], right[...], 1, 0).astype(LOW)
    kept[...] = dot(left[:half, :], right[...], 1, 0)


def row_terms(left, right):
    rows, units = left.shape
    half, width = rows // 2, right.shape[1]
    step = 256
    return pl.pallas_call(
        row_kernel,
        out_shape=(
            jax.ShapeDtypeStruct((half, width), LOW),
            jax.ShapeDtypeStruct((half, width), jnp.float32),
        ),
        grid=(width // step,),
        in_specs=[
            pl.BlockSpec((rows, units), lambda i: (0, 0)),
            pl.BlockSpec((units, step), lambda i: (0, i)),
        ],
        out_specs=[pl.BlockSpec((half, step), lambda i: (0, i))] * 2,
        compiler_params=pltpu.CompilerParams(vmem_limit_bytes=16 << 20),
        cost_estimate=pl.CostEstimate(
            flops=8 * rows * units * width, bytes_accessed=2 * units * width, transcendentals=0
        ),
        name="row_terms",
    )(left, right)


def turn(values, cosine, sine):
    half = cosine.shape[0]
    heads = values.shape[0] // (2 * half)
    pieces = values.reshape(heads, 2, half, values.shape[1])
    first, second = pieces[:, 0], pieces[:, 1]
    return jnp.stack(
        [first * cosine - second * sine, second * cosine + first * sine], 1
    ).reshape(values.shape)


def turn_back(grads, cosine, sine):
    return turn(grads, cosine, -sine)


def norm_back(grad_rows, values, scale_rows, gain):
    scaled = grad_rows * gain
    inner_mean = jnp.mean(scaled * values, -1, keepdims=True)
    return (
        scale_rows * (scaled - values * scale_rows * scale_rows * inner_mean),
        jnp.sum(grad_rows * values * scale_rows, 0),
    )


def shards(
    tokens,
    positions,
    norm1_gain,
    w_query,
    w_key,
    w_value,
    w_out,
    norm2_gain,
    w_gate,
    w_up,
    w_down,
    cotangent,
):
    rows_here, width = tokens.shape
    size = w_key.shape[1]
    dp = lax.axis_size("dp")
    tp_count = len(ROW_MASKS)
    own_rows = rows_here // tp_count
    block = width // dp
    bits = dp.bit_length() - 1
    half_count = dp // 2

    def exchange_order(order):
        return np.array(
            [
                sum(((j >> (len(order) - 1 - k)) & 1) << b for k, b in enumerate(order))
                for j in range(1 << len(order))
            ],
            np.int32,
        )

    down_bits = [0] + list(range(2, bits))
    rest_bits = list(range(1, bits))

    place = lax.axis_index("dp").astype(jnp.int32)
    spot = lax.axis_index("tp").astype(jnp.int32)
    natural = np.arange(half_count, dtype=np.int32)
    down_here, rest_here = place ^ exchange_order(down_bits), place ^ exchange_order(rest_bits)
    table = Table(
        mine=2 * natural + (place & 1),
        theirs=2 * natural + (1 - (place & 1)),
        natural=jnp.asarray(natural),
        down=down_here,
        down_far=down_here ^ 2,
        rest=rest_here,
        rest_far=rest_here ^ 1,
        rest_block=rest_here >> 1,
        core=(spot & 1)[None],
    )
    at = jnp.stack([place & (SPAN - 1), spot])
    row_starts = [((spot ^ m) * own_rows).astype(jnp.uint32) for m in ROW_MASKS]
    core_starts = [(c * (rows_here // 2)).astype(jnp.uint32) for c in (spot & 1, 1 - (spot & 1))]
    tokens, table.values, at, row_starts, core_starts = lax.optimization_barrier(
        (tokens, table.values, at, row_starts, core_starts)
    )
    pos = positions.reshape(1, rows_here)

    def own(values):
        return take(values, row_starts[0], own_rows, 0)

    inputs = tokens.astype(jnp.float32)
    scale_one = lax.rsqrt(jnp.mean(inputs * inputs, -1, keepdims=True) + EPSILON)
    normed_one = (inputs * scale_one * norm1_gain).astype(LOW)
    half = size // 2
    frequency = jnp.exp(
        -jnp.log(10000.0) * (2.0 * jnp.arange(half, dtype=jnp.float32) / size)
    )
    angles = frequency[:, None] * positions.astype(jnp.float32)[None, :]
    cosine, sine = jnp.cos(angles), jnp.sin(angles)
    w_kv = jnp.concatenate([w_key.T, w_value.T], 0)
    paired = dot(w_kv, normed_one, 1, 1)
    paired = jnp.concatenate([turn(paired[:size], cosine, sine), paired[size:]], 0).astype(LOW)
    blocks = [paired] + [flip(paired, "dp", m) for m in range(1, SPAN)]
    queries = (turn(dot(w_query, normed_one, 0, 1), cosine, sine) * size ** (-0.5)).astype(LOW)

    wide = w_query.shape[1]

    def near_sum(part):
        send = part(2, 4).astype(LOW)
        near, kept = lax.optimization_barrier((flip(send, "tp", 1), part(0, 2)))
        pair = kept + near
        return pair[:own_rows], pair[own_rows:].astype(LOW)

    attended, lse = attention_forward(at, pos, queries, blocks, size, 8)

    branch, branch_out = near_sum(
        lambda lo, hi: dot(attended[:, lo * own_rows : hi * own_rows], w_out, 0, 0)
    )
    branch_far = flip(branch_out, "tp", 2)
    cot = jnp.concatenate(
        [take(after(cotangent, branch_out), start, own_rows, 0) for start in row_starts], 0
    )
    cot_send = pick_columns(table, "down_far", cot)
    cot_theirs = flip(cot_send, "dp", 2)
    own_inputs = own(tokens).astype(jnp.float32)
    one_send = pick_columns(table, "theirs", after(normed_one, cot_send), "core", 2)
    one_near = flip(one_send, "dp", 1)
    grad_hidden = dot(after(cot, one_send), w_down, 1, 1)
    middle = own_inputs + (after(branch, grad_hidden) + branch_far)

    scale_two = lax.rsqrt(jnp.mean(middle * middle, -1, keepdims=True) + EPSILON)
    own_two = (middle * scale_two * norm2_gain).astype(LOW)
    far_two = flip(own_two, "tp", 2)
    gate_w, up_w = load_weights(after(w_gate, own_two), w_up)
    pair_two = jnp.concatenate([after(own_two, gate_w), far_two], 0)
    core_two = flip(pair_two, "tp", 1)
    two_send = pick_columns(table, "theirs", pair_two)
    two_near = flip(two_send, "dp", 1)
    normed_two = jnp.concatenate([after(pair_two, two_send), core_two], 0)

    hidden, grad_gate_pre, grad_up_pre = feed_forward(normed_two, gate_w, up_w, grad_hidden)
    gate_theirs = flip(grad_gate_pre, "dp", 1)
    hidden_theirs = flip(hidden, "dp", 2)
    up_theirs = flip(grad_up_pre, "dp", 1)
    gate_late, cot_theirs, one_near = lax.optimization_barrier((grad_gate_pre, cot_theirs, one_near))

    def two_terms(lo, hi):
        rows = slice(lo * own_rows, hi * own_rows)
        return dot(gate_late[rows], gate_w, 1, 1) + dot(grad_up_pre[rows], up_w, 1, 1)

    grad_normed_two, two_out = near_sum(two_terms)
    two_out, two_near = lax.optimization_barrier((two_out, two_near))
    two_far = flip(two_out, "tp", 2)
    cores = jnp.concatenate([two_near, one_near], 1)
    cores_far = flip(cores, "tp", 1)
    two_theirs = jnp.concatenate([two_near, cores_far[:, : width // 2]], 0)

    down_near, down = row_terms(after(hidden, two_out), w_down)
    grad_normed_two = after(grad_normed_two, down) + two_far

    grad_mid_norm, gain_two = norm_back(grad_normed_two, middle, scale_two, norm2_gain)
    grad_middle = own(cotangent).astype(jnp.float32) + grad_mid_norm
    branch_grad = grad_middle.astype(LOW)
    grad_far = flip(branch_grad, "tp", 2)

    down_near = flip(after(down_near, branch_grad), "tp", 1)
    gate_terms = weight_terms(
        table,
        "mine",
        "natural",
        0,
        half_count,
        after(normed_two, branch_grad),
        two_theirs,
        grad_gate_pre,
        gate_theirs,
        keep=False,
    )
    grad_gate = parity_sum(gate_terms, 0)
    grad_pair = jnp.concatenate([after(branch_grad, gate_terms), grad_far], 0)
    grad_core = flip(grad_pair, "tp", 1)
    branch_send = pick_columns(table, "theirs", grad_pair)
    att_theirs = flip(after(attended, branch_send), "dp", 1)

    def near_flip(terms, bit):
        half = terms.shape[0] // 2
        return [flip(terms[half:], "dp", 1 << bit), flip(terms[:half], "dp", 1 << bit)]

    def down_terms(lo, hi, *late):
        g = after(hidden, *late)
        return weight_terms(table, "down", "natural", lo, hi, cot, cot_theirs, g, hidden_theirs)

    down_sent = down_terms(half_count // 2, half_count, branch_send)
    half = down_sent.shape[0] // 2
    down_first = flip(down_sent[half:], "dp", 1)
    branch_all = jnp.concatenate([after(grad_pair, down_sent), grad_core], 0)
    grad_attended = dot(w_out, branch_all, 1, 1).astype(LOW)
    grads = attention_backward(
        at, pos, queries, grad_attended, attended, lse, cosine, sine, blocks, size, 2
    )
    grad_query_rows, kv_total = grads[0], grads[1]
    *kv_sends, att_theirs = lax.optimization_barrier((*grads[2:], att_theirs))
    kv_back = [flip(kv_sends[m - 1], "dp", m) for m in range(1, SPAN)]

    def rest_terms(lo, hi, x, x_far, g, g_far, transposed=False):
        return weight_terms(
            table, "rest", "rest_block", lo, hi, x, x_far, g, g_far, transposed
        )

    down = down + after(down_near, grad_query_rows)
    down, down_out = down[:own_rows], down[own_rows:].astype(LOW)
    down_far = flip(down_out, "tp", 2)

    def up_terms(lo, hi, *late):
        return rest_terms(lo, hi, normed_two, two_theirs, after(grad_up_pre, *late), up_theirs)

    up_sent = up_terms(half_count // 2, half_count, grad_query_rows)
    up_first = flip(up_sent[half:], "dp", 2)

    def exchange_mid(terms, first, order, *late):
        got, left = [first], half_count // 2
        for b in order[1:]:
            send = terms(left // 2, left, *late).astype(jnp.float32)
            rows = send.shape[0]
            for other in got:
                send = send + other[other.shape[0] - rows :]
            send = send.astype(LOW)
            got.append(flip(send, "dp", 1 << b))
            left //= 2
        return got[1:], send

    down_late, down_last = exchange_mid(down_terms, down_first, down_bits, grad_query_rows)
    kv_total, grad_gate = lax.optimization_barrier(
        (kv_total, grad_gate, up_sent, down_out, down_last)
    )[:2]
    for back in kv_back:
        kv_total = kv_total + back
    key_grad = turn_back(kv_total[:size], cosine, sine)
    grad_kv_rows = jnp.concatenate([key_grad, kv_total[size:]], 0).astype(LOW)
    proj_rows = jnp.concatenate([grad_query_rows, grad_kv_rows], 0)
    proj_theirs = flip(proj_rows, "dp", 1)
    branch_near = flip(after(branch_send, proj_rows), "dp", 1)

    own_order = jnp.concatenate(
        [take(proj_rows, start, own_rows, 1) for start in row_starts], 1
    )

    def one_terms(lo, hi):
        cut = own_order[:, lo * own_rows : hi * own_rows]
        return dot(cut[:wide], w_query, 0, 1) + dot(cut[wide:], w_kv, 0, 0)

    grad_normed_one, one_out = near_sum(one_terms)
    one_far = flip(one_out, "tp", 2)
    output_rows = (middle + (down + after(down_far, one_out))).astype(LOW)
    one_theirs = join_rows(table, after(one_near, one_out), cores_far[:, width // 2 :])
    up_kept = up_terms(0, 1, one_out)
    grad_gate = grad_gate.astype(jnp.float32)
    grad_normed_one = after(grad_normed_one, output_rows, up_kept, grad_gate, one_theirs) + one_far
    grad_in_norm, gain_one = norm_back(grad_normed_one, own_inputs, own(scale_one), norm1_gain)
    input_rows = grad_middle + grad_in_norm

    up_late, up_last = exchange_mid(up_terms, up_first, rest_bits, input_rows)
    branch_near, down_second = lax.optimization_barrier((branch_near, down_sent[:half], up_last))[:2]
    branch_theirs = jnp.concatenate([branch_near, flip(branch_near, "tp", 1)], 0)
    down_second = flip(down_second, "dp", 1)
    gain_one, *down_late = lax.optimization_barrier((gain_one, *down_late, up_last))[:-1]
    gains = jnp.stack([gain_one, gain_two])
    for m in (1, 2):
        gains = gains + flip(gains, "tp", m)
    gains = pick_columns(table, "rest", gains) + flip(
        pick_columns(table, "rest_far", gains), "dp", 1
    )

    out_late, proj_late = lax.optimization_barrier((attended, proj_rows, up_last))[:2]

    def last_terms(lo, hi, *late):
        first, second = after(proj_late, *late), after(out_late, *late)
        return jnp.concatenate(
            [
                rest_terms(lo, hi, normed_one, one_theirs, first, proj_theirs, True),
                rest_terms(lo, hi, branch_all, branch_theirs, second, att_theirs, True),
            ],
            1,
        )

    def with_gains(terms, lo, hi, *others):
        extra = gains[:, lo * block : hi * block]
        for other, other_gains in others:
            terms = terms.astype(jnp.float32) + other
            extra = extra + other_gains
        columns = terms.shape[1]
        extra = jnp.pad(extra, ((0, 14), (0, -extra.shape[1] % columns)))[:, :columns]
        return jnp.concatenate([terms.astype(LOW), extra.astype(LOW)], 0)

    def split(message, count):
        rows = count * block
        return message[:rows], message[rows : rows + 2, :rows]

    quarter = half_count // 4
    sent = last_terms(half_count // 2, half_count)
    cut = quarter * block
    firsts = with_gains(sent[cut:], 3 * quarter, half_count)
    seconds = with_gains(sent[:cut], 2 * quarter, 3 * quarter)
    mids = [split(flip(firsts, "dp", 2), quarter)]
    last_second = split(flip(after(seconds, firsts), "dp", 2), quarter)
    proj_kept = rest_terms(0, 1, normed_one, one_theirs, after(proj_late, firsts), proj_theirs, True)
    out_kept = rest_terms(0, 1, branch_all, branch_theirs, after(out_late, firsts), att_theirs, True)
    down_kept = down_terms(0, 1, firsts)
    left = half_count // 2
    for b in rest_bits[1:]:
        count = left // 2
        terms = last_terms(count, left, firsts)
        terms, *up_late = lax.optimization_barrier((terms, *up_late, proj_kept, out_kept, down_kept))[
            :-3
        ]
        send = with_gains(
            terms, count, left, *((o[-count * block :], g[:, -count * block :]) for o, g in mids)
        )
        mids.append(split(flip(send, "dp", 1 << b), count))
        left = count
    up_second = flip(after(up_sent[:half], send), "dp", 2)

    def ending(kept, *others):
        kept = kept.astype(jnp.float32)
        for other in others:
            kept = kept + other[:block]
        return kept

    down_kept, down_second = lax.optimization_barrier((down_kept, down_second, send))[:2]
    grad_down = ending(down_kept, down_second, *down_late)
    grad_last = ending(
        jnp.concatenate([proj_kept, out_kept], 1), last_second[0], *(m[0] for m in mids[1:])
    )
    gains = gains[:, :block] + last_second[1][:, :block]
    for _, other in mids[1:]:
        gains = gains + other[:, :block]
    grad_up = ending(up_kept, up_second, *up_late)
    narrow = wide + 2 * size

    return (
        output_rows,
        input_rows,
        gains[0],
        grad_last[:, :wide],
        grad_last[:, wide : wide + size],
        grad_last[:, wide + size : narrow],
        grad_last[:, narrow:].T,
        gains[1],
        grad_gate,
        grad_up,
        grad_down.T,
    )


def solution(mesh):
    placed = (
        P("dp", None),
        P("dp"),
        P(),
        P(None, "tp"),
        P(None, "tp"),
        P(None, "tp"),
        P("tp", None),
        P(),
        P(None, "tp"),
        P(None, "tp"),
        P("tp", None),
        P("dp", None),
    )
    return jax.shard_map(
        shards,
        mesh=mesh,
        in_specs=placed,
        out_specs=(
            P(("dp", "tp"), None),
            P(("dp", "tp"), None),
            P("dp"),
            P("dp", "tp"),
            P("dp", "tp"),
            P("dp", "tp"),
            P("tp", "dp"),
            P("dp"),
            P("dp", "tp"),
            P("dp", "tp"),
            P("tp", "dp"),
        ),
        check_vma=False,
    )
```

```python
import functools

import jax
import jax.numpy as jnp
import numpy as np
from jax import lax
from jax.experimental import pallas as pl
from jax.experimental.pallas import tpu as pltpu
from jax.sharding import PartitionSpec as P

SPAN = 4
EPSILON = 1e-05
FAR_BELOW = -1e30
LOW = jnp.bfloat16
ROW_MASKS = (0, 2, 1, 3)


def flip(block, axis, mask):
    return lax.ppermute(block, axis, [(i, i ^ mask) for i in range(lax.axis_size(axis))])


def dot(left, right, left_dim, right_dim):
    return lax.dot_general(
        left,
        right,
        (((left_dim,), (right_dim,)), ((), ())),
        preferred_element_type=jnp.float32,
    )


def in_hbm(*arrays):
    return [pltpu.with_memory_space_constraint(a, pltpu.HBM) for a in arrays]


def own_mask(pos, begin, keys, queries):
    key_at = lax.broadcasted_iota(jnp.int32, (keys, queries), 0)
    query_at = lax.broadcasted_iota(jnp.int32, (keys, queries), 1) + begin
    return (key_at <= query_at) & (key_at >= query_at - pos)


def row_starts(spot, rows):
    part = rows // len(ROW_MASKS)
    return [pl.multiple_of((spot ^ m) * part, part) for m in ROW_MASKS]


def forward_kernel(
    heads,
    size,
    at_ref,
    pos_ref,
    q_ref,
    kv0,
    kv1,
    kv2,
    kv3,
    o_ref,
    lse_ref,
    keys,
    vals,
    top,
    acc,
    ordered,
):
    rank, spot = at_ref[0], at_ref[1]
    rows = pos_ref.shape[1]
    half = rows // 2

    @pl.when(pl.program_id(0) == 0)
    def _():
        for m, kv in enumerate((kv0, kv1, kv2, kv3)):
            keys[m] = kv[:size, :].T
            vals[m, :size, :] = kv[size:, :]
            vals[m, size:, :] = jnp.ones((16, rows), LOW)

    pos = pos_ref[...]
    for part in range(2):
        cols = slice(part * half, (part + 1) * half)
        count = (part + 1) * half
        mask = own_mask(pos[:, cols], part * half, count, half)
        for h in range(heads):
            scores = dot(keys[0, :count, :], q_ref[h * size : (h + 1) * size, cols], 1, 0)
            scores = jnp.where(mask, scores, FAR_BELOW)
            peak = jnp.max(scores, 0, keepdims=True)
            weights = jnp.exp(scores - peak).astype(LOW)
            acc[h, :, cols] = dot(vals[0, :, :count], weights, 1, 0)
            top[h, :, cols] = peak
    seen = pos > lax.broadcasted_iota(jnp.int32, (1, rows), 1)
    for m in range(1, SPAN):

        @pl.when((rank ^ m) < rank)
        def _():
            for h in range(heads):
                scores = dot(keys[m], q_ref[h * size : (h + 1) * size, :], 1, 0)
                old = top[h]
                peak = jnp.where(seen, jnp.maximum(old, jnp.max(scores, 0, keepdims=True)), old)
                weights = jnp.exp(scores - jnp.where(seen, peak, -FAR_BELOW)).astype(LOW)
                acc[h] = acc[h] * jnp.exp(old - peak) + dot(vals[m], weights, 1, 0)
                top[h] = peak

    for h in range(heads):
        total = acc[h, size : size + 1, :]
        ordered[h * size : (h + 1) * size, :] = (acc[h, :size, :] / total).astype(LOW)
        lse_ref[h] = top[h] + jnp.log(total)
    for j, start in enumerate(row_starts(spot, rows)):
        part = rows // len(ROW_MASKS)
        o_ref[:, j * part : (j + 1) * part] = ordered[:, pl.ds(start, part)]


def backward_kernel(
    heads,
    size,
    at_ref,
    pos_ref,
    q_ref,
    do_in,
    o_in,
    lse_ref,
    cos_ref,
    sin_ref,
    kv0,
    kv1,
    kv2,
    kv3,
    dq_ref,
    g0,
    g1,
    g2,
    g3,
    keys,
    vals,
    dq,
    total,
    do_ref,
    o_ref,
):
    rank, spot = at_ref[0], at_ref[1]
    rows = pos_ref.shape[1]
    half = rows // 2
    blocks = (kv0, kv1, kv2, kv3)
    step = pl.program_id(0)

    @pl.when(step == 0)
    def _():
        for m, kv in enumerate(blocks):
            keys[m] = kv[:size, :].T
            vals[m] = kv[size:, :].T
        total[...] = jnp.zeros_like(total)

    part = rows // len(ROW_MASKS)
    for j, start in enumerate(row_starts(spot, rows)):
        do_ref[:, pl.ds(start, part)] = do_in[:, j * part : (j + 1) * part]
        o_ref[:, pl.ds(start, part)] = o_in[:, j * part : (j + 1) * part]
    pos = pos_ref[...]
    seen = pos > lax.broadcasted_iota(jnp.int32, (1, rows), 1)
    deltas = []
    for h in range(heads):
        span = slice(h * size, (h + 1) * size)
        deltas.append(
            jnp.sum(
                do_ref[span, :].astype(jnp.float32) * o_ref[span, :].astype(jnp.float32),
                0,
                keepdims=True,
            )
        )
    for part in range(2):
        cols = slice(part * half, (part + 1) * half)
        count = (part + 1) * half
        mask = own_mask(pos[:, cols], part * half, count, half)
        for h in range(heads):
            span = slice(h * size, (h + 1) * size)
            query, grad = q_ref[span, cols], do_ref[span, cols]
            scores = dot(keys[0, :count, :], query, 1, 0)
            probs = jnp.exp(jnp.where(mask, scores, FAR_BELOW) - lse_ref[h, :, cols])
            grad_probs = dot(vals[0, :count, :], grad, 1, 0)
            grad_scores = (probs * (grad_probs - deltas[h][:, cols])).astype(LOW)
            total[0, :size, :count] += dot(query, grad_scores, 1, 1)
            total[0, size:, :count] += dot(grad, probs.astype(LOW), 1, 1)
            dq[h, :, cols] = dot(kv0[:size, :count], grad_scores, 1, 0)
    for m in range(1, SPAN):

        @pl.when((rank ^ m) < rank)
        def _():
            for h in range(heads):
                span = slice(h * size, (h + 1) * size)
                query, grad = q_ref[span, :], do_ref[span, :]
                scores = dot(keys[m], query, 1, 0)
                probs = jnp.exp(scores - jnp.where(seen, lse_ref[h], -FAR_BELOW))
                grad_probs = dot(vals[m], grad, 1, 0)
                grad_scores = (probs * (grad_probs - deltas[h])).astype(LOW)
                total[m, :size, :] += dot(query, grad_scores, 1, 1)
                total[m, size:, :] += dot(grad, probs.astype(LOW), 1, 1)
                dq[h] += dot(blocks[m][:size, :], grad_scores, 1, 0)

    middle_at = size // 2
    cosine, sine = cos_ref[...], sin_ref[...]
    for h in range(heads):
        first = dq[h, :middle_at, :] * size ** (-0.5)
        second = dq[h, middle_at:, :] * size ** (-0.5)
        base = h * size
        dq_ref[base : base + middle_at, :] = (first * cosine + second * sine).astype(LOW)
        dq_ref[base + middle_at : base + size, :] = (second * cosine - first * sine).astype(LOW)

    @pl.when(step == pl.num_programs(0) - 1)
    def _():
        g0[...] = total[0]
        for m, out in ((1, g1), (2, g2), (3, g3)):
            out[...] = total[m].astype(LOW)


def attention_forward(at, pos, queries, blocks, size, heads):
    wide, rows = queries.shape
    count = wide // size
    whole = pl.BlockSpec((2 * size, rows), lambda i, r: (0, 0))
    some = pl.BlockSpec((heads * size, rows), lambda i, r: (i, 0))
    return pl.pallas_call(
        functools.partial(forward_kernel, heads, size),
        out_shape=(
            jax.ShapeDtypeStruct((wide, rows), LOW),
            jax.ShapeDtypeStruct((count, 1, rows), jnp.float32),
        ),
        grid_spec=pltpu.PrefetchScalarGridSpec(
            num_scalar_prefetch=1,
            grid=(count // heads,),
            in_specs=[pl.BlockSpec((1, rows), lambda i, r: (0, 0)), some] + [whole] * SPAN,
            out_specs=[some, pl.BlockSpec((heads, 1, rows), lambda i, r: (i, 0, 0))],
            scratch_shapes=[
                pltpu.VMEM((SPAN, rows, size), LOW),
                pltpu.VMEM((SPAN, size + 16, rows), LOW),
                pltpu.VMEM((heads, 1, rows), jnp.float32),
                pltpu.VMEM((heads, size + 16, rows), jnp.float32),
                pltpu.VMEM((heads * size, rows), LOW),
            ],
        ),
        compiler_params=pltpu.CompilerParams(vmem_limit_bytes=24 << 20),
        cost_estimate=pl.CostEstimate(
            flops=32 * wide * rows * rows * SPAN,
            bytes_accessed=4 * wide * rows,
            transcendentals=0,
        ),
        name="attention_forward",
    )(at, pos, queries, *blocks)


def attention_backward(at, pos, queries, grads, attended, lse, cosine, sine, blocks, size, heads):
    wide, rows = queries.shape
    count = wide // size
    whole = pl.BlockSpec((2 * size, rows), lambda i, r: (0, 0))
    table = pl.BlockSpec((size // 2, rows), lambda i, r: (0, 0))
    some = pl.BlockSpec((heads * size, rows), lambda i, r: (i, 0))
    return pl.pallas_call(
        functools.partial(backward_kernel, heads, size),
        out_shape=(
            jax.ShapeDtypeStruct((wide, rows), LOW),
            jax.ShapeDtypeStruct((2 * size, rows), jnp.float32),
        )
        + (jax.ShapeDtypeStruct((2 * size, rows), LOW),) * (SPAN - 1),
        grid_spec=pltpu.PrefetchScalarGridSpec(
            num_scalar_prefetch=1,
            grid=(count // heads,),
            in_specs=[
                pl.BlockSpec((1, rows), lambda i, r: (0, 0)),
                some,
                some,
                some,
                pl.BlockSpec((heads, 1, rows), lambda i, r: (i, 0, 0)),
                table,
                table,
            ]
            + [whole] * SPAN,
            out_specs=[some] + [whole] * SPAN,
            scratch_shapes=[
                pltpu.VMEM((SPAN, rows, size), LOW),
                pltpu.VMEM((SPAN, rows, size), LOW),
                pltpu.VMEM((heads, size, rows), jnp.float32),
                pltpu.VMEM((SPAN, 2 * size, rows), jnp.float32),
                pltpu.VMEM((heads * size, rows), LOW),
                pltpu.VMEM((heads * size, rows), LOW),
            ],
        ),
        compiler_params=pltpu.CompilerParams(vmem_limit_bytes=24 << 20),
        cost_estimate=pl.CostEstimate(
            flops=48 * wide * rows * rows * SPAN,
            bytes_accessed=10 * wide * rows,
            transcendentals=0,
        ),
        name="attention_backward",
    )(at, pos, *in_hbm(queries, grads, attended, lse, cosine, sine, *blocks))


def take(values, start, size, dim):
    starts = [np.uint32(0)] * values.ndim
    starts[dim] = start
    sizes = list(values.shape)
    sizes[dim] = size
    return lax.dynamic_slice(values, starts, sizes)


def pick(values, places, blocks, dim):
    size = values.shape[dim] // blocks
    return jnp.concatenate(
        [lax.dynamic_slice_in_dim(values, p * size, size, dim) for p in places], dim
    )


class Table:
    def __init__(self, **parts):
        self.begin, at = {}, 0
        for name, part in parts.items():
            self.begin[name] = at
            at += part.shape[0]
        self.values = jnp.concatenate([p.astype(jnp.int32) for p in parts.values()])

    def list(self, name, lo, hi):
        return [self.values[self.begin[name] + j] for j in range(lo, hi)]


def after(value, *others):
    return lax.optimization_barrier((value, *others))[0]


def parity_sum(terms, dim):
    count = lax.axis_size("dp")
    groups = [list(range(p, count, 2)) for p in range(2)]
    return lax.psum_scatter(
        terms.astype(LOW), "dp", scatter_dimension=dim, axis_index_groups=groups, tiled=True
    )


def terms_kernel(transposed, places, x, x_far, g, g_far, out):
    del places
    side = 1 if transposed else 0
    out[...] = (dot(x[...], g[...], 0, side) + dot(x_far[...], g_far[...], 0, side)).astype(LOW)


def weight_terms(table, name, far, lo, hi, x, x_far, g, g_far, transposed=False, keep=True):
    count = hi - lo
    size = x.shape[1] // lax.axis_size("dp")
    rows = x.shape[0]
    units = g.shape[0] if transposed else g.shape[1]
    if size % 128:
        side = 1 if transposed else 0
        mine = pick(x, table.list(name, lo, hi), x.shape[1] // size, 1)
        theirs = pick(x_far, table.list(far, lo, hi), x_far.shape[1] // size, 1)
        return (dot(mine, g, 0, side) + dot(theirs, g_far, 0, side)).astype(LOW)
    whole = pl.BlockSpec(g.shape, lambda i, p: (0, 0))
    begin, far_begin = table.begin[name] + lo, table.begin[far] + lo
    return pl.pallas_call(
        functools.partial(terms_kernel, transposed),
        out_shape=(jax.ShapeDtypeStruct if keep else pltpu.HBM)((count * size, units), LOW),
        grid_spec=pltpu.PrefetchScalarGridSpec(
            num_scalar_prefetch=1,
            grid=(count,),
            in_specs=[
                pl.BlockSpec((rows, size), lambda i, p: (0, p[begin + i])),
                pl.BlockSpec((rows, size), lambda i, p: (0, p[far_begin + i])),
                whole,
                whole,
            ],
            out_specs=pl.BlockSpec((size, units), lambda i, p: (i, 0)),
        ),
        compiler_params=pltpu.CompilerParams(vmem_limit_bytes=20 << 20),
        cost_estimate=pl.CostEstimate(
            flops=24 * rows * count * size * units, bytes_accessed=4 * rows * units, transcendentals=0
        ),
        name="weight_terms",
    )(table.values, x, x_far, g, g_far)


def copy_kernel(places, source, target):
    del places
    target[...] = source[...]


def pick_columns(table, name, values, part=None, parts=1):
    blocks = lax.axis_size("dp")
    rows, count = values.shape[0] // parts, blocks // 2
    size = values.shape[1] // blocks
    if size % 128:
        if part is not None:
            values = lax.dynamic_slice_in_dim(values, table.list(part, 0, 1)[0] * rows, rows, 0)
        return pick(values, table.list(name, 0, count), blocks, 1)
    begin = table.begin[name]
    row = 0 if part is None else table.begin[part]
    return pl.pallas_call(
        copy_kernel,
        out_shape=jax.ShapeDtypeStruct((rows, count * size), values.dtype),
        grid_spec=pltpu.PrefetchScalarGridSpec(
            num_scalar_prefetch=1,
            grid=(count,),
            in_specs=[
                pl.BlockSpec(
                    (rows, size), lambda i, p: (0 if part is None else p[row], p[begin + i])
                )
            ],
            out_specs=pl.BlockSpec((rows, size), lambda i, p: (0, i)),
        ),
        compiler_params=pltpu.CompilerParams(vmem_limit_bytes=8 << 20),
        cost_estimate=pl.CostEstimate(
            flops=65536 * rows * count * size, bytes_accessed=4 * rows * count * size, transcendentals=0
        ),
        name="pick_columns",
    )(table.values, values)


def load_kernel(*refs):
    *pairs, sems = refs
    half = len(pairs) // 2
    copies = [
        pltpu.make_async_copy(source, target, sems.at[j])
        for j, (source, target) in enumerate(zip(pairs[:half], pairs[half:]))
    ]
    for copy in copies:
        copy.start()
    for copy in copies:
        copy.wait()


def load_weights(*weights):
    return pl.pallas_call(
        load_kernel,
        out_shape=tuple(pltpu.VMEM(w.shape, w.dtype) for w in weights),
        in_specs=[pl.BlockSpec(memory_space=pl.ANY)] * len(weights),
        out_specs=[pl.BlockSpec(memory_space=pltpu.VMEM)] * len(weights),
        scratch_shapes=[pltpu.SemaphoreType.DMA((len(weights),))],
        compiler_params=pltpu.CompilerParams(vmem_limit_bytes=2 << 20),
        cost_estimate=pl.CostEstimate(
            flops=20_000_000_000,
            bytes_accessed=2 * sum(w.size for w in weights),
            transcendentals=0,
        ),
        name="load_weights",
    )(*in_hbm(*weights))


def in_vmem(*arrays):
    return [pltpu.with_memory_space_constraint(a, pltpu.VMEM) for a in arrays]


def ffn_kernel(rows, gate_w, up_w, grad_in, hidden, grad_gate, grad_up):
    step = 128
    for begin in range(0, hidden.shape[1], step):
        cut = slice(begin, begin + step)
        both = dot(rows[...], jnp.concatenate([gate_w[:, cut], up_w[:, cut]], 1), 1, 0)
        gate, up = both[:, :step], both[:, step:]
        grad = grad_in[:, cut]
        sigma = jax.nn.sigmoid(gate)
        active = gate * sigma
        hidden[:, cut] = (active * up).astype(LOW)
        grad_gate[:, cut] = (grad * up * sigma * (1.0 + gate * (1.0 - sigma))).astype(LOW)
        grad_up[:, cut] = (grad * active).astype(LOW)


def feed_forward(rows, w_gate, w_up, grad_hidden):
    count, width = rows.shape
    units = w_gate.shape[1]
    here = pl.BlockSpec(memory_space=pltpu.VMEM)
    return pl.pallas_call(
        ffn_kernel,
        out_shape=(jax.ShapeDtypeStruct((count, units), LOW),) * 3,
        in_specs=[here] * 4,
        out_specs=[here] * 3,
        compiler_params=pltpu.CompilerParams(vmem_limit_bytes=20 << 20),
        cost_estimate=pl.CostEstimate(
            flops=6 * count * width * units,
            bytes_accessed=4 * width * units,
            transcendentals=count * units,
        ),
        name="feed_forward",
    )(*in_vmem(rows, w_gate, w_up, grad_hidden))


def back_kernel(gate_rows, up_rows, gate_w, up_w, out):
    step = out.shape[1]
    cut = pl.ds(pl.multiple_of(pl.program_id(0) * step, step), step)
    total = dot(gate_rows[...], gate_w[cut, :], 1, 1) + dot(up_rows[...], up_w[cut, :], 1, 1)
    out[...] = total.astype(out.dtype)


def feed_forward_back(grad_gate, grad_up, w_gate, w_up, half, kind):
    count, units = grad_gate.shape
    width = w_gate.shape[0]
    step = width // 2
    rows = pl.BlockSpec((count // 2, units), lambda i: (half, 0))
    here = pl.BlockSpec(memory_space=pltpu.VMEM)
    return pl.pallas_call(
        back_kernel,
        out_shape=jax.ShapeDtypeStruct((count // 2, width), kind),
        grid=(2,),
        in_specs=[rows, rows, here, here],
        out_specs=pl.BlockSpec((count // 2, step), lambda i: (0, i)),
        compiler_params=pltpu.CompilerParams(vmem_limit_bytes=16 << 20),
        cost_estimate=pl.CostEstimate(
            flops=10 * count * width * units, bytes_accessed=4 * width * units, transcendentals=0
        ),
        name="feed_forward_back",
    )(grad_gate, grad_up, *in_vmem(w_gate, w_up))


def join_kernel(places, first, second, out):
    del places

    @pl.when(pl.program_id(0) == 0)
    def _():
        out[...] = first[...]

    @pl.when(pl.program_id(0) == 1)
    def _():
        out[...] = second[...]


def join_rows(table, first, second):
    rows, width = first.shape
    core = table.begin["core"]
    whole = pl.BlockSpec((rows, width), lambda i, p: (0, 0))
    return pl.pallas_call(
        join_kernel,
        out_shape=jax.ShapeDtypeStruct((2 * rows, width), first.dtype),
        grid_spec=pltpu.PrefetchScalarGridSpec(
            num_scalar_prefetch=1,
            grid=(2,),
            in_specs=[whole, whole],
            out_specs=pl.BlockSpec((rows, width), lambda i, p: (p[core] ^ i, 0)),
        ),
        compiler_params=pltpu.CompilerParams(vmem_limit_bytes=8 << 20),
        cost_estimate=pl.CostEstimate(
            flops=1_000_000_000, bytes_accessed=8 * rows * width, transcendentals=0
        ),
        name="join_rows",
    )(table.values, first, second)


def row_kernel(left, right, send, kept):
    half = left.shape[0] // 2
    send[...] = dot(left[half:, :], right[...], 1, 0).astype(LOW)
    kept[...] = dot(left[:half, :], right[...], 1, 0)


def row_terms(left, right):
    rows, units = left.shape
    half, width = rows // 2, right.shape[1]
    step = 256
    return pl.pallas_call(
        row_kernel,
        out_shape=(
            jax.ShapeDtypeStruct((half, width), LOW),
            jax.ShapeDtypeStruct((half, width), jnp.float32),
        ),
        grid=(width // step,),
        in_specs=[
            pl.BlockSpec((rows, units), lambda i: (0, 0)),
            pl.BlockSpec((units, step), lambda i: (0, i)),
        ],
        out_specs=[pl.BlockSpec((half, step), lambda i: (0, i))] * 2,
        compiler_params=pltpu.CompilerParams(vmem_limit_bytes=16 << 20),
        cost_estimate=pl.CostEstimate(
            flops=8 * rows * units * width, bytes_accessed=2 * units * width, transcendentals=0
        ),
        name="row_terms",
    )(left, right)


def turn(values, cosine, sine):
    half = cosine.shape[0]
    heads = values.shape[0] // (2 * half)
    pieces = values.reshape(heads, 2, half, values.shape[1])
    first, second = pieces[:, 0], pieces[:, 1]
    return jnp.stack(
        [first * cosine - second * sine, second * cosine + first * sine], 1
    ).reshape(values.shape)


def turn_back(grads, cosine, sine):
    return turn(grads, cosine, -sine)


def norm_back(grad_rows, values, scale_rows, gain):
    scaled = grad_rows * gain
    inner_mean = jnp.mean(scaled * values, -1, keepdims=True)
    return (
        scale_rows * (scaled - values * scale_rows * scale_rows * inner_mean),
        jnp.sum(grad_rows * values * scale_rows, 0),
    )


def shards(
    tokens,
    positions,
    norm1_gain,
    w_query,
    w_key,
    w_value,
    w_out,
    norm2_gain,
    w_gate,
    w_up,
    w_down,
    cotangent,
):
    rows_here, width = tokens.shape
    size = w_key.shape[1]
    dp = lax.axis_size("dp")
    tp_count = len(ROW_MASKS)
    own_rows = rows_here // tp_count
    block = width // dp
    bits = dp.bit_length() - 1
    half_count = dp // 2

    def exchange_order(order):
        return np.array(
            [
                sum(((j >> (len(order) - 1 - k)) & 1) << b for k, b in enumerate(order))
                for j in range(1 << len(order))
            ],
            np.int32,
        )

    down_bits = [0] + list(range(2, bits))
    rest_bits = list(range(1, bits))

    place = lax.axis_index("dp").astype(jnp.int32)
    spot = lax.axis_index("tp").astype(jnp.int32)
    natural = np.arange(half_count, dtype=np.int32)
    down_here, rest_here = place ^ exchange_order(down_bits), place ^ exchange_order(rest_bits)
    table = Table(
        mine=2 * natural + (place & 1),
        theirs=2 * natural + (1 - (place & 1)),
        natural=jnp.asarray(natural),
        down=down_here,
        down_far=down_here ^ 2,
        rest=rest_here,
        rest_far=rest_here ^ 1,
        rest_block=rest_here >> 1,
        core=(spot & 1)[None],
    )
    at = jnp.stack([place & (SPAN - 1), spot])
    row_starts = [((spot ^ m) * own_rows).astype(jnp.uint32) for m in ROW_MASKS]
    core_starts = [(c * (rows_here // 2)).astype(jnp.uint32) for c in (spot & 1, 1 - (spot & 1))]
    tokens, table.values, at, row_starts, core_starts = lax.optimization_barrier(
        (tokens, table.values, at, row_starts, core_starts)
    )
    pos = positions.reshape(1, rows_here)

    def own(values):
        return take(values, row_starts[0], own_rows, 0)

    inputs = tokens.astype(jnp.float32)
    scale_one = lax.rsqrt(jnp.mean(inputs * inputs, -1, keepdims=True) + EPSILON)
    normed_one = (inputs * scale_one * norm1_gain).astype(LOW)
    half = size // 2
    frequency = jnp.exp(
        -jnp.log(10000.0) * (2.0 * jnp.arange(half, dtype=jnp.float32) / size)
    )
    angles = frequency[:, None] * positions.astype(jnp.float32)[None, :]
    cosine, sine = jnp.cos(angles), jnp.sin(angles)
    w_kv = jnp.concatenate([w_key.T, w_value.T], 0)
    paired = dot(w_kv, normed_one, 1, 1)
    paired = jnp.concatenate([turn(paired[:size], cosine, sine), paired[size:]], 0).astype(LOW)
    blocks = [paired] + [flip(paired, "dp", m) for m in range(1, SPAN)]
    queries = (turn(dot(w_query, normed_one, 0, 1), cosine, sine) * size ** (-0.5)).astype(LOW)

    wide = w_query.shape[1]

    def near_sum(part):
        send = part(2, 4).astype(LOW)
        near, kept = lax.optimization_barrier((flip(send, "tp", 1), part(0, 2)))
        pair = kept + near
        return pair[:own_rows], pair[own_rows:].astype(LOW)

    attended, lse = attention_forward(at, pos, queries, blocks, size, 8)

    branch, branch_out = near_sum(
        lambda lo, hi: dot(attended[:, lo * own_rows : hi * own_rows], w_out, 0, 0)
    )
    branch_far = flip(branch_out, "tp", 2)
    cot = jnp.concatenate(
        [take(after(cotangent, branch_out), start, own_rows, 0) for start in row_starts], 0
    )
    cot_send = pick_columns(table, "down_far", cot)
    cot_theirs = flip(cot_send, "dp", 2)
    own_inputs = own(tokens).astype(jnp.float32)
    one_send = pick_columns(table, "theirs", after(normed_one, cot_send), "core", 2)
    one_near = flip(one_send, "dp", 1)
    grad_hidden = dot(after(cot, one_send), w_down, 1, 1)
    middle = own_inputs + (after(branch, grad_hidden) + branch_far)

    scale_two = lax.rsqrt(jnp.mean(middle * middle, -1, keepdims=True) + EPSILON)
    own_two = (middle * scale_two * norm2_gain).astype(LOW)
    far_two = flip(own_two, "tp", 2)
    gate_w, up_w = load_weights(after(w_gate, own_two), w_up)
    pair_two = jnp.concatenate([after(own_two, gate_w), far_two], 0)
    core_two = flip(pair_two, "tp", 1)
    two_send = pick_columns(table, "theirs", pair_two)
    two_near = flip(two_send, "dp", 1)
    normed_two = jnp.concatenate([after(pair_two, two_send), core_two], 0)

    hidden, grad_gate_pre, grad_up_pre = feed_forward(normed_two, gate_w, up_w, grad_hidden)
    gate_theirs = flip(grad_gate_pre, "dp", 1)
    hidden_theirs = flip(hidden, "dp", 2)
    up_theirs = flip(grad_up_pre, "dp", 1)
    gate_late, cot_theirs, one_near = lax.optimization_barrier((grad_gate_pre, cot_theirs, one_near))

    two_back = functools.partial(feed_forward_back, gate_late, grad_up_pre, gate_w, up_w)
    grad_normed_two, two_out = near_sum(
        lambda lo, hi: two_back(lo // 2, jnp.float32 if lo == 0 else LOW)
    )
    two_out, two_near = lax.optimization_barrier((two_out, two_near))
    two_far = flip(two_out, "tp", 2)
    cores = jnp.concatenate([two_near, one_near], 1)
    cores_far = flip(cores, "tp", 1)
    two_theirs = jnp.concatenate([two_near, cores_far[:, : width // 2]], 0)

    down_near, down = row_terms(after(hidden, two_out), w_down)
    grad_normed_two = after(grad_normed_two, down) + two_far

    grad_mid_norm, gain_two = norm_back(grad_normed_two, middle, scale_two, norm2_gain)
    grad_middle = own(cotangent).astype(jnp.float32) + grad_mid_norm
    branch_grad = grad_middle.astype(LOW)
    grad_far = flip(branch_grad, "tp", 2)

    down_near = flip(after(down_near, branch_grad), "tp", 1)
    gate_terms = weight_terms(
        table,
        "mine",
        "natural",
        0,
        half_count,
        after(normed_two, branch_grad),
        two_theirs,
        grad_gate_pre,
        gate_theirs,
        keep=False,
    )
    grad_gate = parity_sum(gate_terms, 0)
    grad_pair = jnp.concatenate([after(branch_grad, gate_terms), grad_far], 0)
    grad_core = flip(grad_pair, "tp", 1)
    branch_send = pick_columns(table, "theirs", grad_pair)
    att_theirs = flip(after(attended, branch_send), "dp", 1)

    def near_flip(terms, bit):
        half = terms.shape[0] // 2
        return [flip(terms[half:], "dp", 1 << bit), flip(terms[:half], "dp", 1 << bit)]

    def down_terms(lo, hi, *late):
        g = after(hidden, *late)
        return weight_terms(table, "down", "natural", lo, hi, cot, cot_theirs, g, hidden_theirs)

    down_sent = down_terms(half_count // 2, half_count, branch_send)
    half = down_sent.shape[0] // 2
    down_first = flip(down_sent[half:], "dp", 1)
    branch_all = jnp.concatenate([after(grad_pair, down_sent), grad_core], 0)
    grad_attended = dot(w_out, branch_all, 1, 1).astype(LOW)
    grads = attention_backward(
        at, pos, queries, grad_attended, attended, lse, cosine, sine, blocks, size, 2
    )
    grad_query_rows, kv_total = grads[0], grads[1]
    *kv_sends, att_theirs = lax.optimization_barrier((*grads[2:], att_theirs))
    kv_back = [flip(kv_sends[m - 1], "dp", m) for m in range(1, SPAN)]

    def rest_terms(lo, hi, x, x_far, g, g_far, transposed=False):
        return weight_terms(
            table, "rest", "rest_block", lo, hi, x, x_far, g, g_far, transposed
        )

    down = down + after(down_near, grad_query_rows)
    down, down_out = down[:own_rows], down[own_rows:].astype(LOW)
    down_far = flip(down_out, "tp", 2)

    def up_terms(lo, hi, *late):
        return rest_terms(lo, hi, normed_two, two_theirs, after(grad_up_pre, *late), up_theirs)

    up_sent = up_terms(half_count // 2, half_count, grad_query_rows)
    up_first = flip(up_sent[half:], "dp", 2)

    def exchange_mid(terms, first, order, *late):
        got, left = [first], half_count // 2
        for b in order[1:]:
            send = terms(left // 2, left, *late).astype(jnp.float32)
            rows = send.shape[0]
            for other in got:
                send = send + other[other.shape[0] - rows :]
            send = send.astype(LOW)
            got.append(flip(send, "dp", 1 << b))
            left //= 2
        return got[1:], send

    down_late, down_last = exchange_mid(down_terms, down_first, down_bits, grad_query_rows)
    kv_total, grad_gate = lax.optimization_barrier(
        (kv_total, grad_gate, up_sent, down_out, down_last)
    )[:2]
    for back in kv_back:
        kv_total = kv_total + back
    key_grad = turn_back(kv_total[:size], cosine, sine)
    grad_kv_rows = jnp.concatenate([key_grad, kv_total[size:]], 0).astype(LOW)
    proj_rows = jnp.concatenate([grad_query_rows, grad_kv_rows], 0)
    proj_theirs = flip(proj_rows, "dp", 1)
    branch_near = flip(after(branch_send, proj_rows), "dp", 1)

    own_order = jnp.concatenate(
        [take(proj_rows, start, own_rows, 1) for start in row_starts], 1
    )

    def one_terms(lo, hi):
        cut = own_order[:, lo * own_rows : hi * own_rows]
        return dot(cut[:wide], w_query, 0, 1) + dot(cut[wide:], w_kv, 0, 0)

    grad_normed_one, one_out = near_sum(one_terms)
    one_far = flip(one_out, "tp", 2)
    output_rows = (middle + (down + after(down_far, one_out))).astype(LOW)
    one_theirs = join_rows(table, after(one_near, one_out), cores_far[:, width // 2 :])
    up_kept = up_terms(0, 1, one_out)
    grad_gate = grad_gate.astype(jnp.float32)
    grad_normed_one = after(grad_normed_one, output_rows, up_kept, grad_gate, one_theirs) + one_far
    grad_in_norm, gain_one = norm_back(grad_normed_one, own_inputs, own(scale_one), norm1_gain)
    input_rows = grad_middle + grad_in_norm

    up_late, up_last = exchange_mid(up_terms, up_first, rest_bits, input_rows)
    branch_near, down_second = lax.optimization_barrier((branch_near, down_sent[:half], up_last))[:2]
    branch_theirs = jnp.concatenate([branch_near, flip(branch_near, "tp", 1)], 0)
    down_second = flip(down_second, "dp", 1)
    gain_one, *down_late = lax.optimization_barrier((gain_one, *down_late, up_last))[:-1]
    gains = jnp.stack([gain_one, gain_two])
    for m in (1, 2):
        gains = gains + flip(gains, "tp", m)
    gains = pick_columns(table, "rest", gains) + flip(
        pick_columns(table, "rest_far", gains), "dp", 1
    )

    out_late, proj_late = lax.optimization_barrier((attended, proj_rows, up_last))[:2]

    def last_terms(lo, hi, *late):
        first, second = after(proj_late, *late), after(out_late, *late)
        return jnp.concatenate(
            [
                rest_terms(lo, hi, normed_one, one_theirs, first, proj_theirs, True),
                rest_terms(lo, hi, branch_all, branch_theirs, second, att_theirs, True),
            ],
            1,
        )

    def with_gains(terms, lo, hi, *others):
        extra = gains[:, lo * block : hi * block]
        for other, other_gains in others:
            terms = terms.astype(jnp.float32) + other
            extra = extra + other_gains
        columns = terms.shape[1]
        extra = jnp.pad(extra, ((0, 14), (0, -extra.shape[1] % columns)))[:, :columns]
        return jnp.concatenate([terms.astype(LOW), extra.astype(LOW)], 0)

    def split(message, count):
        rows = count * block
        return message[:rows], message[rows : rows + 2, :rows]

    quarter = half_count // 4
    sent = last_terms(half_count // 2, half_count)
    cut = quarter * block
    firsts = with_gains(sent[cut:], 3 * quarter, half_count)
    seconds = with_gains(sent[:cut], 2 * quarter, 3 * quarter)
    mids = [split(flip(firsts, "dp", 2), quarter)]
    last_second = split(flip(after(seconds, firsts), "dp", 2), quarter)
    proj_kept = rest_terms(0, 1, normed_one, one_theirs, after(proj_late, firsts), proj_theirs, True)
    out_kept = rest_terms(0, 1, branch_all, branch_theirs, after(out_late, firsts), att_theirs, True)
    down_kept = down_terms(0, 1, firsts)
    left = half_count // 2
    for b in rest_bits[1:]:
        count = left // 2
        terms = last_terms(count, left, firsts)
        terms, *up_late = lax.optimization_barrier((terms, *up_late, proj_kept, out_kept, down_kept))[
            :-3
        ]
        send = with_gains(
            terms, count, left, *((o[-count * block :], g[:, -count * block :]) for o, g in mids)
        )
        mids.append(split(flip(send, "dp", 1 << b), count))
        left = count
    up_second = flip(after(up_sent[:half], send), "dp", 2)

    def ending(kept, *others):
        kept = kept.astype(jnp.float32)
        for other in others:
            kept = kept + other[:block]
        return kept

    down_kept, down_second = lax.optimization_barrier((down_kept, down_second, send))[:2]
    grad_down = ending(down_kept, down_second, *down_late)
    grad_last = ending(
        jnp.concatenate([proj_kept, out_kept], 1), last_second[0], *(m[0] for m in mids[1:])
    )
    gains = gains[:, :block] + last_second[1][:, :block]
    for _, other in mids[1:]:
        gains = gains + other[:, :block]
    grad_up = ending(up_kept, up_second, *up_late)
    narrow = wide + 2 * size

    return (
        output_rows,
        input_rows,
        gains[0],
        grad_last[:, :wide],
        grad_last[:, wide : wide + size],
        grad_last[:, wide + size : narrow],
        grad_last[:, narrow:].T,
        gains[1],
        grad_gate,
        grad_up,
        grad_down.T,
    )


def solution(mesh):
    placed = (
        P("dp", None),
        P("dp"),
        P(),
        P(None, "tp"),
        P(None, "tp"),
        P(None, "tp"),
        P("tp", None),
        P(),
        P(None, "tp"),
        P(None, "tp"),
        P("tp", None),
        P("dp", None),
    )
    return jax.shard_map(
        shards,
        mesh=mesh,
        in_specs=placed,
        out_specs=(
            P(("dp", "tp"), None),
            P(("dp", "tp"), None),
            P("dp"),
            P("dp", "tp"),
            P("dp", "tp"),
            P("dp", "tp"),
            P("tp", "dp"),
            P("dp"),
            P("dp", "tp"),
            P("dp", "tp"),
            P("tp", "dp"),
        ),
        check_vma=False,
    )
```

```python
import functools

import jax
import jax.numpy as jnp
import numpy as np
from jax import lax
from jax.experimental import pallas as pl
from jax.experimental.pallas import tpu as pltpu
from jax.sharding import PartitionSpec as P

SPAN = 4
EPSILON = 1e-05
FAR_BELOW = -1e30
LOW = jnp.bfloat16
ROW_MASKS = (0, 2, 1, 3)


def flip(block, axis, mask):
    return lax.ppermute(block, axis, [(i, i ^ mask) for i in range(lax.axis_size(axis))])


def dot(left, right, left_dim, right_dim):
    return lax.dot_general(
        left,
        right,
        (((left_dim,), (right_dim,)), ((), ())),
        preferred_element_type=jnp.float32,
    )


def in_hbm(*arrays):
    return [pltpu.with_memory_space_constraint(a, pltpu.HBM) for a in arrays]


def own_mask(pos, begin, keys, queries):
    key_at = lax.broadcasted_iota(jnp.int32, (keys, queries), 0)
    query_at = lax.broadcasted_iota(jnp.int32, (keys, queries), 1) + begin
    return (key_at <= query_at) & (key_at >= query_at - pos)


def row_starts(spot, rows):
    part = rows // len(ROW_MASKS)
    return [pl.multiple_of((spot ^ m) * part, part) for m in ROW_MASKS]


def forward_kernel(
    heads,
    size,
    at_ref,
    pos_ref,
    q_ref,
    kv0,
    kv1,
    kv2,
    kv3,
    o_ref,
    lse_ref,
    keys,
    vals,
    top,
    acc,
    ordered,
):
    rank, spot = at_ref[0], at_ref[1]
    rows = pos_ref.shape[1]
    half = rows // 2

    @pl.when(pl.program_id(0) == 0)
    def _():
        for m, kv in enumerate((kv0, kv1, kv2, kv3)):
            keys[m] = kv[:size, :].T
            vals[m, :size, :] = kv[size:, :]
            vals[m, size:, :] = jnp.ones((16, rows), LOW)

    pos = pos_ref[...]
    for part in range(2):
        cols = slice(part * half, (part + 1) * half)
        count = (part + 1) * half
        mask = own_mask(pos[:, cols], part * half, count, half)
        for h in range(heads):
            scores = dot(keys[0, :count, :], q_ref[h * size : (h + 1) * size, cols], 1, 0)
            scores = jnp.where(mask, scores, FAR_BELOW)
            peak = jnp.max(scores, 0, keepdims=True)
            weights = jnp.exp(scores - peak).astype(LOW)
            acc[h, :, cols] = dot(vals[0, :, :count], weights, 1, 0)
            top[h, :, cols] = peak
    seen = pos > lax.broadcasted_iota(jnp.int32, (1, rows), 1)
    for m in range(1, SPAN):

        @pl.when((rank ^ m) < rank)
        def _():
            for h in range(heads):
                scores = dot(keys[m], q_ref[h * size : (h + 1) * size, :], 1, 0)
                old = top[h]
                peak = jnp.where(seen, jnp.maximum(old, jnp.max(scores, 0, keepdims=True)), old)
                weights = jnp.exp(scores - jnp.where(seen, peak, -FAR_BELOW)).astype(LOW)
                acc[h] = acc[h] * jnp.exp(old - peak) + dot(vals[m], weights, 1, 0)
                top[h] = peak

    for h in range(heads):
        total = acc[h, size : size + 1, :]
        ordered[h * size : (h + 1) * size, :] = (acc[h, :size, :] / total).astype(LOW)
        lse_ref[h] = top[h] + jnp.log(total)
    for j, start in enumerate(row_starts(spot, rows)):
        part = rows // len(ROW_MASKS)
        o_ref[:, j * part : (j + 1) * part] = ordered[:, pl.ds(start, part)]


def backward_kernel(
    heads,
    size,
    at_ref,
    pos_ref,
    q_ref,
    do_in,
    o_in,
    lse_ref,
    cos_ref,
    sin_ref,
    kv0,
    kv1,
    kv2,
    kv3,
    dq_ref,
    g0,
    g1,
    g2,
    g3,
    keys,
    vals,
    dq,
    total,
    do_ref,
    o_ref,
):
    rank, spot = at_ref[0], at_ref[1]
    rows = pos_ref.shape[1]
    half = rows // 2
    blocks = (kv0, kv1, kv2, kv3)
    step = pl.program_id(0)

    @pl.when(step == 0)
    def _():
        for m, kv in enumerate(blocks):
            keys[m] = kv[:size, :].T
            vals[m] = kv[size:, :].T
        total[...] = jnp.zeros_like(total)

    part = rows // len(ROW_MASKS)
    for j, start in enumerate(row_starts(spot, rows)):
        do_ref[:, pl.ds(start, part)] = do_in[:, j * part : (j + 1) * part]
        o_ref[:, pl.ds(start, part)] = o_in[:, j * part : (j + 1) * part]
    pos = pos_ref[...]
    seen = pos > lax.broadcasted_iota(jnp.int32, (1, rows), 1)
    deltas = []
    for h in range(heads):
        span = slice(h * size, (h + 1) * size)
        deltas.append(
            jnp.sum(
                do_ref[span, :].astype(jnp.float32) * o_ref[span, :].astype(jnp.float32),
                0,
                keepdims=True,
            )
        )
    for part in range(2):
        cols = slice(part * half, (part + 1) * half)
        count = (part + 1) * half
        mask = own_mask(pos[:, cols], part * half, count, half)
        for h in range(heads):
            span = slice(h * size, (h + 1) * size)
            query, grad = q_ref[span, cols], do_ref[span, cols]
            scores = dot(keys[0, :count, :], query, 1, 0)
            probs = jnp.exp(jnp.where(mask, scores, FAR_BELOW) - lse_ref[h, :, cols])
            grad_probs = dot(vals[0, :count, :], grad, 1, 0)
            grad_scores = (probs * (grad_probs - deltas[h][:, cols])).astype(LOW)
            total[0, :size, :count] += dot(query, grad_scores, 1, 1)
            total[0, size:, :count] += dot(grad, probs.astype(LOW), 1, 1)
            dq[h, :, cols] = dot(kv0[:size, :count], grad_scores, 1, 0)
    for m in range(1, SPAN):

        @pl.when((rank ^ m) < rank)
        def _():
            for h in range(heads):
                span = slice(h * size, (h + 1) * size)
                query, grad = q_ref[span, :], do_ref[span, :]
                scores = dot(keys[m], query, 1, 0)
                probs = jnp.exp(scores - jnp.where(seen, lse_ref[h], -FAR_BELOW))
                grad_probs = dot(vals[m], grad, 1, 0)
                grad_scores = (probs * (grad_probs - deltas[h])).astype(LOW)
                total[m, :size, :] += dot(query, grad_scores, 1, 1)
                total[m, size:, :] += dot(grad, probs.astype(LOW), 1, 1)
                dq[h] += dot(blocks[m][:size, :], grad_scores, 1, 0)

    middle_at = size // 2
    cosine, sine = cos_ref[...], sin_ref[...]
    for h in range(heads):
        first = dq[h, :middle_at, :] * size ** (-0.5)
        second = dq[h, middle_at:, :] * size ** (-0.5)
        base = h * size
        dq_ref[base : base + middle_at, :] = (first * cosine + second * sine).astype(LOW)
        dq_ref[base + middle_at : base + size, :] = (second * cosine - first * sine).astype(LOW)

    @pl.when(step == pl.num_programs(0) - 1)
    def _():
        g0[...] = total[0]
        for m, out in ((1, g1), (2, g2), (3, g3)):
            out[...] = total[m].astype(LOW)


def attention_forward(at, pos, queries, blocks, size, heads):
    wide, rows = queries.shape
    count = wide // size
    whole = pl.BlockSpec((2 * size, rows), lambda i, r: (0, 0))
    some = pl.BlockSpec((heads * size, rows), lambda i, r: (i, 0))
    return pl.pallas_call(
        functools.partial(forward_kernel, heads, size),
        out_shape=(
            jax.ShapeDtypeStruct((wide, rows), LOW),
            jax.ShapeDtypeStruct((count, 1, rows), jnp.float32),
        ),
        grid_spec=pltpu.PrefetchScalarGridSpec(
            num_scalar_prefetch=1,
            grid=(count // heads,),
            in_specs=[pl.BlockSpec((1, rows), lambda i, r: (0, 0)), some] + [whole] * SPAN,
            out_specs=[some, pl.BlockSpec((heads, 1, rows), lambda i, r: (i, 0, 0))],
            scratch_shapes=[
                pltpu.VMEM((SPAN, rows, size), LOW),
                pltpu.VMEM((SPAN, size + 16, rows), LOW),
                pltpu.VMEM((heads, 1, rows), jnp.float32),
                pltpu.VMEM((heads, size + 16, rows), jnp.float32),
                pltpu.VMEM((heads * size, rows), LOW),
            ],
        ),
        compiler_params=pltpu.CompilerParams(vmem_limit_bytes=24 << 20),
        cost_estimate=pl.CostEstimate(
            flops=32 * wide * rows * rows * SPAN,
            bytes_accessed=4 * wide * rows,
            transcendentals=0,
        ),
        name="attention_forward",
    )(at, pos, queries, *blocks)


def attention_backward(at, pos, queries, grads, attended, lse, cosine, sine, blocks, size, heads):
    wide, rows = queries.shape
    count = wide // size
    whole = pl.BlockSpec((2 * size, rows), lambda i, r: (0, 0))
    table = pl.BlockSpec((size // 2, rows), lambda i, r: (0, 0))
    some = pl.BlockSpec((heads * size, rows), lambda i, r: (i, 0))
    return pl.pallas_call(
        functools.partial(backward_kernel, heads, size),
        out_shape=(
            jax.ShapeDtypeStruct((wide, rows), LOW),
            jax.ShapeDtypeStruct((2 * size, rows), jnp.float32),
        )
        + (jax.ShapeDtypeStruct((2 * size, rows), LOW),) * (SPAN - 1),
        grid_spec=pltpu.PrefetchScalarGridSpec(
            num_scalar_prefetch=1,
            grid=(count // heads,),
            in_specs=[
                pl.BlockSpec((1, rows), lambda i, r: (0, 0)),
                some,
                some,
                some,
                pl.BlockSpec((heads, 1, rows), lambda i, r: (i, 0, 0)),
                table,
                table,
            ]
            + [whole] * SPAN,
            out_specs=[some] + [whole] * SPAN,
            scratch_shapes=[
                pltpu.VMEM((SPAN, rows, size), LOW),
                pltpu.VMEM((SPAN, rows, size), LOW),
                pltpu.VMEM((heads, size, rows), jnp.float32),
                pltpu.VMEM((SPAN, 2 * size, rows), jnp.float32),
                pltpu.VMEM((heads * size, rows), LOW),
                pltpu.VMEM((heads * size, rows), LOW),
            ],
        ),
        compiler_params=pltpu.CompilerParams(vmem_limit_bytes=24 << 20),
        cost_estimate=pl.CostEstimate(
            flops=48 * wide * rows * rows * SPAN,
            bytes_accessed=10 * wide * rows,
            transcendentals=0,
        ),
        name="attention_backward",
    )(at, pos, *in_hbm(queries, grads, attended, lse, cosine, sine, *blocks))


def take(values, start, size, dim):
    starts = [np.uint32(0)] * values.ndim
    starts[dim] = start
    sizes = list(values.shape)
    sizes[dim] = size
    return lax.dynamic_slice(values, starts, sizes)


def pick(values, places, blocks, dim):
    size = values.shape[dim] // blocks
    return jnp.concatenate(
        [lax.dynamic_slice_in_dim(values, p * size, size, dim) for p in places], dim
    )


class Table:
    def __init__(self, **parts):
        self.begin, at = {}, 0
        for name, part in parts.items():
            self.begin[name] = at
            at += part.shape[0]
        self.values = jnp.concatenate([p.astype(jnp.int32) for p in parts.values()])

    def list(self, name, lo, hi):
        return [self.values[self.begin[name] + j] for j in range(lo, hi)]


def after(value, *others):
    return lax.optimization_barrier((value, *others))[0]


def parity_sum(terms, dim):
    count = lax.axis_size("dp")
    groups = [list(range(p, count, 2)) for p in range(2)]
    return lax.psum_scatter(
        terms.astype(LOW), "dp", scatter_dimension=dim, axis_index_groups=groups, tiled=True
    )


def terms_kernel(transposed, places, x, x_far, g, g_far, out):
    del places
    side = 1 if transposed else 0
    out[...] = (dot(x[...], g[...], 0, side) + dot(x_far[...], g_far[...], 0, side)).astype(LOW)


def weight_terms(table, name, far, lo, hi, x, x_far, g, g_far, transposed=False, keep=True):
    count = hi - lo
    size = x.shape[1] // lax.axis_size("dp")
    rows = x.shape[0]
    units = g.shape[0] if transposed else g.shape[1]
    if size % 128:
        side = 1 if transposed else 0
        mine = pick(x, table.list(name, lo, hi), x.shape[1] // size, 1)
        theirs = pick(x_far, table.list(far, lo, hi), x_far.shape[1] // size, 1)
        return (dot(mine, g, 0, side) + dot(theirs, g_far, 0, side)).astype(LOW)
    whole = pl.BlockSpec(g.shape, lambda i, p: (0, 0))
    begin, far_begin = table.begin[name] + lo, table.begin[far] + lo
    return pl.pallas_call(
        functools.partial(terms_kernel, transposed),
        out_shape=(jax.ShapeDtypeStruct if keep else pltpu.HBM)((count * size, units), LOW),
        grid_spec=pltpu.PrefetchScalarGridSpec(
            num_scalar_prefetch=1,
            grid=(count,),
            in_specs=[
                pl.BlockSpec((rows, size), lambda i, p: (0, p[begin + i])),
                pl.BlockSpec((rows, size), lambda i, p: (0, p[far_begin + i])),
                whole,
                whole,
            ],
            out_specs=pl.BlockSpec((size, units), lambda i, p: (i, 0)),
        ),
        compiler_params=pltpu.CompilerParams(vmem_limit_bytes=20 << 20),
        cost_estimate=pl.CostEstimate(
            flops=24 * rows * count * size * units, bytes_accessed=4 * rows * units, transcendentals=0
        ),
        name="weight_terms",
    )(table.values, x, x_far, g, g_far)


def copy_kernel(places, source, target):
    del places
    target[...] = source[...]


def pick_columns(table, name, values, part=None, parts=1):
    blocks = lax.axis_size("dp")
    rows, count = values.shape[0] // parts, blocks // 2
    size = values.shape[1] // blocks
    if size % 128:
        if part is not None:
            values = lax.dynamic_slice_in_dim(values, table.list(part, 0, 1)[0] * rows, rows, 0)
        return pick(values, table.list(name, 0, count), blocks, 1)
    begin = table.begin[name]
    row = 0 if part is None else table.begin[part]
    return pl.pallas_call(
        copy_kernel,
        out_shape=jax.ShapeDtypeStruct((rows, count * size), values.dtype),
        grid_spec=pltpu.PrefetchScalarGridSpec(
            num_scalar_prefetch=1,
            grid=(count,),
            in_specs=[
                pl.BlockSpec(
                    (rows, size), lambda i, p: (0 if part is None else p[row], p[begin + i])
                )
            ],
            out_specs=pl.BlockSpec((rows, size), lambda i, p: (0, i)),
        ),
        compiler_params=pltpu.CompilerParams(vmem_limit_bytes=8 << 20),
        cost_estimate=pl.CostEstimate(
            flops=65536 * rows * count * size, bytes_accessed=4 * rows * count * size, transcendentals=0
        ),
        name="pick_columns",
    )(table.values, values)


def load_kernel(*refs):
    *pairs, sems = refs
    half = len(pairs) // 2
    copies = [
        pltpu.make_async_copy(source, target, sems.at[j])
        for j, (source, target) in enumerate(zip(pairs[:half], pairs[half:]))
    ]
    for copy in copies:
        copy.start()
    for copy in copies:
        copy.wait()


def load_weights(*weights):
    return pl.pallas_call(
        load_kernel,
        out_shape=tuple(pltpu.VMEM(w.shape, w.dtype) for w in weights),
        in_specs=[pl.BlockSpec(memory_space=pl.ANY)] * len(weights),
        out_specs=[pl.BlockSpec(memory_space=pltpu.VMEM)] * len(weights),
        scratch_shapes=[pltpu.SemaphoreType.DMA((len(weights),))],
        compiler_params=pltpu.CompilerParams(vmem_limit_bytes=2 << 20),
        cost_estimate=pl.CostEstimate(
            flops=20_000_000_000,
            bytes_accessed=2 * sum(w.size for w in weights),
            transcendentals=0,
        ),
        name="load_weights",
    )(*in_hbm(*weights))


def in_vmem(*arrays):
    return [pltpu.with_memory_space_constraint(a, pltpu.VMEM) for a in arrays]


def ffn_kernel(rows, gate_w, up_w, grad_in, hidden, grad_gate, grad_up):
    step = 128
    for begin in range(0, hidden.shape[1], step):
        cut = slice(begin, begin + step)
        both = dot(rows[...], jnp.concatenate([gate_w[:, cut], up_w[:, cut]], 1), 1, 0)
        gate, up = both[:, :step], both[:, step:]
        grad = grad_in[:, cut]
        sigma = jax.nn.sigmoid(gate)
        active = gate * sigma
        hidden[:, cut] = (active * up).astype(LOW)
        grad_gate[:, cut] = (grad * up * sigma * (1.0 + gate * (1.0 - sigma))).astype(LOW)
        grad_up[:, cut] = (grad * active).astype(LOW)


def feed_forward(rows, w_gate, w_up, grad_hidden):
    count, width = rows.shape
    units = w_gate.shape[1]
    here = pl.BlockSpec(memory_space=pltpu.VMEM)
    return pl.pallas_call(
        ffn_kernel,
        out_shape=(jax.ShapeDtypeStruct((count, units), LOW),) * 3,
        in_specs=[here] * 4,
        out_specs=[here] * 3,
        compiler_params=pltpu.CompilerParams(vmem_limit_bytes=20 << 20),
        cost_estimate=pl.CostEstimate(
            flops=6 * count * width * units,
            bytes_accessed=4 * width * units,
            transcendentals=count * units,
        ),
        name="feed_forward",
    )(*in_vmem(rows, w_gate, w_up, grad_hidden))


def back_kernel(gate_rows, up_rows, gate_w, up_w, out):
    step = out.shape[1]
    cut = pl.ds(pl.multiple_of(pl.program_id(0) * step, step), step)
    total = dot(gate_rows[...], gate_w[cut, :], 1, 1) + dot(up_rows[...], up_w[cut, :], 1, 1)
    out[...] = total.astype(out.dtype)


def feed_forward_back(grad_gate, grad_up, w_gate, w_up, half, kind):
    count, units = grad_gate.shape
    width = w_gate.shape[0]
    step = width // 2
    rows = pl.BlockSpec((count // 2, units), lambda i: (half, 0))
    here = pl.BlockSpec(memory_space=pltpu.VMEM)
    return pl.pallas_call(
        back_kernel,
        out_shape=jax.ShapeDtypeStruct((count // 2, width), kind),
        grid=(2,),
        in_specs=[rows, rows, here, here],
        out_specs=pl.BlockSpec((count // 2, step), lambda i: (0, i)),
        compiler_params=pltpu.CompilerParams(vmem_limit_bytes=16 << 20),
        cost_estimate=pl.CostEstimate(
            flops=10 * count * width * units, bytes_accessed=4 * width * units, transcendentals=0
        ),
        name="feed_forward_back",
    )(grad_gate, grad_up, *in_vmem(w_gate, w_up))


def join_kernel(places, first, second, out):
    del places

    @pl.when(pl.program_id(0) == 0)
    def _():
        out[...] = first[...]

    @pl.when(pl.program_id(0) == 1)
    def _():
        out[...] = second[...]


def join_rows(table, first, second):
    rows, width = first.shape
    core = table.begin["core"]
    whole = pl.BlockSpec((rows, width), lambda i, p: (0, 0))
    return pl.pallas_call(
        join_kernel,
        out_shape=jax.ShapeDtypeStruct((2 * rows, width), first.dtype),
        grid_spec=pltpu.PrefetchScalarGridSpec(
            num_scalar_prefetch=1,
            grid=(2,),
            in_specs=[whole, whole],
            out_specs=pl.BlockSpec((rows, width), lambda i, p: (p[core] ^ i, 0)),
        ),
        compiler_params=pltpu.CompilerParams(vmem_limit_bytes=8 << 20),
        cost_estimate=pl.CostEstimate(
            flops=1_000_000_000, bytes_accessed=8 * rows * width, transcendentals=0
        ),
        name="join_rows",
    )(table.values, first, second)


def row_kernel(left, right, send, kept):
    half = left.shape[0] // 2
    send[...] = dot(left[half:, :], right[...], 1, 0).astype(LOW)
    kept[...] = dot(left[:half, :], right[...], 1, 0)


def row_terms(left, right):
    rows, units = left.shape
    half, width = rows // 2, right.shape[1]
    step = 256
    return pl.pallas_call(
        row_kernel,
        out_shape=(
            jax.ShapeDtypeStruct((half, width), LOW),
            jax.ShapeDtypeStruct((half, width), jnp.float32),
        ),
        grid=(width // step,),
        in_specs=[
            pl.BlockSpec((rows, units), lambda i: (0, 0)),
            pl.BlockSpec((units, step), lambda i: (0, i)),
        ],
        out_specs=[pl.BlockSpec((half, step), lambda i: (0, i))] * 2,
        compiler_params=pltpu.CompilerParams(vmem_limit_bytes=16 << 20),
        cost_estimate=pl.CostEstimate(
            flops=8 * rows * units * width, bytes_accessed=2 * units * width, transcendentals=0
        ),
        name="row_terms",
    )(left, right)


def turn(values, cosine, sine):
    half = cosine.shape[0]
    heads = values.shape[0] // (2 * half)
    pieces = values.reshape(heads, 2, half, values.shape[1])
    first, second = pieces[:, 0], pieces[:, 1]
    return jnp.stack(
        [first * cosine - second * sine, second * cosine + first * sine], 1
    ).reshape(values.shape)


def turn_back(grads, cosine, sine):
    return turn(grads, cosine, -sine)


def norm_back(grad_rows, values, scale_rows, gain):
    scaled = grad_rows * gain
    inner_mean = jnp.mean(scaled * values, -1, keepdims=True)
    return (
        scale_rows * (scaled - values * scale_rows * scale_rows * inner_mean),
        jnp.sum(grad_rows * values * scale_rows, 0),
    )


def shards(
    tokens,
    positions,
    norm1_gain,
    w_query,
    w_key,
    w_value,
    w_out,
    norm2_gain,
    w_gate,
    w_up,
    w_down,
    cotangent,
):
    rows_here, width = tokens.shape
    size = w_key.shape[1]
    dp = lax.axis_size("dp")
    tp_count = len(ROW_MASKS)
    own_rows = rows_here // tp_count
    block = width // dp
    bits = dp.bit_length() - 1
    half_count = dp // 2

    def exchange_order(order):
        return np.array(
            [
                sum(((j >> (len(order) - 1 - k)) & 1) << b for k, b in enumerate(order))
                for j in range(1 << len(order))
            ],
            np.int32,
        )

    down_bits = [0] + list(range(2, bits))
    rest_bits = list(range(1, bits))

    place = lax.axis_index("dp").astype(jnp.int32)
    spot = lax.axis_index("tp").astype(jnp.int32)
    natural = np.arange(half_count, dtype=np.int32)
    down_here, rest_here = place ^ exchange_order(down_bits), place ^ exchange_order(rest_bits)
    table = Table(
        mine=2 * natural + (place & 1),
        theirs=2 * natural + (1 - (place & 1)),
        natural=jnp.asarray(natural),
        down=down_here,
        down_far=down_here ^ 2,
        rest=rest_here,
        rest_far=rest_here ^ 1,
        rest_block=rest_here >> 1,
        core=(spot & 1)[None],
    )
    at = jnp.stack([place & (SPAN - 1), spot])
    row_starts = [((spot ^ m) * own_rows).astype(jnp.uint32) for m in ROW_MASKS]
    core_starts = [(c * (rows_here // 2)).astype(jnp.uint32) for c in (spot & 1, 1 - (spot & 1))]
    tokens, table.values, at, row_starts, core_starts = lax.optimization_barrier(
        (tokens, table.values, at, row_starts, core_starts)
    )
    pos = positions.reshape(1, rows_here)

    def own(values):
        return take(values, row_starts[0], own_rows, 0)

    inputs = tokens.astype(jnp.float32)
    scale_one = lax.rsqrt(jnp.mean(inputs * inputs, -1, keepdims=True) + EPSILON)
    normed_one = (inputs * scale_one * norm1_gain).astype(LOW)
    half = size // 2
    frequency = jnp.exp(
        -jnp.log(10000.0) * (2.0 * jnp.arange(half, dtype=jnp.float32) / size)
    )
    angles = frequency[:, None] * positions.astype(jnp.float32)[None, :]
    cosine, sine = jnp.cos(angles), jnp.sin(angles)
    w_kv = jnp.concatenate([w_key.T, w_value.T], 0)
    paired = dot(w_kv, normed_one, 1, 1)
    paired = jnp.concatenate([turn(paired[:size], cosine, sine), paired[size:]], 0).astype(LOW)
    blocks = [paired] + [flip(paired, "dp", m) for m in range(1, SPAN)]
    queries = (turn(dot(w_query, normed_one, 0, 1), cosine, sine) * size ** (-0.5)).astype(LOW)

    wide = w_query.shape[1]

    def near_sum(part):
        send = part(2, 4).astype(LOW)
        near, kept = lax.optimization_barrier((flip(send, "tp", 1), part(0, 2)))
        pair = kept + near
        return pair[:own_rows], pair[own_rows:].astype(LOW)

    attended, lse = attention_forward(at, pos, queries, blocks, size, 8)

    branch, branch_out = near_sum(
        lambda lo, hi: dot(attended[:, lo * own_rows : hi * own_rows], w_out, 0, 0)
    )
    branch_far = flip(branch_out, "tp", 2)
    cot = jnp.concatenate(
        [take(after(cotangent, branch_out), start, own_rows, 0) for start in row_starts], 0
    )
    cot_send = pick_columns(table, "down_far", cot)
    cot_theirs = flip(cot_send, "dp", 2)
    own_inputs = own(tokens).astype(jnp.float32)
    one_send = pick_columns(table, "theirs", after(normed_one, cot_send), "core", 2)
    one_near = flip(one_send, "dp", 1)
    grad_hidden = dot(after(cot, one_send), w_down, 1, 1)
    middle = own_inputs + (after(branch, grad_hidden) + branch_far)

    scale_two = lax.rsqrt(jnp.mean(middle * middle, -1, keepdims=True) + EPSILON)
    own_two = (middle * scale_two * norm2_gain).astype(LOW)
    far_two = flip(own_two, "tp", 2)
    gate_w, up_w = load_weights(after(w_gate, own_two), w_up)
    pair_two = jnp.concatenate([after(own_two, gate_w), far_two], 0)
    core_two = flip(pair_two, "tp", 1)
    two_send = pick_columns(table, "theirs", pair_two)
    two_near = flip(two_send, "dp", 1)
    normed_two = jnp.concatenate([after(pair_two, two_send), core_two], 0)

    hidden, grad_gate_pre, grad_up_pre = feed_forward(normed_two, gate_w, up_w, grad_hidden)
    gate_theirs = flip(grad_gate_pre, "dp", 1)
    hidden_theirs = flip(hidden, "dp", 2)
    up_theirs = flip(grad_up_pre, "dp", 1)
    gate_late, cot_theirs, one_near = lax.optimization_barrier((grad_gate_pre, cot_theirs, one_near))

    two_back = functools.partial(feed_forward_back, gate_late, grad_up_pre, gate_w, up_w)
    grad_normed_two, two_out = near_sum(
        lambda lo, hi: two_back(lo // 2, jnp.float32 if lo == 0 else LOW)
    )
    two_out, two_near = lax.optimization_barrier((two_out, two_near))
    two_far = flip(two_out, "tp", 2)
    cores = jnp.concatenate([two_near, one_near], 1)
    cores_far = flip(cores, "tp", 1)
    two_theirs = jnp.concatenate([two_near, cores_far[:, : width // 2]], 0)

    down_near, down = row_terms(after(hidden, two_out), w_down)
    grad_normed_two = after(grad_normed_two, down) + two_far

    grad_mid_norm, gain_two = norm_back(grad_normed_two, middle, scale_two, norm2_gain)
    grad_middle = own(cotangent).astype(jnp.float32) + grad_mid_norm
    branch_grad = grad_middle.astype(LOW)
    grad_far = flip(branch_grad, "tp", 2)

    down_near = flip(after(down_near, branch_grad), "tp", 1)
    gate_terms = weight_terms(
        table,
        "mine",
        "natural",
        0,
        half_count,
        after(normed_two, branch_grad),
        two_theirs,
        grad_gate_pre,
        gate_theirs,
        keep=False,
    )
    grad_gate = parity_sum(gate_terms, 0)
    grad_pair = jnp.concatenate([after(branch_grad, gate_terms), grad_far], 0)
    grad_core = flip(grad_pair, "tp", 1)
    branch_send = pick_columns(table, "theirs", grad_pair)
    att_theirs = flip(after(attended, branch_send), "dp", 1)

    def near_flip(terms, bit):
        half = terms.shape[0] // 2
        return [flip(terms[half:], "dp", 1 << bit), flip(terms[:half], "dp", 1 << bit)]

    def down_terms(lo, hi, *late):
        g = after(hidden, *late)
        return weight_terms(table, "down", "natural", lo, hi, cot, cot_theirs, g, hidden_theirs)

    down_sent = down_terms(half_count // 2, half_count, branch_send)
    half = down_sent.shape[0] // 2
    down_first = flip(down_sent[half:], "dp", 1)
    branch_all = jnp.concatenate([after(grad_pair, down_sent), grad_core], 0)
    grad_attended = dot(w_out, branch_all, 1, 1).astype(LOW)
    grads = attention_backward(
        at, pos, queries, grad_attended, attended, lse, cosine, sine, blocks, size, 2
    )
    grad_query_rows, kv_total = grads[0], grads[1]
    *kv_sends, att_theirs = lax.optimization_barrier((*grads[2:], att_theirs))
    kv_back = [flip(kv_sends[m - 1], "dp", m) for m in range(1, SPAN)]

    def rest_terms(lo, hi, x, x_far, g, g_far, transposed=False):
        return weight_terms(
            table, "rest", "rest_block", lo, hi, x, x_far, g, g_far, transposed
        )

    down = down + after(down_near, grad_query_rows)
    down, down_out = down[:own_rows], down[own_rows:].astype(LOW)
    down_far = flip(down_out, "tp", 2)

    def up_terms(lo, hi, *late):
        return rest_terms(lo, hi, normed_two, two_theirs, after(grad_up_pre, *late), up_theirs)

    up_sent = up_terms(half_count // 2, half_count, grad_query_rows)
    up_first = flip(up_sent[half:], "dp", 2)

    def exchange_mid(terms, first, order, *late):
        got, left = [first], half_count // 2
        for b in order[1:]:
            send = terms(left // 2, left, *late).astype(jnp.float32)
            rows = send.shape[0]
            for other in got:
                send = send + other[other.shape[0] - rows :]
            send = send.astype(LOW)
            got.append(flip(send, "dp", 1 << b))
            left //= 2
        return got[1:], send

    down_late, down_last = exchange_mid(down_terms, down_first, down_bits, grad_query_rows)
    kv_total, grad_gate = lax.optimization_barrier(
        (kv_total, grad_gate, up_sent, down_out, down_last)
    )[:2]
    for back in kv_back:
        kv_total = kv_total + back
    key_grad = turn_back(kv_total[:size], cosine, sine)
    grad_kv_rows = jnp.concatenate([key_grad, kv_total[size:]], 0).astype(LOW)
    proj_rows = jnp.concatenate([grad_query_rows, grad_kv_rows], 0)
    units = proj_rows.shape[0]
    pieces = [
        branch_send[:, begin : begin + rows_here] for begin in range(0, branch_send.shape[1], rows_here)
    ]
    both_theirs = flip(jnp.concatenate([proj_rows, *pieces], 0), "dp", 1)

    own_order = jnp.concatenate(
        [take(proj_rows, start, own_rows, 1) for start in row_starts], 1
    )

    def one_terms(lo, hi):
        cut = own_order[:, lo * own_rows : hi * own_rows]
        return dot(cut[:wide], w_query, 0, 1) + dot(cut[wide:], w_kv, 0, 0)

    grad_normed_one, one_out = near_sum(one_terms)
    one_far = flip(one_out, "tp", 2)
    up_second = flip(after(up_sent[:half], one_out), "dp", 2)
    output_rows = (middle + (down + after(down_far, one_out))).astype(LOW)
    one_theirs = join_rows(table, after(one_near, one_out), cores_far[:, width // 2 :])
    up_kept = up_terms(0, 1, one_out)
    grad_gate = grad_gate.astype(jnp.float32)
    grad_normed_one = after(grad_normed_one, output_rows, up_kept, grad_gate, one_theirs) + one_far
    grad_in_norm, gain_one = norm_back(grad_normed_one, own_inputs, own(scale_one), norm1_gain)
    input_rows = grad_middle + grad_in_norm

    up_late, up_last = exchange_mid(up_terms, up_first, rest_bits, input_rows)
    both_theirs = after(both_theirs, up_last)
    proj_theirs = both_theirs[:units]
    branch_near = jnp.concatenate(
        [
            both_theirs[begin : begin + branch_send.shape[0]]
            for begin in range(units, both_theirs.shape[0], branch_send.shape[0])
        ],
        1,
    )
    branch_theirs = jnp.concatenate([branch_near, flip(branch_near, "tp", 1)], 0)
    gain_one, *down_late = lax.optimization_barrier((gain_one, *down_late, up_last))[:-1]
    gains = jnp.stack([gain_one, gain_two])
    for m in (1, 2):
        gains = gains + flip(gains, "tp", m)
    gains = pick_columns(table, "rest", gains) + flip(
        pick_columns(table, "rest_far", gains), "dp", 1
    )

    out_late, proj_late = lax.optimization_barrier((attended, proj_rows, up_last))[:2]

    def last_terms(lo, hi, *late):
        first, second = after(proj_late, *late), after(out_late, *late)
        return jnp.concatenate(
            [
                rest_terms(lo, hi, normed_one, one_theirs, first, proj_theirs, True),
                rest_terms(lo, hi, branch_all, branch_theirs, second, att_theirs, True),
            ],
            1,
        )

    def with_gains(terms, lo, hi, *others):
        extra = gains[:, lo * block : hi * block]
        for other, other_gains in others:
            terms = terms.astype(jnp.float32) + other
            extra = extra + other_gains
        columns = terms.shape[1]
        extra = jnp.pad(extra, ((0, 14), (0, -extra.shape[1] % columns)))[:, :columns]
        return jnp.concatenate([terms.astype(LOW), extra.astype(LOW)], 0)

    def split(message, count):
        rows = count * block
        return message[:rows], message[rows : rows + 2, :rows]

    quarter = half_count // 4
    sent = last_terms(half_count // 2, half_count)
    cut = quarter * block
    firsts = with_gains(sent[cut:], 3 * quarter, half_count)
    seconds = with_gains(sent[:cut], 2 * quarter, 3 * quarter)
    mids = [split(flip(firsts, "dp", 2), quarter)]
    last_second = split(flip(after(seconds, firsts), "dp", 2), quarter)
    up_late = [*up_late, up_second]
    proj_kept = rest_terms(0, 1, normed_one, one_theirs, after(proj_late, firsts), proj_theirs, True)
    out_kept = rest_terms(0, 1, branch_all, branch_theirs, after(out_late, firsts), att_theirs, True)
    down_kept = down_terms(0, 1, firsts)
    left = half_count // 2
    for b in rest_bits[1:]:
        count = left // 2
        terms = last_terms(count, left, firsts)
        terms, *up_late = lax.optimization_barrier((terms, *up_late, proj_kept, out_kept, down_kept))[
            :-3
        ]
        send = with_gains(
            terms, count, left, *((o[-count * block :], g[:, -count * block :]) for o, g in mids)
        )
        mids.append(split(flip(send, "dp", 1 << b), count))
        left = count
    down_second = flip(after(down_sent[:half], firsts), "dp", 1)

    def ending(kept, *others):
        kept = kept.astype(jnp.float32)
        for other in others:
            kept = kept + other[:block]
        return kept

    down_kept, down_second = lax.optimization_barrier((down_kept, down_second, send))[:2]
    grad_down = ending(down_kept, down_second, *down_late)
    grad_last = ending(
        jnp.concatenate([proj_kept, out_kept], 1), last_second[0], *(m[0] for m in mids[1:])
    )
    gains = gains[:, :block] + last_second[1][:, :block]
    for _, other in mids[1:]:
        gains = gains + other[:, :block]
    grad_up = ending(up_kept, *up_late)
    narrow = wide + 2 * size

    return (
        output_rows,
        input_rows,
        gains[0],
        grad_last[:, :wide],
        grad_last[:, wide : wide + size],
        grad_last[:, wide + size : narrow],
        grad_last[:, narrow:].T,
        gains[1],
        grad_gate,
        grad_up,
        grad_down.T,
    )


def solution(mesh):
    placed = (
        P("dp", None),
        P("dp"),
        P(),
        P(None, "tp"),
        P(None, "tp"),
        P(None, "tp"),
        P("tp", None),
        P(),
        P(None, "tp"),
        P(None, "tp"),
        P("tp", None),
        P("dp", None),
    )
    return jax.shard_map(
        shards,
        mesh=mesh,
        in_specs=placed,
        out_specs=(
            P(("dp", "tp"), None),
            P(("dp", "tp"), None),
            P("dp"),
            P("dp", "tp"),
            P("dp", "tp"),
            P("dp", "tp"),
            P("tp", "dp"),
            P("dp"),
            P("dp", "tp"),
            P("dp", "tp"),
            P("tp", "dp"),
        ),
        check_vma=False,
    )
```

```python
import functools

import jax
import jax.numpy as jnp
import numpy as np
from jax import lax
from jax.experimental import pallas as pl
from jax.experimental.pallas import tpu as pltpu
from jax.sharding import PartitionSpec as P

SPAN = 4
EPSILON = 1e-05
FAR_BELOW = -1e30
LOW = jnp.bfloat16
ROW_MASKS = (0, 2, 1, 3)


def flip(block, axis, mask):
    return lax.ppermute(block, axis, [(i, i ^ mask) for i in range(lax.axis_size(axis))])


def dot(left, right, left_dim, right_dim):
    return lax.dot_general(
        left,
        right,
        (((left_dim,), (right_dim,)), ((), ())),
        preferred_element_type=jnp.float32,
    )


def in_hbm(*arrays):
    return [pltpu.with_memory_space_constraint(a, pltpu.HBM) for a in arrays]


def own_mask(pos, begin, keys, queries):
    key_at = lax.broadcasted_iota(jnp.int32, (keys, queries), 0)
    query_at = lax.broadcasted_iota(jnp.int32, (keys, queries), 1) + begin
    return (key_at <= query_at) & (key_at >= query_at - pos)


def row_starts(spot, rows):
    part = rows // len(ROW_MASKS)
    return [pl.multiple_of((spot ^ m) * part, part) for m in ROW_MASKS]


def forward_kernel(
    heads,
    size,
    at_ref,
    pos_ref,
    q_ref,
    kv0,
    kv1,
    kv2,
    kv3,
    o_ref,
    lse_ref,
    keys,
    vals,
    top,
    acc,
    ordered,
):
    rank, spot = at_ref[0], at_ref[1]
    rows = pos_ref.shape[1]
    half = rows // 2

    @pl.when(pl.program_id(0) == 0)
    def _():
        for m, kv in enumerate((kv0, kv1, kv2, kv3)):
            keys[m] = kv[:size, :].T
            vals[m, :size, :] = kv[size:, :]
            vals[m, size:, :] = jnp.ones((16, rows), LOW)

    pos = pos_ref[...]
    for part in range(2):
        cols = slice(part * half, (part + 1) * half)
        count = (part + 1) * half
        mask = own_mask(pos[:, cols], part * half, count, half)
        for h in range(heads):
            scores = dot(keys[0, :count, :], q_ref[h * size : (h + 1) * size, cols], 1, 0)
            scores = jnp.where(mask, scores, FAR_BELOW)
            peak = jnp.max(scores, 0, keepdims=True)
            weights = jnp.exp(scores - peak).astype(LOW)
            acc[h, :, cols] = dot(vals[0, :, :count], weights, 1, 0)
            top[h, :, cols] = peak
    seen = pos > lax.broadcasted_iota(jnp.int32, (1, rows), 1)
    for m in range(1, SPAN):

        @pl.when((rank ^ m) < rank)
        def _():
            for h in range(heads):
                scores = dot(keys[m], q_ref[h * size : (h + 1) * size, :], 1, 0)
                old = top[h]
                peak = jnp.where(seen, jnp.maximum(old, jnp.max(scores, 0, keepdims=True)), old)
                weights = jnp.exp(scores - jnp.where(seen, peak, -FAR_BELOW)).astype(LOW)
                acc[h] = acc[h] * jnp.exp(old - peak) + dot(vals[m], weights, 1, 0)
                top[h] = peak

    for h in range(heads):
        total = acc[h, size : size + 1, :]
        ordered[h * size : (h + 1) * size, :] = (acc[h, :size, :] / total).astype(LOW)
        lse_ref[h] = top[h] + jnp.log(total)
    for j, start in enumerate(row_starts(spot, rows)):
        part = rows // len(ROW_MASKS)
        o_ref[:, j * part : (j + 1) * part] = ordered[:, pl.ds(start, part)]


def backward_kernel(
    heads,
    size,
    at_ref,
    pos_ref,
    q_ref,
    do_in,
    o_in,
    lse_ref,
    cos_ref,
    sin_ref,
    kv0,
    kv1,
    kv2,
    kv3,
    dq_ref,
    g0,
    g1,
    g2,
    g3,
    keys,
    vals,
    dq,
    total,
    do_ref,
    o_ref,
):
    rank, spot = at_ref[0], at_ref[1]
    rows = pos_ref.shape[1]
    half = rows // 2
    blocks = (kv0, kv1, kv2, kv3)
    step = pl.program_id(0)

    @pl.when(step == 0)
    def _():
        for m, kv in enumerate(blocks):
            keys[m] = kv[:size, :].T
            vals[m] = kv[size:, :].T
        total[...] = jnp.zeros_like(total)

    part = rows // len(ROW_MASKS)
    for j, start in enumerate(row_starts(spot, rows)):
        do_ref[:, pl.ds(start, part)] = do_in[:, j * part : (j + 1) * part]
        o_ref[:, pl.ds(start, part)] = o_in[:, j * part : (j + 1) * part]
    pos = pos_ref[...]
    seen = pos > lax.broadcasted_iota(jnp.int32, (1, rows), 1)
    deltas = []
    for h in range(heads):
        span = slice(h * size, (h + 1) * size)
        deltas.append(
            jnp.sum(
                do_ref[span, :].astype(jnp.float32) * o_ref[span, :].astype(jnp.float32),
                0,
                keepdims=True,
            )
        )
    for part in range(2):
        cols = slice(part * half, (part + 1) * half)
        count = (part + 1) * half
        mask = own_mask(pos[:, cols], part * half, count, half)
        for h in range(heads):
            span = slice(h * size, (h + 1) * size)
            query, grad = q_ref[span, cols], do_ref[span, cols]
            scores = dot(keys[0, :count, :], query, 1, 0)
            probs = jnp.exp(jnp.where(mask, scores, FAR_BELOW) - lse_ref[h, :, cols])
            grad_probs = dot(vals[0, :count, :], grad, 1, 0)
            grad_scores = (probs * (grad_probs - deltas[h][:, cols])).astype(LOW)
            total[0, :size, :count] += dot(query, grad_scores, 1, 1)
            total[0, size:, :count] += dot(grad, probs.astype(LOW), 1, 1)
            dq[h, :, cols] = dot(kv0[:size, :count], grad_scores, 1, 0)
    for m in range(1, SPAN):

        @pl.when((rank ^ m) < rank)
        def _():
            for h in range(heads):
                span = slice(h * size, (h + 1) * size)
                query, grad = q_ref[span, :], do_ref[span, :]
                scores = dot(keys[m], query, 1, 0)
                probs = jnp.exp(scores - jnp.where(seen, lse_ref[h], -FAR_BELOW))
                grad_probs = dot(vals[m], grad, 1, 0)
                grad_scores = (probs * (grad_probs - deltas[h])).astype(LOW)
                total[m, :size, :] += dot(query, grad_scores, 1, 1)
                total[m, size:, :] += dot(grad, probs.astype(LOW), 1, 1)
                dq[h] += dot(blocks[m][:size, :], grad_scores, 1, 0)

    middle_at = size // 2
    cosine, sine = cos_ref[...], sin_ref[...]
    for h in range(heads):
        first = dq[h, :middle_at, :] * size ** (-0.5)
        second = dq[h, middle_at:, :] * size ** (-0.5)
        base = h * size
        dq_ref[base : base + middle_at, :] = (first * cosine + second * sine).astype(LOW)
        dq_ref[base + middle_at : base + size, :] = (second * cosine - first * sine).astype(LOW)

    @pl.when(step == pl.num_programs(0) - 1)
    def _():
        g0[...] = total[0]
        for m, out in ((1, g1), (2, g2), (3, g3)):
            out[...] = total[m].astype(LOW)


def attention_forward(at, pos, queries, blocks, size, heads):
    wide, rows = queries.shape
    count = wide // size
    whole = pl.BlockSpec((2 * size, rows), lambda i, r: (0, 0))
    some = pl.BlockSpec((heads * size, rows), lambda i, r: (i, 0))
    return pl.pallas_call(
        functools.partial(forward_kernel, heads, size),
        out_shape=(
            jax.ShapeDtypeStruct((wide, rows), LOW),
            jax.ShapeDtypeStruct((count, 1, rows), jnp.float32),
        ),
        grid_spec=pltpu.PrefetchScalarGridSpec(
            num_scalar_prefetch=1,
            grid=(count // heads,),
            in_specs=[pl.BlockSpec((1, rows), lambda i, r: (0, 0)), some] + [whole] * SPAN,
            out_specs=[some, pl.BlockSpec((heads, 1, rows), lambda i, r: (i, 0, 0))],
            scratch_shapes=[
                pltpu.VMEM((SPAN, rows, size), LOW),
                pltpu.VMEM((SPAN, size + 16, rows), LOW),
                pltpu.VMEM((heads, 1, rows), jnp.float32),
                pltpu.VMEM((heads, size + 16, rows), jnp.float32),
                pltpu.VMEM((heads * size, rows), LOW),
            ],
        ),
        compiler_params=pltpu.CompilerParams(vmem_limit_bytes=24 << 20),
        cost_estimate=pl.CostEstimate(
            flops=32 * wide * rows * rows * SPAN,
            bytes_accessed=4 * wide * rows,
            transcendentals=0,
        ),
        name="attention_forward",
    )(at, pos, queries, *blocks)


def attention_backward(at, pos, queries, grads, attended, lse, cosine, sine, blocks, size, heads):
    wide, rows = queries.shape
    count = wide // size
    whole = pl.BlockSpec((2 * size, rows), lambda i, r: (0, 0))
    table = pl.BlockSpec((size // 2, rows), lambda i, r: (0, 0))
    some = pl.BlockSpec((heads * size, rows), lambda i, r: (i, 0))
    return pl.pallas_call(
        functools.partial(backward_kernel, heads, size),
        out_shape=(
            jax.ShapeDtypeStruct((wide, rows), LOW),
            jax.ShapeDtypeStruct((2 * size, rows), jnp.float32),
        )
        + (jax.ShapeDtypeStruct((2 * size, rows), LOW),) * (SPAN - 1),
        grid_spec=pltpu.PrefetchScalarGridSpec(
            num_scalar_prefetch=1,
            grid=(count // heads,),
            in_specs=[
                pl.BlockSpec((1, rows), lambda i, r: (0, 0)),
                some,
                some,
                some,
                pl.BlockSpec((heads, 1, rows), lambda i, r: (i, 0, 0)),
                table,
                table,
            ]
            + [whole] * SPAN,
            out_specs=[some] + [whole] * SPAN,
            scratch_shapes=[
                pltpu.VMEM((SPAN, rows, size), LOW),
                pltpu.VMEM((SPAN, rows, size), LOW),
                pltpu.VMEM((heads, size, rows), jnp.float32),
                pltpu.VMEM((SPAN, 2 * size, rows), jnp.float32),
                pltpu.VMEM((heads * size, rows), LOW),
                pltpu.VMEM((heads * size, rows), LOW),
            ],
        ),
        compiler_params=pltpu.CompilerParams(vmem_limit_bytes=24 << 20),
        cost_estimate=pl.CostEstimate(
            flops=48 * wide * rows * rows * SPAN,
            bytes_accessed=10 * wide * rows,
            transcendentals=0,
        ),
        name="attention_backward",
    )(at, pos, *in_hbm(queries, grads, attended, lse, cosine, sine, *blocks))


def take(values, start, size, dim):
    starts = [np.uint32(0)] * values.ndim
    starts[dim] = start
    sizes = list(values.shape)
    sizes[dim] = size
    return lax.dynamic_slice(values, starts, sizes)


def pick(values, places, blocks, dim):
    size = values.shape[dim] // blocks
    return jnp.concatenate(
        [lax.dynamic_slice_in_dim(values, p * size, size, dim) for p in places], dim
    )


class Table:
    def __init__(self, **parts):
        self.begin, at = {}, 0
        for name, part in parts.items():
            self.begin[name] = at
            at += part.shape[0]
        self.values = jnp.concatenate([p.astype(jnp.int32) for p in parts.values()])

    def list(self, name, lo, hi):
        return [self.values[self.begin[name] + j] for j in range(lo, hi)]


def after(value, *others):
    return lax.optimization_barrier((value, *others))[0]


def parity_sum(terms, dim):
    count = lax.axis_size("dp")
    groups = [list(range(p, count, 2)) for p in range(2)]
    return lax.psum_scatter(
        terms.astype(LOW), "dp", scatter_dimension=dim, axis_index_groups=groups, tiled=True
    )


def terms_kernel(transposed, places, x, x_far, g, g_far, out):
    del places
    side = 1 if transposed else 0
    out[...] = (dot(x[...], g[...], 0, side) + dot(x_far[...], g_far[...], 0, side)).astype(LOW)


def weight_terms(table, name, far, lo, hi, x, x_far, g, g_far, transposed=False, keep=True):
    count = hi - lo
    size = x.shape[1] // lax.axis_size("dp")
    rows = x.shape[0]
    units = g.shape[0] if transposed else g.shape[1]
    if size % 128:
        side = 1 if transposed else 0
        mine = pick(x, table.list(name, lo, hi), x.shape[1] // size, 1)
        theirs = pick(x_far, table.list(far, lo, hi), x_far.shape[1] // size, 1)
        return (dot(mine, g, 0, side) + dot(theirs, g_far, 0, side)).astype(LOW)
    whole = pl.BlockSpec(g.shape, lambda i, p: (0, 0))
    begin, far_begin = table.begin[name] + lo, table.begin[far] + lo
    return pl.pallas_call(
        functools.partial(terms_kernel, transposed),
        out_shape=(jax.ShapeDtypeStruct if keep else pltpu.HBM)((count * size, units), LOW),
        grid_spec=pltpu.PrefetchScalarGridSpec(
            num_scalar_prefetch=1,
            grid=(count,),
            in_specs=[
                pl.BlockSpec((rows, size), lambda i, p: (0, p[begin + i])),
                pl.BlockSpec((rows, size), lambda i, p: (0, p[far_begin + i])),
                whole,
                whole,
            ],
            out_specs=pl.BlockSpec((size, units), lambda i, p: (i, 0)),
        ),
        compiler_params=pltpu.CompilerParams(vmem_limit_bytes=20 << 20),
        cost_estimate=pl.CostEstimate(
            flops=40 * rows * count * size * units, bytes_accessed=4 * rows * units, transcendentals=0
        ),
        name="weight_terms",
    )(table.values, x, x_far, g, g_far)


def copy_kernel(places, source, target):
    del places
    target[...] = source[...]


def pick_columns(table, name, values, part=None, parts=1):
    blocks = lax.axis_size("dp")
    rows, count = values.shape[0] // parts, blocks // 2
    size = values.shape[1] // blocks
    if size % 128:
        if part is not None:
            values = lax.dynamic_slice_in_dim(values, table.list(part, 0, 1)[0] * rows, rows, 0)
        return pick(values, table.list(name, 0, count), blocks, 1)
    begin = table.begin[name]
    row = 0 if part is None else table.begin[part]
    return pl.pallas_call(
        copy_kernel,
        out_shape=jax.ShapeDtypeStruct((rows, count * size), values.dtype),
        grid_spec=pltpu.PrefetchScalarGridSpec(
            num_scalar_prefetch=1,
            grid=(count,),
            in_specs=[
                pl.BlockSpec(
                    (rows, size), lambda i, p: (0 if part is None else p[row], p[begin + i])
                )
            ],
            out_specs=pl.BlockSpec((rows, size), lambda i, p: (0, i)),
        ),
        compiler_params=pltpu.CompilerParams(vmem_limit_bytes=8 << 20),
        cost_estimate=pl.CostEstimate(
            flops=65536 * rows * count * size, bytes_accessed=4 * rows * count * size, transcendentals=0
        ),
        name="pick_columns",
    )(table.values, values)


def load_kernel(*refs):
    *pairs, sems = refs
    half = len(pairs) // 2
    copies = [
        pltpu.make_async_copy(source, target, sems.at[j])
        for j, (source, target) in enumerate(zip(pairs[:half], pairs[half:]))
    ]
    for copy in copies:
        copy.start()
    for copy in copies:
        copy.wait()


def load_weights(*weights):
    return pl.pallas_call(
        load_kernel,
        out_shape=tuple(pltpu.VMEM(w.shape, w.dtype) for w in weights),
        in_specs=[pl.BlockSpec(memory_space=pl.ANY)] * len(weights),
        out_specs=[pl.BlockSpec(memory_space=pltpu.VMEM)] * len(weights),
        scratch_shapes=[pltpu.SemaphoreType.DMA((len(weights),))],
        compiler_params=pltpu.CompilerParams(vmem_limit_bytes=2 << 20),
        cost_estimate=pl.CostEstimate(
            flops=20_000_000_000,
            bytes_accessed=2 * sum(w.size for w in weights),
            transcendentals=0,
        ),
        name="load_weights",
    )(*in_hbm(*weights))


def in_vmem(*arrays):
    return [pltpu.with_memory_space_constraint(a, pltpu.VMEM) for a in arrays]


def ffn_kernel(rows, gate_w, up_w, grad_in, hidden, grad_gate, grad_up):
    step = 128
    for begin in range(0, hidden.shape[1], step):
        cut = slice(begin, begin + step)
        both = dot(rows[...], jnp.concatenate([gate_w[:, cut], up_w[:, cut]], 1), 1, 0)
        gate, up = both[:, :step], both[:, step:]
        grad = grad_in[:, cut]
        sigma = jax.nn.sigmoid(gate)
        active = gate * sigma
        hidden[:, cut] = (active * up).astype(LOW)
        grad_gate[:, cut] = (grad * up * sigma * (1.0 + gate * (1.0 - sigma))).astype(LOW)
        grad_up[:, cut] = (grad * active).astype(LOW)


def feed_forward(rows, w_gate, w_up, grad_hidden):
    count, width = rows.shape
    units = w_gate.shape[1]
    here = pl.BlockSpec(memory_space=pltpu.VMEM)
    return pl.pallas_call(
        ffn_kernel,
        out_shape=(jax.ShapeDtypeStruct((count, units), LOW),) * 3,
        in_specs=[here] * 4,
        out_specs=[here] * 3,
        compiler_params=pltpu.CompilerParams(vmem_limit_bytes=20 << 20),
        cost_estimate=pl.CostEstimate(
            flops=6 * count * width * units,
            bytes_accessed=4 * width * units,
            transcendentals=count * units,
        ),
        name="feed_forward",
    )(*in_vmem(rows, w_gate, w_up, grad_hidden))


def back_kernel(gate_rows, up_rows, gate_w, up_w, out):
    step = out.shape[1]
    cut = pl.ds(pl.multiple_of(pl.program_id(0) * step, step), step)
    total = dot(gate_rows[...], gate_w[cut, :], 1, 1) + dot(up_rows[...], up_w[cut, :], 1, 1)
    out[...] = total.astype(out.dtype)


def feed_forward_back(grad_gate, grad_up, w_gate, w_up, half, kind):
    count, units = grad_gate.shape
    width = w_gate.shape[0]
    step = width // 2
    rows = pl.BlockSpec((count // 2, units), lambda i: (half, 0))
    here = pl.BlockSpec(memory_space=pltpu.VMEM)
    return pl.pallas_call(
        back_kernel,
        out_shape=jax.ShapeDtypeStruct((count // 2, width), kind),
        grid=(2,),
        in_specs=[rows, rows, here, here],
        out_specs=pl.BlockSpec((count // 2, step), lambda i: (0, i)),
        compiler_params=pltpu.CompilerParams(vmem_limit_bytes=16 << 20),
        cost_estimate=pl.CostEstimate(
            flops=10 * count * width * units, bytes_accessed=4 * width * units, transcendentals=0
        ),
        name="feed_forward_back",
    )(grad_gate, grad_up, *in_vmem(w_gate, w_up))


def join_kernel(places, first, second, out):
    del places

    @pl.when(pl.program_id(0) == 0)
    def _():
        out[...] = first[...]

    @pl.when(pl.program_id(0) == 1)
    def _():
        out[...] = second[...]


def join_rows(table, first, second):
    rows, width = first.shape
    core = table.begin["core"]
    whole = pl.BlockSpec((rows, width), lambda i, p: (0, 0))
    return pl.pallas_call(
        join_kernel,
        out_shape=jax.ShapeDtypeStruct((2 * rows, width), first.dtype),
        grid_spec=pltpu.PrefetchScalarGridSpec(
            num_scalar_prefetch=1,
            grid=(2,),
            in_specs=[whole, whole],
            out_specs=pl.BlockSpec((rows, width), lambda i, p: (p[core] ^ i, 0)),
        ),
        compiler_params=pltpu.CompilerParams(vmem_limit_bytes=8 << 20),
        cost_estimate=pl.CostEstimate(
            flops=1_000_000_000, bytes_accessed=8 * rows * width, transcendentals=0
        ),
        name="join_rows",
    )(table.values, first, second)


def row_kernel(left, right, send, kept):
    half = left.shape[0] // 2
    send[...] = dot(left[half:, :], right[...], 1, 0).astype(LOW)
    kept[...] = dot(left[:half, :], right[...], 1, 0)


def row_terms(left, right):
    rows, units = left.shape
    half, width = rows // 2, right.shape[1]
    step = 256
    return pl.pallas_call(
        row_kernel,
        out_shape=(
            jax.ShapeDtypeStruct((half, width), LOW),
            jax.ShapeDtypeStruct((half, width), jnp.float32),
        ),
        grid=(width // step,),
        in_specs=[
            pl.BlockSpec((rows, units), lambda i: (0, 0)),
            pl.BlockSpec((units, step), lambda i: (0, i)),
        ],
        out_specs=[pl.BlockSpec((half, step), lambda i: (0, i))] * 2,
        compiler_params=pltpu.CompilerParams(vmem_limit_bytes=16 << 20),
        cost_estimate=pl.CostEstimate(
            flops=8 * rows * units * width, bytes_accessed=2 * units * width, transcendentals=0
        ),
        name="row_terms",
    )(left, right)


def turn(values, cosine, sine):
    half = cosine.shape[0]
    heads = values.shape[0] // (2 * half)
    pieces = values.reshape(heads, 2, half, values.shape[1])
    first, second = pieces[:, 0], pieces[:, 1]
    return jnp.stack(
        [first * cosine - second * sine, second * cosine + first * sine], 1
    ).reshape(values.shape)


def turn_back(grads, cosine, sine):
    return turn(grads, cosine, -sine)


def norm_back(grad_rows, values, scale_rows, gain):
    scaled = grad_rows * gain
    inner_mean = jnp.mean(scaled * values, -1, keepdims=True)
    return (
        scale_rows * (scaled - values * scale_rows * scale_rows * inner_mean),
        jnp.sum(grad_rows * values * scale_rows, 0),
    )


def shards(
    tokens,
    positions,
    norm1_gain,
    w_query,
    w_key,
    w_value,
    w_out,
    norm2_gain,
    w_gate,
    w_up,
    w_down,
    cotangent,
):
    rows_here, width = tokens.shape
    size = w_key.shape[1]
    dp = lax.axis_size("dp")
    tp_count = len(ROW_MASKS)
    own_rows = rows_here // tp_count
    block = width // dp
    bits = dp.bit_length() - 1
    half_count = dp // 2

    def exchange_order(order):
        return np.array(
            [
                sum(((j >> (len(order) - 1 - k)) & 1) << b for k, b in enumerate(order))
                for j in range(1 << len(order))
            ],
            np.int32,
        )

    down_bits = [0] + list(range(2, bits))
    rest_bits = list(range(1, bits))

    place = lax.axis_index("dp").astype(jnp.int32)
    spot = lax.axis_index("tp").astype(jnp.int32)
    natural = np.arange(half_count, dtype=np.int32)
    down_here, rest_here = place ^ exchange_order(down_bits), place ^ exchange_order(rest_bits)
    gain_bits = rest_bits[::-1]
    gain_here = place ^ exchange_order(gain_bits)
    table = Table(
        mine=2 * natural + (place & 1),
        theirs=2 * natural + (1 - (place & 1)),
        natural=jnp.asarray(natural),
        down=down_here,
        down_far=down_here ^ 2,
        rest=rest_here,
        gain=gain_here,
        gain_far=gain_here ^ 1,
        rest_block=rest_here >> 1,
        core=(spot & 1)[None],
    )
    at = jnp.stack([place & (SPAN - 1), spot])
    row_starts = [((spot ^ m) * own_rows).astype(jnp.uint32) for m in ROW_MASKS]
    core_starts = [(c * (rows_here // 2)).astype(jnp.uint32) for c in (spot & 1, 1 - (spot & 1))]
    tokens, table.values, at, row_starts, core_starts = lax.optimization_barrier(
        (tokens, table.values, at, row_starts, core_starts)
    )
    pos = positions.reshape(1, rows_here)

    def own(values):
        return take(values, row_starts[0], own_rows, 0)

    inputs = tokens.astype(jnp.float32)
    scale_one = lax.rsqrt(jnp.mean(inputs * inputs, -1, keepdims=True) + EPSILON)
    normed_one = (inputs * scale_one * norm1_gain).astype(LOW)
    half = size // 2
    frequency = jnp.exp(
        -jnp.log(10000.0) * (2.0 * jnp.arange(half, dtype=jnp.float32) / size)
    )
    angles = frequency[:, None] * positions.astype(jnp.float32)[None, :]
    cosine, sine = jnp.cos(angles), jnp.sin(angles)
    w_kv = jnp.concatenate([w_key.T, w_value.T], 0)
    paired = dot(w_kv, normed_one, 1, 1)
    paired = jnp.concatenate([turn(paired[:size], cosine, sine), paired[size:]], 0).astype(LOW)
    blocks = [paired] + [flip(paired, "dp", m) for m in range(1, SPAN)]
    queries = (turn(dot(w_query, normed_one, 0, 1), cosine, sine) * size ** (-0.5)).astype(LOW)

    wide = w_query.shape[1]

    def near_sum(part):
        send = part(2, 4).astype(LOW)
        near, kept = lax.optimization_barrier((flip(send, "tp", 1), part(0, 2)))
        pair = kept + near
        return pair[:own_rows], pair[own_rows:].astype(LOW)

    attended, lse = attention_forward(at, pos, queries, blocks, size, 8)

    branch, branch_out = near_sum(
        lambda lo, hi: dot(attended[:, lo * own_rows : hi * own_rows], w_out, 0, 0)
    )
    branch_far = flip(branch_out, "tp", 2)
    cot = jnp.concatenate(
        [take(after(cotangent, branch_out), start, own_rows, 0) for start in row_starts], 0
    )
    cot_send = pick_columns(table, "down_far", cot)
    cot_theirs = flip(cot_send, "dp", 2)
    own_inputs = own(tokens).astype(jnp.float32)
    one_send = pick_columns(table, "theirs", after(normed_one, cot_send), "core", 2)
    one_near = flip(one_send, "dp", 1)
    grad_hidden = dot(after(cot, one_send), w_down, 1, 1)
    middle = own_inputs + (after(branch, grad_hidden) + branch_far)

    scale_two = lax.rsqrt(jnp.mean(middle * middle, -1, keepdims=True) + EPSILON)
    own_two = (middle * scale_two * norm2_gain).astype(LOW)
    far_two = flip(own_two, "tp", 2)
    gate_w, up_w = load_weights(after(w_gate, own_two), w_up)
    pair_two = jnp.concatenate([after(own_two, gate_w), far_two], 0)
    core_two = flip(pair_two, "tp", 1)
    two_send = pick_columns(table, "theirs", pair_two)
    two_near = flip(two_send, "dp", 1)
    normed_two = jnp.concatenate([after(pair_two, two_send), core_two], 0)

    hidden, grad_gate_pre, grad_up_pre = feed_forward(normed_two, gate_w, up_w, grad_hidden)
    gate_theirs = flip(grad_gate_pre, "dp", 1)
    hidden_theirs = flip(hidden, "dp", 2)
    up_theirs = flip(grad_up_pre, "dp", 1)
    gate_late, cot_theirs, one_near = lax.optimization_barrier((grad_gate_pre, cot_theirs, one_near))

    two_back = functools.partial(feed_forward_back, gate_late, grad_up_pre, gate_w, up_w)
    grad_normed_two, two_out = near_sum(
        lambda lo, hi: two_back(lo // 2, jnp.float32 if lo == 0 else LOW)
    )
    two_out, two_near = lax.optimization_barrier((two_out, two_near))
    two_far = flip(two_out, "tp", 2)
    cores = jnp.concatenate([two_near, one_near], 1)
    cores_far = flip(cores, "tp", 1)
    two_theirs = jnp.concatenate([two_near, cores_far[:, : width // 2]], 0)

    down_near, down = row_terms(after(hidden, two_out), w_down)
    grad_normed_two = after(grad_normed_two, down) + two_far

    grad_mid_norm, gain_two = norm_back(grad_normed_two, middle, scale_two, norm2_gain)
    grad_middle = own(cotangent).astype(jnp.float32) + grad_mid_norm
    branch_grad = grad_middle.astype(LOW)
    grad_far = flip(branch_grad, "tp", 2)

    down_near = flip(after(down_near, branch_grad), "tp", 1)
    gate_terms = weight_terms(
        table,
        "mine",
        "natural",
        0,
        half_count,
        after(normed_two, branch_grad),
        two_theirs,
        grad_gate_pre,
        gate_theirs,
        keep=False,
    )
    grad_gate = parity_sum(gate_terms, 0)
    grad_pair = jnp.concatenate([after(branch_grad, gate_terms), grad_far], 0)
    grad_core = flip(grad_pair, "tp", 1)
    branch_send = pick_columns(table, "theirs", grad_pair)
    att_theirs = flip(after(attended, branch_send), "dp", 1)

    def near_flip(terms, bit):
        half = terms.shape[0] // 2
        return [flip(terms[half:], "dp", 1 << bit), flip(terms[:half], "dp", 1 << bit)]

    def down_terms(lo, hi, *late):
        g = after(hidden, *late)
        return weight_terms(table, "down", "natural", lo, hi, cot, cot_theirs, g, hidden_theirs)

    down_sent = down_terms(half_count // 2, half_count, branch_send)
    half = down_sent.shape[0] // 2
    down_first = flip(down_sent[half:], "dp", 1)
    branch_all = jnp.concatenate([after(grad_pair, down_sent), grad_core], 0)
    grad_attended = dot(w_out, branch_all, 1, 1).astype(LOW)
    grads = attention_backward(
        at, pos, queries, grad_attended, attended, lse, cosine, sine, blocks, size, 2
    )
    grad_query_rows, kv_total = grads[0], grads[1]
    *kv_sends, att_theirs = lax.optimization_barrier((*grads[2:], att_theirs))
    kv_back = [flip(kv_sends[m - 1], "dp", m) for m in range(1, SPAN)]

    def rest_terms(lo, hi, x, x_far, g, g_far, transposed=False):
        return weight_terms(
            table, "rest", "rest_block", lo, hi, x, x_far, g, g_far, transposed
        )

    down = down + after(down_near, grad_query_rows)
    down, down_out = down[:own_rows], down[own_rows:].astype(LOW)
    down_far = flip(down_out, "tp", 2)

    def up_terms(lo, hi, *late):
        return rest_terms(lo, hi, normed_two, two_theirs, after(grad_up_pre, *late), up_theirs)

    up_sent = up_terms(half_count // 2, half_count, grad_query_rows)
    up_first = flip(up_sent[half:], "dp", 2)

    def exchange_mid(terms, first, order, *late):
        got, left = [first], half_count // 2
        for b in order[1:]:
            send = terms(left // 2, left, *late).astype(jnp.float32)
            rows = send.shape[0]
            for other in got:
                send = send + other[other.shape[0] - rows :]
            send = send.astype(LOW)
            got.append(flip(send, "dp", 1 << b))
            left //= 2
        return got[1:], send

    down_late, down_last = exchange_mid(down_terms, down_first, down_bits, grad_query_rows)
    kv_total, grad_gate = lax.optimization_barrier(
        (kv_total, grad_gate, up_sent, down_out, down_last)
    )[:2]
    for back in kv_back:
        kv_total = kv_total + back
    key_grad = turn_back(kv_total[:size], cosine, sine)
    grad_kv_rows = jnp.concatenate([key_grad, kv_total[size:]], 0).astype(LOW)
    proj_rows = jnp.concatenate([grad_query_rows, grad_kv_rows], 0)
    units = proj_rows.shape[0]
    pieces = [
        branch_send[:, begin : begin + rows_here] for begin in range(0, branch_send.shape[1], rows_here)
    ]
    both_theirs = flip(jnp.concatenate([proj_rows, *pieces], 0), "dp", 1)

    own_order = jnp.concatenate(
        [take(proj_rows, start, own_rows, 1) for start in row_starts], 1
    )

    def one_terms(lo, hi):
        cut = own_order[:, lo * own_rows : hi * own_rows]
        return dot(cut[:wide], w_query, 0, 1) + dot(cut[wide:], w_kv, 0, 0)

    grad_normed_one, one_out = near_sum(one_terms)
    one_far = flip(one_out, "tp", 2)
    up_second = flip(after(up_sent[:half], one_out), "dp", 2)
    output_rows = (middle + (down + after(down_far, one_out))).astype(LOW)
    one_theirs = join_rows(table, after(one_near, one_out), cores_far[:, width // 2 :])
    up_kept = up_terms(0, 1, one_out)
    grad_gate = grad_gate.astype(jnp.float32)
    grad_normed_one = after(grad_normed_one, output_rows, up_kept, grad_gate, one_theirs) + one_far
    grad_in_norm, gain_one = norm_back(grad_normed_one, own_inputs, own(scale_one), norm1_gain)
    input_rows = grad_middle + grad_in_norm

    up_late, up_last = exchange_mid(up_terms, up_first, rest_bits, input_rows)
    both_theirs = after(both_theirs, up_last)
    proj_theirs = both_theirs[:units]
    branch_near = jnp.concatenate(
        [
            both_theirs[begin : begin + branch_send.shape[0]]
            for begin in range(units, both_theirs.shape[0], branch_send.shape[0])
        ],
        1,
    )
    branch_theirs = jnp.concatenate([branch_near, flip(branch_near, "tp", 1)], 0)
    *down_late, up_last = lax.optimization_barrier((*down_late, up_last))

    out_late, proj_late = lax.optimization_barrier((attended, proj_rows, up_last))[:2]

    def last_terms(lo, hi, *late):
        first, second = after(proj_late, *late), after(out_late, *late)
        return jnp.concatenate(
            [
                rest_terms(lo, hi, normed_one, one_theirs, first, proj_theirs, True),
                rest_terms(lo, hi, branch_all, branch_theirs, second, att_theirs, True),
            ],
            1,
        )

    quarter = half_count // 4
    sent = last_terms(half_count // 2, half_count)
    firsts, seconds = sent[quarter * block :], sent[: quarter * block]
    mids = [flip(firsts, "dp", 2)]
    last_second = flip(after(seconds, firsts), "dp", 2)
    up_late = [*up_late, up_second]
    proj_kept = rest_terms(0, 1, normed_one, one_theirs, after(proj_late, firsts), proj_theirs, True)
    out_kept = rest_terms(0, 1, branch_all, branch_theirs, after(out_late, firsts), att_theirs, True)
    down_kept = down_terms(0, 1, firsts)

    gains = jnp.stack([after(gain_one, firsts), gain_two])
    for m in (1, 2):
        gains = gains + flip(gains, "tp", m)
    gains = pick_columns(table, "gain", gains) + flip(
        pick_columns(table, "gain_far", gains), "dp", 1
    )

    def gain_exchange(gains, bit):
        half = gains.shape[1] // 2
        return gains[:, :half] + flip(gains[:, half:], "dp", 1 << bit)

    gains = gain_exchange(gains, gain_bits[0])
    left = half_count // 2
    for b in rest_bits[1:]:
        count = left // 2
        terms = last_terms(count, left, firsts)
        terms, *up_late = lax.optimization_barrier((terms, *up_late, proj_kept, out_kept, down_kept))[
            :-3
        ]
        send = terms.astype(jnp.float32)
        for other in mids:
            send = send + other[-count * block :]
        send = send.astype(LOW)
        mids.append(flip(send, "dp", 1 << b))
        left = count
    down_second = flip(after(down_sent[:half], send), "dp", 1)
    for b in gain_bits[1:]:
        gains = gain_exchange(after(gains, send), b)

    def ending(kept, *others):
        kept = kept.astype(jnp.float32)
        for other in others:
            kept = kept + other[:block]
        return kept

    down_kept, down_second = lax.optimization_barrier((down_kept, down_second, send))[:2]
    grad_down = ending(down_kept, down_second, *down_late)
    grad_last = ending(
        jnp.concatenate([proj_kept, out_kept], 1), last_second, *mids[1:]
    )
    grad_up = ending(up_kept, *up_late)
    narrow = wide + 2 * size

    return (
        output_rows,
        input_rows,
        gains[0],
        grad_last[:, :wide],
        grad_last[:, wide : wide + size],
        grad_last[:, wide + size : narrow],
        grad_last[:, narrow:].T,
        gains[1],
        grad_gate,
        grad_up,
        grad_down.T,
    )


def solution(mesh):
    placed = (
        P("dp", None),
        P("dp"),
        P(),
        P(None, "tp"),
        P(None, "tp"),
        P(None, "tp"),
        P("tp", None),
        P(),
        P(None, "tp"),
        P(None, "tp"),
        P("tp", None),
        P("dp", None),
    )
    return jax.shard_map(
        shards,
        mesh=mesh,
        in_specs=placed,
        out_specs=(
            P(("dp", "tp"), None),
            P(("dp", "tp"), None),
            P("dp"),
            P("dp", "tp"),
            P("dp", "tp"),
            P("dp", "tp"),
            P("tp", "dp"),
            P("dp"),
            P("dp", "tp"),
            P("dp", "tp"),
            P("tp", "dp"),
        ),
        check_vma=False,
    )
```

```python
import functools

import jax
import jax.numpy as jnp
import numpy as np
from jax import lax
from jax.experimental import pallas as pl
from jax.experimental.pallas import tpu as pltpu
from jax.sharding import PartitionSpec as P

SPAN = 4
EPSILON = 1e-05
FAR_BELOW = -1e30
LOW = jnp.bfloat16
ROW_MASKS = (0, 2, 1, 3)


def flip(block, axis, mask):
    return lax.ppermute(block, axis, [(i, i ^ mask) for i in range(lax.axis_size(axis))])


def dot(left, right, left_dim, right_dim):
    return lax.dot_general(
        left,
        right,
        (((left_dim,), (right_dim,)), ((), ())),
        preferred_element_type=jnp.float32,
    )


def in_hbm(*arrays):
    return [pltpu.with_memory_space_constraint(a, pltpu.HBM) for a in arrays]


def own_mask(pos, begin, keys, queries):
    key_at = lax.broadcasted_iota(jnp.int32, (keys, queries), 0)
    query_at = lax.broadcasted_iota(jnp.int32, (keys, queries), 1) + begin
    return (key_at <= query_at) & (key_at >= query_at - pos)


def row_starts(spot, rows):
    part = rows // len(ROW_MASKS)
    return [pl.multiple_of((spot ^ m) * part, part) for m in ROW_MASKS]


def forward_kernel(
    heads,
    size,
    at_ref,
    pos_ref,
    q_ref,
    kv0,
    kv1,
    kv2,
    kv3,
    o_ref,
    lse_ref,
    keys,
    vals,
    top,
    acc,
    ordered,
):
    rank, spot = at_ref[0], at_ref[1]
    rows = pos_ref.shape[1]
    half = rows // 2

    @pl.when(pl.program_id(0) == 0)
    def _():
        for m, kv in enumerate((kv0, kv1, kv2, kv3)):
            keys[m] = kv[:size, :].T
            vals[m, :size, :] = kv[size:, :]
            vals[m, size:, :] = jnp.ones((16, rows), LOW)

    pos = pos_ref[...]
    for part in range(2):
        cols = slice(part * half, (part + 1) * half)
        count = (part + 1) * half
        mask = own_mask(pos[:, cols], part * half, count, half)
        for h in range(heads):
            scores = dot(keys[0, :count, :], q_ref[h * size : (h + 1) * size, cols], 1, 0)
            scores = jnp.where(mask, scores, FAR_BELOW)
            peak = jnp.max(scores, 0, keepdims=True)
            weights = jnp.exp(scores - peak).astype(LOW)
            acc[h, :, cols] = dot(vals[0, :, :count], weights, 1, 0)
            top[h, :, cols] = peak
    seen = pos > lax.broadcasted_iota(jnp.int32, (1, rows), 1)
    for m in range(1, SPAN):

        @pl.when((rank ^ m) < rank)
        def _():
            for h in range(heads):
                scores = dot(keys[m], q_ref[h * size : (h + 1) * size, :], 1, 0)
                old = top[h]
                peak = jnp.where(seen, jnp.maximum(old, jnp.max(scores, 0, keepdims=True)), old)
                weights = jnp.exp(scores - jnp.where(seen, peak, -FAR_BELOW)).astype(LOW)
                acc[h] = acc[h] * jnp.exp(old - peak) + dot(vals[m], weights, 1, 0)
                top[h] = peak

    for h in range(heads):
        total = acc[h, size : size + 1, :]
        ordered[h * size : (h + 1) * size, :] = (acc[h, :size, :] / total).astype(LOW)
        lse_ref[h] = top[h] + jnp.log(total)
    for j, start in enumerate(row_starts(spot, rows)):
        part = rows // len(ROW_MASKS)
        o_ref[:, j * part : (j + 1) * part] = ordered[:, pl.ds(start, part)]


def backward_kernel(
    heads,
    size,
    at_ref,
    pos_ref,
    q_ref,
    do_in,
    o_in,
    lse_ref,
    cos_ref,
    sin_ref,
    kv0,
    kv1,
    kv2,
    kv3,
    dq_ref,
    g0,
    g1,
    g2,
    g3,
    keys,
    vals,
    dq,
    total,
    do_ref,
    o_ref,
):
    rank, spot = at_ref[0], at_ref[1]
    rows = pos_ref.shape[1]
    half = rows // 2
    blocks = (kv0, kv1, kv2, kv3)
    step = pl.program_id(0)

    @pl.when(step == 0)
    def _():
        for m, kv in enumerate(blocks):
            keys[m] = kv[:size, :].T
            vals[m] = kv[size:, :].T
        total[...] = jnp.zeros_like(total)

    part = rows // len(ROW_MASKS)
    for j, start in enumerate(row_starts(spot, rows)):
        do_ref[:, pl.ds(start, part)] = do_in[:, j * part : (j + 1) * part]
        o_ref[:, pl.ds(start, part)] = o_in[:, j * part : (j + 1) * part]
    pos = pos_ref[...]
    seen = pos > lax.broadcasted_iota(jnp.int32, (1, rows), 1)
    deltas = []
    for h in range(heads):
        span = slice(h * size, (h + 1) * size)
        deltas.append(
            jnp.sum(
                do_ref[span, :].astype(jnp.float32) * o_ref[span, :].astype(jnp.float32),
                0,
                keepdims=True,
            )
        )
    for part in range(2):
        cols = slice(part * half, (part + 1) * half)
        count = (part + 1) * half
        mask = own_mask(pos[:, cols], part * half, count, half)
        for h in range(heads):
            span = slice(h * size, (h + 1) * size)
            query, grad = q_ref[span, cols], do_ref[span, cols]
            scores = dot(keys[0, :count, :], query, 1, 0)
            probs = jnp.exp(jnp.where(mask, scores, FAR_BELOW) - lse_ref[h, :, cols])
            grad_probs = dot(vals[0, :count, :], grad, 1, 0)
            grad_scores = (probs * (grad_probs - deltas[h][:, cols])).astype(LOW)
            total[0, :size, :count] += dot(query, grad_scores, 1, 1)
            total[0, size:, :count] += dot(grad, probs.astype(LOW), 1, 1)
            dq[h, :, cols] = dot(kv0[:size, :count], grad_scores, 1, 0)
    for m in range(1, SPAN):

        @pl.when((rank ^ m) < rank)
        def _():
            for h in range(heads):
                span = slice(h * size, (h + 1) * size)
                query, grad = q_ref[span, :], do_ref[span, :]
                scores = dot(keys[m], query, 1, 0)
                probs = jnp.exp(scores - jnp.where(seen, lse_ref[h], -FAR_BELOW))
                grad_probs = dot(vals[m], grad, 1, 0)
                grad_scores = (probs * (grad_probs - deltas[h])).astype(LOW)
                total[m, :size, :] += dot(query, grad_scores, 1, 1)
                total[m, size:, :] += dot(grad, probs.astype(LOW), 1, 1)
                dq[h] += dot(blocks[m][:size, :], grad_scores, 1, 0)

    middle_at = size // 2
    cosine, sine = cos_ref[...], sin_ref[...]
    for h in range(heads):
        first = dq[h, :middle_at, :] * size ** (-0.5)
        second = dq[h, middle_at:, :] * size ** (-0.5)
        base = h * size
        dq_ref[base : base + middle_at, :] = (first * cosine + second * sine).astype(LOW)
        dq_ref[base + middle_at : base + size, :] = (second * cosine - first * sine).astype(LOW)

    @pl.when(step == pl.num_programs(0) - 1)
    def _():
        g0[...] = total[0]
        for m, out in ((1, g1), (2, g2), (3, g3)):
            out[...] = total[m].astype(LOW)


def attention_forward(at, pos, queries, blocks, size, heads):
    wide, rows = queries.shape
    count = wide // size
    whole = pl.BlockSpec((2 * size, rows), lambda i, r: (0, 0))
    some = pl.BlockSpec((heads * size, rows), lambda i, r: (i, 0))
    return pl.pallas_call(
        functools.partial(forward_kernel, heads, size),
        out_shape=(
            jax.ShapeDtypeStruct((wide, rows), LOW),
            jax.ShapeDtypeStruct((count, 1, rows), jnp.float32),
        ),
        grid_spec=pltpu.PrefetchScalarGridSpec(
            num_scalar_prefetch=1,
            grid=(count // heads,),
            in_specs=[pl.BlockSpec((1, rows), lambda i, r: (0, 0)), some] + [whole] * SPAN,
            out_specs=[some, pl.BlockSpec((heads, 1, rows), lambda i, r: (i, 0, 0))],
            scratch_shapes=[
                pltpu.VMEM((SPAN, rows, size), LOW),
                pltpu.VMEM((SPAN, size + 16, rows), LOW),
                pltpu.VMEM((heads, 1, rows), jnp.float32),
                pltpu.VMEM((heads, size + 16, rows), jnp.float32),
                pltpu.VMEM((heads * size, rows), LOW),
            ],
        ),
        compiler_params=pltpu.CompilerParams(vmem_limit_bytes=24 << 20),
        cost_estimate=pl.CostEstimate(
            flops=32 * wide * rows * rows * SPAN,
            bytes_accessed=4 * wide * rows,
            transcendentals=0,
        ),
        name="attention_forward",
    )(at, pos, queries, *blocks)


def attention_backward(at, pos, queries, grads, attended, lse, cosine, sine, blocks, size, heads):
    wide, rows = queries.shape
    count = wide // size
    whole = pl.BlockSpec((2 * size, rows), lambda i, r: (0, 0))
    table = pl.BlockSpec((size // 2, rows), lambda i, r: (0, 0))
    some = pl.BlockSpec((heads * size, rows), lambda i, r: (i, 0))
    return pl.pallas_call(
        functools.partial(backward_kernel, heads, size),
        out_shape=(
            jax.ShapeDtypeStruct((wide, rows), LOW),
            jax.ShapeDtypeStruct((2 * size, rows), jnp.float32),
        )
        + (jax.ShapeDtypeStruct((2 * size, rows), LOW),) * (SPAN - 1),
        grid_spec=pltpu.PrefetchScalarGridSpec(
            num_scalar_prefetch=1,
            grid=(count // heads,),
            in_specs=[
                pl.BlockSpec((1, rows), lambda i, r: (0, 0)),
                some,
                some,
                some,
                pl.BlockSpec((heads, 1, rows), lambda i, r: (i, 0, 0)),
                table,
                table,
            ]
            + [whole] * SPAN,
            out_specs=[some] + [whole] * SPAN,
            scratch_shapes=[
                pltpu.VMEM((SPAN, rows, size), LOW),
                pltpu.VMEM((SPAN, rows, size), LOW),
                pltpu.VMEM((heads, size, rows), jnp.float32),
                pltpu.VMEM((SPAN, 2 * size, rows), jnp.float32),
                pltpu.VMEM((heads * size, rows), LOW),
                pltpu.VMEM((heads * size, rows), LOW),
            ],
        ),
        compiler_params=pltpu.CompilerParams(vmem_limit_bytes=24 << 20),
        cost_estimate=pl.CostEstimate(
            flops=48 * wide * rows * rows * SPAN,
            bytes_accessed=10 * wide * rows,
            transcendentals=0,
        ),
        name="attention_backward",
    )(at, pos, *in_hbm(queries, grads, attended, lse, cosine, sine, *blocks))


def take(values, start, size, dim):
    starts = [np.uint32(0)] * values.ndim
    starts[dim] = start
    sizes = list(values.shape)
    sizes[dim] = size
    return lax.dynamic_slice(values, starts, sizes)


def pick(values, places, blocks, dim):
    size = values.shape[dim] // blocks
    return jnp.concatenate(
        [lax.dynamic_slice_in_dim(values, p * size, size, dim) for p in places], dim
    )


class Table:
    def __init__(self, **parts):
        self.begin, at = {}, 0
        for name, part in parts.items():
            self.begin[name] = at
            at += part.shape[0]
        self.values = jnp.concatenate([p.astype(jnp.int32) for p in parts.values()])

    def list(self, name, lo, hi):
        return [self.values[self.begin[name] + j] for j in range(lo, hi)]


def after(value, *others):
    return lax.optimization_barrier((value, *others))[0]


def parity_sum(terms, dim):
    count = lax.axis_size("dp")
    groups = [list(range(p, count, 2)) for p in range(2)]
    return lax.psum_scatter(
        terms.astype(LOW), "dp", scatter_dimension=dim, axis_index_groups=groups, tiled=True
    )


def terms_kernel(transposed, places, x, x_far, g, g_far, out):
    del places
    side = 1 if transposed else 0
    out[...] = (dot(x[...], g[...], 0, side) + dot(x_far[...], g_far[...], 0, side)).astype(LOW)


def weight_terms(table, name, far, lo, hi, x, x_far, g, g_far, transposed=False, keep=True):
    count = hi - lo
    size = x.shape[1] // lax.axis_size("dp")
    rows = x.shape[0]
    units = g.shape[0] if transposed else g.shape[1]
    if size % 128:
        side = 1 if transposed else 0
        mine = pick(x, table.list(name, lo, hi), x.shape[1] // size, 1)
        theirs = pick(x_far, table.list(far, lo, hi), x_far.shape[1] // size, 1)
        return (dot(mine, g, 0, side) + dot(theirs, g_far, 0, side)).astype(LOW)
    whole = pl.BlockSpec(g.shape, lambda i, p: (0, 0))
    begin, far_begin = table.begin[name] + lo, table.begin[far] + lo
    return pl.pallas_call(
        functools.partial(terms_kernel, transposed),
        out_shape=(jax.ShapeDtypeStruct if keep else pltpu.HBM)((count * size, units), LOW),
        grid_spec=pltpu.PrefetchScalarGridSpec(
            num_scalar_prefetch=1,
            grid=(count,),
            in_specs=[
                pl.BlockSpec((rows, size), lambda i, p: (0, p[begin + i])),
                pl.BlockSpec((rows, size), lambda i, p: (0, p[far_begin + i])),
                whole,
                whole,
            ],
            out_specs=pl.BlockSpec((size, units), lambda i, p: (i, 0)),
        ),
        compiler_params=pltpu.CompilerParams(vmem_limit_bytes=20 << 20),
        cost_estimate=pl.CostEstimate(
            flops=24 * rows * count * size * units, bytes_accessed=4 * rows * units, transcendentals=0
        ),
        name="weight_terms",
    )(table.values, x, x_far, g, g_far)


def copy_kernel(places, source, target):
    del places
    target[...] = source[...]


def pick_columns(table, name, values, part=None, parts=1):
    blocks = lax.axis_size("dp")
    rows, count = values.shape[0] // parts, blocks // 2
    size = values.shape[1] // blocks
    if size % 128:
        if part is not None:
            values = lax.dynamic_slice_in_dim(values, table.list(part, 0, 1)[0] * rows, rows, 0)
        return pick(values, table.list(name, 0, count), blocks, 1)
    begin = table.begin[name]
    row = 0 if part is None else table.begin[part]
    return pl.pallas_call(
        copy_kernel,
        out_shape=jax.ShapeDtypeStruct((rows, count * size), values.dtype),
        grid_spec=pltpu.PrefetchScalarGridSpec(
            num_scalar_prefetch=1,
            grid=(count,),
            in_specs=[
                pl.BlockSpec(
                    (rows, size), lambda i, p: (0 if part is None else p[row], p[begin + i])
                )
            ],
            out_specs=pl.BlockSpec((rows, size), lambda i, p: (0, i)),
        ),
        compiler_params=pltpu.CompilerParams(vmem_limit_bytes=8 << 20),
        cost_estimate=pl.CostEstimate(
            flops=65536 * rows * count * size, bytes_accessed=4 * rows * count * size, transcendentals=0
        ),
        name="pick_columns",
    )(table.values, values)


def load_kernel(*refs):
    *pairs, sems = refs
    half = len(pairs) // 2
    copies = [
        pltpu.make_async_copy(source, target, sems.at[j])
        for j, (source, target) in enumerate(zip(pairs[:half], pairs[half:]))
    ]
    for copy in copies:
        copy.start()
    for copy in copies:
        copy.wait()


def load_weights(*weights):
    return pl.pallas_call(
        load_kernel,
        out_shape=tuple(pltpu.VMEM(w.shape, w.dtype) for w in weights),
        in_specs=[pl.BlockSpec(memory_space=pl.ANY)] * len(weights),
        out_specs=[pl.BlockSpec(memory_space=pltpu.VMEM)] * len(weights),
        scratch_shapes=[pltpu.SemaphoreType.DMA((len(weights),))],
        compiler_params=pltpu.CompilerParams(vmem_limit_bytes=2 << 20),
        cost_estimate=pl.CostEstimate(
            flops=20_000_000_000,
            bytes_accessed=2 * sum(w.size for w in weights),
            transcendentals=0,
        ),
        name="load_weights",
    )(*in_hbm(*weights))


def in_vmem(*arrays):
    return [pltpu.with_memory_space_constraint(a, pltpu.VMEM) for a in arrays]


def ffn_kernel(rows, gate_w, up_w, grad_in, hidden, grad_gate, grad_up):
    step = 128
    for begin in range(0, hidden.shape[1], step):
        cut = slice(begin, begin + step)
        both = dot(rows[...], jnp.concatenate([gate_w[:, cut], up_w[:, cut]], 1), 1, 0)
        gate, up = both[:, :step], both[:, step:]
        grad = grad_in[:, cut]
        sigma = jax.nn.sigmoid(gate)
        active = gate * sigma
        hidden[:, cut] = (active * up).astype(LOW)
        grad_gate[:, cut] = (grad * up * sigma * (1.0 + gate * (1.0 - sigma))).astype(LOW)
        grad_up[:, cut] = (grad * active).astype(LOW)


def feed_forward(rows, w_gate, w_up, grad_hidden):
    count, width = rows.shape
    units = w_gate.shape[1]
    here = pl.BlockSpec(memory_space=pltpu.VMEM)
    return pl.pallas_call(
        ffn_kernel,
        out_shape=(jax.ShapeDtypeStruct((count, units), LOW),) * 3,
        in_specs=[here] * 4,
        out_specs=[here] * 3,
        compiler_params=pltpu.CompilerParams(vmem_limit_bytes=20 << 20),
        cost_estimate=pl.CostEstimate(
            flops=6 * count * width * units,
            bytes_accessed=4 * width * units,
            transcendentals=count * units,
        ),
        name="feed_forward",
    )(*in_vmem(rows, w_gate, w_up, grad_hidden))


def back_kernel(gate_rows, up_rows, gate_w, up_w, out):
    step = out.shape[1]
    cut = pl.ds(pl.multiple_of(pl.program_id(0) * step, step), step)
    total = dot(gate_rows[...], gate_w[cut, :], 1, 1) + dot(up_rows[...], up_w[cut, :], 1, 1)
    out[...] = total.astype(out.dtype)


def feed_forward_back(grad_gate, grad_up, w_gate, w_up, half, kind):
    count, units = grad_gate.shape
    width = w_gate.shape[0]
    step = width // 2
    rows = pl.BlockSpec((count // 2, units), lambda i: (half, 0))
    here = pl.BlockSpec(memory_space=pltpu.VMEM)
    return pl.pallas_call(
        back_kernel,
        out_shape=jax.ShapeDtypeStruct((count // 2, width), kind),
        grid=(2,),
        in_specs=[rows, rows, here, here],
        out_specs=pl.BlockSpec((count // 2, step), lambda i: (0, i)),
        compiler_params=pltpu.CompilerParams(vmem_limit_bytes=16 << 20),
        cost_estimate=pl.CostEstimate(
            flops=10 * count * width * units, bytes_accessed=4 * width * units, transcendentals=0
        ),
        name="feed_forward_back",
    )(grad_gate, grad_up, *in_vmem(w_gate, w_up))


def join_kernel(places, first, second, out):
    del places

    @pl.when(pl.program_id(0) == 0)
    def _():
        out[...] = first[...]

    @pl.when(pl.program_id(0) == 1)
    def _():
        out[...] = second[...]


def join_rows(table, first, second):
    rows, width = first.shape
    core = table.begin["core"]
    whole = pl.BlockSpec((rows, width), lambda i, p: (0, 0))
    return pl.pallas_call(
        join_kernel,
        out_shape=jax.ShapeDtypeStruct((2 * rows, width), first.dtype),
        grid_spec=pltpu.PrefetchScalarGridSpec(
            num_scalar_prefetch=1,
            grid=(2,),
            in_specs=[whole, whole],
            out_specs=pl.BlockSpec((rows, width), lambda i, p: (p[core] ^ i, 0)),
        ),
        compiler_params=pltpu.CompilerParams(vmem_limit_bytes=8 << 20),
        cost_estimate=pl.CostEstimate(
            flops=1_000_000_000, bytes_accessed=8 * rows * width, transcendentals=0
        ),
        name="join_rows",
    )(table.values, first, second)


def row_kernel(left, right, send, kept):
    half = left.shape[0] // 2
    send[...] = dot(left[half:, :], right[...], 1, 0).astype(LOW)
    kept[...] = dot(left[:half, :], right[...], 1, 0)


def row_terms(left, right):
    rows, units = left.shape
    half, width = rows // 2, right.shape[1]
    step = 256
    return pl.pallas_call(
        row_kernel,
        out_shape=(
            jax.ShapeDtypeStruct((half, width), LOW),
            jax.ShapeDtypeStruct((half, width), jnp.float32),
        ),
        grid=(width // step,),
        in_specs=[
            pl.BlockSpec((rows, units), lambda i: (0, 0)),
            pl.BlockSpec((units, step), lambda i: (0, i)),
        ],
        out_specs=[pl.BlockSpec((half, step), lambda i: (0, i))] * 2,
        compiler_params=pltpu.CompilerParams(vmem_limit_bytes=16 << 20),
        cost_estimate=pl.CostEstimate(
            flops=8 * rows * units * width, bytes_accessed=2 * units * width, transcendentals=0
        ),
        name="row_terms",
    )(left, right)


def turn(values, cosine, sine):
    half = cosine.shape[0]
    heads = values.shape[0] // (2 * half)
    pieces = values.reshape(heads, 2, half, values.shape[1])
    first, second = pieces[:, 0], pieces[:, 1]
    return jnp.stack(
        [first * cosine - second * sine, second * cosine + first * sine], 1
    ).reshape(values.shape)


def turn_back(grads, cosine, sine):
    return turn(grads, cosine, -sine)


def norm_back(grad_rows, values, scale_rows, gain):
    scaled = grad_rows * gain
    inner_mean = jnp.mean(scaled * values, -1, keepdims=True)
    return (
        scale_rows * (scaled - values * scale_rows * scale_rows * inner_mean),
        jnp.sum(grad_rows * values * scale_rows, 0),
    )


def shards(
    tokens,
    positions,
    norm1_gain,
    w_query,
    w_key,
    w_value,
    w_out,
    norm2_gain,
    w_gate,
    w_up,
    w_down,
    cotangent,
):
    rows_here, width = tokens.shape
    size = w_key.shape[1]
    dp = lax.axis_size("dp")
    tp_count = len(ROW_MASKS)
    own_rows = rows_here // tp_count
    block = width // dp
    bits = dp.bit_length() - 1
    half_count = dp // 2

    def exchange_order(order):
        return np.array(
            [
                sum(((j >> (len(order) - 1 - k)) & 1) << b for k, b in enumerate(order))
                for j in range(1 << len(order))
            ],
            np.int32,
        )

    down_bits = [0] + list(range(2, bits))
    rest_bits = list(range(1, bits))

    place = lax.axis_index("dp").astype(jnp.int32)
    spot = lax.axis_index("tp").astype(jnp.int32)
    natural = np.arange(half_count, dtype=np.int32)
    down_here, rest_here = place ^ exchange_order(down_bits), place ^ exchange_order(rest_bits)
    table = Table(
        mine=2 * natural + (place & 1),
        theirs=2 * natural + (1 - (place & 1)),
        natural=jnp.asarray(natural),
        down=down_here,
        down_far=down_here ^ 2,
        rest=rest_here,
        rest_far=rest_here ^ 1,
        rest_block=rest_here >> 1,
        core=(spot & 1)[None],
    )
    at = jnp.stack([place & (SPAN - 1), spot])
    row_starts = [((spot ^ m) * own_rows).astype(jnp.uint32) for m in ROW_MASKS]
    core_starts = [(c * (rows_here // 2)).astype(jnp.uint32) for c in (spot & 1, 1 - (spot & 1))]
    tokens, table.values, at, row_starts, core_starts = lax.optimization_barrier(
        (tokens, table.values, at, row_starts, core_starts)
    )
    pos = positions.reshape(1, rows_here)

    def own(values):
        return take(values, row_starts[0], own_rows, 0)

    inputs = tokens.astype(jnp.float32)
    scale_one = lax.rsqrt(jnp.mean(inputs * inputs, -1, keepdims=True) + EPSILON)
    normed_one = (inputs * scale_one * norm1_gain).astype(LOW)
    half = size // 2
    frequency = jnp.exp(
        -jnp.log(10000.0) * (2.0 * jnp.arange(half, dtype=jnp.float32) / size)
    )
    angles = frequency[:, None] * positions.astype(jnp.float32)[None, :]
    cosine, sine = jnp.cos(angles), jnp.sin(angles)
    w_kv = jnp.concatenate([w_key.T, w_value.T], 0)
    paired = dot(w_kv, normed_one, 1, 1)
    paired = jnp.concatenate([turn(paired[:size], cosine, sine), paired[size:]], 0).astype(LOW)
    blocks = [paired] + [flip(paired, "dp", m) for m in range(1, SPAN)]
    queries = (turn(dot(w_query, normed_one, 0, 1), cosine, sine) * size ** (-0.5)).astype(LOW)

    wide = w_query.shape[1]

    def near_sum(part):
        send = part(2, 4).astype(LOW)
        near, kept = lax.optimization_barrier((flip(send, "tp", 1), part(0, 2)))
        pair = kept + near
        return pair[:own_rows], pair[own_rows:].astype(LOW)

    attended, lse = attention_forward(at, pos, queries, blocks, size, 8)

    branch, branch_out = near_sum(
        lambda lo, hi: dot(attended[:, lo * own_rows : hi * own_rows], w_out, 0, 0)
    )
    branch_far = flip(branch_out, "tp", 2)
    cot = jnp.concatenate(
        [take(after(cotangent, branch_out), start, own_rows, 0) for start in row_starts], 0
    )
    cot_send = pick_columns(table, "down_far", cot)
    cot_theirs = flip(cot_send, "dp", 2)
    own_inputs = own(tokens).astype(jnp.float32)
    one_send = pick_columns(table, "theirs", after(normed_one, cot_send), "core", 2)
    one_near = flip(one_send, "dp", 1)
    grad_hidden = dot(after(cot, one_send), w_down, 1, 1)
    middle = own_inputs + (after(branch, grad_hidden) + branch_far)

    scale_two = lax.rsqrt(jnp.mean(middle * middle, -1, keepdims=True) + EPSILON)
    own_two = (middle * scale_two * norm2_gain).astype(LOW)
    far_two = flip(own_two, "tp", 2)
    gate_w, up_w = load_weights(after(w_gate, own_two), w_up)
    pair_two = jnp.concatenate([after(own_two, gate_w), far_two], 0)
    core_two = flip(pair_two, "tp", 1)
    two_send = pick_columns(table, "theirs", pair_two)
    two_near = flip(two_send, "dp", 1)
    normed_two = jnp.concatenate([after(pair_two, two_send), core_two], 0)

    hidden, grad_gate_pre, grad_up_pre = feed_forward(normed_two, gate_w, up_w, grad_hidden)
    gate_theirs = flip(grad_gate_pre, "dp", 1)
    hidden_theirs = flip(hidden, "dp", 2)
    up_theirs = flip(grad_up_pre, "dp", 1)
    gate_late, cot_theirs, one_near = lax.optimization_barrier((grad_gate_pre, cot_theirs, one_near))

    two_back = functools.partial(feed_forward_back, gate_late, grad_up_pre, gate_w, up_w)
    grad_normed_two, two_out = near_sum(
        lambda lo, hi: two_back(lo // 2, jnp.float32 if lo == 0 else LOW)
    )
    two_out, two_near = lax.optimization_barrier((two_out, two_near))
    two_far = flip(two_out, "tp", 2)
    cores = jnp.concatenate([two_near, one_near], 1)
    cores_far = flip(cores, "tp", 1)
    two_theirs = jnp.concatenate([two_near, cores_far[:, : width // 2]], 0)

    down_near, down = row_terms(after(hidden, two_out), w_down)
    grad_normed_two = after(grad_normed_two, down) + two_far

    grad_mid_norm, gain_two = norm_back(grad_normed_two, middle, scale_two, norm2_gain)
    grad_middle = own(cotangent).astype(jnp.float32) + grad_mid_norm
    branch_grad = grad_middle.astype(LOW)
    grad_far = flip(branch_grad, "tp", 2)

    down_near = flip(after(down_near, branch_grad), "tp", 1)
    gate_terms = weight_terms(
        table,
        "mine",
        "natural",
        0,
        half_count,
        after(normed_two, branch_grad),
        two_theirs,
        grad_gate_pre,
        gate_theirs,
        keep=False,
    )
    grad_gate = parity_sum(gate_terms, 0)
    grad_pair = jnp.concatenate([after(branch_grad, gate_terms), grad_far], 0)
    grad_core = flip(grad_pair, "tp", 1)
    att_theirs = flip(after(attended, grad_pair), "dp", 1)

    def near_flip(terms, bit):
        half = terms.shape[0] // 2
        return [flip(terms[half:], "dp", 1 << bit), flip(terms[:half], "dp", 1 << bit)]

    def down_terms(lo, hi, *late):
        g = after(hidden, *late)
        return weight_terms(table, "down", "natural", lo, hi, cot, cot_theirs, g, hidden_theirs)

    down_sent = down_terms(half_count // 2, half_count, grad_pair)
    half = down_sent.shape[0] // 2
    down_first = flip(down_sent[half:], "dp", 1)
    branch_all = jnp.concatenate([after(grad_pair, down_sent), grad_core], 0)
    grad_attended = dot(w_out, branch_all, 1, 1).astype(LOW)
    grads = attention_backward(
        at, pos, queries, grad_attended, attended, lse, cosine, sine, blocks, size, 4
    )
    grad_query_rows, kv_total = grads[0], grads[1]
    branch_send = pick_columns(table, "theirs", after(grad_pair, grad_query_rows))
    *kv_sends, att_theirs = lax.optimization_barrier((*grads[2:], att_theirs))
    kv_back = [flip(kv_sends[m - 1], "dp", m) for m in range(1, SPAN)]

    def rest_terms(lo, hi, x, x_far, g, g_far, transposed=False):
        return weight_terms(
            table, "rest", "rest_block", lo, hi, x, x_far, g, g_far, transposed
        )

    down = down + after(down_near, grad_query_rows)
    down, down_out = down[:own_rows], down[own_rows:].astype(LOW)
    down_far = flip(down_out, "tp", 2)

    def up_terms(lo, hi, *late):
        return rest_terms(lo, hi, normed_two, two_theirs, after(grad_up_pre, *late), up_theirs)

    up_sent = up_terms(half_count // 2, half_count, grad_query_rows)
    up_first = flip(up_sent[half:], "dp", 2)

    def exchange_mid(terms, first, order, *late):
        got, left = [first], half_count // 2
        for b in order[1:]:
            send = terms(left // 2, left, *late).astype(jnp.float32)
            rows = send.shape[0]
            for other in got:
                send = send + other[other.shape[0] - rows :]
            send = send.astype(LOW)
            got.append(flip(send, "dp", 1 << b))
            left //= 2
        return got[1:], send

    down_late, down_last = exchange_mid(down_terms, down_first, down_bits, grad_query_rows)
    kv_total, grad_gate = lax.optimization_barrier(
        (kv_total, grad_gate, up_sent, down_out, down_last)
    )[:2]
    for back in kv_back:
        kv_total = kv_total + back
    key_grad = turn_back(kv_total[:size], cosine, sine)
    grad_kv_rows = jnp.concatenate([key_grad, kv_total[size:]], 0).astype(LOW)
    proj_rows = jnp.concatenate([grad_query_rows, grad_kv_rows], 0)
    units = proj_rows.shape[0]
    pieces = [
        branch_send[:, begin : begin + rows_here] for begin in range(0, branch_send.shape[1], rows_here)
    ]
    both_theirs = flip(jnp.concatenate([proj_rows, *pieces], 0), "dp", 1)

    own_order = jnp.concatenate(
        [take(proj_rows, start, own_rows, 1) for start in row_starts], 1
    )

    def one_terms(lo, hi):
        cut = own_order[:, lo * own_rows : hi * own_rows]
        return dot(cut[:wide], w_query, 0, 1) + dot(cut[wide:], w_kv, 0, 0)

    grad_normed_one, one_out = near_sum(one_terms)
    one_far = flip(one_out, "tp", 2)
    up_second = flip(after(up_sent[:half], one_out), "dp", 2)
    output_rows = (middle + (down + after(down_far, one_out))).astype(LOW)
    one_theirs = join_rows(table, after(one_near, one_out), cores_far[:, width // 2 :])
    up_kept = up_terms(0, 1, one_out)
    grad_gate = grad_gate.astype(jnp.float32)
    grad_normed_one = after(grad_normed_one, output_rows, up_kept, grad_gate, one_theirs) + one_far
    grad_in_norm, gain_one = norm_back(grad_normed_one, own_inputs, own(scale_one), norm1_gain)
    input_rows = grad_middle + grad_in_norm

    up_late, up_last = exchange_mid(up_terms, up_first, rest_bits, input_rows)
    both_theirs = after(both_theirs, up_last)
    proj_theirs = both_theirs[:units]
    branch_near = jnp.concatenate(
        [
            both_theirs[begin : begin + branch_send.shape[0]]
            for begin in range(units, both_theirs.shape[0], branch_send.shape[0])
        ],
        1,
    )
    branch_theirs = jnp.concatenate([branch_near, flip(branch_near, "tp", 1)], 0)
    gain_one, *down_late = lax.optimization_barrier((gain_one, *down_late, up_last))[:-1]
    gains = jnp.stack([gain_one, gain_two])
    for m in (1, 2):
        gains = gains + flip(gains, "tp", m)
    gains = pick_columns(table, "rest", gains) + flip(
        pick_columns(table, "rest_far", gains), "dp", 1
    )

    out_late, proj_late = lax.optimization_barrier((attended, proj_rows, up_last))[:2]

    def last_terms(lo, hi, *late):
        first, second = after(proj_late, *late), after(out_late, *late)
        return jnp.concatenate(
            [
                rest_terms(lo, hi, normed_one, one_theirs, first, proj_theirs, True),
                rest_terms(lo, hi, branch_all, branch_theirs, second, att_theirs, True),
            ],
            1,
        )

    def with_gains(terms, lo, hi, *others):
        extra = gains[:, lo * block : hi * block]
        for other, other_gains in others:
            terms = terms.astype(jnp.float32) + other
            extra = extra + other_gains
        columns = terms.shape[1]
        extra = jnp.pad(extra, ((0, 14), (0, -extra.shape[1] % columns)))[:, :columns]
        return jnp.concatenate([terms.astype(LOW), extra.astype(LOW)], 0)

    def split(message, count):
        rows = count * block
        return message[:rows], message[rows : rows + 2, :rows]

    quarter = half_count // 4
    sent = last_terms(half_count // 2, half_count)
    cut = quarter * block
    firsts = with_gains(sent[cut:], 3 * quarter, half_count)
    seconds = with_gains(sent[:cut], 2 * quarter, 3 * quarter)
    mids = [split(flip(firsts, "dp", 2), quarter)]
    last_second = split(flip(after(seconds, firsts), "dp", 2), quarter)
    up_late = [*up_late, up_second]
    proj_kept = rest_terms(0, 1, normed_one, one_theirs, after(proj_late, firsts), proj_theirs, True)
    out_kept = rest_terms(0, 1, branch_all, branch_theirs, after(out_late, firsts), att_theirs, True)
    down_kept = down_terms(0, 1, firsts)
    left = half_count // 2
    for b in rest_bits[1:]:
        count = left // 2
        terms = last_terms(count, left, firsts)
        terms, *up_late = lax.optimization_barrier((terms, *up_late, proj_kept, out_kept, down_kept))[
            :-3
        ]
        send = with_gains(
            terms, count, left, *((o[-count * block :], g[:, -count * block :]) for o, g in mids)
        )
        mids.append(split(flip(send, "dp", 1 << b), count))
        left = count
    down_second = flip(after(down_sent[:half], firsts), "dp", 1)

    def ending(kept, *others):
        kept = kept.astype(jnp.float32)
        for other in others:
            kept = kept + other[:block]
        return kept

    down_kept, down_second = lax.optimization_barrier((down_kept, down_second, send))[:2]
    grad_down = ending(down_kept, down_second, *down_late)
    grad_last = ending(
        jnp.concatenate([proj_kept, out_kept], 1), last_second[0], *(m[0] for m in mids[1:])
    )
    gains = gains[:, :block] + last_second[1][:, :block]
    for _, other in mids[1:]:
        gains = gains + other[:, :block]
    grad_up = ending(up_kept, *up_late)
    narrow = wide + 2 * size

    return (
        output_rows,
        input_rows,
        gains[0],
        grad_last[:, :wide],
        grad_last[:, wide : wide + size],
        grad_last[:, wide + size : narrow],
        grad_last[:, narrow:].T,
        gains[1],
        grad_gate,
        grad_up,
        grad_down.T,
    )


def solution(mesh):
    placed = (
        P("dp", None),
        P("dp"),
        P(),
        P(None, "tp"),
        P(None, "tp"),
        P(None, "tp"),
        P("tp", None),
        P(),
        P(None, "tp"),
        P(None, "tp"),
        P("tp", None),
        P("dp", None),
    )
    return jax.shard_map(
        shards,
        mesh=mesh,
        in_specs=placed,
        out_specs=(
            P(("dp", "tp"), None),
            P(("dp", "tp"), None),
            P("dp"),
            P("dp", "tp"),
            P("dp", "tp"),
            P("dp", "tp"),
            P("tp", "dp"),
            P("dp"),
            P("dp", "tp"),
            P("dp", "tp"),
            P("tp", "dp"),
        ),
        check_vma=False,
    )
```

```python
import functools

import jax
import jax.numpy as jnp
import numpy as np
from jax import lax
from jax.experimental import pallas as pl
from jax.experimental.pallas import tpu as pltpu
from jax.sharding import PartitionSpec as P

SPAN = 4
EPSILON = 1e-05
FAR_BELOW = -1e30
LOW = jnp.bfloat16
ROW_MASKS = (0, 2, 1, 3)


def flip(block, axis, mask):
    return lax.ppermute(block, axis, [(i, i ^ mask) for i in range(lax.axis_size(axis))])


def dot(left, right, left_dim, right_dim):
    return lax.dot_general(
        left,
        right,
        (((left_dim,), (right_dim,)), ((), ())),
        preferred_element_type=jnp.float32,
    )


def in_hbm(*arrays):
    return [pltpu.with_memory_space_constraint(a, pltpu.HBM) for a in arrays]


def own_mask(pos, begin, keys, queries):
    key_at = lax.broadcasted_iota(jnp.int32, (keys, queries), 0)
    query_at = lax.broadcasted_iota(jnp.int32, (keys, queries), 1) + begin
    return (key_at <= query_at) & (key_at >= query_at - pos)


def row_starts(spot, rows):
    part = rows // len(ROW_MASKS)
    return [pl.multiple_of((spot ^ m) * part, part) for m in ROW_MASKS]


def forward_kernel(
    heads,
    size,
    at_ref,
    pos_ref,
    q_ref,
    kv0,
    kv1,
    kv2,
    kv3,
    o_ref,
    lse_ref,
    keys,
    vals,
    top,
    acc,
    ordered,
):
    rank, spot = at_ref[0], at_ref[1]
    rows = pos_ref.shape[1]
    half = rows // 2

    @pl.when(pl.program_id(0) == 0)
    def _():
        for m, kv in enumerate((kv0, kv1, kv2, kv3)):
            keys[m] = kv[:size, :].T
            vals[m, :size, :] = kv[size:, :]
            vals[m, size:, :] = jnp.ones((16, rows), LOW)

    pos = pos_ref[...]
    for part in range(2):
        cols = slice(part * half, (part + 1) * half)
        count = (part + 1) * half
        mask = own_mask(pos[:, cols], part * half, count, half)
        for h in range(heads):
            scores = dot(keys[0, :count, :], q_ref[h * size : (h + 1) * size, cols], 1, 0)
            scores = jnp.where(mask, scores, FAR_BELOW)
            peak = jnp.max(scores, 0, keepdims=True)
            weights = jnp.exp(scores - peak).astype(LOW)
            acc[h, :, cols] = dot(vals[0, :, :count], weights, 1, 0)
            top[h, :, cols] = peak
    seen = pos > lax.broadcasted_iota(jnp.int32, (1, rows), 1)
    for m in range(1, SPAN):

        @pl.when((rank ^ m) < rank)
        def _():
            for h in range(heads):
                scores = dot(keys[m], q_ref[h * size : (h + 1) * size, :], 1, 0)
                old = top[h]
                peak = jnp.where(seen, jnp.maximum(old, jnp.max(scores, 0, keepdims=True)), old)
                weights = jnp.exp(scores - jnp.where(seen, peak, -FAR_BELOW)).astype(LOW)
                acc[h] = acc[h] * jnp.exp(old - peak) + dot(vals[m], weights, 1, 0)
                top[h] = peak

    for h in range(heads):
        total = acc[h, size : size + 1, :]
        ordered[h * size : (h + 1) * size, :] = (acc[h, :size, :] / total).astype(LOW)
        lse_ref[h] = top[h] + jnp.log(total)
    for j, start in enumerate(row_starts(spot, rows)):
        part = rows // len(ROW_MASKS)
        o_ref[:, j * part : (j + 1) * part] = ordered[:, pl.ds(start, part)]


def backward_kernel(
    heads,
    size,
    at_ref,
    pos_ref,
    q_ref,
    do_in,
    o_in,
    lse_ref,
    cos_ref,
    sin_ref,
    kv0,
    kv1,
    kv2,
    kv3,
    dq_ref,
    g0,
    g1,
    g2,
    g3,
    keys,
    vals,
    dq,
    total,
    do_ref,
    o_ref,
):
    rank, spot = at_ref[0], at_ref[1]
    rows = pos_ref.shape[1]
    half = rows // 2
    blocks = (kv0, kv1, kv2, kv3)
    step = pl.program_id(0)

    @pl.when(step == 0)
    def _():
        for m, kv in enumerate(blocks):
            keys[m] = kv[:size, :].T
            vals[m] = kv[size:, :].T
        total[...] = jnp.zeros_like(total)

    part = rows // len(ROW_MASKS)
    for j, start in enumerate(row_starts(spot, rows)):
        do_ref[:, pl.ds(start, part)] = do_in[:, j * part : (j + 1) * part]
        o_ref[:, pl.ds(start, part)] = o_in[:, j * part : (j + 1) * part]
    pos = pos_ref[...]
    seen = pos > lax.broadcasted_iota(jnp.int32, (1, rows), 1)
    deltas = []
    for h in range(heads):
        span = slice(h * size, (h + 1) * size)
        deltas.append(
            jnp.sum(
                do_ref[span, :].astype(jnp.float32) * o_ref[span, :].astype(jnp.float32),
                0,
                keepdims=True,
            )
        )
    for part in range(2):
        cols = slice(part * half, (part + 1) * half)
        count = (part + 1) * half
        mask = own_mask(pos[:, cols], part * half, count, half)
        for h in range(heads):
            span = slice(h * size, (h + 1) * size)
            query, grad = q_ref[span, cols], do_ref[span, cols]
            scores = dot(keys[0, :count, :], query, 1, 0)
            probs = jnp.exp(jnp.where(mask, scores, FAR_BELOW) - lse_ref[h, :, cols])
            grad_probs = dot(vals[0, :count, :], grad, 1, 0)
            grad_scores = (probs * (grad_probs - deltas[h][:, cols])).astype(LOW)
            total[0, :size, :count] += dot(query, grad_scores, 1, 1)
            total[0, size:, :count] += dot(grad, probs.astype(LOW), 1, 1)
            dq[h, :, cols] = dot(kv0[:size, :count], grad_scores, 1, 0)
    for m in range(1, SPAN):

        @pl.when((rank ^ m) < rank)
        def _():
            for h in range(heads):
                span = slice(h * size, (h + 1) * size)
                query, grad = q_ref[span, :], do_ref[span, :]
                scores = dot(keys[m], query, 1, 0)
                probs = jnp.exp(scores - jnp.where(seen, lse_ref[h], -FAR_BELOW))
                grad_probs = dot(vals[m], grad, 1, 0)
                grad_scores = (probs * (grad_probs - deltas[h])).astype(LOW)
                total[m, :size, :] += dot(query, grad_scores, 1, 1)
                total[m, size:, :] += dot(grad, probs.astype(LOW), 1, 1)
                dq[h] += dot(blocks[m][:size, :], grad_scores, 1, 0)

    middle_at = size // 2
    cosine, sine = cos_ref[...], sin_ref[...]
    for h in range(heads):
        first = dq[h, :middle_at, :] * size ** (-0.5)
        second = dq[h, middle_at:, :] * size ** (-0.5)
        base = h * size
        dq_ref[base : base + middle_at, :] = (first * cosine + second * sine).astype(LOW)
        dq_ref[base + middle_at : base + size, :] = (second * cosine - first * sine).astype(LOW)

    @pl.when(step == pl.num_programs(0) - 1)
    def _():
        g0[...] = total[0]
        for m, out in ((1, g1), (2, g2), (3, g3)):
            out[...] = total[m].astype(LOW)


def attention_forward(at, pos, queries, blocks, size, heads):
    wide, rows = queries.shape
    count = wide // size
    whole = pl.BlockSpec((2 * size, rows), lambda i, r: (0, 0))
    some = pl.BlockSpec((heads * size, rows), lambda i, r: (i, 0))
    return pl.pallas_call(
        functools.partial(forward_kernel, heads, size),
        out_shape=(
            jax.ShapeDtypeStruct((wide, rows), LOW),
            jax.ShapeDtypeStruct((count, 1, rows), jnp.float32),
        ),
        grid_spec=pltpu.PrefetchScalarGridSpec(
            num_scalar_prefetch=1,
            grid=(count // heads,),
            in_specs=[pl.BlockSpec((1, rows), lambda i, r: (0, 0)), some] + [whole] * SPAN,
            out_specs=[some, pl.BlockSpec((heads, 1, rows), lambda i, r: (i, 0, 0))],
            scratch_shapes=[
                pltpu.VMEM((SPAN, rows, size), LOW),
                pltpu.VMEM((SPAN, size + 16, rows), LOW),
                pltpu.VMEM((heads, 1, rows), jnp.float32),
                pltpu.VMEM((heads, size + 16, rows), jnp.float32),
                pltpu.VMEM((heads * size, rows), LOW),
            ],
        ),
        compiler_params=pltpu.CompilerParams(vmem_limit_bytes=24 << 20),
        cost_estimate=pl.CostEstimate(
            flops=32 * wide * rows * rows * SPAN,
            bytes_accessed=4 * wide * rows,
            transcendentals=0,
        ),
        name="attention_forward",
    )(at, pos, queries, *blocks)


def attention_backward(at, pos, queries, grads, attended, lse, cosine, sine, blocks, size, heads):
    wide, rows = queries.shape
    count = wide // size
    whole = pl.BlockSpec((2 * size, rows), lambda i, r: (0, 0))
    table = pl.BlockSpec((size // 2, rows), lambda i, r: (0, 0))
    some = pl.BlockSpec((heads * size, rows), lambda i, r: (i, 0))
    return pl.pallas_call(
        functools.partial(backward_kernel, heads, size),
        out_shape=(
            jax.ShapeDtypeStruct((wide, rows), LOW),
            jax.ShapeDtypeStruct((2 * size, rows), jnp.float32),
        )
        + (jax.ShapeDtypeStruct((2 * size, rows), LOW),) * (SPAN - 1),
        grid_spec=pltpu.PrefetchScalarGridSpec(
            num_scalar_prefetch=1,
            grid=(count // heads,),
            in_specs=[
                pl.BlockSpec((1, rows), lambda i, r: (0, 0)),
                some,
                some,
                some,
                pl.BlockSpec((heads, 1, rows), lambda i, r: (i, 0, 0)),
                table,
                table,
            ]
            + [whole] * SPAN,
            out_specs=[some] + [whole] * SPAN,
            scratch_shapes=[
                pltpu.VMEM((SPAN, rows, size), LOW),
                pltpu.VMEM((SPAN, rows, size), LOW),
                pltpu.VMEM((heads, size, rows), jnp.float32),
                pltpu.VMEM((SPAN, 2 * size, rows), jnp.float32),
                pltpu.VMEM((heads * size, rows), LOW),
                pltpu.VMEM((heads * size, rows), LOW),
            ],
        ),
        compiler_params=pltpu.CompilerParams(vmem_limit_bytes=24 << 20),
        cost_estimate=pl.CostEstimate(
            flops=48 * wide * rows * rows * SPAN,
            bytes_accessed=10 * wide * rows,
            transcendentals=0,
        ),
        name="attention_backward",
    )(at, pos, *in_hbm(queries, grads, attended, lse, cosine, sine, *blocks))


def take(values, start, size, dim):
    starts = [np.uint32(0)] * values.ndim
    starts[dim] = start
    sizes = list(values.shape)
    sizes[dim] = size
    return lax.dynamic_slice(values, starts, sizes)


def pick(values, places, blocks, dim):
    size = values.shape[dim] // blocks
    return jnp.concatenate(
        [lax.dynamic_slice_in_dim(values, p * size, size, dim) for p in places], dim
    )


class Table:
    def __init__(self, **parts):
        self.begin, at = {}, 0
        for name, part in parts.items():
            self.begin[name] = at
            at += part.shape[0]
        self.values = jnp.concatenate([p.astype(jnp.int32) for p in parts.values()])

    def list(self, name, lo, hi):
        return [self.values[self.begin[name] + j] for j in range(lo, hi)]


def after(value, *others):
    return lax.optimization_barrier((value, *others))[0]


def parity_sum(terms, dim):
    count = lax.axis_size("dp")
    groups = [list(range(p, count, 2)) for p in range(2)]
    return lax.psum_scatter(
        terms.astype(LOW), "dp", scatter_dimension=dim, axis_index_groups=groups, tiled=True
    )


def terms_kernel(transposed, places, x, x_far, g, g_far, out):
    del places
    side = 1 if transposed else 0
    out[...] = (dot(x[...], g[...], 0, side) + dot(x_far[...], g_far[...], 0, side)).astype(LOW)


def weight_terms(table, name, far, lo, hi, x, x_far, g, g_far, transposed=False, keep=True):
    count = hi - lo
    size = x.shape[1] // lax.axis_size("dp")
    rows = x.shape[0]
    units = g.shape[0] if transposed else g.shape[1]
    if size % 128:
        side = 1 if transposed else 0
        mine = pick(x, table.list(name, lo, hi), x.shape[1] // size, 1)
        theirs = pick(x_far, table.list(far, lo, hi), x_far.shape[1] // size, 1)
        return (dot(mine, g, 0, side) + dot(theirs, g_far, 0, side)).astype(LOW)
    whole = pl.BlockSpec(g.shape, lambda i, p: (0, 0))
    begin, far_begin = table.begin[name] + lo, table.begin[far] + lo
    return pl.pallas_call(
        functools.partial(terms_kernel, transposed),
        out_shape=(jax.ShapeDtypeStruct if keep else pltpu.HBM)((count * size, units), LOW),
        grid_spec=pltpu.PrefetchScalarGridSpec(
            num_scalar_prefetch=1,
            grid=(count,),
            in_specs=[
                pl.BlockSpec((rows, size), lambda i, p: (0, p[begin + i])),
                pl.BlockSpec((rows, size), lambda i, p: (0, p[far_begin + i])),
                whole,
                whole,
            ],
            out_specs=pl.BlockSpec((size, units), lambda i, p: (i, 0)),
        ),
        compiler_params=pltpu.CompilerParams(vmem_limit_bytes=20 << 20),
        cost_estimate=pl.CostEstimate(
            flops=24 * rows * count * size * units, bytes_accessed=4 * rows * units, transcendentals=0
        ),
        name="weight_terms",
    )(table.values, x, x_far, g, g_far)


def copy_kernel(places, source, target):
    del places
    target[...] = source[...]


def pick_columns(table, name, values, part=None, parts=1):
    blocks = lax.axis_size("dp")
    rows, count = values.shape[0] // parts, blocks // 2
    size = values.shape[1] // blocks
    if size % 128:
        if part is not None:
            values = lax.dynamic_slice_in_dim(values, table.list(part, 0, 1)[0] * rows, rows, 0)
        return pick(values, table.list(name, 0, count), blocks, 1)
    begin = table.begin[name]
    row = 0 if part is None else table.begin[part]
    return pl.pallas_call(
        copy_kernel,
        out_shape=jax.ShapeDtypeStruct((rows, count * size), values.dtype),
        grid_spec=pltpu.PrefetchScalarGridSpec(
            num_scalar_prefetch=1,
            grid=(count,),
            in_specs=[
                pl.BlockSpec(
                    (rows, size), lambda i, p: (0 if part is None else p[row], p[begin + i])
                )
            ],
            out_specs=pl.BlockSpec((rows, size), lambda i, p: (0, i)),
        ),
        compiler_params=pltpu.CompilerParams(vmem_limit_bytes=8 << 20),
        cost_estimate=pl.CostEstimate(
            flops=65536 * rows * count * size, bytes_accessed=4 * rows * count * size, transcendentals=0
        ),
        name="pick_columns",
    )(table.values, values)


def load_kernel(*refs):
    *pairs, sems = refs
    half = len(pairs) // 2
    copies = [
        pltpu.make_async_copy(source, target, sems.at[j])
        for j, (source, target) in enumerate(zip(pairs[:half], pairs[half:]))
    ]
    for copy in copies:
        copy.start()
    for copy in copies:
        copy.wait()


def load_weights(*weights):
    return pl.pallas_call(
        load_kernel,
        out_shape=tuple(pltpu.VMEM(w.shape, w.dtype) for w in weights),
        in_specs=[pl.BlockSpec(memory_space=pl.ANY)] * len(weights),
        out_specs=[pl.BlockSpec(memory_space=pltpu.VMEM)] * len(weights),
        scratch_shapes=[pltpu.SemaphoreType.DMA((len(weights),))],
        compiler_params=pltpu.CompilerParams(vmem_limit_bytes=2 << 20),
        cost_estimate=pl.CostEstimate(
            flops=20_000_000_000,
            bytes_accessed=2 * sum(w.size for w in weights),
            transcendentals=0,
        ),
        name="load_weights",
    )(*in_hbm(*weights))


def in_vmem(*arrays):
    return [pltpu.with_memory_space_constraint(a, pltpu.VMEM) for a in arrays]


def ffn_kernel(rows, gate_w, up_w, grad_in, hidden, grad_gate, grad_up):
    step = 128
    for begin in range(0, hidden.shape[1], step):
        cut = slice(begin, begin + step)
        both = dot(rows[...], jnp.concatenate([gate_w[:, cut], up_w[:, cut]], 1), 1, 0)
        gate, up = both[:, :step], both[:, step:]
        grad = grad_in[:, cut]
        sigma = jax.nn.sigmoid(gate)
        active = gate * sigma
        hidden[:, cut] = (active * up).astype(LOW)
        grad_gate[:, cut] = (grad * up * sigma * (1.0 + gate * (1.0 - sigma))).astype(LOW)
        grad_up[:, cut] = (grad * active).astype(LOW)


def feed_forward(rows, w_gate, w_up, grad_hidden):
    count, width = rows.shape
    units = w_gate.shape[1]
    here = pl.BlockSpec(memory_space=pltpu.VMEM)
    return pl.pallas_call(
        ffn_kernel,
        out_shape=(jax.ShapeDtypeStruct((count, units), LOW),) * 3,
        in_specs=[here] * 4,
        out_specs=[here] * 3,
        compiler_params=pltpu.CompilerParams(vmem_limit_bytes=20 << 20),
        cost_estimate=pl.CostEstimate(
            flops=6 * count * width * units,
            bytes_accessed=4 * width * units,
            transcendentals=count * units,
        ),
        name="feed_forward",
    )(*in_vmem(rows, w_gate, w_up, grad_hidden))


def back_kernel(gate_rows, up_rows, gate_w, up_w, out):
    step = out.shape[1]
    cut = pl.ds(pl.multiple_of(pl.program_id(0) * step, step), step)
    total = dot(gate_rows[...], gate_w[cut, :], 1, 1) + dot(up_rows[...], up_w[cut, :], 1, 1)
    out[...] = total.astype(out.dtype)


def feed_forward_back(grad_gate, grad_up, w_gate, w_up, half, kind):
    count, units = grad_gate.shape
    width = w_gate.shape[0]
    step = width // 2
    rows = pl.BlockSpec((count // 2, units), lambda i: (half, 0))
    here = pl.BlockSpec(memory_space=pltpu.VMEM)
    return pl.pallas_call(
        back_kernel,
        out_shape=jax.ShapeDtypeStruct((count // 2, width), kind),
        grid=(2,),
        in_specs=[rows, rows, here, here],
        out_specs=pl.BlockSpec((count // 2, step), lambda i: (0, i)),
        compiler_params=pltpu.CompilerParams(vmem_limit_bytes=16 << 20),
        cost_estimate=pl.CostEstimate(
            flops=10 * count * width * units, bytes_accessed=4 * width * units, transcendentals=0
        ),
        name="feed_forward_back",
    )(grad_gate, grad_up, *in_vmem(w_gate, w_up))


def join_kernel(places, first, second, out):
    del places

    @pl.when(pl.program_id(0) == 0)
    def _():
        out[...] = first[...]

    @pl.when(pl.program_id(0) == 1)
    def _():
        out[...] = second[...]


def join_rows(table, first, second):
    rows, width = first.shape
    core = table.begin["core"]
    whole = pl.BlockSpec((rows, width), lambda i, p: (0, 0))
    return pl.pallas_call(
        join_kernel,
        out_shape=jax.ShapeDtypeStruct((2 * rows, width), first.dtype),
        grid_spec=pltpu.PrefetchScalarGridSpec(
            num_scalar_prefetch=1,
            grid=(2,),
            in_specs=[whole, whole],
            out_specs=pl.BlockSpec((rows, width), lambda i, p: (p[core] ^ i, 0)),
        ),
        compiler_params=pltpu.CompilerParams(vmem_limit_bytes=8 << 20),
        cost_estimate=pl.CostEstimate(
            flops=1_000_000_000, bytes_accessed=8 * rows * width, transcendentals=0
        ),
        name="join_rows",
    )(table.values, first, second)


def row_kernel(left, right, send, kept):
    half = left.shape[0] // 2
    send[...] = dot(left[half:, :], right[...], 1, 0).astype(LOW)
    kept[...] = dot(left[:half, :], right[...], 1, 0)


def row_terms(left, right):
    rows, units = left.shape
    half, width = rows // 2, right.shape[1]
    step = 256
    return pl.pallas_call(
        row_kernel,
        out_shape=(
            jax.ShapeDtypeStruct((half, width), LOW),
            jax.ShapeDtypeStruct((half, width), jnp.float32),
        ),
        grid=(width // step,),
        in_specs=[
            pl.BlockSpec((rows, units), lambda i: (0, 0)),
            pl.BlockSpec((units, step), lambda i: (0, i)),
        ],
        out_specs=[pl.BlockSpec((half, step), lambda i: (0, i))] * 2,
        compiler_params=pltpu.CompilerParams(vmem_limit_bytes=16 << 20),
        cost_estimate=pl.CostEstimate(
            flops=8 * rows * units * width, bytes_accessed=2 * units * width, transcendentals=0
        ),
        name="row_terms",
    )(left, right)


def turn(values, cosine, sine):
    half = cosine.shape[0]
    heads = values.shape[0] // (2 * half)
    pieces = values.reshape(heads, 2, half, values.shape[1])
    first, second = pieces[:, 0], pieces[:, 1]
    return jnp.stack(
        [first * cosine - second * sine, second * cosine + first * sine], 1
    ).reshape(values.shape)


def turn_back(grads, cosine, sine):
    return turn(grads, cosine, -sine)


def norm_back(grad_rows, values, scale_rows, gain):
    scaled = grad_rows * gain
    inner_mean = jnp.mean(scaled * values, -1, keepdims=True)
    return (
        scale_rows * (scaled - values * scale_rows * scale_rows * inner_mean),
        jnp.sum(grad_rows * values * scale_rows, 0),
    )


def shards(
    tokens,
    positions,
    norm1_gain,
    w_query,
    w_key,
    w_value,
    w_out,
    norm2_gain,
    w_gate,
    w_up,
    w_down,
    cotangent,
):
    rows_here, width = tokens.shape
    size = w_key.shape[1]
    dp = lax.axis_size("dp")
    tp_count = len(ROW_MASKS)
    own_rows = rows_here // tp_count
    block = width // dp
    bits = dp.bit_length() - 1
    half_count = dp // 2

    def exchange_order(order):
        return np.array(
            [
                sum(((j >> (len(order) - 1 - k)) & 1) << b for k, b in enumerate(order))
                for j in range(1 << len(order))
            ],
            np.int32,
        )

    down_bits = [0] + list(range(2, bits))
    rest_bits = list(range(1, bits))

    place = lax.axis_index("dp").astype(jnp.int32)
    spot = lax.axis_index("tp").astype(jnp.int32)
    natural = np.arange(half_count, dtype=np.int32)
    down_here, rest_here = place ^ exchange_order(down_bits), place ^ exchange_order(rest_bits)
    table = Table(
        mine=2 * natural + (place & 1),
        theirs=2 * natural + (1 - (place & 1)),
        natural=jnp.asarray(natural),
        down=down_here,
        down_far=down_here ^ 2,
        rest=rest_here,
        rest_far=rest_here ^ 1,
        rest_block=rest_here >> 1,
        core=(spot & 1)[None],
    )
    at = jnp.stack([place & (SPAN - 1), spot])
    row_starts = [((spot ^ m) * own_rows).astype(jnp.uint32) for m in ROW_MASKS]
    core_starts = [(c * (rows_here // 2)).astype(jnp.uint32) for c in (spot & 1, 1 - (spot & 1))]
    tokens, table.values, at, row_starts, core_starts = lax.optimization_barrier(
        (tokens, table.values, at, row_starts, core_starts)
    )
    pos = positions.reshape(1, rows_here)

    def own(values):
        return take(values, row_starts[0], own_rows, 0)

    inputs = tokens.astype(jnp.float32)
    scale_one = lax.rsqrt(jnp.mean(inputs * inputs, -1, keepdims=True) + EPSILON)
    normed_one = (inputs * scale_one * norm1_gain).astype(LOW)
    half = size // 2
    frequency = jnp.exp(
        -jnp.log(10000.0) * (2.0 * jnp.arange(half, dtype=jnp.float32) / size)
    )
    angles = frequency[:, None] * positions.astype(jnp.float32)[None, :]
    cosine, sine = jnp.cos(angles), jnp.sin(angles)
    w_kv = jnp.concatenate([w_key.T, w_value.T], 0)
    paired = dot(w_kv, normed_one, 1, 1)
    paired = jnp.concatenate([turn(paired[:size], cosine, sine), paired[size:]], 0).astype(LOW)
    blocks = [paired] + [flip(paired, "dp", m) for m in range(1, SPAN)]
    queries = (turn(dot(w_query, normed_one, 0, 1), cosine, sine) * size ** (-0.5)).astype(LOW)

    wide = w_query.shape[1]

    def near_sum(part):
        send = part(2, 4).astype(LOW)
        near, kept = lax.optimization_barrier((flip(send, "tp", 1), part(0, 2)))
        pair = kept + near
        return pair[:own_rows], pair[own_rows:].astype(LOW)

    attended, lse = attention_forward(at, pos, queries, blocks, size, 8)

    branch, branch_out = near_sum(
        lambda lo, hi: dot(attended[:, lo * own_rows : hi * own_rows], w_out, 0, 0)
    )
    branch_far = flip(branch_out, "tp", 2)
    cot = jnp.concatenate(
        [take(after(cotangent, branch_out), start, own_rows, 0) for start in row_starts], 0
    )
    cot_send = pick_columns(table, "down_far", cot)
    cot_theirs = flip(cot_send, "dp", 2)
    own_inputs = own(tokens).astype(jnp.float32)
    one_send = pick_columns(table, "theirs", after(normed_one, cot_send), "core", 2)
    one_near = flip(one_send, "dp", 1)
    grad_hidden = dot(after(cot, one_send), w_down, 1, 1)
    middle = own_inputs + (after(branch, grad_hidden) + branch_far)

    scale_two = lax.rsqrt(jnp.mean(middle * middle, -1, keepdims=True) + EPSILON)
    own_two = (middle * scale_two * norm2_gain).astype(LOW)
    far_two = flip(own_two, "tp", 2)
    gate_w, up_w = load_weights(after(w_gate, own_two), w_up)
    pair_two = jnp.concatenate([after(own_two, gate_w), far_two], 0)
    core_two = flip(pair_two, "tp", 1)
    two_send = pick_columns(table, "theirs", pair_two)
    two_near = flip(two_send, "dp", 1)
    normed_two = jnp.concatenate([after(pair_two, two_send), core_two], 0)

    hidden, grad_gate_pre, grad_up_pre = feed_forward(normed_two, gate_w, up_w, grad_hidden)
    gate_theirs = flip(grad_gate_pre, "dp", 1)
    hidden_theirs = flip(hidden, "dp", 2)
    up_theirs = flip(grad_up_pre, "dp", 1)
    gate_late, cot_theirs, one_near = lax.optimization_barrier((grad_gate_pre, cot_theirs, one_near))

    two_back = functools.partial(feed_forward_back, gate_late, grad_up_pre, gate_w, up_w)
    grad_normed_two, two_out = near_sum(
        lambda lo, hi: two_back(lo // 2, jnp.float32 if lo == 0 else LOW)
    )
    two_out, two_near = lax.optimization_barrier((two_out, two_near))
    two_far = flip(two_out, "tp", 2)
    cores = jnp.concatenate([two_near, one_near], 1)
    cores_far = flip(cores, "tp", 1)
    two_theirs = jnp.concatenate([two_near, cores_far[:, : width // 2]], 0)

    down_near, down = row_terms(after(hidden, two_out), w_down)
    grad_normed_two = after(grad_normed_two, down) + two_far

    grad_mid_norm, gain_two = norm_back(grad_normed_two, middle, scale_two, norm2_gain)
    grad_middle = own(cotangent).astype(jnp.float32) + grad_mid_norm
    branch_grad = grad_middle.astype(LOW)
    grad_far = flip(branch_grad, "tp", 2)

    down_near = flip(after(down_near, branch_grad), "tp", 1)
    gate_terms = weight_terms(
        table,
        "mine",
        "natural",
        0,
        half_count,
        after(normed_two, branch_grad),
        two_theirs,
        grad_gate_pre,
        gate_theirs,
        keep=False,
    )
    grad_gate = parity_sum(gate_terms, 0)
    grad_pair = jnp.concatenate([after(branch_grad, gate_terms), grad_far], 0)
    grad_core = flip(grad_pair, "tp", 1)
    att_theirs = flip(after(attended, grad_pair), "dp", 1)

    def near_flip(terms, bit):
        half = terms.shape[0] // 2
        return [flip(terms[half:], "dp", 1 << bit), flip(terms[:half], "dp", 1 << bit)]

    def down_terms(lo, hi, *late):
        g = after(hidden, *late)
        return weight_terms(table, "down", "natural", lo, hi, cot, cot_theirs, g, hidden_theirs)

    down_sent = down_terms(half_count // 2, half_count, grad_pair)
    half = down_sent.shape[0] // 2
    down_first = flip(down_sent[half:], "dp", 1)
    branch_all = jnp.concatenate([after(grad_pair, down_sent), grad_core], 0)
    grad_attended = dot(w_out, branch_all, 1, 1).astype(LOW)
    grads = attention_backward(
        at, pos, queries, grad_attended, attended, lse, cosine, sine, blocks, size, 4
    )
    grad_query_rows, kv_total = grads[0], grads[1]
    branch_send = pick_columns(table, "theirs", after(grad_pair, grad_query_rows))
    *kv_sends, att_theirs = lax.optimization_barrier((*grads[2:], att_theirs))
    kv_back = [flip(kv_sends[m - 1], "dp", m) for m in range(1, SPAN)]

    def rest_terms(lo, hi, x, x_far, g, g_far, transposed=False):
        return weight_terms(
            table, "rest", "rest_block", lo, hi, x, x_far, g, g_far, transposed
        )

    down = down + after(down_near, grad_query_rows)
    down, down_out = down[:own_rows], down[own_rows:].astype(LOW)
    down_far = flip(down_out, "tp", 2)

    def up_terms(lo, hi, *late):
        return rest_terms(lo, hi, normed_two, two_theirs, after(grad_up_pre, *late), up_theirs)

    up_sent = up_terms(half_count // 2, half_count, grad_query_rows)
    up_first = flip(up_sent[half:], "dp", 2)

    def exchange_mid(terms, first, order, *late):
        got, left = [first], half_count // 2
        for b in order[1:]:
            send = terms(left // 2, left, *late).astype(jnp.float32)
            rows = send.shape[0]
            for other in got:
                send = send + other[other.shape[0] - rows :]
            send = send.astype(LOW)
            got.append(flip(send, "dp", 1 << b))
            left //= 2
        return got[1:], send

    down_late, down_last = exchange_mid(down_terms, down_first, down_bits, grad_query_rows)
    kv_total, grad_gate = lax.optimization_barrier(
        (kv_total, grad_gate, up_sent, down_out, down_last)
    )[:2]
    for back in kv_back:
        kv_total = kv_total + back
    key_grad = turn_back(kv_total[:size], cosine, sine)
    grad_kv_rows = jnp.concatenate([key_grad, kv_total[size:]], 0).astype(LOW)
    proj_rows = jnp.concatenate([grad_query_rows, grad_kv_rows], 0)
    units = proj_rows.shape[0]
    pieces = [
        branch_send[:, begin : begin + rows_here] for begin in range(0, branch_send.shape[1], rows_here)
    ]
    both_theirs = flip(jnp.concatenate([proj_rows, *pieces], 0), "dp", 1)

    own_order = jnp.concatenate(
        [take(proj_rows, start, own_rows, 1) for start in row_starts], 1
    )

    def one_terms(lo, hi):
        cut = own_order[:, lo * own_rows : hi * own_rows]
        return dot(cut[:wide], w_query, 0, 1) + dot(cut[wide:], w_kv, 0, 0)

    grad_normed_one, one_out = near_sum(one_terms)
    one_far = flip(one_out, "tp", 2)
    up_second = flip(after(up_sent[:half], one_out), "dp", 2)
    output_rows = (middle + (down + after(down_far, one_out))).astype(LOW)
    one_theirs = join_rows(table, after(one_near, one_out), cores_far[:, width // 2 :])
    up_kept = up_terms(0, 1, one_out)
    grad_gate = grad_gate.astype(jnp.float32)
    grad_normed_one = after(grad_normed_one, output_rows, up_kept, grad_gate, one_theirs) + one_far
    grad_in_norm, gain_one = norm_back(grad_normed_one, own_inputs, own(scale_one), norm1_gain)
    input_rows = grad_middle + grad_in_norm

    gains = jnp.stack([after(gain_one, input_rows), gain_two])
    gains_core = flip(gains, "tp", 1)
    up_mid = up_terms(half_count // 4, half_count // 2, gains)
    gains, gains_core, up_first = lax.optimization_barrier((gains, gains_core, up_first, up_mid))[:3]
    gains = gains + gains_core
    up_late, up_last = exchange_mid(
        lambda lo, hi, *late: up_mid if hi == half_count // 2 else up_terms(lo, hi, *late),
        up_first,
        rest_bits,
        gains,
    )
    both_theirs = after(both_theirs, up_last)
    proj_theirs = both_theirs[:units]
    branch_near = jnp.concatenate(
        [
            both_theirs[begin : begin + branch_send.shape[0]]
            for begin in range(units, both_theirs.shape[0], branch_send.shape[0])
        ],
        1,
    )
    branch_theirs = jnp.concatenate([branch_near, flip(branch_near, "tp", 1)], 0)
    gains, *down_late = lax.optimization_barrier((gains, *down_late, up_last))[:-1]
    gains = gains + flip(gains, "tp", 2)
    gains = pick_columns(table, "rest", gains) + flip(
        pick_columns(table, "rest_far", gains), "dp", 1
    )

    out_late, proj_late = lax.optimization_barrier((attended, proj_rows, up_last))[:2]

    def last_terms(lo, hi, *late):
        first, second = after(proj_late, *late), after(out_late, *late)
        return jnp.concatenate(
            [
                rest_terms(lo, hi, normed_one, one_theirs, first, proj_theirs, True),
                rest_terms(lo, hi, branch_all, branch_theirs, second, att_theirs, True),
            ],
            1,
        )

    def with_gains(terms, lo, hi, *others):
        extra = gains[:, lo * block : hi * block]
        for other, other_gains in others:
            terms = terms.astype(jnp.float32) + other
            extra = extra + other_gains
        columns = terms.shape[1]
        extra = jnp.pad(extra, ((0, 14), (0, -extra.shape[1] % columns)))[:, :columns]
        return jnp.concatenate([terms.astype(LOW), extra.astype(LOW)], 0)

    def split(message, count):
        rows = count * block
        return message[:rows], message[rows : rows + 2, :rows]

    quarter = half_count // 4
    sent = last_terms(half_count // 2, half_count)
    cut = quarter * block
    firsts = with_gains(sent[cut:], 3 * quarter, half_count)
    seconds = with_gains(sent[:cut], 2 * quarter, 3 * quarter)
    mids = [split(flip(firsts, "dp", 2), quarter)]
    last_second = split(flip(after(seconds, firsts), "dp", 2), quarter)
    up_late = [*up_late, up_second]
    proj_kept = rest_terms(0, 1, normed_one, one_theirs, after(proj_late, firsts), proj_theirs, True)
    out_kept = rest_terms(0, 1, branch_all, branch_theirs, after(out_late, firsts), att_theirs, True)
    down_kept = down_terms(0, 1, firsts)
    left = half_count // 2
    for b in rest_bits[1:]:
        count = left // 2
        terms = last_terms(count, left, firsts)
        terms, *up_late = lax.optimization_barrier((terms, *up_late, proj_kept, out_kept, down_kept))[
            :-3
        ]
        send = with_gains(
            terms, count, left, *((o[-count * block :], g[:, -count * block :]) for o, g in mids)
        )
        mids.append(split(flip(send, "dp", 1 << b), count))
        left = count
    down_second = flip(after(down_sent[:half], firsts), "dp", 1)

    def ending(kept, *others):
        kept = kept.astype(jnp.float32)
        for other in others:
            kept = kept + other[:block]
        return kept

    down_kept, down_second = lax.optimization_barrier((down_kept, down_second, send))[:2]
    grad_down = ending(down_kept, down_second, *down_late)
    grad_last = ending(
        jnp.concatenate([proj_kept, out_kept], 1), last_second[0], *(m[0] for m in mids[1:])
    )
    gains = gains[:, :block] + last_second[1][:, :block]
    for _, other in mids[1:]:
        gains = gains + other[:, :block]
    grad_up = ending(up_kept, *up_late)
    narrow = wide + 2 * size

    return (
        output_rows,
        input_rows,
        gains[0],
        grad_last[:, :wide],
        grad_last[:, wide : wide + size],
        grad_last[:, wide + size : narrow],
        grad_last[:, narrow:].T,
        gains[1],
        grad_gate,
        grad_up,
        grad_down.T,
    )


def solution(mesh):
    placed = (
        P("dp", None),
        P("dp"),
        P(),
        P(None, "tp"),
        P(None, "tp"),
        P(None, "tp"),
        P("tp", None),
        P(),
        P(None, "tp"),
        P(None, "tp"),
        P("tp", None),
        P("dp", None),
    )
    return jax.shard_map(
        shards,
        mesh=mesh,
        in_specs=placed,
        out_specs=(
            P(("dp", "tp"), None),
            P(("dp", "tp"), None),
            P("dp"),
            P("dp", "tp"),
            P("dp", "tp"),
            P("dp", "tp"),
            P("tp", "dp"),
            P("dp"),
            P("dp", "tp"),
            P("dp", "tp"),
            P("tp", "dp"),
        ),
        check_vma=False,
    )
```

```python
import functools

import jax
import jax.numpy as jnp
import numpy as np
from jax import lax
from jax.experimental import pallas as pl
from jax.experimental.pallas import tpu as pltpu
from jax.sharding import PartitionSpec as P

SPAN = 4
EPSILON = 1e-05
FAR_BELOW = -1e30
LOW = jnp.bfloat16
ROW_MASKS = (0, 2, 1, 3)


def flip(block, axis, mask):
    return lax.ppermute(block, axis, [(i, i ^ mask) for i in range(lax.axis_size(axis))])


def dot(left, right, left_dim, right_dim):
    return lax.dot_general(
        left,
        right,
        (((left_dim,), (right_dim,)), ((), ())),
        preferred_element_type=jnp.float32,
    )


def in_hbm(*arrays):
    return [pltpu.with_memory_space_constraint(a, pltpu.HBM) for a in arrays]


def own_mask(pos, begin, keys, queries):
    key_at = lax.broadcasted_iota(jnp.int32, (keys, queries), 0)
    query_at = lax.broadcasted_iota(jnp.int32, (keys, queries), 1) + begin
    return (key_at <= query_at) & (key_at >= query_at - pos)


def row_starts(spot, rows):
    part = rows // len(ROW_MASKS)
    return [pl.multiple_of((spot ^ m) * part, part) for m in ROW_MASKS]


def forward_kernel(
    heads,
    size,
    at_ref,
    pos_ref,
    q_ref,
    kv0,
    kv1,
    kv2,
    kv3,
    o_ref,
    lse_ref,
    keys,
    vals,
    top,
    acc,
    ordered,
):
    rank, spot = at_ref[0], at_ref[1]
    rows = pos_ref.shape[1]

    @pl.when(pl.program_id(0) == 0)
    def _():
        for m, kv in enumerate((kv0, kv1, kv2, kv3)):
            keys[m] = kv[:size, :].T
            vals[m, :size, :] = kv[size:, :]
            vals[m, size:, :] = jnp.ones((16, rows), LOW)

    pos = pos_ref[...]
    mask = own_mask(pos, 0, rows, rows)
    for h in range(heads):
        scores = dot(keys[0], q_ref[h * size : (h + 1) * size, :], 1, 0)
        scores = jnp.where(mask, scores, FAR_BELOW)
        peak = jnp.max(scores, 0, keepdims=True)
        acc[h] = dot(vals[0], jnp.exp(scores - peak).astype(LOW), 1, 0)
        top[h] = peak
    seen = pos > lax.broadcasted_iota(jnp.int32, (1, rows), 1)
    for m in range(1, SPAN):

        @pl.when((rank ^ m) < rank)
        def _():
            for h in range(heads):
                scores = dot(keys[m], q_ref[h * size : (h + 1) * size, :], 1, 0)
                old = top[h]
                peak = jnp.where(seen, jnp.maximum(old, jnp.max(scores, 0, keepdims=True)), old)
                weights = jnp.exp(scores - jnp.where(seen, peak, -FAR_BELOW)).astype(LOW)
                acc[h] = acc[h] * jnp.exp(old - peak) + dot(vals[m], weights, 1, 0)
                top[h] = peak

    for h in range(heads):
        total = acc[h, size : size + 1, :]
        ordered[h * size : (h + 1) * size, :] = (acc[h, :size, :] / total).astype(LOW)
        lse_ref[h] = top[h] + jnp.log(total)
    for j, start in enumerate(row_starts(spot, rows)):
        part = rows // len(ROW_MASKS)
        o_ref[:, j * part : (j + 1) * part] = ordered[:, pl.ds(start, part)]


def backward_kernel(
    heads,
    size,
    at_ref,
    pos_ref,
    q_ref,
    do_in,
    o_in,
    lse_ref,
    cos_ref,
    sin_ref,
    kv0,
    kv1,
    kv2,
    kv3,
    dq_ref,
    g0,
    g1,
    g2,
    g3,
    keys,
    vals,
    dq,
    total,
    do_ref,
    o_ref,
):
    rank, spot = at_ref[0], at_ref[1]
    rows = pos_ref.shape[1]
    half = rows // 2
    blocks = (kv0, kv1, kv2, kv3)
    step = pl.program_id(0)

    @pl.when(step == 0)
    def _():
        for m, kv in enumerate(blocks):
            keys[m] = kv[:size, :].T
            vals[m] = kv[size:, :].T
        total[...] = jnp.zeros_like(total)

    part = rows // len(ROW_MASKS)
    for j, start in enumerate(row_starts(spot, rows)):
        do_ref[:, pl.ds(start, part)] = do_in[:, j * part : (j + 1) * part]
        o_ref[:, pl.ds(start, part)] = o_in[:, j * part : (j + 1) * part]
    pos = pos_ref[...]
    seen = pos > lax.broadcasted_iota(jnp.int32, (1, rows), 1)
    deltas = []
    for h in range(heads):
        span = slice(h * size, (h + 1) * size)
        deltas.append(
            jnp.sum(
                do_ref[span, :].astype(jnp.float32) * o_ref[span, :].astype(jnp.float32),
                0,
                keepdims=True,
            )
        )
    for part in range(2):
        cols = slice(part * half, (part + 1) * half)
        count = (part + 1) * half
        mask = own_mask(pos[:, cols], part * half, count, half)
        for h in range(heads):
            span = slice(h * size, (h + 1) * size)
            query, grad = q_ref[span, cols], do_ref[span, cols]
            scores = dot(keys[0, :count, :], query, 1, 0)
            probs = jnp.exp(jnp.where(mask, scores, FAR_BELOW) - lse_ref[h, :, cols])
            grad_probs = dot(vals[0, :count, :], grad, 1, 0)
            grad_scores = (probs * (grad_probs - deltas[h][:, cols])).astype(LOW)
            total[0, :size, :count] += dot(query, grad_scores, 1, 1)
            total[0, size:, :count] += dot(grad, probs.astype(LOW), 1, 1)
            dq[h, :, cols] = dot(kv0[:size, :count], grad_scores, 1, 0)
    for m in range(1, SPAN):

        @pl.when((rank ^ m) < rank)
        def _():
            for h in range(heads):
                span = slice(h * size, (h + 1) * size)
                query, grad = q_ref[span, :], do_ref[span, :]
                scores = dot(keys[m], query, 1, 0)
                probs = jnp.exp(scores - jnp.where(seen, lse_ref[h], -FAR_BELOW))
                grad_probs = dot(vals[m], grad, 1, 0)
                grad_scores = (probs * (grad_probs - deltas[h])).astype(LOW)
                total[m, :size, :] += dot(query, grad_scores, 1, 1)
                total[m, size:, :] += dot(grad, probs.astype(LOW), 1, 1)
                dq[h] += dot(blocks[m][:size, :], grad_scores, 1, 0)

    middle_at = size // 2
    cosine, sine = cos_ref[...], sin_ref[...]
    for h in range(heads):
        first = dq[h, :middle_at, :] * size ** (-0.5)
        second = dq[h, middle_at:, :] * size ** (-0.5)
        base = h * size
        dq_ref[base : base + middle_at, :] = (first * cosine + second * sine).astype(LOW)
        dq_ref[base + middle_at : base + size, :] = (second * cosine - first * sine).astype(LOW)

    @pl.when(step == pl.num_programs(0) - 1)
    def _():
        g0[...] = total[0]
        for m, out in ((1, g1), (2, g2), (3, g3)):
            out[...] = total[m].astype(LOW)


def attention_forward(at, pos, queries, blocks, size, heads):
    wide, rows = queries.shape
    count = wide // size
    whole = pl.BlockSpec((2 * size, rows), lambda i, r: (0, 0))
    some = pl.BlockSpec((heads * size, rows), lambda i, r: (i, 0))
    return pl.pallas_call(
        functools.partial(forward_kernel, heads, size),
        out_shape=(
            jax.ShapeDtypeStruct((wide, rows), LOW),
            jax.ShapeDtypeStruct((count, 1, rows), jnp.float32),
        ),
        grid_spec=pltpu.PrefetchScalarGridSpec(
            num_scalar_prefetch=1,
            grid=(count // heads,),
            in_specs=[pl.BlockSpec((1, rows), lambda i, r: (0, 0)), some] + [whole] * SPAN,
            out_specs=[some, pl.BlockSpec((heads, 1, rows), lambda i, r: (i, 0, 0))],
            scratch_shapes=[
                pltpu.VMEM((SPAN, rows, size), LOW),
                pltpu.VMEM((SPAN, size + 16, rows), LOW),
                pltpu.VMEM((heads, 1, rows), jnp.float32),
                pltpu.VMEM((heads, size + 16, rows), jnp.float32),
                pltpu.VMEM((heads * size, rows), LOW),
            ],
        ),
        compiler_params=pltpu.CompilerParams(vmem_limit_bytes=24 << 20),
        cost_estimate=pl.CostEstimate(
            flops=32 * wide * rows * rows * SPAN,
            bytes_accessed=4 * wide * rows,
            transcendentals=0,
        ),
        name="attention_forward",
    )(at, pos, queries, *blocks)


def attention_backward(at, pos, queries, grads, attended, lse, cosine, sine, blocks, size, heads):
    wide, rows = queries.shape
    count = wide // size
    whole = pl.BlockSpec((2 * size, rows), lambda i, r: (0, 0))
    table = pl.BlockSpec((size // 2, rows), lambda i, r: (0, 0))
    some = pl.BlockSpec((heads * size, rows), lambda i, r: (i, 0))
    return pl.pallas_call(
        functools.partial(backward_kernel, heads, size),
        out_shape=(
            jax.ShapeDtypeStruct((wide, rows), LOW),
            jax.ShapeDtypeStruct((2 * size, rows), jnp.float32),
        )
        + (jax.ShapeDtypeStruct((2 * size, rows), LOW),) * (SPAN - 1),
        grid_spec=pltpu.PrefetchScalarGridSpec(
            num_scalar_prefetch=1,
            grid=(count // heads,),
            in_specs=[
                pl.BlockSpec((1, rows), lambda i, r: (0, 0)),
                some,
                some,
                some,
                pl.BlockSpec((heads, 1, rows), lambda i, r: (i, 0, 0)),
                table,
                table,
            ]
            + [whole] * SPAN,
            out_specs=[some] + [whole] * SPAN,
            scratch_shapes=[
                pltpu.VMEM((SPAN, rows, size), LOW),
                pltpu.VMEM((SPAN, rows, size), LOW),
                pltpu.VMEM((heads, size, rows), jnp.float32),
                pltpu.VMEM((SPAN, 2 * size, rows), jnp.float32),
                pltpu.VMEM((heads * size, rows), LOW),
                pltpu.VMEM((heads * size, rows), LOW),
            ],
        ),
        compiler_params=pltpu.CompilerParams(vmem_limit_bytes=24 << 20),
        cost_estimate=pl.CostEstimate(
            flops=48 * wide * rows * rows * SPAN,
            bytes_accessed=10 * wide * rows,
            transcendentals=0,
        ),
        name="attention_backward",
    )(at, pos, *in_hbm(queries, grads, attended, lse, cosine, sine, *blocks))


def take(values, start, size, dim):
    starts = [np.uint32(0)] * values.ndim
    starts[dim] = start
    sizes = list(values.shape)
    sizes[dim] = size
    return lax.dynamic_slice(values, starts, sizes)


def pick(values, places, blocks, dim):
    size = values.shape[dim] // blocks
    return jnp.concatenate(
        [lax.dynamic_slice_in_dim(values, p * size, size, dim) for p in places], dim
    )


class Table:
    def __init__(self, **parts):
        self.begin, at = {}, 0
        for name, part in parts.items():
            self.begin[name] = at
            at += part.shape[0]
        self.values = jnp.concatenate([p.astype(jnp.int32) for p in parts.values()])

    def list(self, name, lo, hi):
        return [self.values[self.begin[name] + j] for j in range(lo, hi)]


def after(value, *others):
    return lax.optimization_barrier((value, *others))[0]


def parity_sum(terms, dim):
    count = lax.axis_size("dp")
    groups = [list(range(p, count, 2)) for p in range(2)]
    return lax.psum_scatter(
        terms.astype(LOW), "dp", scatter_dimension=dim, axis_index_groups=groups, tiled=True
    )


def terms_kernel(transposed, places, x, x_far, g, g_far, out):
    del places
    side = 1 if transposed else 0
    out[...] = (dot(x[...], g[...], 0, side) + dot(x_far[...], g_far[...], 0, side)).astype(LOW)


def weight_terms(table, name, far, lo, hi, x, x_far, g, g_far, transposed=False, keep=True):
    count = hi - lo
    size = x.shape[1] // lax.axis_size("dp")
    rows = x.shape[0]
    units = g.shape[0] if transposed else g.shape[1]
    if size % 128:
        side = 1 if transposed else 0
        mine = pick(x, table.list(name, lo, hi), x.shape[1] // size, 1)
        theirs = pick(x_far, table.list(far, lo, hi), x_far.shape[1] // size, 1)
        return (dot(mine, g, 0, side) + dot(theirs, g_far, 0, side)).astype(LOW)
    whole = pl.BlockSpec(g.shape, lambda i, p: (0, 0))
    begin, far_begin = table.begin[name] + lo, table.begin[far] + lo
    return pl.pallas_call(
        functools.partial(terms_kernel, transposed),
        out_shape=(jax.ShapeDtypeStruct if keep else pltpu.HBM)((count * size, units), LOW),
        grid_spec=pltpu.PrefetchScalarGridSpec(
            num_scalar_prefetch=1,
            grid=(count,),
            in_specs=[
                pl.BlockSpec((rows, size), lambda i, p: (0, p[begin + i])),
                pl.BlockSpec((rows, size), lambda i, p: (0, p[far_begin + i])),
                whole,
                whole,
            ],
            out_specs=pl.BlockSpec((size, units), lambda i, p: (i, 0)),
        ),
        compiler_params=pltpu.CompilerParams(vmem_limit_bytes=20 << 20),
        cost_estimate=pl.CostEstimate(
            flops=24 * rows * count * size * units, bytes_accessed=4 * rows * units, transcendentals=0
        ),
        name="weight_terms",
    )(table.values, x, x_far, g, g_far)


def copy_kernel(places, source, target):
    del places
    target[...] = source[...]


def pick_columns(table, name, values, part=None, parts=1):
    blocks = lax.axis_size("dp")
    rows, count = values.shape[0] // parts, blocks // 2
    size = values.shape[1] // blocks
    if size % 128:
        if part is not None:
            values = lax.dynamic_slice_in_dim(values, table.list(part, 0, 1)[0] * rows, rows, 0)
        return pick(values, table.list(name, 0, count), blocks, 1)
    begin = table.begin[name]
    row = 0 if part is None else table.begin[part]
    return pl.pallas_call(
        copy_kernel,
        out_shape=jax.ShapeDtypeStruct((rows, count * size), values.dtype),
        grid_spec=pltpu.PrefetchScalarGridSpec(
            num_scalar_prefetch=1,
            grid=(count,),
            in_specs=[
                pl.BlockSpec(
                    (rows, size), lambda i, p: (0 if part is None else p[row], p[begin + i])
                )
            ],
            out_specs=pl.BlockSpec((rows, size), lambda i, p: (0, i)),
        ),
        compiler_params=pltpu.CompilerParams(vmem_limit_bytes=8 << 20),
        cost_estimate=pl.CostEstimate(
            flops=65536 * rows * count * size, bytes_accessed=4 * rows * count * size, transcendentals=0
        ),
        name="pick_columns",
    )(table.values, values)


def load_kernel(*refs):
    *pairs, sems = refs
    half = len(pairs) // 2
    copies = [
        pltpu.make_async_copy(source, target, sems.at[j])
        for j, (source, target) in enumerate(zip(pairs[:half], pairs[half:]))
    ]
    for copy in copies:
        copy.start()
    for copy in copies:
        copy.wait()


def load_weights(*weights):
    return pl.pallas_call(
        load_kernel,
        out_shape=tuple(pltpu.VMEM(w.shape, w.dtype) for w in weights),
        in_specs=[pl.BlockSpec(memory_space=pl.ANY)] * len(weights),
        out_specs=[pl.BlockSpec(memory_space=pltpu.VMEM)] * len(weights),
        scratch_shapes=[pltpu.SemaphoreType.DMA((len(weights),))],
        compiler_params=pltpu.CompilerParams(vmem_limit_bytes=2 << 20),
        cost_estimate=pl.CostEstimate(
            flops=20_000_000_000,
            bytes_accessed=2 * sum(w.size for w in weights),
            transcendentals=0,
        ),
        name="load_weights",
    )(*in_hbm(*weights))


def in_vmem(*arrays):
    return [pltpu.with_memory_space_constraint(a, pltpu.VMEM) for a in arrays]


def ffn_kernel(rows, gate_w, up_w, grad_in, hidden, grad_gate, grad_up):
    step = 128
    for begin in range(0, hidden.shape[1], step):
        cut = slice(begin, begin + step)
        both = dot(rows[...], jnp.concatenate([gate_w[:, cut], up_w[:, cut]], 1), 1, 0)
        gate, up = both[:, :step], both[:, step:]
        grad = grad_in[:, cut]
        sigma = jax.nn.sigmoid(gate)
        active = gate * sigma
        hidden[:, cut] = (active * up).astype(LOW)
        grad_gate[:, cut] = (grad * up * sigma * (1.0 + gate * (1.0 - sigma))).astype(LOW)
        grad_up[:, cut] = (grad * active).astype(LOW)


def feed_forward(rows, w_gate, w_up, grad_hidden):
    count, width = rows.shape
    units = w_gate.shape[1]
    here = pl.BlockSpec(memory_space=pltpu.VMEM)
    return pl.pallas_call(
        ffn_kernel,
        out_shape=(jax.ShapeDtypeStruct((count, units), LOW),) * 3,
        in_specs=[here] * 4,
        out_specs=[here] * 3,
        compiler_params=pltpu.CompilerParams(vmem_limit_bytes=20 << 20),
        cost_estimate=pl.CostEstimate(
            flops=6 * count * width * units,
            bytes_accessed=4 * width * units,
            transcendentals=count * units,
        ),
        name="feed_forward",
    )(*in_vmem(rows, w_gate, w_up, grad_hidden))


def back_kernel(gate_rows, up_rows, gate_w, up_w, out):
    step = out.shape[1]
    cut = pl.ds(pl.multiple_of(pl.program_id(0) * step, step), step)
    total = dot(gate_rows[...], gate_w[cut, :], 1, 1) + dot(up_rows[...], up_w[cut, :], 1, 1)
    out[...] = total.astype(out.dtype)


def feed_forward_back(grad_gate, grad_up, w_gate, w_up, half, kind):
    count, units = grad_gate.shape
    width = w_gate.shape[0]
    step = width // 2
    rows = pl.BlockSpec((count // 2, units), lambda i: (half, 0))
    here = pl.BlockSpec(memory_space=pltpu.VMEM)
    return pl.pallas_call(
        back_kernel,
        out_shape=jax.ShapeDtypeStruct((count // 2, width), kind),
        grid=(2,),
        in_specs=[rows, rows, here, here],
        out_specs=pl.BlockSpec((count // 2, step), lambda i: (0, i)),
        compiler_params=pltpu.CompilerParams(vmem_limit_bytes=16 << 20),
        cost_estimate=pl.CostEstimate(
            flops=10 * count * width * units, bytes_accessed=4 * width * units, transcendentals=0
        ),
        name="feed_forward_back",
    )(grad_gate, grad_up, *in_vmem(w_gate, w_up))


def join_kernel(places, first, second, out):
    del places

    @pl.when(pl.program_id(0) == 0)
    def _():
        out[...] = first[...]

    @pl.when(pl.program_id(0) == 1)
    def _():
        out[...] = second[...]


def join_rows(table, first, second):
    rows, width = first.shape
    core = table.begin["core"]
    whole = pl.BlockSpec((rows, width), lambda i, p: (0, 0))
    return pl.pallas_call(
        join_kernel,
        out_shape=jax.ShapeDtypeStruct((2 * rows, width), first.dtype),
        grid_spec=pltpu.PrefetchScalarGridSpec(
            num_scalar_prefetch=1,
            grid=(2,),
            in_specs=[whole, whole],
            out_specs=pl.BlockSpec((rows, width), lambda i, p: (p[core] ^ i, 0)),
        ),
        compiler_params=pltpu.CompilerParams(vmem_limit_bytes=8 << 20),
        cost_estimate=pl.CostEstimate(
            flops=1_000_000_000, bytes_accessed=8 * rows * width, transcendentals=0
        ),
        name="join_rows",
    )(table.values, first, second)


def row_kernel(left, right, send, kept):
    half = left.shape[0] // 2
    send[...] = dot(left[half:, :], right[...], 1, 0).astype(LOW)
    kept[...] = dot(left[:half, :], right[...], 1, 0)


def row_terms(left, right):
    rows, units = left.shape
    half, width = rows // 2, right.shape[1]
    step = 256
    return pl.pallas_call(
        row_kernel,
        out_shape=(
            jax.ShapeDtypeStruct((half, width), LOW),
            jax.ShapeDtypeStruct((half, width), jnp.float32),
        ),
        grid=(width // step,),
        in_specs=[
            pl.BlockSpec((rows, units), lambda i: (0, 0)),
            pl.BlockSpec((units, step), lambda i: (0, i)),
        ],
        out_specs=[pl.BlockSpec((half, step), lambda i: (0, i))] * 2,
        compiler_params=pltpu.CompilerParams(vmem_limit_bytes=16 << 20),
        cost_estimate=pl.CostEstimate(
            flops=8 * rows * units * width, bytes_accessed=2 * units * width, transcendentals=0
        ),
        name="row_terms",
    )(left, right)


def turn(values, cosine, sine):
    half = cosine.shape[0]
    heads = values.shape[0] // (2 * half)
    pieces = values.reshape(heads, 2, half, values.shape[1])
    first, second = pieces[:, 0], pieces[:, 1]
    return jnp.stack(
        [first * cosine - second * sine, second * cosine + first * sine], 1
    ).reshape(values.shape)


def turn_back(grads, cosine, sine):
    return turn(grads, cosine, -sine)


def norm_back(grad_rows, values, scale_rows, gain):
    scaled = grad_rows * gain
    inner_mean = jnp.mean(scaled * values, -1, keepdims=True)
    return (
        scale_rows * (scaled - values * scale_rows * scale_rows * inner_mean),
        jnp.sum(grad_rows * values * scale_rows, 0),
    )


def shards(
    tokens,
    positions,
    norm1_gain,
    w_query,
    w_key,
    w_value,
    w_out,
    norm2_gain,
    w_gate,
    w_up,
    w_down,
    cotangent,
):
    rows_here, width = tokens.shape
    size = w_key.shape[1]
    dp = lax.axis_size("dp")
    tp_count = len(ROW_MASKS)
    own_rows = rows_here // tp_count
    block = width // dp
    bits = dp.bit_length() - 1
    half_count = dp // 2

    def exchange_order(order):
        return np.array(
            [
                sum(((j >> (len(order) - 1 - k)) & 1) << b for k, b in enumerate(order))
                for j in range(1 << len(order))
            ],
            np.int32,
        )

    down_bits = [0] + list(range(2, bits))
    rest_bits = list(range(1, bits))

    place = lax.axis_index("dp").astype(jnp.int32)
    spot = lax.axis_index("tp").astype(jnp.int32)
    natural = np.arange(half_count, dtype=np.int32)
    down_here, rest_here = place ^ exchange_order(down_bits), place ^ exchange_order(rest_bits)
    table = Table(
        mine=2 * natural + (place & 1),
        theirs=2 * natural + (1 - (place & 1)),
        natural=jnp.asarray(natural),
        down=down_here,
        down_far=down_here ^ 2,
        rest=rest_here,
        rest_far=rest_here ^ 1,
        rest_block=rest_here >> 1,
        core=(spot & 1)[None],
    )
    at = jnp.stack([place & (SPAN - 1), spot])
    row_starts = [((spot ^ m) * own_rows).astype(jnp.uint32) for m in ROW_MASKS]
    core_starts = [(c * (rows_here // 2)).astype(jnp.uint32) for c in (spot & 1, 1 - (spot & 1))]
    tokens, table.values, at, row_starts, core_starts = lax.optimization_barrier(
        (tokens, table.values, at, row_starts, core_starts)
    )
    pos = positions.reshape(1, rows_here)

    def own(values):
        return take(values, row_starts[0], own_rows, 0)

    inputs = tokens.astype(jnp.float32)
    scale_one = lax.rsqrt(jnp.mean(inputs * inputs, -1, keepdims=True) + EPSILON)
    normed_one = (inputs * scale_one * norm1_gain).astype(LOW)
    half = size // 2
    frequency = jnp.exp(
        -jnp.log(10000.0) * (2.0 * jnp.arange(half, dtype=jnp.float32) / size)
    )
    angles = frequency[:, None] * positions.astype(jnp.float32)[None, :]
    cosine, sine = jnp.cos(angles), jnp.sin(angles)
    w_kv = jnp.concatenate([w_key.T, w_value.T], 0)
    paired = dot(w_kv, normed_one, 1, 1)
    paired = jnp.concatenate([turn(paired[:size], cosine, sine), paired[size:]], 0).astype(LOW)
    blocks = [paired] + [flip(paired, "dp", m) for m in range(1, SPAN)]
    queries = (turn(dot(w_query, normed_one, 0, 1), cosine, sine) * size ** (-0.5)).astype(LOW)

    wide = w_query.shape[1]

    def near_sum(part):
        send = part(2, 4).astype(LOW)
        near, kept = lax.optimization_barrier((flip(send, "tp", 1), part(0, 2)))
        pair = kept + near
        return pair[:own_rows], pair[own_rows:].astype(LOW)

    attended, lse = attention_forward(at, pos, queries, blocks, size, 8)

    branch, branch_out = near_sum(
        lambda lo, hi: dot(attended[:, lo * own_rows : hi * own_rows], w_out, 0, 0)
    )
    branch_far = flip(branch_out, "tp", 2)
    cot = jnp.concatenate(
        [take(after(cotangent, branch_out), start, own_rows, 0) for start in row_starts], 0
    )
    cot_send = pick_columns(table, "down_far", cot)
    cot_theirs = flip(cot_send, "dp", 2)
    own_inputs = own(tokens).astype(jnp.float32)
    one_send = pick_columns(table, "theirs", after(normed_one, cot_send), "core", 2)
    one_near = flip(one_send, "dp", 1)
    grad_hidden = dot(after(cot, one_send), w_down, 1, 1)
    middle = own_inputs + (after(branch, grad_hidden) + branch_far)

    scale_two = lax.rsqrt(jnp.mean(middle * middle, -1, keepdims=True) + EPSILON)
    own_two = (middle * scale_two * norm2_gain).astype(LOW)
    far_two = flip(own_two, "tp", 2)
    gate_w, up_w = load_weights(after(w_gate, own_two), w_up)
    pair_two = jnp.concatenate([after(own_two, gate_w), far_two], 0)
    core_two = flip(pair_two, "tp", 1)
    two_send = pick_columns(table, "theirs", pair_two)
    two_near = flip(two_send, "dp", 1)
    normed_two = jnp.concatenate([after(pair_two, two_send), core_two], 0)

    hidden, grad_gate_pre, grad_up_pre = feed_forward(normed_two, gate_w, up_w, grad_hidden)
    gate_theirs = flip(grad_gate_pre, "dp", 1)
    hidden_theirs = flip(hidden, "dp", 2)
    up_theirs = flip(grad_up_pre, "dp", 1)
    gate_late, cot_theirs, one_near = lax.optimization_barrier((grad_gate_pre, cot_theirs, one_near))

    two_back = functools.partial(feed_forward_back, gate_late, grad_up_pre, gate_w, up_w)
    grad_normed_two, two_out = near_sum(
        lambda lo, hi: two_back(lo // 2, jnp.float32 if lo == 0 else LOW)
    )
    two_out, two_near = lax.optimization_barrier((two_out, two_near))
    two_far = flip(two_out, "tp", 2)
    cores = jnp.concatenate([two_near, one_near], 1)
    cores_far = flip(cores, "tp", 1)
    two_theirs = jnp.concatenate([two_near, cores_far[:, : width // 2]], 0)

    down_near, down = row_terms(after(hidden, two_out), w_down)
    grad_normed_two = after(grad_normed_two, down) + two_far

    grad_mid_norm, gain_two = norm_back(grad_normed_two, middle, scale_two, norm2_gain)
    grad_middle = own(cotangent).astype(jnp.float32) + grad_mid_norm
    branch_grad = grad_middle.astype(LOW)
    grad_far = flip(branch_grad, "tp", 2)

    down_near = flip(after(down_near, branch_grad), "tp", 1)
    gate_terms = weight_terms(
        table,
        "mine",
        "natural",
        0,
        half_count,
        after(normed_two, branch_grad),
        two_theirs,
        grad_gate_pre,
        gate_theirs,
        keep=False,
    )
    grad_gate = parity_sum(gate_terms, 0)
    grad_pair = jnp.concatenate([after(branch_grad, gate_terms), grad_far], 0)
    grad_core = flip(grad_pair, "tp", 1)
    att_theirs = flip(after(attended, grad_pair), "dp", 1)

    def near_flip(terms, bit):
        half = terms.shape[0] // 2
        return [flip(terms[half:], "dp", 1 << bit), flip(terms[:half], "dp", 1 << bit)]

    def down_terms(lo, hi, *late):
        g = after(hidden, *late)
        return weight_terms(table, "down", "natural", lo, hi, cot, cot_theirs, g, hidden_theirs)

    down_sent = down_terms(half_count // 2, half_count, grad_pair)
    half = down_sent.shape[0] // 2
    down_first = flip(down_sent[half:], "dp", 1)
    branch_all = jnp.concatenate([after(grad_pair, down_sent), grad_core], 0)
    grad_attended = dot(w_out, branch_all, 1, 1).astype(LOW)
    grads = attention_backward(
        at, pos, queries, grad_attended, attended, lse, cosine, sine, blocks, size, 4
    )
    grad_query_rows, kv_total = grads[0], grads[1]
    branch_send = pick_columns(table, "theirs", after(grad_pair, grad_query_rows))
    *kv_sends, att_theirs = lax.optimization_barrier((*grads[2:], att_theirs))
    kv_back = [flip(kv_sends[m - 1], "dp", m) for m in range(1, SPAN)]

    def rest_terms(lo, hi, x, x_far, g, g_far, transposed=False):
        return weight_terms(
            table, "rest", "rest_block", lo, hi, x, x_far, g, g_far, transposed
        )

    down = down + after(down_near, grad_query_rows)
    down, down_out = down[:own_rows], down[own_rows:].astype(LOW)
    down_far = flip(down_out, "tp", 2)

    def up_terms(lo, hi, *late):
        return rest_terms(lo, hi, normed_two, two_theirs, after(grad_up_pre, *late), up_theirs)

    up_sent = up_terms(half_count // 2, half_count, grad_query_rows)
    up_first = flip(up_sent[half:], "dp", 2)

    def exchange_mid(terms, first, order, *late):
        got, left = [first], half_count // 2
        for b in order[1:]:
            send = terms(left // 2, left, *late).astype(jnp.float32)
            rows = send.shape[0]
            for other in got:
                send = send + other[other.shape[0] - rows :]
            send = send.astype(LOW)
            got.append(flip(send, "dp", 1 << b))
            left //= 2
        return got[1:], send

    down_late, down_last = exchange_mid(down_terms, down_first, down_bits, grad_query_rows)
    kv_total, grad_gate = lax.optimization_barrier(
        (kv_total, grad_gate, up_sent, down_out, down_last)
    )[:2]
    for back in kv_back:
        kv_total = kv_total + back
    key_grad = turn_back(kv_total[:size], cosine, sine)
    grad_kv_rows = jnp.concatenate([key_grad, kv_total[size:]], 0).astype(LOW)
    proj_rows = jnp.concatenate([grad_query_rows, grad_kv_rows], 0)
    units = proj_rows.shape[0]
    pieces = [
        branch_send[:, begin : begin + rows_here] for begin in range(0, branch_send.shape[1], rows_here)
    ]
    both_theirs = flip(jnp.concatenate([proj_rows, *pieces], 0), "dp", 1)

    own_order = jnp.concatenate(
        [take(proj_rows, start, own_rows, 1) for start in row_starts], 1
    )

    def one_terms(lo, hi):
        cut = own_order[:, lo * own_rows : hi * own_rows]
        return dot(cut[:wide], w_query, 0, 1) + dot(cut[wide:], w_kv, 0, 0)

    grad_normed_one, one_out = near_sum(one_terms)
    one_far = flip(one_out, "tp", 2)
    up_second = flip(after(up_sent[:half], one_out), "dp", 2)
    output_rows = (middle + (down + after(down_far, one_out))).astype(LOW)
    one_theirs = join_rows(table, after(one_near, one_out), cores_far[:, width // 2 :])
    up_kept = up_terms(0, 1, one_out)
    grad_gate = grad_gate.astype(jnp.float32)
    grad_normed_one = after(grad_normed_one, output_rows, up_kept, grad_gate, one_theirs) + one_far
    grad_in_norm, gain_one = norm_back(grad_normed_one, own_inputs, own(scale_one), norm1_gain)
    input_rows = grad_middle + grad_in_norm

    gains = jnp.stack([after(gain_one, input_rows), gain_two])
    gains_core = flip(gains, "tp", 1)
    up_mid = up_terms(half_count // 4, half_count // 2, gains)
    gains, gains_core, up_first = lax.optimization_barrier((gains, gains_core, up_first, up_mid))[:3]
    gains = gains + gains_core
    up_late, up_last = exchange_mid(
        lambda lo, hi, *late: up_mid if hi == half_count // 2 else up_terms(lo, hi, *late),
        up_first,
        rest_bits,
        gains,
    )
    both_theirs = after(both_theirs, up_last)
    proj_theirs = both_theirs[:units]
    branch_near = jnp.concatenate(
        [
            both_theirs[begin : begin + branch_send.shape[0]]
            for begin in range(units, both_theirs.shape[0], branch_send.shape[0])
        ],
        1,
    )
    branch_theirs = jnp.concatenate([branch_near, flip(branch_near, "tp", 1)], 0)
    gains, *down_late = lax.optimization_barrier((gains, *down_late, up_last))[:-1]
    gains = gains + flip(gains, "tp", 2)
    gains = pick_columns(table, "rest", gains) + flip(
        pick_columns(table, "rest_far", gains), "dp", 1
    )

    out_late, proj_late = lax.optimization_barrier((attended, proj_rows, up_last))[:2]

    def last_terms(lo, hi, *late):
        first, second = after(proj_late, *late), after(out_late, *late)
        return jnp.concatenate(
            [
                rest_terms(lo, hi, normed_one, one_theirs, first, proj_theirs, True),
                rest_terms(lo, hi, branch_all, branch_theirs, second, att_theirs, True),
            ],
            1,
        )

    def with_gains(terms, lo, hi, *others):
        extra = gains[:, lo * block : hi * block]
        for other, other_gains in others:
            terms = terms.astype(jnp.float32) + other
            extra = extra + other_gains
        columns = terms.shape[1]
        extra = jnp.pad(extra, ((0, 14), (0, -extra.shape[1] % columns)))[:, :columns]
        return jnp.concatenate([terms.astype(LOW), extra.astype(LOW)], 0)

    def split(message, count):
        rows = count * block
        return message[:rows], message[rows : rows + 2, :rows]

    quarter = half_count // 4
    sent = last_terms(half_count // 2, half_count)
    cut = quarter * block
    firsts = with_gains(sent[cut:], 3 * quarter, half_count)
    seconds = with_gains(sent[:cut], 2 * quarter, 3 * quarter)
    mids = [split(flip(firsts, "dp", 2), quarter)]
    last_second = split(flip(after(seconds, firsts), "dp", 2), quarter)
    up_late = [*up_late, up_second]
    proj_kept = rest_terms(0, 1, normed_one, one_theirs, after(proj_late, firsts), proj_theirs, True)
    out_kept = rest_terms(0, 1, branch_all, branch_theirs, after(out_late, firsts), att_theirs, True)
    down_kept = down_terms(0, 1, firsts)
    left = half_count // 2
    for b in rest_bits[1:]:
        count = left // 2
        terms = last_terms(count, left, firsts)
        terms, *up_late = lax.optimization_barrier((terms, *up_late, proj_kept, out_kept, down_kept))[
            :-3
        ]
        send = with_gains(
            terms, count, left, *((o[-count * block :], g[:, -count * block :]) for o, g in mids)
        )
        mids.append(split(flip(send, "dp", 1 << b), count))
        left = count
    down_second = flip(after(down_sent[:half], firsts), "dp", 1)

    def ending(kept, *others):
        kept = kept.astype(jnp.float32)
        for other in others:
            kept = kept + other[:block]
        return kept

    down_kept, down_second = lax.optimization_barrier((down_kept, down_second, send))[:2]
    grad_down = ending(down_kept, down_second, *down_late)
    grad_last = ending(
        jnp.concatenate([proj_kept, out_kept], 1), last_second[0], *(m[0] for m in mids[1:])
    )
    gains = gains[:, :block] + last_second[1][:, :block]
    for _, other in mids[1:]:
        gains = gains + other[:, :block]
    grad_up = ending(up_kept, *up_late)
    narrow = wide + 2 * size

    return (
        output_rows,
        input_rows,
        gains[0],
        grad_last[:, :wide],
        grad_last[:, wide : wide + size],
        grad_last[:, wide + size : narrow],
        grad_last[:, narrow:].T,
        gains[1],
        grad_gate,
        grad_up,
        grad_down.T,
    )


def solution(mesh):
    placed = (
        P("dp", None),
        P("dp"),
        P(),
        P(None, "tp"),
        P(None, "tp"),
        P(None, "tp"),
        P("tp", None),
        P(),
        P(None, "tp"),
        P(None, "tp"),
        P("tp", None),
        P("dp", None),
    )
    return jax.shard_map(
        shards,
        mesh=mesh,
        in_specs=placed,
        out_specs=(
            P(("dp", "tp"), None),
            P(("dp", "tp"), None),
            P("dp"),
            P("dp", "tp"),
            P("dp", "tp"),
            P("dp", "tp"),
            P("tp", "dp"),
            P("dp"),
            P("dp", "tp"),
            P("dp", "tp"),
            P("tp", "dp"),
        ),
        check_vma=False,
    )
```

```python
import functools

import jax
import jax.numpy as jnp
import numpy as np
from jax import lax
from jax.experimental import pallas as pl
from jax.experimental.pallas import tpu as pltpu
from jax.sharding import PartitionSpec as P

SPAN = 4
EPSILON = 1e-05
FAR_BELOW = -1e30
LOW = jnp.bfloat16
ROW_MASKS = (0, 2, 1, 3)


def flip(block, axis, mask):
    return lax.ppermute(block, axis, [(i, i ^ mask) for i in range(lax.axis_size(axis))])


def dot(left, right, left_dim, right_dim):
    return lax.dot_general(
        left,
        right,
        (((left_dim,), (right_dim,)), ((), ())),
        preferred_element_type=jnp.float32,
    )


def in_hbm(*arrays):
    return [pltpu.with_memory_space_constraint(a, pltpu.HBM) for a in arrays]


def own_mask(pos, begin, keys, queries):
    key_at = lax.broadcasted_iota(jnp.int32, (keys, queries), 0)
    query_at = lax.broadcasted_iota(jnp.int32, (keys, queries), 1) + begin
    return (key_at <= query_at) & (key_at >= query_at - pos)


def row_starts(spot, rows):
    part = rows // len(ROW_MASKS)
    return [pl.multiple_of((spot ^ m) * part, part) for m in ROW_MASKS]


def forward_kernel(
    heads,
    size,
    at_ref,
    pos_ref,
    q_ref,
    kv0,
    kv1,
    kv2,
    kv3,
    o_ref,
    lse_ref,
    keys,
    vals,
    top,
    acc,
    ordered,
):
    rank, spot = at_ref[0], at_ref[1]
    rows = pos_ref.shape[1]

    @pl.when(pl.program_id(0) == 0)
    def _():
        for m, kv in enumerate((kv0, kv1, kv2, kv3)):
            keys[m] = kv[:size, :].T
            vals[m, :size, :] = kv[size:, :]
            vals[m, size:, :] = jnp.ones((16, rows), LOW)

    pos = pos_ref[...]
    mask = own_mask(pos, 0, rows, rows)
    for h in range(heads):
        scores = dot(keys[0], q_ref[h * size : (h + 1) * size, :], 1, 0)
        scores = jnp.where(mask, scores, FAR_BELOW)
        peak = jnp.max(scores, 0, keepdims=True)
        acc[h] = dot(vals[0], jnp.exp(scores - peak).astype(LOW), 1, 0)
        top[h] = peak
    seen = pos > lax.broadcasted_iota(jnp.int32, (1, rows), 1)
    for m in range(1, SPAN):

        @pl.when((rank ^ m) < rank)
        def _():
            for h in range(heads):
                scores = dot(keys[m], q_ref[h * size : (h + 1) * size, :], 1, 0)
                old = top[h]
                peak = jnp.where(seen, jnp.maximum(old, jnp.max(scores, 0, keepdims=True)), old)
                weights = jnp.exp(scores - jnp.where(seen, peak, -FAR_BELOW)).astype(LOW)
                acc[h] = acc[h] * jnp.exp(old - peak) + dot(vals[m], weights, 1, 0)
                top[h] = peak

    for h in range(heads):
        total = acc[h, size : size + 1, :]
        ordered[h * size : (h + 1) * size, :] = (acc[h, :size, :] / total).astype(LOW)
        lse_ref[h] = top[h] + jnp.log(total)
    for j, start in enumerate(row_starts(spot, rows)):
        part = rows // len(ROW_MASKS)
        o_ref[:, j * part : (j + 1) * part] = ordered[:, pl.ds(start, part)]


def backward_kernel(
    heads,
    size,
    at_ref,
    pos_ref,
    q_ref,
    do_in,
    o_in,
    lse_ref,
    cos_ref,
    sin_ref,
    kv0,
    kv1,
    kv2,
    kv3,
    dq_ref,
    g0,
    g1,
    g2,
    g3,
    keys,
    vals,
    dq,
    total,
    do_ref,
    o_ref,
):
    rank, spot = at_ref[0], at_ref[1]
    rows = pos_ref.shape[1]
    half = rows // 2
    blocks = (kv0, kv1, kv2, kv3)
    step = pl.program_id(0)

    @pl.when(step == 0)
    def _():
        for m, kv in enumerate(blocks):
            keys[m] = kv[:size, :].T
            vals[m] = kv[size:, :].T
        total[...] = jnp.zeros_like(total)

    part = rows // len(ROW_MASKS)
    for j, start in enumerate(row_starts(spot, rows)):
        do_ref[:, pl.ds(start, part)] = do_in[:, j * part : (j + 1) * part]
        o_ref[:, pl.ds(start, part)] = o_in[:, j * part : (j + 1) * part]
    pos = pos_ref[...]
    seen = pos > lax.broadcasted_iota(jnp.int32, (1, rows), 1)
    deltas = []
    for h in range(heads):
        span = slice(h * size, (h + 1) * size)
        deltas.append(
            jnp.sum(
                do_ref[span, :].astype(jnp.float32) * o_ref[span, :].astype(jnp.float32),
                0,
                keepdims=True,
            )
        )
    for part in range(2):
        cols = slice(part * half, (part + 1) * half)
        count = (part + 1) * half
        mask = own_mask(pos[:, cols], part * half, count, half)
        for h in range(heads):
            span = slice(h * size, (h + 1) * size)
            query, grad = q_ref[span, cols], do_ref[span, cols]
            scores = dot(keys[0, :count, :], query, 1, 0)
            probs = jnp.exp(jnp.where(mask, scores, FAR_BELOW) - lse_ref[h, :, cols])
            grad_probs = dot(vals[0, :count, :], grad, 1, 0)
            grad_scores = (probs * (grad_probs - deltas[h][:, cols])).astype(LOW)
            total[0, :size, :count] += dot(query, grad_scores, 1, 1)
            total[0, size:, :count] += dot(grad, probs.astype(LOW), 1, 1)
            dq[h, :, cols] = dot(kv0[:size, :count], grad_scores, 1, 0)
    for m in range(1, SPAN):

        @pl.when((rank ^ m) < rank)
        def _():
            for h in range(heads):
                span = slice(h * size, (h + 1) * size)
                query, grad = q_ref[span, :], do_ref[span, :]
                scores = dot(keys[m], query, 1, 0)
                probs = jnp.exp(scores - jnp.where(seen, lse_ref[h], -FAR_BELOW))
                grad_probs = dot(vals[m], grad, 1, 0)
                grad_scores = (probs * (grad_probs - deltas[h])).astype(LOW)
                total[m, :size, :] += dot(query, grad_scores, 1, 1)
                total[m, size:, :] += dot(grad, probs.astype(LOW), 1, 1)
                dq[h] += dot(blocks[m][:size, :], grad_scores, 1, 0)

    middle_at = size // 2
    cosine, sine = cos_ref[...], sin_ref[...]
    for h in range(heads):
        first = dq[h, :middle_at, :] * size ** (-0.5)
        second = dq[h, middle_at:, :] * size ** (-0.5)
        base = h * size
        dq_ref[base : base + middle_at, :] = (first * cosine + second * sine).astype(LOW)
        dq_ref[base + middle_at : base + size, :] = (second * cosine - first * sine).astype(LOW)

    @pl.when(step == pl.num_programs(0) - 1)
    def _():
        g0[...] = total[0]
        for m, out in ((1, g1), (2, g2), (3, g3)):
            out[...] = total[m].astype(LOW)


def attention_forward(at, pos, queries, blocks, size, heads):
    wide, rows = queries.shape
    count = wide // size
    whole = pl.BlockSpec((2 * size, rows), lambda i, r: (0, 0))
    some = pl.BlockSpec((heads * size, rows), lambda i, r: (i, 0))
    return pl.pallas_call(
        functools.partial(forward_kernel, heads, size),
        out_shape=(
            jax.ShapeDtypeStruct((wide, rows), LOW),
            jax.ShapeDtypeStruct((count, 1, rows), jnp.float32),
        ),
        grid_spec=pltpu.PrefetchScalarGridSpec(
            num_scalar_prefetch=1,
            grid=(count // heads,),
            in_specs=[pl.BlockSpec((1, rows), lambda i, r: (0, 0)), some] + [whole] * SPAN,
            out_specs=[some, pl.BlockSpec((heads, 1, rows), lambda i, r: (i, 0, 0))],
            scratch_shapes=[
                pltpu.VMEM((SPAN, rows, size), LOW),
                pltpu.VMEM((SPAN, size + 16, rows), LOW),
                pltpu.VMEM((heads, 1, rows), jnp.float32),
                pltpu.VMEM((heads, size + 16, rows), jnp.float32),
                pltpu.VMEM((heads * size, rows), LOW),
            ],
        ),
        compiler_params=pltpu.CompilerParams(vmem_limit_bytes=24 << 20),
        cost_estimate=pl.CostEstimate(
            flops=32 * wide * rows * rows * SPAN,
            bytes_accessed=4 * wide * rows,
            transcendentals=0,
        ),
        name="attention_forward",
    )(at, pos, queries, *blocks)


def attention_backward(at, pos, queries, grads, attended, lse, cosine, sine, blocks, size, heads):
    wide, rows = queries.shape
    count = wide // size
    whole = pl.BlockSpec((2 * size, rows), lambda i, r: (0, 0))
    table = pl.BlockSpec((size // 2, rows), lambda i, r: (0, 0))
    some = pl.BlockSpec((heads * size, rows), lambda i, r: (i, 0))
    return pl.pallas_call(
        functools.partial(backward_kernel, heads, size),
        out_shape=(
            jax.ShapeDtypeStruct((wide, rows), LOW),
            jax.ShapeDtypeStruct((2 * size, rows), jnp.float32),
        )
        + (jax.ShapeDtypeStruct((2 * size, rows), LOW),) * (SPAN - 1),
        grid_spec=pltpu.PrefetchScalarGridSpec(
            num_scalar_prefetch=1,
            grid=(count // heads,),
            in_specs=[
                pl.BlockSpec((1, rows), lambda i, r: (0, 0)),
                some,
                some,
                some,
                pl.BlockSpec((heads, 1, rows), lambda i, r: (i, 0, 0)),
                table,
                table,
            ]
            + [whole] * SPAN,
            out_specs=[some] + [whole] * SPAN,
            scratch_shapes=[
                pltpu.VMEM((SPAN, rows, size), LOW),
                pltpu.VMEM((SPAN, rows, size), LOW),
                pltpu.VMEM((heads, size, rows), jnp.float32),
                pltpu.VMEM((SPAN, 2 * size, rows), jnp.float32),
                pltpu.VMEM((heads * size, rows), LOW),
                pltpu.VMEM((heads * size, rows), LOW),
            ],
        ),
        compiler_params=pltpu.CompilerParams(vmem_limit_bytes=24 << 20),
        cost_estimate=pl.CostEstimate(
            flops=48 * wide * rows * rows * SPAN,
            bytes_accessed=10 * wide * rows,
            transcendentals=0,
        ),
        name="attention_backward",
    )(at, pos, *in_hbm(queries, grads, attended, lse, cosine, sine, *blocks))


def take(values, start, size, dim):
    starts = [np.uint32(0)] * values.ndim
    starts[dim] = start
    sizes = list(values.shape)
    sizes[dim] = size
    return lax.dynamic_slice(values, starts, sizes)


def pick(values, places, blocks, dim):
    size = values.shape[dim] // blocks
    return jnp.concatenate(
        [lax.dynamic_slice_in_dim(values, p * size, size, dim) for p in places], dim
    )


class Table:
    def __init__(self, **parts):
        self.begin, at = {}, 0
        for name, part in parts.items():
            self.begin[name] = at
            at += part.shape[0]
        self.values = jnp.concatenate([p.astype(jnp.int32) for p in parts.values()])

    def list(self, name, lo, hi):
        return [self.values[self.begin[name] + j] for j in range(lo, hi)]


def after(value, *others):
    return lax.optimization_barrier((value, *others))[0]


def parity_sum(terms, dim):
    count = lax.axis_size("dp")
    groups = [list(range(p, count, 2)) for p in range(2)]
    return lax.psum_scatter(
        terms.astype(LOW), "dp", scatter_dimension=dim, axis_index_groups=groups, tiled=True
    )


def terms_kernel(transposed, places, x, x_far, g, g_far, out):
    del places
    side = 1 if transposed else 0
    out[...] = (dot(x[...], g[...], 0, side) + dot(x_far[...], g_far[...], 0, side)).astype(LOW)


def weight_terms(table, name, far, lo, hi, x, x_far, g, g_far, transposed=False, keep=True):
    count = hi - lo
    size = x.shape[1] // lax.axis_size("dp")
    rows = x.shape[0]
    units = g.shape[0] if transposed else g.shape[1]
    if size % 128:
        side = 1 if transposed else 0
        mine = pick(x, table.list(name, lo, hi), x.shape[1] // size, 1)
        theirs = pick(x_far, table.list(far, lo, hi), x_far.shape[1] // size, 1)
        return (dot(mine, g, 0, side) + dot(theirs, g_far, 0, side)).astype(LOW)
    whole = pl.BlockSpec(g.shape, lambda i, p: (0, 0))
    begin, far_begin = table.begin[name] + lo, table.begin[far] + lo
    return pl.pallas_call(
        functools.partial(terms_kernel, transposed),
        out_shape=(jax.ShapeDtypeStruct if keep else pltpu.HBM)((count * size, units), LOW),
        grid_spec=pltpu.PrefetchScalarGridSpec(
            num_scalar_prefetch=1,
            grid=(count,),
            in_specs=[
                pl.BlockSpec((rows, size), lambda i, p: (0, p[begin + i])),
                pl.BlockSpec((rows, size), lambda i, p: (0, p[far_begin + i])),
                whole,
                whole,
            ],
            out_specs=pl.BlockSpec((size, units), lambda i, p: (i, 0)),
        ),
        compiler_params=pltpu.CompilerParams(vmem_limit_bytes=20 << 20),
        cost_estimate=pl.CostEstimate(
            flops=24 * rows * count * size * units, bytes_accessed=4 * rows * units, transcendentals=0
        ),
        name="weight_terms",
    )(table.values, x, x_far, g, g_far)


def copy_kernel(places, source, target):
    del places
    target[...] = source[...]


def pick_columns(table, name, values, part=None, parts=1):
    blocks = lax.axis_size("dp")
    rows, count = values.shape[0] // parts, blocks // 2
    size = values.shape[1] // blocks
    if size % 128:
        if part is not None:
            values = lax.dynamic_slice_in_dim(values, table.list(part, 0, 1)[0] * rows, rows, 0)
        return pick(values, table.list(name, 0, count), blocks, 1)
    begin = table.begin[name]
    row = 0 if part is None else table.begin[part]
    return pl.pallas_call(
        copy_kernel,
        out_shape=jax.ShapeDtypeStruct((rows, count * size), values.dtype),
        grid_spec=pltpu.PrefetchScalarGridSpec(
            num_scalar_prefetch=1,
            grid=(count,),
            in_specs=[
                pl.BlockSpec(
                    (rows, size), lambda i, p: (0 if part is None else p[row], p[begin + i])
                )
            ],
            out_specs=pl.BlockSpec((rows, size), lambda i, p: (0, i)),
        ),
        compiler_params=pltpu.CompilerParams(vmem_limit_bytes=8 << 20),
        cost_estimate=pl.CostEstimate(
            flops=65536 * rows * count * size, bytes_accessed=4 * rows * count * size, transcendentals=0
        ),
        name="pick_columns",
    )(table.values, values)


def load_kernel(*refs):
    *pairs, sems = refs
    half = len(pairs) // 2
    copies = [
        pltpu.make_async_copy(source, target, sems.at[j])
        for j, (source, target) in enumerate(zip(pairs[:half], pairs[half:]))
    ]
    for copy in copies:
        copy.start()
    for copy in copies:
        copy.wait()


def load_weights(*weights):
    return pl.pallas_call(
        load_kernel,
        out_shape=tuple(pltpu.VMEM(w.shape, w.dtype) for w in weights),
        in_specs=[pl.BlockSpec(memory_space=pl.ANY)] * len(weights),
        out_specs=[pl.BlockSpec(memory_space=pltpu.VMEM)] * len(weights),
        scratch_shapes=[pltpu.SemaphoreType.DMA((len(weights),))],
        compiler_params=pltpu.CompilerParams(vmem_limit_bytes=2 << 20),
        cost_estimate=pl.CostEstimate(
            flops=20_000_000_000,
            bytes_accessed=2 * sum(w.size for w in weights),
            transcendentals=0,
        ),
        name="load_weights",
    )(*in_hbm(*weights))


def in_vmem(*arrays):
    return [pltpu.with_memory_space_constraint(a, pltpu.VMEM) for a in arrays]


def ffn_kernel(rows, gate_w, up_w, grad_in, hidden, grad_gate, grad_up):
    step = 128
    for begin in range(0, hidden.shape[1], step):
        cut = slice(begin, begin + step)
        both = dot(rows[...], jnp.concatenate([gate_w[:, cut], up_w[:, cut]], 1), 1, 0)
        gate, up = both[:, :step], both[:, step:]
        grad = grad_in[:, cut]
        sigma = jax.nn.sigmoid(gate)
        active = gate * sigma
        hidden[:, cut] = (active * up).astype(LOW)
        grad_gate[:, cut] = (grad * up * sigma * (1.0 + gate * (1.0 - sigma))).astype(LOW)
        grad_up[:, cut] = (grad * active).astype(LOW)


def feed_forward(rows, w_gate, w_up, grad_hidden):
    count, width = rows.shape
    units = w_gate.shape[1]
    here = pl.BlockSpec(memory_space=pltpu.VMEM)
    return pl.pallas_call(
        ffn_kernel,
        out_shape=(jax.ShapeDtypeStruct((count, units), LOW),) * 3,
        in_specs=[here] * 4,
        out_specs=[here] * 3,
        compiler_params=pltpu.CompilerParams(vmem_limit_bytes=20 << 20),
        cost_estimate=pl.CostEstimate(
            flops=6 * count * width * units,
            bytes_accessed=4 * width * units,
            transcendentals=count * units,
        ),
        name="feed_forward",
    )(*in_vmem(rows, w_gate, w_up, grad_hidden))


def back_kernel(gate_rows, up_rows, gate_w, up_w, out):
    step = out.shape[1]
    cut = pl.ds(pl.multiple_of(pl.program_id(0) * step, step), step)
    total = dot(gate_rows[...], gate_w[cut, :], 1, 1) + dot(up_rows[...], up_w[cut, :], 1, 1)
    out[...] = total.astype(out.dtype)


def feed_forward_back(grad_gate, grad_up, w_gate, w_up, half, kind):
    count, units = grad_gate.shape
    width = w_gate.shape[0]
    step = width // 2
    rows = pl.BlockSpec((count // 2, units), lambda i: (half, 0))
    here = pl.BlockSpec(memory_space=pltpu.VMEM)
    return pl.pallas_call(
        back_kernel,
        out_shape=jax.ShapeDtypeStruct((count // 2, width), kind),
        grid=(2,),
        in_specs=[rows, rows, here, here],
        out_specs=pl.BlockSpec((count // 2, step), lambda i: (0, i)),
        compiler_params=pltpu.CompilerParams(vmem_limit_bytes=16 << 20),
        cost_estimate=pl.CostEstimate(
            flops=10 * count * width * units, bytes_accessed=4 * width * units, transcendentals=0
        ),
        name="feed_forward_back",
    )(grad_gate, grad_up, *in_vmem(w_gate, w_up))


def join_kernel(places, first, second, out):
    del places

    @pl.when(pl.program_id(0) == 0)
    def _():
        out[...] = first[...]

    @pl.when(pl.program_id(0) == 1)
    def _():
        out[...] = second[...]


def join_rows(table, first, second):
    rows, width = first.shape
    core = table.begin["core"]
    whole = pl.BlockSpec((rows, width), lambda i, p: (0, 0))
    return pl.pallas_call(
        join_kernel,
        out_shape=jax.ShapeDtypeStruct((2 * rows, width), first.dtype),
        grid_spec=pltpu.PrefetchScalarGridSpec(
            num_scalar_prefetch=1,
            grid=(2,),
            in_specs=[whole, whole],
            out_specs=pl.BlockSpec((rows, width), lambda i, p: (p[core] ^ i, 0)),
        ),
        compiler_params=pltpu.CompilerParams(vmem_limit_bytes=8 << 20),
        cost_estimate=pl.CostEstimate(
            flops=1_000_000_000, bytes_accessed=8 * rows * width, transcendentals=0
        ),
        name="join_rows",
    )(table.values, first, second)


def row_kernel(left, right, send, kept):
    half = left.shape[0] // 2
    send[...] = dot(left[half:, :], right[...], 1, 0).astype(LOW)
    kept[...] = dot(left[:half, :], right[...], 1, 0)


def row_terms(left, right):
    rows, units = left.shape
    half, width = rows // 2, right.shape[1]
    step = 256
    return pl.pallas_call(
        row_kernel,
        out_shape=(
            jax.ShapeDtypeStruct((half, width), LOW),
            jax.ShapeDtypeStruct((half, width), jnp.float32),
        ),
        grid=(width // step,),
        in_specs=[
            pl.BlockSpec((rows, units), lambda i: (0, 0)),
            pl.BlockSpec((units, step), lambda i: (0, i)),
        ],
        out_specs=[pl.BlockSpec((half, step), lambda i: (0, i))] * 2,
        compiler_params=pltpu.CompilerParams(vmem_limit_bytes=16 << 20),
        cost_estimate=pl.CostEstimate(
            flops=8 * rows * units * width, bytes_accessed=2 * units * width, transcendentals=0
        ),
        name="row_terms",
    )(left, right)


def turn(values, cosine, sine):
    half = cosine.shape[0]
    heads = values.shape[0] // (2 * half)
    pieces = values.reshape(heads, 2, half, values.shape[1])
    first, second = pieces[:, 0], pieces[:, 1]
    return jnp.stack(
        [first * cosine - second * sine, second * cosine + first * sine], 1
    ).reshape(values.shape)


def turn_back(grads, cosine, sine):
    return turn(grads, cosine, -sine)


def norm_back(grad_rows, values, scale_rows, gain):
    scaled = grad_rows * gain
    inner_mean = jnp.mean(scaled * values, -1, keepdims=True)
    return (
        scale_rows * (scaled - values * scale_rows * scale_rows * inner_mean),
        jnp.sum(grad_rows * values * scale_rows, 0),
    )


def shards(
    tokens,
    positions,
    norm1_gain,
    w_query,
    w_key,
    w_value,
    w_out,
    norm2_gain,
    w_gate,
    w_up,
    w_down,
    cotangent,
):
    rows_here, width = tokens.shape
    size = w_key.shape[1]
    dp = lax.axis_size("dp")
    tp_count = len(ROW_MASKS)
    own_rows = rows_here // tp_count
    block = width // dp
    bits = dp.bit_length() - 1
    half_count = dp // 2

    def exchange_order(order):
        return np.array(
            [
                sum(((j >> (len(order) - 1 - k)) & 1) << b for k, b in enumerate(order))
                for j in range(1 << len(order))
            ],
            np.int32,
        )

    down_bits = [0] + list(range(2, bits))
    rest_bits = list(range(1, bits))

    place = lax.axis_index("dp").astype(jnp.int32)
    spot = lax.axis_index("tp").astype(jnp.int32)
    natural = np.arange(half_count, dtype=np.int32)
    down_here, rest_here = place ^ exchange_order(down_bits), place ^ exchange_order(rest_bits)
    table = Table(
        mine=2 * natural + (place & 1),
        theirs=2 * natural + (1 - (place & 1)),
        natural=jnp.asarray(natural),
        down=down_here,
        down_far=down_here ^ 2,
        rest=rest_here,
        rest_far=rest_here ^ 1,
        rest_block=rest_here >> 1,
        core=(spot & 1)[None],
    )
    at = jnp.stack([place & (SPAN - 1), spot])
    row_starts = [((spot ^ m) * own_rows).astype(jnp.uint32) for m in ROW_MASKS]
    core_starts = [(c * (rows_here // 2)).astype(jnp.uint32) for c in (spot & 1, 1 - (spot & 1))]
    tokens, table.values, at, row_starts, core_starts = lax.optimization_barrier(
        (tokens, table.values, at, row_starts, core_starts)
    )
    pos = positions.reshape(1, rows_here)

    def own(values):
        return take(values, row_starts[0], own_rows, 0)

    inputs = tokens.astype(jnp.float32)
    scale_one = lax.rsqrt(jnp.mean(inputs * inputs, -1, keepdims=True) + EPSILON)
    normed_one = (inputs * scale_one * norm1_gain).astype(LOW)
    half = size // 2
    frequency = jnp.exp(
        -jnp.log(10000.0) * (2.0 * jnp.arange(half, dtype=jnp.float32) / size)
    )
    angles = frequency[:, None] * positions.astype(jnp.float32)[None, :]
    cosine, sine = jnp.cos(angles), jnp.sin(angles)
    w_kv = jnp.concatenate([w_key.T, w_value.T], 0)
    paired = dot(w_kv, normed_one, 1, 1)
    paired = jnp.concatenate([turn(paired[:size], cosine, sine), paired[size:]], 0).astype(LOW)
    blocks = [paired] + [flip(paired, "dp", m) for m in range(1, SPAN)]
    queries = (turn(dot(w_query, normed_one, 0, 1), cosine, sine) * size ** (-0.5)).astype(LOW)

    wide = w_query.shape[1]

    def near_sum(part):
        send = part(2, 4).astype(LOW)
        near, kept = lax.optimization_barrier((flip(send, "tp", 1), part(0, 2)))
        pair = kept + near
        return pair[:own_rows], pair[own_rows:].astype(LOW)

    attended, lse = attention_forward(at, pos, queries, blocks, size, 8)

    branch, branch_out = near_sum(
        lambda lo, hi: dot(attended[:, lo * own_rows : hi * own_rows], w_out, 0, 0)
    )
    branch_far = flip(branch_out, "tp", 2)
    cot = jnp.concatenate(
        [take(after(cotangent, branch_out), start, own_rows, 0) for start in row_starts], 0
    )
    cot_send = pick_columns(table, "down_far", cot)
    cot_theirs = flip(cot_send, "dp", 2)
    own_inputs = own(tokens).astype(jnp.float32)
    one_send = pick_columns(table, "theirs", after(normed_one, cot_send), "core", 2)
    one_near = flip(one_send, "dp", 1)
    grad_hidden = dot(after(cot, one_send), w_down, 1, 1)
    middle = own_inputs + (after(branch, grad_hidden) + branch_far)

    scale_two = lax.rsqrt(jnp.mean(middle * middle, -1, keepdims=True) + EPSILON)
    own_two = (middle * scale_two * norm2_gain).astype(LOW)
    far_two = flip(own_two, "tp", 2)
    gate_w, up_w = load_weights(after(w_gate, own_two), w_up)
    pair_two = jnp.concatenate([after(own_two, gate_w), far_two], 0)
    core_two = flip(pair_two, "tp", 1)
    two_send = pick_columns(table, "theirs", pair_two)
    two_near = flip(two_send, "dp", 1)
    normed_two = jnp.concatenate([after(pair_two, two_send), core_two], 0)

    hidden, grad_gate_pre, grad_up_pre = feed_forward(normed_two, gate_w, up_w, grad_hidden)
    gate_theirs = flip(grad_gate_pre, "dp", 1)
    hidden_theirs = flip(hidden, "dp", 2)
    up_theirs = flip(grad_up_pre, "dp", 1)
    gate_late, cot_theirs, one_near = lax.optimization_barrier((grad_gate_pre, cot_theirs, one_near))

    two_back = functools.partial(feed_forward_back, gate_late, grad_up_pre, gate_w, up_w)
    grad_normed_two, two_out = near_sum(
        lambda lo, hi: two_back(lo // 2, jnp.float32 if lo == 0 else LOW)
    )
    two_out, two_near = lax.optimization_barrier((two_out, two_near))
    two_far = flip(two_out, "tp", 2)
    cores = jnp.concatenate([two_near, one_near], 1)
    cores_far = flip(cores, "tp", 1)
    two_theirs = jnp.concatenate([two_near, cores_far[:, : width // 2]], 0)

    down_near, down = row_terms(after(hidden, two_out), w_down)
    grad_normed_two = after(grad_normed_two, down) + two_far

    grad_mid_norm, gain_two = norm_back(grad_normed_two, middle, scale_two, norm2_gain)
    grad_middle = own(cotangent).astype(jnp.float32) + grad_mid_norm
    branch_grad = grad_middle.astype(LOW)
    grad_far = flip(branch_grad, "tp", 2)

    down_near = flip(after(down_near, branch_grad), "tp", 1)
    gate_terms = weight_terms(
        table,
        "mine",
        "natural",
        0,
        half_count,
        after(normed_two, branch_grad),
        two_theirs,
        grad_gate_pre,
        gate_theirs,
        keep=False,
    )
    grad_gate = parity_sum(gate_terms, 0)
    grad_pair = jnp.concatenate([after(branch_grad, gate_terms), grad_far], 0)
    grad_core = flip(grad_pair, "tp", 1)
    att_theirs = flip(after(attended, grad_pair), "dp", 1)

    def near_flip(terms, bit):
        half = terms.shape[0] // 2
        return [flip(terms[half:], "dp", 1 << bit), flip(terms[:half], "dp", 1 << bit)]

    def down_terms(lo, hi, *late):
        g = after(hidden, *late)
        return weight_terms(table, "down", "natural", lo, hi, cot, cot_theirs, g, hidden_theirs)

    down_sent = down_terms(half_count // 2, half_count, grad_pair)
    half = down_sent.shape[0] // 2
    down_first = flip(down_sent[half:], "dp", 1)
    branch_all = jnp.concatenate([after(grad_pair, down_sent), grad_core], 0)
    grad_attended = dot(w_out, branch_all, 1, 1).astype(LOW)
    grads = attention_backward(
        at, pos, queries, grad_attended, attended, lse, cosine, sine, blocks, size, 8
    )
    grad_query_rows, kv_total = grads[0], grads[1]
    branch_send = pick_columns(table, "theirs", after(grad_pair, grad_query_rows))
    *kv_sends, att_theirs = lax.optimization_barrier((*grads[2:], att_theirs))
    kv_back = [flip(kv_sends[m - 1], "dp", m) for m in range(1, SPAN)]

    def rest_terms(lo, hi, x, x_far, g, g_far, transposed=False):
        return weight_terms(
            table, "rest", "rest_block", lo, hi, x, x_far, g, g_far, transposed
        )

    down = down + after(down_near, grad_query_rows)
    down, down_out = down[:own_rows], down[own_rows:].astype(LOW)
    down_far = flip(down_out, "tp", 2)

    def up_terms(lo, hi, *late):
        return rest_terms(lo, hi, normed_two, two_theirs, after(grad_up_pre, *late), up_theirs)

    up_sent = up_terms(half_count // 2, half_count, grad_query_rows)
    up_first = flip(up_sent[half:], "dp", 2)

    def exchange_mid(terms, first, order, *late):
        got, left = [first], half_count // 2
        for b in order[1:]:
            send = terms(left // 2, left, *late).astype(jnp.float32)
            rows = send.shape[0]
            for other in got:
                send = send + other[other.shape[0] - rows :]
            send = send.astype(LOW)
            got.append(flip(send, "dp", 1 << b))
            left //= 2
        return got[1:], send

    down_late, down_last = exchange_mid(down_terms, down_first, down_bits, grad_query_rows)
    kv_total, grad_gate = lax.optimization_barrier(
        (kv_total, grad_gate, up_sent, down_out, down_last)
    )[:2]
    for back in kv_back:
        kv_total = kv_total + back
    key_grad = turn_back(kv_total[:size], cosine, sine)
    grad_kv_rows = jnp.concatenate([key_grad, kv_total[size:]], 0).astype(LOW)
    proj_rows = jnp.concatenate([grad_query_rows, grad_kv_rows], 0)
    units = proj_rows.shape[0]
    pieces = [
        branch_send[:, begin : begin + rows_here] for begin in range(0, branch_send.shape[1], rows_here)
    ]
    both_theirs = flip(jnp.concatenate([proj_rows, *pieces], 0), "dp", 1)

    own_order = jnp.concatenate(
        [take(proj_rows, start, own_rows, 1) for start in row_starts], 1
    )

    def one_terms(lo, hi):
        cut = own_order[:, lo * own_rows : hi * own_rows]
        return dot(cut[:wide], w_query, 0, 1) + dot(cut[wide:], w_kv, 0, 0)

    grad_normed_one, one_out = near_sum(one_terms)
    one_far = flip(one_out, "tp", 2)
    up_second = flip(after(up_sent[:half], one_out), "dp", 2)
    output_rows = (middle + (down + after(down_far, one_out))).astype(LOW)
    one_theirs = join_rows(table, after(one_near, one_out), cores_far[:, width // 2 :])
    up_kept = up_terms(0, 1, one_out)
    grad_gate = grad_gate.astype(jnp.float32)
    grad_normed_one = after(grad_normed_one, output_rows, up_kept, grad_gate, one_theirs) + one_far
    grad_in_norm, gain_one = norm_back(grad_normed_one, own_inputs, own(scale_one), norm1_gain)
    input_rows = grad_middle + grad_in_norm

    gains = jnp.stack([after(gain_one, input_rows), gain_two])
    gains_core = flip(gains, "tp", 1)
    up_mid = up_terms(half_count // 4, half_count // 2, gains)
    gains, gains_core, up_first = lax.optimization_barrier((gains, gains_core, up_first, up_mid))[:3]
    gains = gains + gains_core
    up_late, up_last = exchange_mid(
        lambda lo, hi, *late: up_mid if hi == half_count // 2 else up_terms(lo, hi, *late),
        up_first,
        rest_bits,
        gains,
    )
    both_theirs = after(both_theirs, up_last)
    proj_theirs = both_theirs[:units]
    branch_near = jnp.concatenate(
        [
            both_theirs[begin : begin + branch_send.shape[0]]
            for begin in range(units, both_theirs.shape[0], branch_send.shape[0])
        ],
        1,
    )
    branch_theirs = jnp.concatenate([branch_near, flip(branch_near, "tp", 1)], 0)
    gains, *down_late = lax.optimization_barrier((gains, *down_late, up_last))[:-1]
    gains = gains + flip(gains, "tp", 2)
    gains = pick_columns(table, "rest", gains) + flip(
        pick_columns(table, "rest_far", gains), "dp", 1
    )

    out_late, proj_late = lax.optimization_barrier((attended, proj_rows, up_last))[:2]

    def last_terms(lo, hi, *late):
        first, second = after(proj_late, *late), after(out_late, *late)
        return jnp.concatenate(
            [
                rest_terms(lo, hi, normed_one, one_theirs, first, proj_theirs, True),
                rest_terms(lo, hi, branch_all, branch_theirs, second, att_theirs, True),
            ],
            1,
        )

    def with_gains(terms, lo, hi, *others):
        extra = gains[:, lo * block : hi * block]
        for other, other_gains in others:
            terms = terms.astype(jnp.float32) + other
            extra = extra + other_gains
        columns = terms.shape[1]
        extra = jnp.pad(extra, ((0, 14), (0, -extra.shape[1] % columns)))[:, :columns]
        return jnp.concatenate([terms.astype(LOW), extra.astype(LOW)], 0)

    def split(message, count):
        rows = count * block
        return message[:rows], message[rows : rows + 2, :rows]

    quarter = half_count // 4
    sent = last_terms(half_count // 2, half_count)
    cut = quarter * block
    firsts = with_gains(sent[cut:], 3 * quarter, half_count)
    seconds = with_gains(sent[:cut], 2 * quarter, 3 * quarter)
    mids = [split(flip(firsts, "dp", 2), quarter)]
    last_second = split(flip(after(seconds, firsts), "dp", 2), quarter)
    up_late = [*up_late, up_second]
    proj_kept = rest_terms(0, 1, normed_one, one_theirs, after(proj_late, firsts), proj_theirs, True)
    out_kept = rest_terms(0, 1, branch_all, branch_theirs, after(out_late, firsts), att_theirs, True)
    down_kept = down_terms(0, 1, firsts)
    left = half_count // 2
    for b in rest_bits[1:]:
        count = left // 2
        terms = last_terms(count, left, firsts)
        terms, *up_late = lax.optimization_barrier((terms, *up_late, proj_kept, out_kept, down_kept))[
            :-3
        ]
        send = with_gains(
            terms, count, left, *((o[-count * block :], g[:, -count * block :]) for o, g in mids)
        )
        mids.append(split(flip(send, "dp", 1 << b), count))
        left = count
    down_second = flip(after(down_sent[:half], firsts), "dp", 1)

    def ending(kept, *others):
        kept = kept.astype(jnp.float32)
        for other in others:
            kept = kept + other[:block]
        return kept

    down_kept, down_second = lax.optimization_barrier((down_kept, down_second, send))[:2]
    grad_down = ending(down_kept, down_second, *down_late)
    grad_last = ending(
        jnp.concatenate([proj_kept, out_kept], 1), last_second[0], *(m[0] for m in mids[1:])
    )
    gains = gains[:, :block] + last_second[1][:, :block]
    for _, other in mids[1:]:
        gains = gains + other[:, :block]
    grad_up = ending(up_kept, *up_late)
    narrow = wide + 2 * size

    return (
        output_rows,
        input_rows,
        gains[0],
        grad_last[:, :wide],
        grad_last[:, wide : wide + size],
        grad_last[:, wide + size : narrow],
        grad_last[:, narrow:].T,
        gains[1],
        grad_gate,
        grad_up,
        grad_down.T,
    )


def solution(mesh):
    placed = (
        P("dp", None),
        P("dp"),
        P(),
        P(None, "tp"),
        P(None, "tp"),
        P(None, "tp"),
        P("tp", None),
        P(),
        P(None, "tp"),
        P(None, "tp"),
        P("tp", None),
        P("dp", None),
    )
    return jax.shard_map(
        shards,
        mesh=mesh,
        in_specs=placed,
        out_specs=(
            P(("dp", "tp"), None),
            P(("dp", "tp"), None),
            P("dp"),
            P("dp", "tp"),
            P("dp", "tp"),
            P("dp", "tp"),
            P("tp", "dp"),
            P("dp"),
            P("dp", "tp"),
            P("dp", "tp"),
            P("tp", "dp"),
        ),
        check_vma=False,
    )
```

```python
import functools

import jax
import jax.numpy as jnp
import numpy as np
from jax import lax
from jax.experimental import pallas as pl
from jax.experimental.pallas import tpu as pltpu
from jax.sharding import PartitionSpec as P

SPAN = 4
EPSILON = 1e-05
FAR_BELOW = -1e30
LOW = jnp.bfloat16
ROW_MASKS = (0, 2, 1, 3)


def flip(block, axis, mask):
    return lax.ppermute(block, axis, [(i, i ^ mask) for i in range(lax.axis_size(axis))])


def dot(left, right, left_dim, right_dim):
    return lax.dot_general(
        left,
        right,
        (((left_dim,), (right_dim,)), ((), ())),
        preferred_element_type=jnp.float32,
    )


def in_hbm(*arrays):
    return [pltpu.with_memory_space_constraint(a, pltpu.HBM) for a in arrays]


def own_mask(pos, begin, keys, queries):
    key_at = lax.broadcasted_iota(jnp.int32, (keys, queries), 0)
    query_at = lax.broadcasted_iota(jnp.int32, (keys, queries), 1) + begin
    return (key_at <= query_at) & (key_at >= query_at - pos)


def row_starts(spot, rows):
    part = rows // len(ROW_MASKS)
    return [pl.multiple_of((spot ^ m) * part, part) for m in ROW_MASKS]


def forward_kernel(
    heads,
    size,
    at_ref,
    pos_ref,
    q_ref,
    kv0,
    kv1,
    kv2,
    kv3,
    o_ref,
    lse_ref,
    keys,
    vals,
    top,
    acc,
    ordered,
):
    rank, spot = at_ref[0], at_ref[1]
    rows = pos_ref.shape[1]

    @pl.when(pl.program_id(0) == 0)
    def _():
        for m, kv in enumerate((kv0, kv1, kv2, kv3)):
            keys[m] = kv[:size, :].T
            vals[m, :size, :] = kv[size:, :]
            vals[m, size:, :] = jnp.ones((16, rows), LOW)

    pos = pos_ref[...]
    mask = own_mask(pos, 0, rows, rows)
    for h in range(heads):
        scores = dot(keys[0], q_ref[h * size : (h + 1) * size, :], 1, 0)
        scores = jnp.where(mask, scores, FAR_BELOW)
        peak = jnp.max(scores, 0, keepdims=True)
        acc[h] = dot(vals[0], jnp.exp(scores - peak).astype(LOW), 1, 0)
        top[h] = peak
    seen = pos > lax.broadcasted_iota(jnp.int32, (1, rows), 1)
    for m in range(1, SPAN):

        @pl.when((rank ^ m) < rank)
        def _():
            for h in range(heads):
                scores = dot(keys[m], q_ref[h * size : (h + 1) * size, :], 1, 0)
                old = top[h]
                peak = jnp.where(seen, jnp.maximum(old, jnp.max(scores, 0, keepdims=True)), old)
                weights = jnp.exp(scores - jnp.where(seen, peak, -FAR_BELOW)).astype(LOW)
                acc[h] = acc[h] * jnp.exp(old - peak) + dot(vals[m], weights, 1, 0)
                top[h] = peak

    for h in range(heads):
        total = acc[h, size : size + 1, :]
        ordered[h * size : (h + 1) * size, :] = (acc[h, :size, :] / total).astype(LOW)
        lse_ref[h] = top[h] + jnp.log(total)
    for j, start in enumerate(row_starts(spot, rows)):
        part = rows // len(ROW_MASKS)
        o_ref[:, j * part : (j + 1) * part] = ordered[:, pl.ds(start, part)]


def backward_kernel(
    heads,
    size,
    at_ref,
    pos_ref,
    q_ref,
    do_in,
    o_in,
    lse_ref,
    cos_ref,
    sin_ref,
    kv0,
    kv1,
    kv2,
    kv3,
    dq_ref,
    g0,
    g1,
    g2,
    g3,
    keys,
    vals,
    dq,
    total,
    do_ref,
    o_ref,
):
    rank, spot = at_ref[0], at_ref[1]
    rows = pos_ref.shape[1]
    half = rows // 2
    blocks = (kv0, kv1, kv2, kv3)
    step = pl.program_id(0)

    @pl.when(step == 0)
    def _():
        for m, kv in enumerate(blocks):
            keys[m] = kv[:size, :].T
            vals[m] = kv[size:, :].T
        total[...] = jnp.zeros_like(total)

    part = rows // len(ROW_MASKS)
    for j, start in enumerate(row_starts(spot, rows)):
        do_ref[:, pl.ds(start, part)] = do_in[:, j * part : (j + 1) * part]
        o_ref[:, pl.ds(start, part)] = o_in[:, j * part : (j + 1) * part]
    pos = pos_ref[...]
    seen = pos > lax.broadcasted_iota(jnp.int32, (1, rows), 1)
    deltas = []
    for h in range(heads):
        span = slice(h * size, (h + 1) * size)
        deltas.append(
            jnp.sum(
                do_ref[span, :].astype(jnp.float32) * o_ref[span, :].astype(jnp.float32),
                0,
                keepdims=True,
            )
        )
    for part in range(2):
        cols = slice(part * half, (part + 1) * half)
        count = (part + 1) * half
        mask = own_mask(pos[:, cols], part * half, count, half)
        for h in range(heads):
            span = slice(h * size, (h + 1) * size)
            query, grad = q_ref[span, cols], do_ref[span, cols]
            scores = dot(keys[0, :count, :], query, 1, 0)
            probs = jnp.exp(jnp.where(mask, scores, FAR_BELOW) - lse_ref[h, :, cols])
            grad_probs = dot(vals[0, :count, :], grad, 1, 0)
            grad_scores = (probs * (grad_probs - deltas[h][:, cols])).astype(LOW)
            total[0, :size, :count] += dot(query, grad_scores, 1, 1)
            total[0, size:, :count] += dot(grad, probs.astype(LOW), 1, 1)
            dq[h, :, cols] = dot(kv0[:size, :count], grad_scores, 1, 0)
    for m in range(1, SPAN):

        @pl.when((rank ^ m) < rank)
        def _():
            for h in range(heads):
                span = slice(h * size, (h + 1) * size)
                query, grad = q_ref[span, :], do_ref[span, :]
                scores = dot(keys[m], query, 1, 0)
                probs = jnp.exp(scores - jnp.where(seen, lse_ref[h], -FAR_BELOW))
                grad_probs = dot(vals[m], grad, 1, 0)
                grad_scores = (probs * (grad_probs - deltas[h])).astype(LOW)
                total[m, :size, :] += dot(query, grad_scores, 1, 1)
                total[m, size:, :] += dot(grad, probs.astype(LOW), 1, 1)
                dq[h] += dot(blocks[m][:size, :], grad_scores, 1, 0)

    middle_at = size // 2
    cosine, sine = cos_ref[...], sin_ref[...]
    for h in range(heads):
        first = dq[h, :middle_at, :] * size ** (-0.5)
        second = dq[h, middle_at:, :] * size ** (-0.5)
        base = h * size
        dq_ref[base : base + middle_at, :] = (first * cosine + second * sine).astype(LOW)
        dq_ref[base + middle_at : base + size, :] = (second * cosine - first * sine).astype(LOW)

    @pl.when(step == pl.num_programs(0) - 1)
    def _():
        g0[...] = total[0]
        for m, out in ((1, g1), (2, g2), (3, g3)):
            out[...] = total[m].astype(LOW)


def attention_forward(at, pos, queries, blocks, size, heads):
    wide, rows = queries.shape
    count = wide // size
    whole = pl.BlockSpec((2 * size, rows), lambda i, r: (0, 0))
    some = pl.BlockSpec((heads * size, rows), lambda i, r: (i, 0))
    return pl.pallas_call(
        functools.partial(forward_kernel, heads, size),
        out_shape=(
            jax.ShapeDtypeStruct((wide, rows), LOW),
            jax.ShapeDtypeStruct((count, 1, rows), jnp.float32),
        ),
        grid_spec=pltpu.PrefetchScalarGridSpec(
            num_scalar_prefetch=1,
            grid=(count // heads,),
            in_specs=[pl.BlockSpec((1, rows), lambda i, r: (0, 0)), some] + [whole] * SPAN,
            out_specs=[some, pl.BlockSpec((heads, 1, rows), lambda i, r: (i, 0, 0))],
            scratch_shapes=[
                pltpu.VMEM((SPAN, rows, size), LOW),
                pltpu.VMEM((SPAN, size + 16, rows), LOW),
                pltpu.VMEM((heads, 1, rows), jnp.float32),
                pltpu.VMEM((heads, size + 16, rows), jnp.float32),
                pltpu.VMEM((heads * size, rows), LOW),
            ],
        ),
        compiler_params=pltpu.CompilerParams(vmem_limit_bytes=24 << 20),
        cost_estimate=pl.CostEstimate(
            flops=32 * wide * rows * rows * SPAN,
            bytes_accessed=4 * wide * rows,
            transcendentals=0,
        ),
        name="attention_forward",
    )(at, pos, queries, *blocks)


def attention_backward(at, pos, queries, grads, attended, lse, cosine, sine, blocks, size, heads):
    wide, rows = queries.shape
    count = wide // size
    whole = pl.BlockSpec((2 * size, rows), lambda i, r: (0, 0))
    table = pl.BlockSpec((size // 2, rows), lambda i, r: (0, 0))
    some = pl.BlockSpec((heads * size, rows), lambda i, r: (i, 0))
    return pl.pallas_call(
        functools.partial(backward_kernel, heads, size),
        out_shape=(
            jax.ShapeDtypeStruct((wide, rows), LOW),
            jax.ShapeDtypeStruct((2 * size, rows), jnp.float32),
        )
        + (jax.ShapeDtypeStruct((2 * size, rows), LOW),) * (SPAN - 1),
        grid_spec=pltpu.PrefetchScalarGridSpec(
            num_scalar_prefetch=1,
            grid=(count // heads,),
            in_specs=[
                pl.BlockSpec((1, rows), lambda i, r: (0, 0)),
                some,
                some,
                some,
                pl.BlockSpec((heads, 1, rows), lambda i, r: (i, 0, 0)),
                table,
                table,
            ]
            + [whole] * SPAN,
            out_specs=[some] + [whole] * SPAN,
            scratch_shapes=[
                pltpu.VMEM((SPAN, rows, size), LOW),
                pltpu.VMEM((SPAN, rows, size), LOW),
                pltpu.VMEM((heads, size, rows), jnp.float32),
                pltpu.VMEM((SPAN, 2 * size, rows), jnp.float32),
                pltpu.VMEM((heads * size, rows), LOW),
                pltpu.VMEM((heads * size, rows), LOW),
            ],
        ),
        compiler_params=pltpu.CompilerParams(vmem_limit_bytes=24 << 20),
        cost_estimate=pl.CostEstimate(
            flops=48 * wide * rows * rows * SPAN,
            bytes_accessed=10 * wide * rows,
            transcendentals=0,
        ),
        name="attention_backward",
    )(at, pos, *in_hbm(queries, grads, attended, lse, cosine, sine, *blocks))


def take(values, start, size, dim):
    starts = [np.uint32(0)] * values.ndim
    starts[dim] = start
    sizes = list(values.shape)
    sizes[dim] = size
    return lax.dynamic_slice(values, starts, sizes)


def pick(values, places, blocks, dim):
    size = values.shape[dim] // blocks
    return jnp.concatenate(
        [lax.dynamic_slice_in_dim(values, p * size, size, dim) for p in places], dim
    )


class Table:
    def __init__(self, **parts):
        self.begin, at = {}, 0
        for name, part in parts.items():
            self.begin[name] = at
            at += part.shape[0]
        self.values = jnp.concatenate([p.astype(jnp.int32) for p in parts.values()])

    def list(self, name, lo, hi):
        return [self.values[self.begin[name] + j] for j in range(lo, hi)]


def after(value, *others):
    return lax.optimization_barrier((value, *others))[0]


def parity_sum(terms, dim):
    count = lax.axis_size("dp")
    groups = [list(range(p, count, 2)) for p in range(2)]
    return lax.psum_scatter(
        terms.astype(LOW), "dp", scatter_dimension=dim, axis_index_groups=groups, tiled=True
    )


def terms_kernel(transposed, places, x, x_far, g, g_far, out):
    del places
    side = 1 if transposed else 0
    out[...] = (dot(x[...], g[...], 0, side) + dot(x_far[...], g_far[...], 0, side)).astype(LOW)


def weight_terms(table, name, far, lo, hi, x, x_far, g, g_far, transposed=False, keep=True):
    count = hi - lo
    size = x.shape[1] // lax.axis_size("dp")
    rows = x.shape[0]
    units = g.shape[0] if transposed else g.shape[1]
    if size % 128:
        side = 1 if transposed else 0
        mine = pick(x, table.list(name, lo, hi), x.shape[1] // size, 1)
        theirs = pick(x_far, table.list(far, lo, hi), x_far.shape[1] // size, 1)
        return (dot(mine, g, 0, side) + dot(theirs, g_far, 0, side)).astype(LOW)
    whole = pl.BlockSpec(g.shape, lambda i, p: (0, 0))
    begin, far_begin = table.begin[name] + lo, table.begin[far] + lo
    return pl.pallas_call(
        functools.partial(terms_kernel, transposed),
        out_shape=(jax.ShapeDtypeStruct if keep else pltpu.HBM)((count * size, units), LOW),
        grid_spec=pltpu.PrefetchScalarGridSpec(
            num_scalar_prefetch=1,
            grid=(count,),
            in_specs=[
                pl.BlockSpec((rows, size), lambda i, p: (0, p[begin + i])),
                pl.BlockSpec((rows, size), lambda i, p: (0, p[far_begin + i])),
                whole,
                whole,
            ],
            out_specs=pl.BlockSpec((size, units), lambda i, p: (i, 0)),
        ),
        compiler_params=pltpu.CompilerParams(vmem_limit_bytes=20 << 20),
        cost_estimate=pl.CostEstimate(
            flops=24 * rows * count * size * units, bytes_accessed=4 * rows * units, transcendentals=0
        ),
        name="weight_terms",
    )(table.values, x, x_far, g, g_far)


def copy_kernel(places, source, target):
    del places
    target[...] = source[...]


def pick_columns(table, name, values, part=None, parts=1):
    blocks = lax.axis_size("dp")
    rows, count = values.shape[0] // parts, blocks // 2
    size = values.shape[1] // blocks
    if size % 128:
        if part is not None:
            values = lax.dynamic_slice_in_dim(values, table.list(part, 0, 1)[0] * rows, rows, 0)
        return pick(values, table.list(name, 0, count), blocks, 1)
    begin = table.begin[name]
    row = 0 if part is None else table.begin[part]
    return pl.pallas_call(
        copy_kernel,
        out_shape=jax.ShapeDtypeStruct((rows, count * size), values.dtype),
        grid_spec=pltpu.PrefetchScalarGridSpec(
            num_scalar_prefetch=1,
            grid=(count,),
            in_specs=[
                pl.BlockSpec(
                    (rows, size), lambda i, p: (0 if part is None else p[row], p[begin + i])
                )
            ],
            out_specs=pl.BlockSpec((rows, size), lambda i, p: (0, i)),
        ),
        compiler_params=pltpu.CompilerParams(vmem_limit_bytes=8 << 20),
        cost_estimate=pl.CostEstimate(
            flops=65536 * rows * count * size, bytes_accessed=4 * rows * count * size, transcendentals=0
        ),
        name="pick_columns",
    )(table.values, values)


def load_kernel(*refs):
    *pairs, sems = refs
    half = len(pairs) // 2
    copies = [
        pltpu.make_async_copy(source, target, sems.at[j])
        for j, (source, target) in enumerate(zip(pairs[:half], pairs[half:]))
    ]
    for copy in copies:
        copy.start()
    for copy in copies:
        copy.wait()


def load_weights(*weights):
    return pl.pallas_call(
        load_kernel,
        out_shape=tuple(pltpu.VMEM(w.shape, w.dtype) for w in weights),
        in_specs=[pl.BlockSpec(memory_space=pl.ANY)] * len(weights),
        out_specs=[pl.BlockSpec(memory_space=pltpu.VMEM)] * len(weights),
        scratch_shapes=[pltpu.SemaphoreType.DMA((len(weights),))],
        compiler_params=pltpu.CompilerParams(vmem_limit_bytes=2 << 20),
        cost_estimate=pl.CostEstimate(
            flops=20_000_000_000,
            bytes_accessed=2 * sum(w.size for w in weights),
            transcendentals=0,
        ),
        name="load_weights",
    )(*in_hbm(*weights))


def in_vmem(*arrays):
    return [pltpu.with_memory_space_constraint(a, pltpu.VMEM) for a in arrays]


def ffn_kernel(rows, gate_w, up_w, grad_in, hidden, grad_gate, grad_up):
    step = 128
    for begin in range(0, hidden.shape[1], step):
        cut = slice(begin, begin + step)
        both = dot(rows[...], jnp.concatenate([gate_w[:, cut], up_w[:, cut]], 1), 1, 0)
        gate, up = both[:, :step], both[:, step:]
        grad = grad_in[:, cut]
        sigma = jax.nn.sigmoid(gate)
        active = gate * sigma
        hidden[:, cut] = (active * up).astype(LOW)
        grad_gate[:, cut] = (grad * up * sigma * (1.0 + gate * (1.0 - sigma))).astype(LOW)
        grad_up[:, cut] = (grad * active).astype(LOW)


def feed_forward(rows, w_gate, w_up, grad_hidden):
    count, width = rows.shape
    units = w_gate.shape[1]
    here = pl.BlockSpec(memory_space=pltpu.VMEM)
    return pl.pallas_call(
        ffn_kernel,
        out_shape=(jax.ShapeDtypeStruct((count, units), LOW),) * 3,
        in_specs=[here] * 4,
        out_specs=[here] * 3,
        compiler_params=pltpu.CompilerParams(vmem_limit_bytes=20 << 20),
        cost_estimate=pl.CostEstimate(
            flops=6 * count * width * units,
            bytes_accessed=4 * width * units,
            transcendentals=count * units,
        ),
        name="feed_forward",
    )(*in_vmem(rows, w_gate, w_up, grad_hidden))


def back_kernel(gate_rows, up_rows, gate_w, up_w, out):
    step = out.shape[1]
    cut = pl.ds(pl.multiple_of(pl.program_id(0) * step, step), step)
    total = dot(gate_rows[...], gate_w[cut, :], 1, 1) + dot(up_rows[...], up_w[cut, :], 1, 1)
    out[...] = total.astype(out.dtype)


def feed_forward_back(grad_gate, grad_up, w_gate, w_up, half, kind):
    count, units = grad_gate.shape
    width = w_gate.shape[0]
    step = width // 2
    rows = pl.BlockSpec((count // 2, units), lambda i: (half, 0))
    here = pl.BlockSpec(memory_space=pltpu.VMEM)
    return pl.pallas_call(
        back_kernel,
        out_shape=jax.ShapeDtypeStruct((count // 2, width), kind),
        grid=(2,),
        in_specs=[rows, rows, here, here],
        out_specs=pl.BlockSpec((count // 2, step), lambda i: (0, i)),
        compiler_params=pltpu.CompilerParams(vmem_limit_bytes=16 << 20),
        cost_estimate=pl.CostEstimate(
            flops=10 * count * width * units, bytes_accessed=4 * width * units, transcendentals=0
        ),
        name="feed_forward_back",
    )(grad_gate, grad_up, *in_vmem(w_gate, w_up))


def join_kernel(places, first, second, out):
    del places

    @pl.when(pl.program_id(0) == 0)
    def _():
        out[...] = first[...]

    @pl.when(pl.program_id(0) == 1)
    def _():
        out[...] = second[...]


def join_rows(table, first, second):
    rows, width = first.shape
    core = table.begin["core"]
    whole = pl.BlockSpec((rows, width), lambda i, p: (0, 0))
    return pl.pallas_call(
        join_kernel,
        out_shape=jax.ShapeDtypeStruct((2 * rows, width), first.dtype),
        grid_spec=pltpu.PrefetchScalarGridSpec(
            num_scalar_prefetch=1,
            grid=(2,),
            in_specs=[whole, whole],
            out_specs=pl.BlockSpec((rows, width), lambda i, p: (p[core] ^ i, 0)),
        ),
        compiler_params=pltpu.CompilerParams(vmem_limit_bytes=8 << 20),
        cost_estimate=pl.CostEstimate(
            flops=1_000_000_000, bytes_accessed=8 * rows * width, transcendentals=0
        ),
        name="join_rows",
    )(table.values, first, second)


def row_kernel(left, right, send, kept):
    half = left.shape[0] // 2
    send[...] = dot(left[half:, :], right[...], 1, 0).astype(LOW)
    kept[...] = dot(left[:half, :], right[...], 1, 0)


def row_terms(left, right):
    rows, units = left.shape
    half, width = rows // 2, right.shape[1]
    step = 256
    return pl.pallas_call(
        row_kernel,
        out_shape=(
            jax.ShapeDtypeStruct((half, width), LOW),
            jax.ShapeDtypeStruct((half, width), jnp.float32),
        ),
        grid=(width // step,),
        in_specs=[
            pl.BlockSpec((rows, units), lambda i: (0, 0)),
            pl.BlockSpec((units, step), lambda i: (0, i)),
        ],
        out_specs=[pl.BlockSpec((half, step), lambda i: (0, i))] * 2,
        compiler_params=pltpu.CompilerParams(vmem_limit_bytes=16 << 20),
        cost_estimate=pl.CostEstimate(
            flops=8 * rows * units * width, bytes_accessed=2 * units * width, transcendentals=0
        ),
        name="row_terms",
    )(left, right)


def turn(values, cosine, sine):
    half = cosine.shape[0]
    heads = values.shape[0] // (2 * half)
    pieces = values.reshape(heads, 2, half, values.shape[1])
    first, second = pieces[:, 0], pieces[:, 1]
    return jnp.stack(
        [first * cosine - second * sine, second * cosine + first * sine], 1
    ).reshape(values.shape)


def turn_back(grads, cosine, sine):
    return turn(grads, cosine, -sine)


def norm_back(grad_rows, values, scale_rows, gain):
    scaled = grad_rows * gain
    inner_mean = jnp.mean(scaled * values, -1, keepdims=True)
    return (
        scale_rows * (scaled - values * scale_rows * scale_rows * inner_mean),
        jnp.sum(grad_rows * values * scale_rows, 0),
    )


def shards(
    tokens,
    positions,
    norm1_gain,
    w_query,
    w_key,
    w_value,
    w_out,
    norm2_gain,
    w_gate,
    w_up,
    w_down,
    cotangent,
):
    rows_here, width = tokens.shape
    size = w_key.shape[1]
    dp = lax.axis_size("dp")
    tp_count = len(ROW_MASKS)
    own_rows = rows_here // tp_count
    block = width // dp
    bits = dp.bit_length() - 1
    half_count = dp // 2

    def exchange_order(order):
        return np.array(
            [
                sum(((j >> (len(order) - 1 - k)) & 1) << b for k, b in enumerate(order))
                for j in range(1 << len(order))
            ],
            np.int32,
        )

    down_bits = [0] + list(range(2, bits))
    rest_bits = list(range(1, bits))

    place = lax.axis_index("dp").astype(jnp.int32)
    spot = lax.axis_index("tp").astype(jnp.int32)
    natural = np.arange(half_count, dtype=np.int32)
    down_here, rest_here = place ^ exchange_order(down_bits), place ^ exchange_order(rest_bits)
    table = Table(
        mine=2 * natural + (place & 1),
        theirs=2 * natural + (1 - (place & 1)),
        natural=jnp.asarray(natural),
        down=down_here,
        down_far=down_here ^ 2,
        rest=rest_here,
        rest_far=rest_here ^ 1,
        rest_block=rest_here >> 1,
        core=(spot & 1)[None],
    )
    at = jnp.stack([place & (SPAN - 1), spot])
    row_starts = [((spot ^ m) * own_rows).astype(jnp.uint32) for m in ROW_MASKS]
    core_starts = [(c * (rows_here // 2)).astype(jnp.uint32) for c in (spot & 1, 1 - (spot & 1))]
    tokens, table.values, at, row_starts, core_starts = lax.optimization_barrier(
        (tokens, table.values, at, row_starts, core_starts)
    )
    pos = positions.reshape(1, rows_here)

    def own(values):
        return take(values, row_starts[0], own_rows, 0)

    inputs = tokens.astype(jnp.float32)
    scale_one = lax.rsqrt(jnp.mean(inputs * inputs, -1, keepdims=True) + EPSILON)
    normed_one = (inputs * scale_one * norm1_gain).astype(LOW)
    half = size // 2
    frequency = jnp.exp(
        -jnp.log(10000.0) * (2.0 * jnp.arange(half, dtype=jnp.float32) / size)
    )
    angles = frequency[:, None] * positions.astype(jnp.float32)[None, :]
    cosine, sine = jnp.cos(angles), jnp.sin(angles)
    w_kv = jnp.concatenate([w_key.T, w_value.T], 0)
    paired = dot(w_kv, normed_one, 1, 1)
    paired = jnp.concatenate([turn(paired[:size], cosine, sine), paired[size:]], 0).astype(LOW)
    blocks = [paired] + [flip(paired, "dp", m) for m in range(1, SPAN)]
    queries = (turn(dot(w_query, normed_one, 0, 1), cosine, sine) * size ** (-0.5)).astype(LOW)

    wide = w_query.shape[1]

    def near_sum(part):
        send = part(2, 4).astype(LOW)
        near, kept = lax.optimization_barrier((flip(send, "tp", 1), part(0, 2)))
        pair = kept + near
        return pair[:own_rows], pair[own_rows:].astype(LOW)

    attended, lse = attention_forward(at, pos, queries, blocks, size, 8)

    branch, branch_out = near_sum(
        lambda lo, hi: dot(attended[:, lo * own_rows : hi * own_rows], w_out, 0, 0)
    )
    branch_far = flip(branch_out, "tp", 2)
    cot = jnp.concatenate(
        [take(after(cotangent, branch_out), start, own_rows, 0) for start in row_starts], 0
    )
    cot_send = pick_columns(table, "down_far", cot)
    cot_theirs = flip(cot_send, "dp", 2)
    own_inputs = own(tokens).astype(jnp.float32)
    one_send = pick_columns(table, "theirs", after(normed_one, cot_send), "core", 2)
    one_near = flip(one_send, "dp", 1)
    grad_hidden = dot(after(cot, one_send), w_down, 1, 1)
    middle = own_inputs + (after(branch, grad_hidden) + branch_far)

    scale_two = lax.rsqrt(jnp.mean(middle * middle, -1, keepdims=True) + EPSILON)
    own_two = (middle * scale_two * norm2_gain).astype(LOW)
    far_two = flip(own_two, "tp", 2)
    gate_w, up_w = load_weights(after(w_gate, own_two), w_up)
    pair_two = jnp.concatenate([after(own_two, gate_w), far_two], 0)
    core_two = flip(pair_two, "tp", 1)
    two_send = pick_columns(table, "theirs", pair_two)
    two_near = flip(two_send, "dp", 1)
    normed_two = jnp.concatenate([after(pair_two, two_send), core_two], 0)

    hidden, grad_gate_pre, grad_up_pre = feed_forward(normed_two, gate_w, up_w, grad_hidden)
    gate_theirs = flip(grad_gate_pre, "dp", 1)
    hidden_theirs = flip(hidden, "dp", 2)
    up_theirs = flip(grad_up_pre, "dp", 1)
    gate_late, cot_theirs, one_near = lax.optimization_barrier((grad_gate_pre, cot_theirs, one_near))

    two_back = functools.partial(feed_forward_back, gate_late, grad_up_pre, gate_w, up_w)
    grad_normed_two, two_out = near_sum(
        lambda lo, hi: two_back(lo // 2, jnp.float32 if lo == 0 else LOW)
    )
    two_out, two_near = lax.optimization_barrier((two_out, two_near))
    two_far = flip(two_out, "tp", 2)
    cores = jnp.concatenate([two_near, one_near], 1)
    cores_far = flip(cores, "tp", 1)
    two_theirs = jnp.concatenate([two_near, cores_far[:, : width // 2]], 0)

    down_near, down = row_terms(after(hidden, two_out), w_down)
    grad_normed_two = after(grad_normed_two, down) + two_far

    grad_mid_norm, gain_two = norm_back(grad_normed_two, middle, scale_two, norm2_gain)
    grad_middle = own(cotangent).astype(jnp.float32) + grad_mid_norm
    branch_grad = grad_middle.astype(LOW)
    grad_far = flip(branch_grad, "tp", 2)

    down_near = flip(after(down_near, branch_grad), "tp", 1)
    gate_terms = weight_terms(
        table,
        "mine",
        "natural",
        0,
        half_count,
        after(normed_two, branch_grad),
        two_theirs,
        grad_gate_pre,
        gate_theirs,
        keep=False,
    )
    grad_gate = parity_sum(gate_terms, 0)
    grad_pair = jnp.concatenate([after(branch_grad, gate_terms), grad_far], 0)
    grad_core = flip(grad_pair, "tp", 1)
    att_theirs = flip(after(attended, grad_pair), "dp", 1)

    def near_flip(terms, bit):
        half = terms.shape[0] // 2
        return [flip(terms[half:], "dp", 1 << bit), flip(terms[:half], "dp", 1 << bit)]

    def down_terms(lo, hi, *late):
        g = after(hidden, *late)
        return weight_terms(table, "down", "natural", lo, hi, cot, cot_theirs, g, hidden_theirs)

    down_sent = down_terms(half_count // 2, half_count, grad_pair)
    half = down_sent.shape[0] // 2
    down_first = flip(down_sent[half:], "dp", 1)
    branch_all = jnp.concatenate([after(grad_pair, down_sent), grad_core], 0)
    grad_attended = dot(w_out, branch_all, 1, 1).astype(LOW)
    grads = attention_backward(
        at, pos, queries, grad_attended, attended, lse, cosine, sine, blocks, size, 4
    )
    grad_query_rows, kv_total = grads[0], grads[1]
    branch_send = pick_columns(table, "theirs", after(grad_pair, grad_query_rows))
    *kv_sends, att_theirs = lax.optimization_barrier((*grads[2:], att_theirs))
    kv_back = [flip(kv_sends[m - 1], "dp", m) for m in range(1, SPAN)]

    def rest_terms(lo, hi, x, x_far, g, g_far, transposed=False):
        return weight_terms(
            table, "rest", "rest_block", lo, hi, x, x_far, g, g_far, transposed
        )

    down = down + after(down_near, grad_query_rows)
    down, down_out = down[:own_rows], down[own_rows:].astype(LOW)
    down_far = flip(down_out, "tp", 2)

    def up_terms(lo, hi, *late):
        return rest_terms(lo, hi, normed_two, two_theirs, after(grad_up_pre, *late), up_theirs)

    up_sent = up_terms(half_count // 2, half_count, grad_query_rows)
    up_first = flip(up_sent[half:], "dp", 2)

    def exchange_mid(terms, first, order, *late):
        got, left = [first], half_count // 2
        for b in order[1:]:
            send = terms(left // 2, left, *late).astype(jnp.float32)
            rows = send.shape[0]
            for other in got:
                send = send + other[other.shape[0] - rows :]
            send = send.astype(LOW)
            got.append(flip(send, "dp", 1 << b))
            left //= 2
        return got[1:], send

    down_late, down_last = exchange_mid(down_terms, down_first, down_bits, grad_query_rows)
    kv_total, grad_gate = lax.optimization_barrier(
        (kv_total, grad_gate, up_sent, down_out, down_last)
    )[:2]
    for back in kv_back:
        kv_total = kv_total + back
    key_grad = turn_back(kv_total[:size], cosine, sine)
    grad_kv_rows = jnp.concatenate([key_grad, kv_total[size:]], 0).astype(LOW)
    proj_rows = jnp.concatenate([grad_query_rows, grad_kv_rows], 0)
    units = proj_rows.shape[0]
    pieces = [
        branch_send[:, begin : begin + rows_here] for begin in range(0, branch_send.shape[1], rows_here)
    ]
    both_theirs = flip(jnp.concatenate([proj_rows, *pieces], 0), "dp", 1)

    own_order = jnp.concatenate(
        [take(proj_rows, start, own_rows, 1) for start in row_starts], 1
    )

    def one_terms(lo, hi):
        cut = own_order[:, lo * own_rows : hi * own_rows]
        return dot(cut[:wide], w_query, 0, 1) + dot(cut[wide:], w_kv, 0, 0)

    grad_normed_one, one_out = near_sum(one_terms)
    one_far = flip(one_out, "tp", 2)
    output_rows = (middle + (down + after(down_far, one_out))).astype(LOW)
    one_theirs = join_rows(table, after(one_near, one_out), cores_far[:, width // 2 :])
    up_kept = up_terms(0, 1, one_out)
    grad_gate = grad_gate.astype(jnp.float32)
    grad_normed_one = after(grad_normed_one, output_rows, up_kept, grad_gate, one_theirs) + one_far
    grad_in_norm, gain_one = norm_back(grad_normed_one, own_inputs, own(scale_one), norm1_gain)
    input_rows = grad_middle + grad_in_norm

    gains = jnp.stack([after(gain_one, input_rows), gain_two])
    gains_core = flip(gains, "tp", 1)
    up_mid = up_terms(half_count // 4, half_count // 2, gains)
    gains, gains_core, up_first = lax.optimization_barrier((gains, gains_core, up_first, up_mid))[:3]
    gains = gains + gains_core
    up_late, up_last = exchange_mid(
        lambda lo, hi, *late: up_mid if hi == half_count // 2 else up_terms(lo, hi, *late),
        up_first,
        rest_bits,
        gains,
    )
    both_theirs = after(both_theirs, up_last)
    proj_theirs = both_theirs[:units]
    branch_near = jnp.concatenate(
        [
            both_theirs[begin : begin + branch_send.shape[0]]
            for begin in range(units, both_theirs.shape[0], branch_send.shape[0])
        ],
        1,
    )
    branch_theirs = jnp.concatenate([branch_near, flip(branch_near, "tp", 1)], 0)
    up_second = flip(after(up_sent[:half], up_last), "dp", 2)
    gains, *down_late = lax.optimization_barrier((gains, *down_late, up_last))[:-1]
    gains = gains + flip(gains, "tp", 2)
    gains = pick_columns(table, "rest", gains) + flip(
        pick_columns(table, "rest_far", gains), "dp", 1
    )

    out_late, proj_late = lax.optimization_barrier((attended, proj_rows, up_last))[:2]

    def last_terms(lo, hi, *late):
        first, second = after(proj_late, *late), after(out_late, *late)
        return jnp.concatenate(
            [
                rest_terms(lo, hi, normed_one, one_theirs, first, proj_theirs, True),
                rest_terms(lo, hi, branch_all, branch_theirs, second, att_theirs, True),
            ],
            1,
        )

    def with_gains(terms, lo, hi, *others):
        extra = gains[:, lo * block : hi * block]
        for other, other_gains in others:
            terms = terms.astype(jnp.float32) + other
            extra = extra + other_gains
        columns = terms.shape[1]
        extra = jnp.pad(extra, ((0, 14), (0, -extra.shape[1] % columns)))[:, :columns]
        return jnp.concatenate([terms.astype(LOW), extra.astype(LOW)], 0)

    def split(message, count):
        rows = count * block
        return message[:rows], message[rows : rows + 2, :rows]

    quarter = half_count // 4
    sent = last_terms(half_count // 2, half_count)
    cut = quarter * block
    firsts = with_gains(sent[cut:], 3 * quarter, half_count)
    seconds = with_gains(sent[:cut], 2 * quarter, 3 * quarter)
    mids = [split(flip(firsts, "dp", 2), quarter)]
    last_second = split(flip(after(seconds, firsts), "dp", 2), quarter)
    up_late = [*up_late, up_second]
    proj_kept = rest_terms(0, 1, normed_one, one_theirs, after(proj_late, firsts), proj_theirs, True)
    out_kept = rest_terms(0, 1, branch_all, branch_theirs, after(out_late, firsts), att_theirs, True)
    down_kept = down_terms(0, 1, firsts)
    left = half_count // 2
    for b in rest_bits[1:]:
        count = left // 2
        terms = last_terms(count, left, firsts)
        terms, *up_late = lax.optimization_barrier((terms, *up_late, proj_kept, out_kept, down_kept))[
            :-3
        ]
        send = with_gains(
            terms, count, left, *((o[-count * block :], g[:, -count * block :]) for o, g in mids)
        )
        mids.append(split(flip(send, "dp", 1 << b), count))
        left = count
    down_second = flip(after(down_sent[:half], firsts), "dp", 1)

    def ending(kept, *others):
        kept = kept.astype(jnp.float32)
        for other in others:
            kept = kept + other[:block]
        return kept

    down_kept, down_second = lax.optimization_barrier((down_kept, down_second, send))[:2]
    grad_down = ending(down_kept, down_second, *down_late)
    grad_last = ending(
        jnp.concatenate([proj_kept, out_kept], 1), last_second[0], *(m[0] for m in mids[1:])
    )
    gains = gains[:, :block] + last_second[1][:, :block]
    for _, other in mids[1:]:
        gains = gains + other[:, :block]
    grad_up = ending(up_kept, *up_late)
    narrow = wide + 2 * size

    return (
        output_rows,
        input_rows,
        gains[0],
        grad_last[:, :wide],
        grad_last[:, wide : wide + size],
        grad_last[:, wide + size : narrow],
        grad_last[:, narrow:].T,
        gains[1],
        grad_gate,
        grad_up,
        grad_down.T,
    )


def solution(mesh):
    placed = (
        P("dp", None),
        P("dp"),
        P(),
        P(None, "tp"),
        P(None, "tp"),
        P(None, "tp"),
        P("tp", None),
        P(),
        P(None, "tp"),
        P(None, "tp"),
        P("tp", None),
        P("dp", None),
    )
    return jax.shard_map(
        shards,
        mesh=mesh,
        in_specs=placed,
        out_specs=(
            P(("dp", "tp"), None),
            P(("dp", "tp"), None),
            P("dp"),
            P("dp", "tp"),
            P("dp", "tp"),
            P("dp", "tp"),
            P("tp", "dp"),
            P("dp"),
            P("dp", "tp"),
            P("dp", "tp"),
            P("tp", "dp"),
        ),
        check_vma=False,
    )
```
